32 devices in a mesh: dp: 16 (over z, y, core), tensor: 2 (over x).
Axes of the slice: x: 2, y: 2, z: 4, core: 2. Of those that a mesh axis runs over, the one named last changes fastest.
Arguments:
- tokens: bfloat16 [8192, 768], P(('dp', 'tensor')), may hold values from -6 to 6
- positions: int32 [8192], P('dp'), may hold values from 0 to 1533, as said below
- span_sizes: int32 [16], P('dp'), may hold values from 32 to 128, as said below
- w_query: bfloat16 [768, 768], replicated, may hold values from -0.21875 to 0.21875
- b_query: bfloat16 [768], replicated, may hold values from -3 to 3
- w_key: bfloat16 [768, 768], replicated, may hold values from -0.21875 to 0.21875
- b_key: bfloat16 [768], replicated, may hold values from -3 to 3
- w_value: bfloat16 [768, 768], replicated, may hold values from -0.21875 to 0.21875
- b_value: bfloat16 [768], replicated, may hold values from -3 to 3
- w_out: bfloat16 [768, 768], replicated, may hold values from -1.75 to 1.75
- b_out: bfloat16 [768], replicated, may hold values from -3 to 3
- norm1_gain: bfloat16 [768], replicated, may hold values from 0.5 to 1.5
- norm1_bias: bfloat16 [768], replicated, may hold values from -3 to 3
- w_up: bfloat16 [768, 3072], P(None, 'tensor'), may hold values from -0.21875 to 0.21875
- b_up: bfloat16 [3072], P('tensor'), may hold values from -3 to 3
- w_down: bfloat16 [3072, 768], P('tensor'), may hold values from -0.109375 to 0.109375
- b_down: bfloat16 [768], replicated, may hold values from -3 to 3
- norm2_gain: bfloat16 [768], replicated, may hold values from 0.5 to 1.5
- norm2_bias: bfloat16 [768], replicated, may hold values from -3 to 3
- out_grad: bfloat16 [8192, 768], P(('dp', 'tensor')), may hold values from -6 to 6
Outputs:
- block_out: bfloat16 [8192, 768], P(('dp', 'tensor'))
- tokens_grad: float32 [8192, 768], P(('dp', 'tensor'))
- w_query_grad: float32 [768, 768], replicated
- b_query_grad: float32 [768], replicated
- w_key_grad: float32 [768, 768], replicated
- b_key_grad: float32 [768], replicated
- w_value_grad: float32 [768, 768], replicated
- b_value_grad: float32 [768], replicated
- w_out_grad: float32 [768, 768], replicated
- b_out_grad: float32 [768], replicated
- norm1_gain_grad: float32 [768], replicated
- norm1_bias_grad: float32 [768], replicated
- w_up_grad: float32 [768, 3072], P(None, 'tensor')
- b_up_grad: float32 [3072], P('tensor')
- w_down_grad: float32 [3072, 768], P('tensor')
- b_down_grad: float32 [768], replicated
- norm2_gain_grad: float32 [768], replicated
- norm2_bias_grad: float32 [768], replicated
The draws below stay inside these ranges and needn't reach their ends.
Inputs may be any that keep to these rules, and one draw needn't show every extreme that they name: Within each sequence of 512 rows the positions rise strictly and the first is 0; consecutive positions of a sequence differ by at most 5. The largest value is reached at the last row of some sequence. `span_sizes`: each span size is 32, 64 or 128; the smallest and the largest both occur.
All inputs are finite; a program needn't handle non-finite values.
Results may differ from the reference program's by a relative error of at most 0.018.
Values may be sent and summed in bfloat16 or wider, within the bound.
A program may use at most 320 MiB of HBM per device.

```python
import math
import jax
import jax.numpy as jnp
from jax import lax

D = 768
HEADS = 12
HD = 64
FF = 3072
SUBLEN = 32
GROUP = 512
LENGTH = 512
SEQS = 1
SEQUENCES = 16
TOKENS = 8192
N_DP = 16


def draw_positions(key, part):
    stride_key, jitter_key, chosen_key = jax.random.split(key, 3)
    stride = jax.random.randint(stride_key, (SEQUENCES, 1), 1, 4)
    chosen = jax.random.randint(chosen_key, (), 0, SEQUENCES)
    seq_index = jnp.arange(SEQUENCES, dtype=jnp.int32)[:, None]
    stride = jnp.where(seq_index == chosen, 3, stride)
    column = jnp.arange(LENGTH, dtype=jnp.int32)[None, :]
    jitter = jax.random.randint(jitter_key, (SEQUENCES, LENGTH), 0, 3) % stride
    jitter = jnp.where(column == 0, 0, jitter)
    jitter = jnp.where(column == LENGTH - 1, 0, jitter)
    rising = stride * column + jitter
    return rising.reshape(TOKENS).astype(jnp.int32)


def draw_span_sizes(key, part):
    levels_key, largest_key, smallest_key = jax.random.split(key, 3)
    levels = jax.random.randint(levels_key, (SEQUENCES,), 0, 3)
    span_values = jnp.where(levels == 0, SUBLEN, jnp.where(levels == 1, 2 * SUBLEN, 4 * SUBLEN))
    largest_at = jax.random.randint(largest_key, (), 0, SEQUENCES)
    smallest_at = (largest_at + 1 + jax.random.randint(smallest_key, (), 0, SEQUENCES - 1)) % SEQUENCES
    slot_index = jnp.arange(SEQUENCES, dtype=jnp.int32)
    span_values = jnp.where(slot_index == largest_at, 4 * SUBLEN, span_values)
    span_values = jnp.where(slot_index == smallest_at, SUBLEN, span_values)
    return span_values.astype(jnp.int32)


def steps_of(rng, shape, cuts, smallest, top_value):
    loudness = 1.0
    for position, parts in cuts:
        heights = jax.random.uniform(jax.random.fold_in(jax.random.fold_in(rng, 6), position), (parts,), jnp.float32, smallest / len(cuts), top_value / len(cuts))
        loudness = loudness * jnp.repeat(jnp.exp(heights), shape[position] // parts).reshape((-1,) + (1,) * (len(shape) - 1 - position))
    return loudness


def normal_values(rng, extent, scale, bound, cuts=(), kind=jnp.bfloat16):
    drawn = jax.random.normal(rng, extent, jnp.float32) * scale
    if len(cuts) > 0:
        drawn = steps_of(rng, extent, cuts, -0.22, 0.18) * drawn
    return jnp.clip(drawn, min=-bound, max=bound).astype(kind)


def setup_inputs(seed: int = 0) -> dict:
    arg_keys = jax.random.split(jax.random.key(seed), 21)
    tokens = normal_values(arg_keys[0], (TOKENS, D), 1.0, 6.0, ((0, 32),))
    positions = draw_positions(jax.random.fold_in(arg_keys[20], 71), 0)
    span_sizes = draw_span_sizes(jax.random.fold_in(arg_keys[20], 71), 0)
    w_query = normal_values(arg_keys[3], (D, D), D ** -0.5, 0.21875)
    b_query = normal_values(arg_keys[4], (D,), 0.5, 3.0)
    w_key = normal_values(arg_keys[5], (D, D), D ** -0.5, 0.21875)
    b_key = normal_values(arg_keys[6], (D,), 0.5, 3.0)
    w_value = normal_values(arg_keys[7], (D, D), D ** -0.5, 0.21875)
    b_value = normal_values(arg_keys[8], (D,), 0.2, 3.0)
    w_out = normal_values(arg_keys[9], (D, D), (D // 64) ** -0.5, 1.75)
    b_out = normal_values(arg_keys[10], (D,), 0.2, 3.0)
    norm1_gain = jnp.clip(1.0 + 0.1 * jax.random.normal(arg_keys[11], (D,), jnp.float32), 0.5, 1.5).astype(jnp.bfloat16)
    norm1_bias = normal_values(arg_keys[12], (D,), 0.2, 3.0)
    w_up = normal_values(arg_keys[13], (D, FF), D ** -0.5, 0.21875, ((1, 2),))
    b_up = normal_values(arg_keys[14], (FF,), 0.5, 3.0, ((0, 2),))
    w_down = normal_values(arg_keys[15], (FF, D), FF ** -0.5, 0.109375, ((0, 2),))
    b_down = normal_values(arg_keys[16], (D,), 0.2, 3.0)
    norm2_gain = jnp.clip(1.0 + 0.1 * jax.random.normal(arg_keys[17], (D,), jnp.float32), 0.5, 1.5).astype(jnp.bfloat16)
    norm2_bias = normal_values(arg_keys[18], (D,), 0.2, 3.0)
    out_grad = normal_values(arg_keys[19], (TOKENS, D), 1.0, 6.0, ((0, 32),))
    return dict(tokens=tokens, positions=positions, span_sizes=span_sizes, w_query=w_query, b_query=b_query, w_key=w_key, b_key=b_key, w_value=w_value, b_value=b_value, w_out=w_out, b_out=b_out, norm1_gain=norm1_gain, norm1_bias=norm1_bias, w_up=w_up, b_up=b_up, w_down=w_down, b_down=b_down, norm2_gain=norm2_gain, norm2_bias=norm2_bias, out_grad=out_grad)


@jax.custom_vjp
def low(v):
    return lax.optimization_barrier(v.astype(jnp.bfloat16)).astype(jnp.float32)

@jax.custom_vjp
def low_back(v):
    return v

def low_keep(v):
    return (low(v), None)

def low_pass(kept, grad):
    return (grad,)

def back_keep(v):
    return (v, None)

def back_low(kept, grad):
    return (low(grad),)
low.defvjp(low_keep, low_pass)
low_back.defvjp(back_keep, back_low)
highest = lax.Precision.HIGHEST

def matmul(left, right):
    return jnp.dot(left, right, precision=highest, preferred_element_type=jnp.float32)

def layer_norm(value, gain, shift):
    mean = lax.optimization_barrier(jnp.mean(value, axis=-1, keepdims=True))
    centred = value - mean
    spread = lax.optimization_barrier(jnp.mean(centred * centred, axis=-1, keepdims=True))
    return centred * lax.rsqrt(spread + 1e-05) * gain + shift

def reach_table(count, span):
    slot_index = jnp.arange(count, dtype=jnp.int32)
    final = (slot_index * SUBLEN // span + 1) * span // SUBLEN - 1
    return (slot_index[None, :] <= final[:, None]).astype(jnp.float32)

def attend(items):
    q_feat, k_feat, values, span = items
    count = LENGTH // SUBLEN
    q_sub = q_feat.reshape(count, SUBLEN, HEADS, 2 * HD)
    k_sub = k_feat.reshape(count, SUBLEN, HEADS, 2 * HD)
    v_sub = values.reshape(count, SUBLEN, HEADS, HD)
    blocks = jnp.einsum('tjhf,tjhd->thfd', k_sub, v_sub, precision=highest)
    k_total = lax.optimization_barrier(jnp.sum(k_sub, axis=1))
    reach = reach_table(count, span)
    state = low(jnp.einsum('st,thfd->shfd', reach, blocks, precision=highest))
    z_sum = jnp.einsum('st,thf->shf', reach, k_total, precision=highest)
    numer = jnp.einsum('sihf,shfd->sihd', q_sub, state, precision=highest)
    denom = jnp.einsum('sihf,shf->sih', q_sub, z_sum, precision=highest) + 1.0
    return (numer / denom[..., None]).reshape(LENGTH, HEADS * HD)

def group_forward(rows, weights, places, spans):
    w_query, b_query, w_key, b_key, w_value, b_value, w_out, b_out, gain_one, bias_one, w_up, b_up, w_down, b_down, gain_two, bias_two = weights
    angle = math.pi / 2 * places.astype(jnp.float32) / (3 * LENGTH)
    cosine = jnp.cos(angle)[:, None, None]
    sine = jnp.sin(angle)[:, None, None]
    query = low_back(matmul(rows, w_query)) + b_query
    key = low_back(matmul(rows, w_key)) + b_key
    value = low_back(matmul(rows, w_value)) + b_value
    relu_query = jax.nn.relu(query).reshape(GROUP, HEADS, HD)
    relu_key = jax.nn.relu(key).reshape(GROUP, HEADS, HD) * (1.0 / HD)
    q_feat = low(jnp.concatenate([relu_query * cosine, relu_query * sine], axis=-1))
    k_feat = low(jnp.concatenate([relu_key * cosine, relu_key * sine], axis=-1))
    v_low = low(value)
    shaped = (q_feat.reshape(SEQS, LENGTH, HEADS, 2 * HD), k_feat.reshape(SEQS, LENGTH, HEADS, 2 * HD), v_low.reshape(SEQS, LENGTH, HEADS, HD), spans)
    mixed = lax.map(jax.checkpoint(attend), shaped).reshape(GROUP, D)
    mixed = low(low_back(mixed))
    resid = rows + (low_back(matmul(mixed, w_out)) + b_out)
    hidden = layer_norm(resid, gain_one, bias_one)
    hidden_low = low(hidden)
    pre = low_back(matmul(hidden_low, w_up)) + b_up
    act = low(jax.nn.gelu(pre, approximate=False))
    summed = hidden + (low_back(matmul(act, w_down)) + b_down)
    return layer_norm(summed, gain_two, bias_two)

def reference(tokens, positions, span_sizes, w_query, b_query, w_key, b_key, w_value, b_value, w_out, b_out, norm1_gain, norm1_bias, w_up, b_up, w_down, b_down, norm2_gain, norm2_bias, out_grad):
    weights = tuple((item.astype(jnp.float32) for item in (w_query, b_query, w_key, b_key, w_value, b_value, w_out, b_out, norm1_gain, norm1_bias, w_up, b_up, w_down, b_down, norm2_gain, norm2_bias)))
    rows = tokens.astype(jnp.float32).reshape(N_DP, GROUP, D)
    places = positions.reshape(N_DP, GROUP)
    spans = span_sizes.reshape(N_DP, SEQS)
    cotangent = out_grad.astype(jnp.float32).reshape(N_DP, GROUP, D)

    def advance(total, items):
        block, place, span, grad = items
        result, pull = jax.vjp(lambda left, right: group_forward(left, right, place, span), block, weights)
        d_rows, d_weights = pull(grad)
        total = jax.tree.map(lambda first, second: first + second, total, d_weights)
        return (total, (result.astype(jnp.bfloat16), d_rows))
    start_total = jax.tree.map(jnp.zeros_like, weights)
    total, (results, d_rows) = lax.scan(advance, start_total, (rows, places, spans, cotangent))
    return (results.reshape(TOKENS, D), d_rows.reshape(TOKENS, D), total[0], total[1], total[2], total[3], total[4], total[5], total[6], total[7], total[8], total[9], total[10], total[11], total[12], total[13], total[14], total[15])
```

```python
import functools
import math

import jax
import jax.numpy as jnp
from jax import lax
from jax.experimental import pallas as pl
from jax.experimental.pallas import tpu as pltpu
from jax.sharding import PartitionSpec as P

HEADS = 12
HD = 64
SUBLEN = 32


highest = lax.Precision.HIGHEST
norm_eps = 1e-05


def norm_forward(value, gain, shift):
    mean = jnp.mean(value, axis=-1, keepdims=True)
    centred = value - mean
    scale = lax.rsqrt(jnp.mean(centred * centred, axis=-1, keepdims=True) + norm_eps)
    normal = centred * scale
    return (normal * gain + shift, normal, scale)


def norm_backward(grad, normal, scale, gain):
    along = grad * gain
    inner = (
        along
        - jnp.mean(along, axis=-1, keepdims=True)
        - normal * jnp.mean(along * normal, axis=-1, keepdims=True)
    )
    return (inner * scale, jnp.sum(grad * normal, axis=0), jnp.sum(grad, axis=0))


def gelu_slope(pre):
    normal_cdf = 0.5 * (1.0 + jax.scipy.special.erf(pre * (1.0 / math.sqrt(2.0))))
    return normal_cdf + pre * jnp.exp(-0.5 * pre * pre) * (1.0 / math.sqrt(2.0 * math.pi))


def reach_table(count, span):
    slot_index = jnp.arange(count, dtype=jnp.int32)
    final = (slot_index * SUBLEN // span + 1) * span // SUBLEN - 1
    return (slot_index[None, :] <= final[:, None]).astype(jnp.float32)


def features(rows, w_joint, b_joint, cosine, sine):
    length = rows.shape[0]
    width = rows.shape[1]
    proj = jnp.dot(rows, w_joint, preferred_element_type=jnp.float32) + b_joint
    relu_query = jax.nn.relu(proj[:, :width]).reshape(length, HEADS, HD)
    relu_key = jax.nn.relu(proj[:, width : 2 * width]).reshape(length, HEADS, HD) * (1.0 / HD)
    q_feat = jnp.concatenate([relu_query * cosine, relu_query * sine], axis=-1).astype(jnp.bfloat16)
    k_feat = jnp.concatenate([relu_key * cosine, relu_key * sine], axis=-1).astype(jnp.bfloat16)
    v_low = proj[:, 2 * width :].astype(jnp.bfloat16)
    return (q_feat, k_feat, v_low)


def local_blocks(k_feat, v_low):
    count = k_feat.shape[0] // SUBLEN
    k_sub = k_feat.reshape(count, SUBLEN, HEADS, 2 * HD)
    v_sub = v_low.reshape(count, SUBLEN, HEADS, HD)
    blocks = jnp.einsum("tjhf,tjhd->thfd", k_sub, v_sub, preferred_element_type=jnp.float32)
    k_total = jnp.sum(k_sub.astype(jnp.float32), axis=1)
    return (blocks, k_total)


def attend_core(q_feat, k_feat, v_low, blocks, k_total, reach, extra_blocks, extra_keys):
    count = q_feat.shape[0] // SUBLEN
    q_sub = q_feat.reshape(count, SUBLEN, HEADS, 2 * HD)
    k_sub = k_feat.reshape(count, SUBLEN, HEADS, 2 * HD)
    v_sub = v_low.reshape(count, SUBLEN, HEADS, HD)
    state_low = (
        jnp.einsum("st,thfd->shfd", reach, blocks, precision=highest) + extra_blocks
    ).astype(jnp.bfloat16)
    z_sum = jnp.einsum("st,thf->shf", reach, k_total, precision=highest) + extra_keys
    numer = jnp.einsum("sihf,shfd->sihd", q_sub, state_low, preferred_element_type=jnp.float32)
    denom = jnp.einsum("sihf,shf->sih", q_sub.astype(jnp.float32), z_sum, precision=highest) + 1.0
    return (q_sub, k_sub, v_sub, state_low, z_sum, numer, denom)


def back_first(parts, grad_mixed):
    q_sub, k_sub, v_sub, state_low, z_sum, numer, denom = parts
    count = q_sub.shape[0]
    grad_out = grad_mixed.reshape(count, SUBLEN, HEADS, HD).astype(jnp.float32)
    d_numer = grad_out / denom[..., None]
    d_denom = -jnp.sum(grad_out * numer, axis=-1) / (denom * denom)
    q_wide = q_sub.astype(jnp.float32)
    d_query = jnp.einsum(
        "sihd,shfd->sihf", d_numer, state_low.astype(jnp.float32), precision=highest
    )
    d_query = d_query + d_denom[..., None] * z_sum[:, None]
    d_state = jnp.einsum("sihf,sihd->shfd", q_wide, d_numer, precision=highest)
    d_zsum = jnp.einsum("sihf,sih->shf", q_wide, d_denom, precision=highest)
    return (d_query, d_state, d_zsum)


def back_second(parts, reach, d_state, d_zsum, later_blocks, later_keys):
    q_sub, k_sub, v_sub = (parts[0], parts[1], parts[2])
    d_blocks = jnp.einsum("st,shfd->thfd", reach, d_state, precision=highest) + later_blocks
    d_ktotal = jnp.einsum("st,shf->thf", reach, d_zsum, precision=highest) + later_keys
    d_key = (
        jnp.einsum("thfd,tjhd->tjhf", d_blocks, v_sub.astype(jnp.float32), precision=highest)
        + d_ktotal[:, None]
    )
    d_value = jnp.einsum("thfd,tjhf->tjhd", d_blocks, k_sub.astype(jnp.float32), precision=highest)
    return (d_key, d_value)


def feature_grads(q_feat, k_feat, d_qf, d_kf, d_val, cos_part, sin_part):
    size = q_feat.shape[0]
    d_qf = d_qf.reshape(size, HEADS, 2 * HD)
    d_kf = d_kf.reshape(size, HEADS, 2 * HD)
    d_query = jnp.where(
        q_feat[..., :HD] > 0, d_qf[..., :HD] * cos_part + d_qf[..., HD:] * sin_part, 0.0
    )
    d_key = jnp.where(
        k_feat[..., :HD] > 0,
        (d_kf[..., :HD] * cos_part + d_kf[..., HD:] * sin_part) * (1.0 / HD),
        0.0,
    )
    return jnp.concatenate(
        [
            d_query.reshape(size, HEADS * HD),
            d_key.reshape(size, HEADS * HD),
            d_val.reshape(size, HEADS * HD),
        ],
        axis=1,
    )


def general_device(
    tokens,
    positions,
    span_sizes,
    w_query,
    b_query,
    w_key,
    b_key,
    w_value,
    b_value,
    w_out,
    b_out,
    norm1_gain,
    norm1_bias,
    w_up,
    b_up,
    w_down,
    b_down,
    norm2_gain,
    norm2_bias,
    out_grad,
):
    rank = lax.axis_index("tensor")
    tensor_count = lax.axis_size("tensor")
    own = tokens.shape[0]
    width = tokens.shape[1]
    seqs = span_sizes.shape[0]
    group = own * tensor_count
    length = group // seqs
    start = rank * own
    w_joint = jnp.concatenate([w_query, w_key, w_value], axis=1)
    b_joint = jnp.concatenate([b_query, b_key, b_value]).astype(jnp.float32)
    gain_one = norm1_gain.astype(jnp.float32)
    gain_two = norm2_gain.astype(jnp.float32)
    gathered = lax.all_gather(tokens, "tensor", axis=0, tiled=True)
    angle = math.pi / 2 * positions.astype(jnp.float32) / (3 * length)
    cosine = jnp.cos(angle).reshape(seqs, length, 1, 1)
    sine = jnp.sin(angle).reshape(seqs, length, 1, 1)

    def seq_forward(items):
        rows, cos_part, sin_part, span = items
        q_feat, k_feat, v_low = features(rows, w_joint, b_joint, cos_part, sin_part)
        blocks_seq, ktot_seq = local_blocks(k_feat, v_low)
        parts = attend_core(
            q_feat,
            k_feat,
            v_low,
            blocks_seq,
            ktot_seq,
            reach_table(q_feat.shape[0] // SUBLEN, span),
            0.0,
            0.0,
        )
        mixed_seq = (
            (parts[5] / parts[6][..., None]).reshape(rows.shape[0], width).astype(jnp.bfloat16)
        )
        return (mixed_seq, q_feat, k_feat, v_low)

    mixed, q_all, k_all, v_all = lax.map(
        seq_forward, (gathered.reshape(seqs, length, width), cosine, sine, span_sizes)
    )
    mixed = mixed.reshape(group, width)
    mixed_own = lax.dynamic_slice_in_dim(mixed, start, own, 0)
    resid = (
        tokens.astype(jnp.float32)
        + jnp.dot(mixed_own, w_out, preferred_element_type=jnp.float32)
        + b_out.astype(jnp.float32)
    )
    hidden, normal_one, scale_one = norm_forward(resid, gain_one, norm1_bias.astype(jnp.float32))
    hidden_low = hidden.astype(jnp.bfloat16)
    rows_in = lax.all_gather(hidden_low, "tensor", axis=0, tiled=True)
    pre = jnp.dot(rows_in, w_up, preferred_element_type=jnp.float32) + b_up.astype(jnp.float32)
    act_low = jax.nn.gelu(pre, approximate=False).astype(jnp.bfloat16)
    branch = lax.psum_scatter(
        jnp.dot(act_low, w_down, preferred_element_type=jnp.float32),
        "tensor",
        scatter_dimension=0,
        tiled=True,
    )
    summed = hidden + branch + b_down.astype(jnp.float32)
    result, normal_two, scale_two = norm_forward(summed, gain_two, norm2_bias.astype(jnp.float32))
    d_sum, d_gain_two, d_bias_two = norm_backward(
        out_grad.astype(jnp.float32), normal_two, scale_two, gain_two
    )
    d_bdown = jnp.sum(d_sum, axis=0)
    d_sum_low = d_sum.astype(jnp.bfloat16)
    rows_grad = lax.all_gather(d_sum_low, "tensor", axis=0, tiled=True)
    g_down = jnp.dot(act_low.T, rows_grad, preferred_element_type=jnp.float32)
    d_pre = jnp.dot(rows_grad, w_down.T, preferred_element_type=jnp.float32) * gelu_slope(pre)
    g_upbias = jnp.sum(d_pre, axis=0)
    d_pre_low = d_pre.astype(jnp.bfloat16)
    g_up = jnp.dot(rows_in.T, d_pre_low, preferred_element_type=jnp.float32)
    d_hidden = lax.psum_scatter(
        jnp.dot(d_pre_low, w_up.T, preferred_element_type=jnp.float32),
        "tensor",
        scatter_dimension=0,
        tiled=True,
    )
    g_up, g_upbias, g_down = (
        lax.psum(g_up.astype(jnp.bfloat16), "dp").astype(jnp.float32),
        lax.psum(g_upbias.astype(jnp.bfloat16), "dp").astype(jnp.float32),
        lax.psum(g_down.astype(jnp.bfloat16), "dp").astype(jnp.float32),
    )
    d_hidden = d_hidden + d_sum
    d_resid, d_gain_one, d_bias_one = norm_backward(d_hidden, normal_one, scale_one, gain_one)
    d_bout = jnp.sum(d_resid, axis=0)
    d_gain_one, d_bias_one, d_gain_two, d_bias_two, d_bout, d_bdown = lax.psum(
        (d_gain_one, d_bias_one, d_gain_two, d_bias_two, d_bout, d_bdown), ("dp", "tensor")
    )
    d_resid_low = d_resid.astype(jnp.bfloat16)
    rows_back = lax.all_gather(d_resid_low, "tensor", axis=0, tiled=True)
    g_out = jnp.dot(mixed.T, rows_back, preferred_element_type=jnp.float32)
    d_mixed = jnp.dot(rows_back, w_out.T, preferred_element_type=jnp.float32).astype(jnp.bfloat16)

    def seq_backward(items):
        q_feat, k_feat, v_low, cos_part, sin_part, span, grad_mixed = items
        blocks_seq, ktot_seq = local_blocks(k_feat, v_low)
        reach = reach_table(q_feat.shape[0] // SUBLEN, span)
        parts = attend_core(q_feat, k_feat, v_low, blocks_seq, ktot_seq, reach, 0.0, 0.0)
        d_qf, d_state, d_zsum = back_first(parts, grad_mixed)
        d_kf, d_val = back_second(parts, reach, d_state, d_zsum, 0.0, 0.0)
        joint = feature_grads(q_feat, k_feat, d_qf, d_kf, d_val, cos_part, sin_part)
        return (joint.astype(jnp.bfloat16), jnp.sum(joint, axis=0))

    d_joint, d_jbias = lax.map(
        seq_backward,
        (q_all, k_all, v_all, cosine, sine, span_sizes, d_mixed.reshape(seqs, length, width)),
    )
    d_joint = d_joint.reshape(group, 3 * width)
    d_jbias = jnp.sum(d_jbias, axis=0)
    g_joint = jnp.dot(gathered.T, d_joint, preferred_element_type=jnp.float32)
    d_joint_own = lax.dynamic_slice_in_dim(d_joint, start, own, 0)
    d_tokens = d_resid + jnp.dot(d_joint_own, w_joint.T, preferred_element_type=jnp.float32)
    g_joint, g_out, d_jbias = lax.psum((g_joint, g_out, d_jbias), "dp")
    return (
        result.astype(jnp.bfloat16),
        d_tokens,
        g_joint[:, :width],
        d_jbias[:width],
        g_joint[:, width : 2 * width],
        d_jbias[width : 2 * width],
        g_joint[:, 2 * width :],
        d_jbias[2 * width :],
        g_out,
        d_bout,
        d_gain_one,
        d_bias_one,
        g_up,
        g_upbias,
        g_down,
        d_bdown,
        d_gain_two,
        d_bias_two,
    )


f32 = jnp.float32
bf16 = jnp.bfloat16
MESH = pl.DeviceIdType.MESH
LANES = 2 * HD
TILE = 256
ROWBLOCK = 32


def tile_at(index, size):
    return pl.ds(pl.multiple_of(index * size, size), size)


def contract(left, right, left_dim, right_dim, precision=None):
    return lax.dot_general(
        left,
        right,
        (((left_dim,), (right_dim,)), ((), ())),
        precision=precision,
        preferred_element_type=f32,
    )


def mm(left, right):
    return contract(left, right, 1, 0)


def mm_nt(left, right):
    return contract(left, right, 1, 1)


def mm_tn(left, right):
    return contract(left, right, 0, 0)


def head_masks():
    lane = lax.broadcasted_iota(jnp.int32, (1, LANES), 1)
    first = (lane < HD).astype(f32)
    return first, 1.0 - first


def pair_mask():
    row = lax.broadcasted_iota(jnp.int32, (LANES, LANES), 0)
    col = lax.broadcasted_iota(jnp.int32, (LANES, LANES), 1)
    return ((row < HD) == (col < HD)).astype(f32)


def first_row(block, which):
    row = lax.broadcasted_iota(jnp.int32, block.shape, 0)
    return jnp.where(row == which, block, 0.0)


def column_of(block, which):
    return contract(first_row(block, which), jnp.ones((8, LANES), f32), 0, 0, highest)


def squeeze_pair(square):
    return square[:HD] + square[HD:]


def spread_pair(half, mask):
    return jnp.concatenate([half, half], axis=0).astype(f32) * mask


def fold8(value):
    total = value[0:8]
    for start in range(8, value.shape[0], 8):
        total = total + value[start : start + 8]
    return total


def angle_tables(trig, span, cosb, sinb, ctab):
    rows = cosb.shape[0]
    block = trig[...]
    cosb[...] = column_of(block, 0)
    sinb[...] = column_of(block, 1)
    both = contract(block, block, 0, 0, highest)
    row = lax.broadcasted_iota(jnp.int32, (rows, rows), 0)
    col = lax.broadcasted_iota(jnp.int32, (rows, rows), 1)
    seen = col <= (row | (span[0, 0] - 1))
    ctab[...] = jnp.where(seen, both * (1.0 / HD), 0.0)


def peer_copy(src, dst, sems, slot, device):
    return pltpu.make_async_remote_copy(
        src_ref=src,
        dst_ref=dst,
        send_sem=sems[0].at[slot],
        recv_sem=sems[1].at[slot],
        device_id=device,
        device_id_type=MESH,
    )


def meet(devices):
    barrier = pltpu.get_barrier_semaphore()
    for device in devices:
        pl.semaphore_signal(barrier, inc=1, device_id=device, device_id_type=MESH)
    pl.semaphore_wait(barrier, len(devices))


def front_kernel(
    tok, trig, span, vec, wq, wk, wv, wo, wup, wdn, og,
    res_o, small_o, gff_o, dhs_o, dho_o, mixb, mixf, inv, rq, rk, vv, nrm, scl, st_o, z_o,
    hbuf, act, slope, dbuf, dpre, hid, tsend, trecv, zsend, zrecv, bsend, brecv,
    numer, denom, ctab, cosb, sinb, acc, bup, send, recv,
):
    sems = (send, recv)
    rows, width = tok.shape
    units = wup.shape[1]
    pairs = width // LANES
    tiles = width // TILE
    rank = lax.axis_index("tensor")
    peer = (lax.axis_index("dp"), 1 - rank)
    late = rank.astype(f32)
    own, other = pl.ds(0, rows), pl.ds(rows, rows)
    meet([peer])

    for which, (weight, target) in enumerate(((wq, rq), (wk, rk), (wv, vv))):

        @pl.loop(0, tiles)
        def _(j, which=which, weight=weight, target=target):
            cols = tile_at(j, TILE)
            y = mm(tok[...], weight[:, cols]) + vec[which : which + 1, cols]
            if which < 2:
                y = jnp.maximum(y, 0.0)
            target[:, cols] = y.astype(bf16)

    angle_tables(trig, span, cosb, sinb, ctab)
    diag = pair_mask()
    first, second = head_masks()
    first_low, second_low = first.astype(bf16), second.astype(bf16)

    @pl.loop(0, pairs)
    def _(p):
        lanes = tile_at(p, LANES)
        k = rk[:, lanes].astype(f32) * (1.0 / HD)
        v = vv[:, lanes]
        kc, ks = (k * cosb[...]).astype(bf16), (k * sinb[...]).astype(bf16)
        tsend[p, 0] = squeeze_pair(mm_tn(kc, v) * diag).astype(bf16)
        tsend[p, 1] = squeeze_pair(mm_tn(ks, v) * diag).astype(bf16)
        sum_c = jnp.sum(kc.astype(f32), axis=0, keepdims=True)
        sum_s = jnp.sum(ks.astype(f32), axis=0, keepdims=True)
        row = lax.broadcasted_iota(jnp.int32, (8, LANES), 0)
        zsend[p] = jnp.where(row == 0, sum_c, jnp.where(row == 1, sum_s, 0.0))

    state_copy = peer_copy(tsend, trecv, sems, 0, peer)
    key_copy = peer_copy(zsend, zrecv, sems, 1, peer)
    state_copy.start()
    key_copy.start()

    @pl.loop(0, pairs)
    def _(p):
        lanes = tile_at(p, LANES)
        q, k, v = rq[:, lanes], rk[:, lanes], vv[:, lanes]
        parts = []
        for mask, rest in ((first_low, second_low), (second_low, first_low)):
            score = mm_nt(q * mask, k)
            prob = (score * ctab[...]).astype(bf16)
            parts.append(mm(prob, v * mask + rest))
        numer[:, lanes] = parts[0] * first + parts[1] * second
        denom[:, lanes] = pltpu.roll(parts[0] * second + parts[1] * first, HD, 1)

    state_copy.wait()
    key_copy.wait()

    @pl.loop(0, pairs)
    def _(p):
        lanes = tile_at(p, LANES)
        q = rq[:, lanes].astype(f32)
        qc, qs = (q * cosb[...]).astype(bf16), (q * sinb[...]).astype(bf16)
        st_o[p] = (trecv[p].astype(f32) * late).astype(bf16)
        zblock = zrecv[p] * late
        z_o[p] = zblock
        num, den = numer[:, lanes], denom[:, lanes] + 1.0
        for part, feat in ((0, qc), (1, qs)):
            num += mm(feat, spread_pair(st_o[p, part], diag).astype(bf16))
            den += mm(feat, (column_of(zblock, part) * diag).astype(bf16))
        reciprocal = 1.0 / den
        mix = num * reciprocal
        inv[:, lanes] = reciprocal
        mixf[:, lanes] = mix
        mixb[:, lanes] = mix.astype(bf16)

    @pl.loop(0, tiles)
    def _(j):
        cols = tile_at(j, TILE)
        hid[:, cols] = tok[:, cols].astype(f32) + mm(mixb[...], wo[:, cols]) + vec[3:4, cols]

    @pl.loop(0, rows // ROWBLOCK)
    def _(i):
        at = tile_at(i, ROWBLOCK)
        value = hid[at, :]
        centred = value - jnp.mean(value, axis=-1, keepdims=True)
        scale = lax.rsqrt(jnp.mean(centred * centred, axis=-1, keepdims=True) + norm_eps)
        normal = centred * scale
        hidden = normal * vec[4:5, :] + vec[5:6, :]
        nrm[at, :] = normal
        scl[at, :] = jnp.broadcast_to(scale, (ROWBLOCK, LANES))
        hid[at, :] = hidden
        hbuf[at, :] = hidden.astype(bf16)

    hidden_copy = peer_copy(hbuf.at[own], hbuf.at[other], sems, 2, peer)
    hidden_copy.start()

    def raise_rows(part):
        for half in range(units // width):

            @pl.loop(0, tiles)
            def _(j, half=half):
                cols = tile_at(half * tiles + j, TILE)
                pre = mm(hbuf[part, :], wup[:, cols]) + vec[9 + half : 10 + half, tile_at(j, TILE)]
                cdf = 0.5 * (1.0 + lax.erf(pre * (1.0 / math.sqrt(2.0))))
                act[part, cols] = (pre * cdf).astype(bf16)
                slope[part, cols] = cdf + pre * jnp.exp(-0.5 * pre * pre) * (
                    1.0 / math.sqrt(2.0 * math.pi)
                )

    raise_rows(own)
    hidden_copy.wait()
    raise_rows(other)

    @pl.loop(0, tiles)
    def _(j):
        cols = tile_at(j, TILE)
        bsend[:, cols] = mm(act[other, :], wdn[:, cols]).astype(bf16)

    branch_copy = peer_copy(bsend, brecv, sems, 3, peer)
    branch_copy.start()

    @pl.loop(0, tiles)
    def _(j):
        cols = tile_at(j, TILE)
        hid[:, cols] += mm(act[own, :], wdn[:, cols]) + vec[6:7, cols]

    acc[...] = jnp.zeros_like(acc)
    branch_copy.wait()

    @pl.loop(0, rows // ROWBLOCK)
    def _(i):
        at = tile_at(i, ROWBLOCK)
        value = hid[at, :] + brecv[at, :].astype(f32)
        centred = value - jnp.mean(value, axis=-1, keepdims=True)
        scale = lax.rsqrt(jnp.mean(centred * centred, axis=-1, keepdims=True) + norm_eps)
        normal = centred * scale
        res_o[at, :] = (normal * vec[7:8, :] + vec[8:9, :]).astype(bf16)
        grad = og[at, :].astype(f32)
        along = grad * vec[7:8, :]
        inner = (
            along
            - jnp.mean(along, axis=-1, keepdims=True)
            - normal * jnp.mean(along * normal, axis=-1, keepdims=True)
        ) * scale
        dho_o[at, :] = inner
        dbuf[at, :] = inner.astype(bf16)
        acc[0:8, :] += fold8(grad * normal)
        acc[8:16, :] += fold8(grad)
        acc[16:24, :] += fold8(inner)

    grad_copy = peer_copy(dbuf.at[own], dbuf.at[other], sems, 4, peer)
    grad_copy.start()

    small_o[...] = jnp.zeros_like(small_o)
    for slot in range(3):
        small_o[3 + slot : 4 + slot, :] = jnp.sum(
            acc[8 * slot : 8 * slot + 8, :], axis=0, keepdims=True
        )
    bup[...] = jnp.zeros_like(bup)

    def lower_rows(part):
        @pl.loop(0, units // TILE)
        def _(j):
            cols = tile_at(j, TILE)
            d_pre = mm_nt(dbuf[part, :], wdn[cols, :]) * slope[part, cols]
            bup[:, cols] += fold8(d_pre)
            dpre[part, cols] = d_pre.astype(bf16)

    lower_rows(own)
    grad_copy.wait()
    lower_rows(other)

    @pl.loop(0, tiles)
    def _(j):
        cols = tile_at(j, TILE)
        dhs_o[:, cols] = mm_nt(dpre[other, :], wup[cols, :]).astype(bf16)
        dho_o[:, cols] += mm_nt(dpre[own, :], wup[cols, :])

    for half in range(units // width):
        line = jnp.sum(bup[:, half * width : (half + 1) * width], axis=0, keepdims=True)
        small_o[9 + half : 10 + half, :] = line * (1.0 - late)
        small_o[9 + units // width + half : 10 + units // width + half, :] = line * late

    @pl.loop(0, units // TILE)
    def _(j):
        cols = tile_at(j, TILE)
        gff_o[cols, :] = mm_tn(act[:, cols], dbuf[...]).astype(bf16)

    for half in range(units // width):

        @pl.loop(0, tiles)
        def _(j, half=half):
            gff_o[pl.ds(units + half * width, width), tile_at(j, TILE)] = mm_tn(
                hbuf[...], dpre[:, tile_at(half * tiles + j, TILE)]
            ).astype(bf16)


def back_kernel(
    tok, trig, span, vec, wq, wk, wv, wo,
    dhs, dho, mixb, mixf, inv, rq, rk, vv, nrm, scl, st, z, small_in,
    dtok_o, ga_o, small_o,
    dhr, dres, dlow, dn, xs, dsend, drecv, dzs, dzr, dq, dk, dv, dql, dkl, dvl,
    ctab, cosb, sinb, acc, send, recv,
):
    sems = (send, recv)
    rows, width = tok.shape
    pairs = width // LANES
    tiles = width // TILE
    rank = lax.axis_index("tensor")
    peer = (lax.axis_index("dp"), 1 - rank)
    early = 1.0 - rank.astype(f32)
    meet([peer])
    hidden_copy = peer_copy(dhs, dhr, sems, 0, peer)
    hidden_copy.start()
    angle_tables(trig, span, cosb, sinb, ctab)
    diag = pair_mask()
    first, second = head_masks()
    first_low, second_low = first.astype(bf16), second.astype(bf16)
    diag_low = diag.astype(bf16)
    acc[...] = jnp.zeros_like(acc)
    small_o[...] = small_in[...]
    hidden_copy.wait()

    @pl.loop(0, rows // ROWBLOCK)
    def _(i):
        at = tile_at(i, ROWBLOCK)
        grad = dho[at, :] + dhr[at, :].astype(f32)
        normal = nrm[at, :]
        along = grad * vec[4:5, :]
        inner = (
            along
            - jnp.mean(along, axis=-1, keepdims=True)
            - normal * jnp.mean(along * normal, axis=-1, keepdims=True)
        ) * scl[at, 0:1]
        dres[at, :] = inner
        dlow[at, :] = inner.astype(bf16)
        acc[0:8, :] += fold8(grad * normal)
        acc[8:16, :] += fold8(grad)
        acc[16:24, :] += fold8(inner)

    for slot in range(3):
        small_o[slot : slot + 1, :] = jnp.sum(
            acc[8 * slot : 8 * slot + 8, :], axis=0, keepdims=True
        )

    @pl.loop(0, tiles)
    def _(j):
        cols = tile_at(j, TILE)
        d_mixed = mm_nt(dlow[...], wo[cols, :]).astype(bf16).astype(f32)
        d_numer = (d_mixed * inv[:, cols]).astype(bf16)
        dn[:, cols] = d_numer
        xs[:, cols] = (d_numer.astype(f32) * mixf[:, cols]).astype(bf16)

    @pl.loop(0, pairs)
    def _(p):
        lanes = tile_at(p, LANES)
        q = rq[:, lanes].astype(f32)
        qc, qs = (q * cosb[...]).astype(bf16), (q * sinb[...]).astype(bf16)
        d_numer = dn[:, lanes]
        dsend[p, 0] = squeeze_pair(mm_tn(qc, d_numer) * diag).astype(bf16)
        dsend[p, 1] = squeeze_pair(mm_tn(qs, d_numer) * diag).astype(bf16)
        across = mm(xs[:, lanes], diag_low)
        sum_c = jnp.sum(qc.astype(f32) * across, axis=0, keepdims=True)
        sum_s = jnp.sum(qs.astype(f32) * across, axis=0, keepdims=True)
        row = lax.broadcasted_iota(jnp.int32, (8, LANES), 0)
        dzs[p] = -jnp.where(row == 0, sum_c, jnp.where(row == 1, sum_s, 0.0))

    state_copy = peer_copy(dsend, drecv, sems, 1, peer)
    key_copy = peer_copy(dzs, dzr, sems, 2, peer)
    state_copy.start()
    key_copy.start()

    @pl.loop(0, tiles)
    def _(j):
        cols = tile_at(j, TILE)
        ga_o[tile_at(3 * tiles + j, TILE), :] = mm_tn(mixb[:, cols], dlow[...]).astype(bf16)

    @pl.loop(0, pairs)
    def _(p):
        lanes = tile_at(p, LANES)
        q, k, v = rq[:, lanes], rk[:, lanes], vv[:, lanes]
        d_numer = dn[:, lanes]
        turned = -pltpu.roll(xs[:, lanes].astype(f32), HD, 1)
        turned = turned.astype(bf16)
        sum_q = sum_k = sum_v = 0.0
        for mask, rest in ((first_low, second_low), (second_low, first_low)):
            q_head, k_head, d_head = q * mask, k * mask, d_numer * mask
            table = ctab[...]
            prob = (mm_nt(q_head, k) * table).astype(bf16)
            d_prob = mm_nt(d_head + turned * rest, v * mask + rest)
            d_score = (d_prob * table).astype(bf16)
            sum_v += mm_tn(prob, d_head)
            sum_q += mm(d_score, k_head)
            sum_k += mm_tn(d_score, q_head)
        dq[:, lanes] = sum_q
        dk[:, lanes] = sum_k
        dv[:, lanes] = sum_v

    state_copy.wait()
    key_copy.wait()

    @pl.loop(0, pairs)
    def _(p):
        lanes = tile_at(p, LANES)
        q, v = rq[:, lanes].astype(f32), vv[:, lanes]
        k = rk[:, lanes].astype(f32)
        d_numer, x = dn[:, lanes], xs[:, lanes]
        sum_q, sum_k, sum_v = dq[:, lanes], dk[:, lanes], dv[:, lanes]
        zblock, dzblock = z[p], dzr[p] * early
        for part, wave in ((0, cosb[...]), (1, sinb[...])):
            state = spread_pair(st[p, part], diag).astype(bf16)
            zmat = (column_of(zblock, part) * diag).astype(bf16)
            sum_q += wave * (mm_nt(d_numer, state) - mm_nt(x, zmat))
            d_state = (spread_pair(drecv[p, part], diag) * early).astype(bf16)
            sum_k += wave * (mm_nt(v, d_state) + dzblock[part : part + 1, :]) * (1.0 / HD)
            sum_v += mm((k * wave * (1.0 / HD)).astype(bf16), d_state)
        sum_q = jnp.where(q > 0, sum_q, 0.0)
        sum_k = jnp.where(k > 0, sum_k, 0.0)
        dql[:, lanes] = sum_q.astype(bf16)
        dkl[:, lanes] = sum_k.astype(bf16)
        dvl[:, lanes] = sum_v.astype(bf16)
        for slot, value in ((6, sum_q), (7, sum_k), (8, sum_v)):
            small_o[slot : slot + 1, lanes] = jnp.sum(value, axis=0, keepdims=True)

    for which, source in enumerate((dql, dkl, dvl)):

        @pl.loop(0, tiles)
        def _(j, which=which, source=source):
            ga_o[tile_at(which * tiles + j, TILE), :] = mm_tn(
                tok[:, tile_at(j, TILE)], source[...]
            ).astype(bf16)

    @pl.loop(0, tiles)
    def _(j):
        cols = tile_at(j, TILE)
        dtok_o[:, cols] = (
            dres[:, cols]
            + mm_nt(dql[...], wq[cols, :])
            + mm_nt(dkl[...], wk[cols, :])
            + mm_nt(dvl[...], wv[cols, :])
        )


def in_vmem(count):
    return [pl.BlockSpec(memory_space=pltpu.VMEM)] * count


def shaped(*items):
    return tuple(jax.ShapeDtypeStruct(shape, kind) for shape, kind in items)


def pair_device(
    tokens,
    positions,
    span_sizes,
    w_query,
    b_query,
    w_key,
    b_key,
    w_value,
    b_value,
    w_out,
    b_out,
    norm1_gain,
    norm1_bias,
    w_up,
    b_up,
    w_down,
    b_down,
    norm2_gain,
    norm2_bias,
    out_grad,
):
    rank = lax.axis_index("tensor")
    rows, width = tokens.shape
    units = w_up.shape[1]
    pairs = width // LANES
    length = positions.shape[0]
    places = lax.dynamic_slice_in_dim(positions, rank * rows, rows, 0)
    angle = math.pi / 2 * places.astype(f32) / (3 * length)
    line = lax.broadcasted_iota(jnp.int32, (8, rows), 0)
    trig = jnp.where(
        line == 0, jnp.cos(angle)[None], jnp.where(line == 1, jnp.sin(angle)[None], 0.0)
    )
    span = span_sizes.reshape(1, 1)
    vectors = [
        b_query, b_key, b_value, b_out, norm1_gain, norm1_bias, b_down, norm2_gain, norm2_bias, b_up,
    ]
    vec = jnp.concatenate(vectors).astype(f32).reshape(-1, width)
    vec = jnp.pad(vec, ((0, -vec.shape[0] % 8), (0, 0)))
    smalls = 9 + 2 * (units // width)
    smalls += -smalls % 8
    state = (pairs, 2, HD, LANES)
    zrows = (pairs, 8, LANES)
    wide, low, both = ((rows, width), f32), ((rows, width), bf16), (2 * rows, width)
    front_outs = shaped(
        low, ((smalls, width), f32), ((2 * units, width), bf16), low, wide, low, wide, wide,
        low, low, low, wide, ((rows, LANES), f32), (state, bf16), (zrows, f32),
    )
    tables = [
        pltpu.VMEM((rows, rows), f32), pltpu.VMEM((rows, LANES), f32), pltpu.VMEM((rows, LANES), f32),
    ]
    smem = [pl.BlockSpec(memory_space=pltpu.SMEM)]
    (
        result, small, gff, dhs, dho, mixb, mixf, inv, rq, rk, vv, nrm, scl, st, z,
    ) = pl.pallas_call(
        front_kernel,
        out_shape=front_outs,
        in_specs=in_vmem(2) + smem + in_vmem(8),
        out_specs=tuple(in_vmem(len(front_outs))),
        scratch_shapes=[
            pltpu.VMEM(both, bf16),
            pltpu.VMEM((2 * rows, units), bf16),
            pltpu.VMEM((2 * rows, units), f32),
            pltpu.VMEM(both, bf16),
            pltpu.VMEM((2 * rows, units), bf16),
            pltpu.VMEM((rows, width), f32),
            pltpu.VMEM(state, bf16),
            pltpu.VMEM(state, bf16),
            pltpu.VMEM(zrows, f32),
            pltpu.VMEM(zrows, f32),
            pltpu.VMEM((rows, width), bf16),
            pltpu.VMEM((rows, width), bf16),
            pltpu.VMEM((rows, width), f32),
            pltpu.VMEM((rows, width), f32),
            *tables,
            pltpu.VMEM((24, width), f32),
            pltpu.VMEM((8, units), f32),
            pltpu.SemaphoreType.DMA((5,)),
            pltpu.SemaphoreType.DMA((5,)),
        ],
        compiler_params=pltpu.CompilerParams(
            collective_id=0, has_side_effects=True, vmem_limit_bytes=60 << 20
        ),
        name="front",
    )(tokens, trig, span, vec, w_query, w_key, w_value, w_out, w_up, w_down, out_grad)
    back_outs = shaped(wide, ((4 * width, width), bf16), ((smalls, width), f32))
    d_tokens, ga, small = pl.pallas_call(
        back_kernel,
        out_shape=back_outs,
        in_specs=in_vmem(2) + smem + in_vmem(18),
        out_specs=tuple(in_vmem(len(back_outs))),
        scratch_shapes=[
            pltpu.VMEM((rows, width), bf16),
            pltpu.VMEM((rows, width), f32),
            pltpu.VMEM((rows, width), bf16),
            pltpu.VMEM((rows, width), bf16),
            pltpu.VMEM((rows, width), bf16),
            pltpu.VMEM(state, bf16),
            pltpu.VMEM(state, bf16),
            pltpu.VMEM(zrows, f32),
            pltpu.VMEM(zrows, f32),
            pltpu.VMEM((rows, width), f32),
            pltpu.VMEM((rows, width), f32),
            pltpu.VMEM((rows, width), f32),
            pltpu.VMEM((rows, width), bf16),
            pltpu.VMEM((rows, width), bf16),
            pltpu.VMEM((rows, width), bf16),
            *tables,
            pltpu.VMEM((24, width), f32),
            pltpu.SemaphoreType.DMA((3,)),
            pltpu.SemaphoreType.DMA((3,)),
        ],
        compiler_params=pltpu.CompilerParams(
            collective_id=1, has_side_effects=True, vmem_limit_bytes=60 << 20
        ),
        name="back",
    )(
        tokens, trig, span, vec, w_query, w_key, w_value, w_out,
        dhs, dho, mixb, mixf, inv, rq, rk, vv, nrm, scl, st, z, small,
    )
    gff = lax.psum(gff, "dp")
    ga = lax.psum(ga, ("dp", "tensor"))
    small = lax.psum(small, ("dp", "tensor"))
    halves = units // width
    g_up = jnp.concatenate(
        [gff[units + h * width : units + (h + 1) * width] for h in range(halves)], axis=1
    )
    g_upbias = lax.dynamic_slice_in_dim(small, 9 + rank * halves, halves, 0).reshape(units)
    return (
        result,
        d_tokens,
        ga[:width].astype(f32),
        small[6],
        ga[width : 2 * width].astype(f32),
        small[7],
        ga[2 * width : 3 * width].astype(f32),
        small[8],
        ga[3 * width :].astype(f32),
        small[2],
        small[0],
        small[1],
        g_up.astype(f32),
        g_upbias,
        gff[:units].astype(f32),
        small[5],
        small[3],
        small[4],
    )


def pick(mesh):
    def per_device(*args):
        tokens, span_sizes, w_up = args[0], args[2], args[13]
        rows, width = tokens.shape
        fits = (
            mesh.shape["tensor"] == 2
            and span_sizes.shape[0] == 1
            and rows % TILE == 0
            and width % TILE == 0
            and w_up.shape[1] % width == 0
            and w_up.shape[1] // width <= 3
        )
        return pair_device(*args) if fits else general_device(*args)

    return per_device


def solution(mesh):
    return jax.shard_map(
        pick(mesh),
        mesh=mesh,
        in_specs=(
            P(("dp", "tensor"), None),
            P("dp"),
            P("dp"),
            P(),
            P(),
            P(),
            P(),
            P(),
            P(),
            P(),
            P(),
            P(),
            P(),
            P(None, "tensor"),
            P("tensor"),
            P("tensor", None),
            P(),
            P(),
            P(),
            P(("dp", "tensor"), None),
        ),
        out_specs=(
            P(("dp", "tensor"), None),
            P(("dp", "tensor"), None),
            P(),
            P(),
            P(),
            P(),
            P(),
            P(),
            P(),
            P(),
            P(),
            P(),
            P(None, "tensor"),
            P("tensor"),
            P("tensor", None),
            P(),
            P(),
            P(),
        ),
        check_vma=False,
    )
```

```python
import functools
import math

import jax
import jax.numpy as jnp
from jax import lax
from jax.experimental import pallas as pl
from jax.experimental.pallas import tpu as pltpu
from jax.sharding import PartitionSpec as P

HEADS = 12
HD = 64
SUBLEN = 32


highest = lax.Precision.HIGHEST
norm_eps = 1e-05


def norm_forward(value, gain, shift):
    mean = jnp.mean(value, axis=-1, keepdims=True)
    centred = value - mean
    scale = lax.rsqrt(jnp.mean(centred * centred, axis=-1, keepdims=True) + norm_eps)
    normal = centred * scale
    return (normal * gain + shift, normal, scale)


def norm_backward(grad, normal, scale, gain):
    along = grad * gain
    inner = (
        along
        - jnp.mean(along, axis=-1, keepdims=True)
        - normal * jnp.mean(along * normal, axis=-1, keepdims=True)
    )
    return (inner * scale, jnp.sum(grad * normal, axis=0), jnp.sum(grad, axis=0))


def gelu_slope(pre):
    normal_cdf = 0.5 * (1.0 + jax.scipy.special.erf(pre * (1.0 / math.sqrt(2.0))))
    return normal_cdf + pre * jnp.exp(-0.5 * pre * pre) * (1.0 / math.sqrt(2.0 * math.pi))


def reach_table(count, span):
    slot_index = jnp.arange(count, dtype=jnp.int32)
    final = (slot_index * SUBLEN // span + 1) * span // SUBLEN - 1
    return (slot_index[None, :] <= final[:, None]).astype(jnp.float32)


def features(rows, w_joint, b_joint, cosine, sine):
    length = rows.shape[0]
    width = rows.shape[1]
    proj = jnp.dot(rows, w_joint, preferred_element_type=jnp.float32) + b_joint
    relu_query = jax.nn.relu(proj[:, :width]).reshape(length, HEADS, HD)
    relu_key = jax.nn.relu(proj[:, width : 2 * width]).reshape(length, HEADS, HD) * (1.0 / HD)
    q_feat = jnp.concatenate([relu_query * cosine, relu_query * sine], axis=-1).astype(jnp.bfloat16)
    k_feat = jnp.concatenate([relu_key * cosine, relu_key * sine], axis=-1).astype(jnp.bfloat16)
    v_low = proj[:, 2 * width :].astype(jnp.bfloat16)
    return (q_feat, k_feat, v_low)


def local_blocks(k_feat, v_low):
    count = k_feat.shape[0] // SUBLEN
    k_sub = k_feat.reshape(count, SUBLEN, HEADS, 2 * HD)
    v_sub = v_low.reshape(count, SUBLEN, HEADS, HD)
    blocks = jnp.einsum("tjhf,tjhd->thfd", k_sub, v_sub, preferred_element_type=jnp.float32)
    k_total = jnp.sum(k_sub.astype(jnp.float32), axis=1)
    return (blocks, k_total)


def attend_core(q_feat, k_feat, v_low, blocks, k_total, reach, extra_blocks, extra_keys):
    count = q_feat.shape[0] // SUBLEN
    q_sub = q_feat.reshape(count, SUBLEN, HEADS, 2 * HD)
    k_sub = k_feat.reshape(count, SUBLEN, HEADS, 2 * HD)
    v_sub = v_low.reshape(count, SUBLEN, HEADS, HD)
    state_low = (
        jnp.einsum("st,thfd->shfd", reach, blocks, precision=highest) + extra_blocks
    ).astype(jnp.bfloat16)
    z_sum = jnp.einsum("st,thf->shf", reach, k_total, precision=highest) + extra_keys
    numer = jnp.einsum("sihf,shfd->sihd", q_sub, state_low, preferred_element_type=jnp.float32)
    denom = jnp.einsum("sihf,shf->sih", q_sub.astype(jnp.float32), z_sum, precision=highest) + 1.0
    return (q_sub, k_sub, v_sub, state_low, z_sum, numer, denom)


def back_first(parts, grad_mixed):
    q_sub, k_sub, v_sub, state_low, z_sum, numer, denom = parts
    count = q_sub.shape[0]
    grad_out = grad_mixed.reshape(count, SUBLEN, HEADS, HD).astype(jnp.float32)
    d_numer = grad_out / denom[..., None]
    d_denom = -jnp.sum(grad_out * numer, axis=-1) / (denom * denom)
    q_wide = q_sub.astype(jnp.float32)
    d_query = jnp.einsum(
        "sihd,shfd->sihf", d_numer, state_low.astype(jnp.float32), precision=highest
    )
    d_query = d_query + d_denom[..., None] * z_sum[:, None]
    d_state = jnp.einsum("sihf,sihd->shfd", q_wide, d_numer, precision=highest)
    d_zsum = jnp.einsum("sihf,sih->shf", q_wide, d_denom, precision=highest)
    return (d_query, d_state, d_zsum)


def back_second(parts, reach, d_state, d_zsum, later_blocks, later_keys):
    q_sub, k_sub, v_sub = (parts[0], parts[1], parts[2])
    d_blocks = jnp.einsum("st,shfd->thfd", reach, d_state, precision=highest) + later_blocks
    d_ktotal = jnp.einsum("st,shf->thf", reach, d_zsum, precision=highest) + later_keys
    d_key = (
        jnp.einsum("thfd,tjhd->tjhf", d_blocks, v_sub.astype(jnp.float32), precision=highest)
        + d_ktotal[:, None]
    )
    d_value = jnp.einsum("thfd,tjhf->tjhd", d_blocks, k_sub.astype(jnp.float32), precision=highest)
    return (d_key, d_value)


def feature_grads(q_feat, k_feat, d_qf, d_kf, d_val, cos_part, sin_part):
    size = q_feat.shape[0]
    d_qf = d_qf.reshape(size, HEADS, 2 * HD)
    d_kf = d_kf.reshape(size, HEADS, 2 * HD)
    d_query = jnp.where(
        q_feat[..., :HD] > 0, d_qf[..., :HD] * cos_part + d_qf[..., HD:] * sin_part, 0.0
    )
    d_key = jnp.where(
        k_feat[..., :HD] > 0,
        (d_kf[..., :HD] * cos_part + d_kf[..., HD:] * sin_part) * (1.0 / HD),
        0.0,
    )
    return jnp.concatenate(
        [
            d_query.reshape(size, HEADS * HD),
            d_key.reshape(size, HEADS * HD),
            d_val.reshape(size, HEADS * HD),
        ],
        axis=1,
    )


def general_device(
    tokens,
    positions,
    span_sizes,
    w_query,
    b_query,
    w_key,
    b_key,
    w_value,
    b_value,
    w_out,
    b_out,
    norm1_gain,
    norm1_bias,
    w_up,
    b_up,
    w_down,
    b_down,
    norm2_gain,
    norm2_bias,
    out_grad,
):
    rank = lax.axis_index("tensor")
    tensor_count = lax.axis_size("tensor")
    own = tokens.shape[0]
    width = tokens.shape[1]
    seqs = span_sizes.shape[0]
    group = own * tensor_count
    length = group // seqs
    start = rank * own
    w_joint = jnp.concatenate([w_query, w_key, w_value], axis=1)
    b_joint = jnp.concatenate([b_query, b_key, b_value]).astype(jnp.float32)
    gain_one = norm1_gain.astype(jnp.float32)
    gain_two = norm2_gain.astype(jnp.float32)
    gathered = lax.all_gather(tokens, "tensor", axis=0, tiled=True)
    angle = math.pi / 2 * positions.astype(jnp.float32) / (3 * length)
    cosine = jnp.cos(angle).reshape(seqs, length, 1, 1)
    sine = jnp.sin(angle).reshape(seqs, length, 1, 1)

    def seq_forward(items):
        rows, cos_part, sin_part, span = items
        q_feat, k_feat, v_low = features(rows, w_joint, b_joint, cos_part, sin_part)
        blocks_seq, ktot_seq = local_blocks(k_feat, v_low)
        parts = attend_core(
            q_feat,
            k_feat,
            v_low,
            blocks_seq,
            ktot_seq,
            reach_table(q_feat.shape[0] // SUBLEN, span),
            0.0,
            0.0,
        )
        mixed_seq = (
            (parts[5] / parts[6][..., None]).reshape(rows.shape[0], width).astype(jnp.bfloat16)
        )
        return (mixed_seq, q_feat, k_feat, v_low)

    mixed, q_all, k_all, v_all = lax.map(
        seq_forward, (gathered.reshape(seqs, length, width), cosine, sine, span_sizes)
    )
    mixed = mixed.reshape(group, width)
    mixed_own = lax.dynamic_slice_in_dim(mixed, start, own, 0)
    resid = (
        tokens.astype(jnp.float32)
        + jnp.dot(mixed_own, w_out, preferred_element_type=jnp.float32)
        + b_out.astype(jnp.float32)
    )
    hidden, normal_one, scale_one = norm_forward(resid, gain_one, norm1_bias.astype(jnp.float32))
    hidden_low = hidden.astype(jnp.bfloat16)
    rows_in = lax.all_gather(hidden_low, "tensor", axis=0, tiled=True)
    pre = jnp.dot(rows_in, w_up, preferred_element_type=jnp.float32) + b_up.astype(jnp.float32)
    act_low = jax.nn.gelu(pre, approximate=False).astype(jnp.bfloat16)
    branch = lax.psum_scatter(
        jnp.dot(act_low, w_down, preferred_element_type=jnp.float32),
        "tensor",
        scatter_dimension=0,
        tiled=True,
    )
    summed = hidden + branch + b_down.astype(jnp.float32)
    result, normal_two, scale_two = norm_forward(summed, gain_two, norm2_bias.astype(jnp.float32))
    d_sum, d_gain_two, d_bias_two = norm_backward(
        out_grad.astype(jnp.float32), normal_two, scale_two, gain_two
    )
    d_bdown = jnp.sum(d_sum, axis=0)
    d_sum_low = d_sum.astype(jnp.bfloat16)
    rows_grad = lax.all_gather(d_sum_low, "tensor", axis=0, tiled=True)
    g_down = jnp.dot(act_low.T, rows_grad, preferred_element_type=jnp.float32)
    d_pre = jnp.dot(rows_grad, w_down.T, preferred_element_type=jnp.float32) * gelu_slope(pre)
    g_upbias = jnp.sum(d_pre, axis=0)
    d_pre_low = d_pre.astype(jnp.bfloat16)
    g_up = jnp.dot(rows_in.T, d_pre_low, preferred_element_type=jnp.float32)
    d_hidden = lax.psum_scatter(
        jnp.dot(d_pre_low, w_up.T, preferred_element_type=jnp.float32),
        "tensor",
        scatter_dimension=0,
        tiled=True,
    )
    g_up, g_upbias, g_down = (
        lax.psum(g_up.astype(jnp.bfloat16), "dp").astype(jnp.float32),
        lax.psum(g_upbias.astype(jnp.bfloat16), "dp").astype(jnp.float32),
        lax.psum(g_down.astype(jnp.bfloat16), "dp").astype(jnp.float32),
    )
    d_hidden = d_hidden + d_sum
    d_resid, d_gain_one, d_bias_one = norm_backward(d_hidden, normal_one, scale_one, gain_one)
    d_bout = jnp.sum(d_resid, axis=0)
    d_gain_one, d_bias_one, d_gain_two, d_bias_two, d_bout, d_bdown = lax.psum(
        (d_gain_one, d_bias_one, d_gain_two, d_bias_two, d_bout, d_bdown), ("dp", "tensor")
    )
    d_resid_low = d_resid.astype(jnp.bfloat16)
    rows_back = lax.all_gather(d_resid_low, "tensor", axis=0, tiled=True)
    g_out = jnp.dot(mixed.T, rows_back, preferred_element_type=jnp.float32)
    d_mixed = jnp.dot(rows_back, w_out.T, preferred_element_type=jnp.float32).astype(jnp.bfloat16)

    def seq_backward(items):
        q_feat, k_feat, v_low, cos_part, sin_part, span, grad_mixed = items
        blocks_seq, ktot_seq = local_blocks(k_feat, v_low)
        reach = reach_table(q_feat.shape[0] // SUBLEN, span)
        parts = attend_core(q_feat, k_feat, v_low, blocks_seq, ktot_seq, reach, 0.0, 0.0)
        d_qf, d_state, d_zsum = back_first(parts, grad_mixed)
        d_kf, d_val = back_second(parts, reach, d_state, d_zsum, 0.0, 0.0)
        joint = feature_grads(q_feat, k_feat, d_qf, d_kf, d_val, cos_part, sin_part)
        return (joint.astype(jnp.bfloat16), jnp.sum(joint, axis=0))

    d_joint, d_jbias = lax.map(
        seq_backward,
        (q_all, k_all, v_all, cosine, sine, span_sizes, d_mixed.reshape(seqs, length, width)),
    )
    d_joint = d_joint.reshape(group, 3 * width)
    d_jbias = jnp.sum(d_jbias, axis=0)
    g_joint = jnp.dot(gathered.T, d_joint, preferred_element_type=jnp.float32)
    d_joint_own = lax.dynamic_slice_in_dim(d_joint, start, own, 0)
    d_tokens = d_resid + jnp.dot(d_joint_own, w_joint.T, preferred_element_type=jnp.float32)
    g_joint, g_out, d_jbias = lax.psum((g_joint, g_out, d_jbias), "dp")
    return (
        result.astype(jnp.bfloat16),
        d_tokens,
        g_joint[:, :width],
        d_jbias[:width],
        g_joint[:, width : 2 * width],
        d_jbias[width : 2 * width],
        g_joint[:, 2 * width :],
        d_jbias[2 * width :],
        g_out,
        d_bout,
        d_gain_one,
        d_bias_one,
        g_up,
        g_upbias,
        g_down,
        d_bdown,
        d_gain_two,
        d_bias_two,
    )


f32 = jnp.float32
bf16 = jnp.bfloat16
MESH = pl.DeviceIdType.MESH
LANES = 2 * HD
TILE = 256
ROWBLOCK = 32


def tile_at(index, size):
    return pl.ds(pl.multiple_of(index * size, size), size)


def contract(left, right, left_dim, right_dim, precision=None):
    return lax.dot_general(
        left,
        right,
        (((left_dim,), (right_dim,)), ((), ())),
        precision=precision,
        preferred_element_type=f32,
    )


def mm(left, right):
    return contract(left, right, 1, 0)


def mm_nt(left, right):
    return contract(left, right, 1, 1)


def mm_tn(left, right):
    return contract(left, right, 0, 0)


def head_masks():
    lane = lax.broadcasted_iota(jnp.int32, (1, LANES), 1)
    first = (lane < HD).astype(f32)
    return first, 1.0 - first


def pair_mask():
    row = lax.broadcasted_iota(jnp.int32, (LANES, LANES), 0)
    col = lax.broadcasted_iota(jnp.int32, (LANES, LANES), 1)
    return ((row < HD) == (col < HD)).astype(f32)


def first_row(block, which):
    row = lax.broadcasted_iota(jnp.int32, block.shape, 0)
    return jnp.where(row == which, block, 0.0)


def column_of(block, which):
    return contract(first_row(block, which), jnp.ones((8, LANES), f32), 0, 0, highest)


def squeeze_pair(square):
    return square[:HD] + square[HD:]


def spread_pair(half, mask):
    return jnp.concatenate([half, half], axis=0).astype(f32) * mask


def fold8(value):
    total = value[0:8]
    for start in range(8, value.shape[0], 8):
        total = total + value[start : start + 8]
    return total


def angle_tables(trig, span, cosb, sinb, ctab):
    rows = cosb.shape[0]
    block = trig[...]
    cosb[...] = column_of(block, 0)
    sinb[...] = column_of(block, 1)
    both = contract(block, block, 0, 0, highest)
    row = lax.broadcasted_iota(jnp.int32, (rows, rows), 0)
    col = lax.broadcasted_iota(jnp.int32, (rows, rows), 1)
    seen = col <= (row | (span[0, 0] - 1))
    ctab[...] = jnp.where(seen, both * (1.0 / HD), 0.0)


def peer_copy(src, dst, sems, slot, device):
    return pltpu.make_async_remote_copy(
        src_ref=src,
        dst_ref=dst,
        send_sem=sems[0].at[slot],
        recv_sem=sems[1].at[slot],
        device_id=device,
        device_id_type=MESH,
    )


def meet(devices):
    barrier = pltpu.get_barrier_semaphore()
    for device in devices:
        pl.semaphore_signal(barrier, inc=1, device_id=device, device_id_type=MESH)
    pl.semaphore_wait(barrier, len(devices))


def front_kernel(
    tok, trig, span, vec, wq, wk, wv, wo, wup, wdn, og,
    res_o, small_o, gff_o, dhs_o, dho_o, mixb, mixf, inv, rq, rk, vv, nrm, scl, st_o, z_o,
    hbuf, act, slope, dbuf, dpre, hid, tsend, trecv, zsend, zrecv, bsend, brecv,
    numer, denom, ctab, cosb, sinb, acc, bup, send, recv,
):
    sems = (send, recv)
    rows, width = tok.shape
    units = wup.shape[1]
    pairs = width // LANES
    tiles = width // TILE
    rank = lax.axis_index("tensor")
    peer = (lax.axis_index("dp"), 1 - rank)
    late = rank.astype(f32)
    own, other = pl.ds(0, rows), pl.ds(rows, rows)
    meet([peer])

    for which, (weight, target) in enumerate(((wq, rq), (wk, rk), (wv, vv))):

        @pl.loop(0, tiles)
        def _(j, which=which, weight=weight, target=target):
            cols = tile_at(j, TILE)
            y = mm(tok[...], weight[:, cols]) + vec[which : which + 1, cols]
            if which < 2:
                y = jnp.maximum(y, 0.0)
            target[:, cols] = y.astype(bf16)

    angle_tables(trig, span, cosb, sinb, ctab)
    diag = pair_mask()
    first, second = head_masks()
    first_low, second_low = first.astype(bf16), second.astype(bf16)

    @pl.loop(0, pairs)
    def _(p):
        lanes = tile_at(p, LANES)
        k = rk[:, lanes].astype(f32) * (1.0 / HD)
        v = vv[:, lanes]
        kc, ks = (k * cosb[...]).astype(bf16), (k * sinb[...]).astype(bf16)
        tsend[p, 0] = squeeze_pair(mm_tn(kc, v) * diag).astype(bf16)
        tsend[p, 1] = squeeze_pair(mm_tn(ks, v) * diag).astype(bf16)
        sum_c = jnp.sum(kc.astype(f32), axis=0, keepdims=True)
        sum_s = jnp.sum(ks.astype(f32), axis=0, keepdims=True)
        row = lax.broadcasted_iota(jnp.int32, (8, LANES), 0)
        zsend[p] = jnp.where(row == 0, sum_c, jnp.where(row == 1, sum_s, 0.0))

    state_copy = peer_copy(tsend, trecv, sems, 0, peer)
    key_copy = peer_copy(zsend, zrecv, sems, 1, peer)
    state_copy.start()
    key_copy.start()

    @pl.loop(0, pairs)
    def _(p):
        lanes = tile_at(p, LANES)
        q, k, v = rq[:, lanes], rk[:, lanes], vv[:, lanes]
        parts = []
        for mask, rest in ((first_low, second_low), (second_low, first_low)):
            score = mm_nt(q * mask, k)
            prob = (score * ctab[...]).astype(bf16)
            parts.append(mm(prob, v * mask + rest))
        numer[:, lanes] = parts[0] * first + parts[1] * second
        denom[:, lanes] = pltpu.roll(parts[0] * second + parts[1] * first, HD, 1)

    state_copy.wait()
    key_copy.wait()

    @pl.loop(0, pairs)
    def _(p):
        lanes = tile_at(p, LANES)
        q = rq[:, lanes].astype(f32)
        qc, qs = (q * cosb[...]).astype(bf16), (q * sinb[...]).astype(bf16)
        st_o[p] = (trecv[p].astype(f32) * late).astype(bf16)
        zblock = zrecv[p] * late
        z_o[p] = zblock
        num, den = numer[:, lanes], denom[:, lanes] + 1.0
        for part, feat in ((0, qc), (1, qs)):
            num += mm(feat, spread_pair(st_o[p, part], diag).astype(bf16))
            den += mm(feat, (column_of(zblock, part) * diag).astype(bf16))
        reciprocal = 1.0 / den
        mix = num * reciprocal
        inv[:, lanes] = reciprocal
        mixf[:, lanes] = mix
        mixb[:, lanes] = mix.astype(bf16)

    @pl.loop(0, tiles)
    def _(j):
        cols = tile_at(j, TILE)
        hid[:, cols] = tok[:, cols].astype(f32) + mm(mixb[...], wo[:, cols]) + vec[3:4, cols]

    @pl.loop(0, rows // ROWBLOCK)
    def _(i):
        at = tile_at(i, ROWBLOCK)
        value = hid[at, :]
        centred = value - jnp.mean(value, axis=-1, keepdims=True)
        scale = lax.rsqrt(jnp.mean(centred * centred, axis=-1, keepdims=True) + norm_eps)
        normal = centred * scale
        hidden = normal * vec[4:5, :] + vec[5:6, :]
        nrm[at, :] = normal
        scl[at, :] = jnp.broadcast_to(scale, (ROWBLOCK, LANES))
        hid[at, :] = hidden
        hbuf[at, :] = hidden.astype(bf16)

    hidden_copy = peer_copy(hbuf.at[own], hbuf.at[other], sems, 2, peer)
    hidden_copy.start()

    def raise_rows(part):
        for half in range(units // width):

            @pl.loop(0, tiles)
            def _(j, half=half):
                cols = tile_at(half * tiles + j, TILE)
                pre = mm(hbuf[part, :], wup[:, cols]) + vec[9 + half : 10 + half, tile_at(j, TILE)]
                cdf = 0.5 * (1.0 + lax.erf(pre * (1.0 / math.sqrt(2.0))))
                act[part, cols] = (pre * cdf).astype(bf16)
                slope[part, cols] = cdf + pre * jnp.exp(-0.5 * pre * pre) * (
                    1.0 / math.sqrt(2.0 * math.pi)
                )

    raise_rows(own)
    hidden_copy.wait()
    raise_rows(other)

    @pl.loop(0, tiles)
    def _(j):
        cols = tile_at(j, TILE)
        bsend[:, cols] = mm(act[other, :], wdn[:, cols]).astype(bf16)

    branch_copy = peer_copy(bsend, brecv, sems, 3, peer)
    branch_copy.start()

    @pl.loop(0, tiles)
    def _(j):
        cols = tile_at(j, TILE)
        hid[:, cols] += mm(act[own, :], wdn[:, cols]) + vec[6:7, cols]

    acc[...] = jnp.zeros_like(acc)
    branch_copy.wait()

    @pl.loop(0, rows // ROWBLOCK)
    def _(i):
        at = tile_at(i, ROWBLOCK)
        value = hid[at, :] + brecv[at, :].astype(f32)
        centred = value - jnp.mean(value, axis=-1, keepdims=True)
        scale = lax.rsqrt(jnp.mean(centred * centred, axis=-1, keepdims=True) + norm_eps)
        normal = centred * scale
        res_o[at, :] = (normal * vec[7:8, :] + vec[8:9, :]).astype(bf16)
        grad = og[at, :].astype(f32)
        along = grad * vec[7:8, :]
        inner = (
            along
            - jnp.mean(along, axis=-1, keepdims=True)
            - normal * jnp.mean(along * normal, axis=-1, keepdims=True)
        ) * scale
        dho_o[at, :] = inner
        dbuf[at, :] = inner.astype(bf16)
        acc[0:8, :] += fold8(grad * normal)
        acc[8:16, :] += fold8(grad)
        acc[16:24, :] += fold8(inner)

    grad_copy = peer_copy(dbuf.at[own], dbuf.at[other], sems, 4, peer)
    grad_copy.start()

    small_o[...] = jnp.zeros_like(small_o)
    for slot in range(3):
        small_o[3 + slot : 4 + slot, :] = jnp.sum(
            acc[8 * slot : 8 * slot + 8, :], axis=0, keepdims=True
        )
    bup[...] = jnp.zeros_like(bup)

    def lower_rows(part):
        @pl.loop(0, units // TILE)
        def _(j):
            cols = tile_at(j, TILE)
            d_pre = mm_nt(dbuf[part, :], wdn[cols, :]) * slope[part, cols]
            bup[:, cols] += fold8(d_pre)
            dpre[part, cols] = d_pre.astype(bf16)

    lower_rows(own)
    grad_copy.wait()
    lower_rows(other)

    @pl.loop(0, tiles)
    def _(j):
        cols = tile_at(j, TILE)
        dhs_o[:, cols] = mm_nt(dpre[other, :], wup[cols, :]).astype(bf16)
        dho_o[:, cols] += mm_nt(dpre[own, :], wup[cols, :])

    for half in range(units // width):
        line = jnp.sum(bup[:, half * width : (half + 1) * width], axis=0, keepdims=True)
        small_o[9 + half : 10 + half, :] = line * (1.0 - late)
        small_o[9 + units // width + half : 10 + units // width + half, :] = line * late

    @pl.loop(0, units // TILE)
    def _(j):
        cols = tile_at(j, TILE)
        gff_o[cols, :] = mm_tn(act[:, cols], dbuf[...]).astype(bf16)

    for half in range(units // width):

        @pl.loop(0, tiles)
        def _(j, half=half):
            gff_o[pl.ds(units + half * width, width), tile_at(j, TILE)] = mm_tn(
                hbuf[...], dpre[:, tile_at(half * tiles + j, TILE)]
            ).astype(bf16)


def back_kernel(
    tok, trig, span, vec, wq, wk, wv, wo,
    dhs, dho, mixb, mixf, inv, rq, rk, vv, nrm, scl, st, z, small_in,
    dtok_o, ga_o, small_o,
    dhr, dres, dlow, dn, xs, dsend, drecv, dzs, dzr, dq, dk, dv, dql, dkl, dvl,
    ctab, cosb, sinb, acc, send, recv,
):
    sems = (send, recv)
    rows, width = tok.shape
    pairs = width // LANES
    tiles = width // TILE
    rank = lax.axis_index("tensor")
    peer = (lax.axis_index("dp"), 1 - rank)
    early = 1.0 - rank.astype(f32)
    meet([peer])
    hidden_copy = peer_copy(dhs, dhr, sems, 0, peer)
    hidden_copy.start()
    angle_tables(trig, span, cosb, sinb, ctab)
    diag = pair_mask()
    first, second = head_masks()
    first_low, second_low = first.astype(bf16), second.astype(bf16)
    diag_low = diag.astype(bf16)
    acc[...] = jnp.zeros_like(acc)
    small_o[...] = small_in[...]
    hidden_copy.wait()

    @pl.loop(0, rows // ROWBLOCK)
    def _(i):
        at = tile_at(i, ROWBLOCK)
        grad = dho[at, :] + dhr[at, :].astype(f32)
        normal = nrm[at, :]
        along = grad * vec[4:5, :]
        inner = (
            along
            - jnp.mean(along, axis=-1, keepdims=True)
            - normal * jnp.mean(along * normal, axis=-1, keepdims=True)
        ) * scl[at, 0:1]
        dres[at, :] = inner
        dlow[at, :] = inner.astype(bf16)
        acc[0:8, :] += fold8(grad * normal)
        acc[8:16, :] += fold8(grad)
        acc[16:24, :] += fold8(inner)

    for slot in range(3):
        small_o[slot : slot + 1, :] = jnp.sum(
            acc[8 * slot : 8 * slot + 8, :], axis=0, keepdims=True
        )

    @pl.loop(0, tiles)
    def _(j):
        cols = tile_at(j, TILE)
        d_mixed = mm_nt(dlow[...], wo[cols, :]).astype(bf16).astype(f32)
        d_numer = (d_mixed * inv[:, cols]).astype(bf16)
        dn[:, cols] = d_numer
        xs[:, cols] = (d_numer.astype(f32) * mixf[:, cols]).astype(bf16)

    @pl.loop(0, pairs)
    def _(p):
        lanes = tile_at(p, LANES)
        q = rq[:, lanes].astype(f32)
        qc, qs = (q * cosb[...]).astype(bf16), (q * sinb[...]).astype(bf16)
        d_numer = dn[:, lanes]
        dsend[p, 0] = squeeze_pair(mm_tn(qc, d_numer) * diag).astype(bf16)
        dsend[p, 1] = squeeze_pair(mm_tn(qs, d_numer) * diag).astype(bf16)
        across = mm(xs[:, lanes], diag_low)
        sum_c = jnp.sum(qc.astype(f32) * across, axis=0, keepdims=True)
        sum_s = jnp.sum(qs.astype(f32) * across, axis=0, keepdims=True)
        row = lax.broadcasted_iota(jnp.int32, (8, LANES), 0)
        dzs[p] = -jnp.where(row == 0, sum_c, jnp.where(row == 1, sum_s, 0.0))

    state_copy = peer_copy(dsend, drecv, sems, 1, peer)
    key_copy = peer_copy(dzs, dzr, sems, 2, peer)
    state_copy.start()
    key_copy.start()

    @pl.loop(0, tiles)
    def _(j):
        cols = tile_at(j, TILE)
        ga_o[tile_at(3 * tiles + j, TILE), :] = mm_tn(mixb[:, cols], dlow[...]).astype(bf16)

    @pl.loop(0, pairs)
    def _(p):
        lanes = tile_at(p, LANES)
        q, k, v = rq[:, lanes], rk[:, lanes], vv[:, lanes]
        d_numer = dn[:, lanes]
        turned = -pltpu.roll(xs[:, lanes].astype(f32), HD, 1)
        turned = turned.astype(bf16)
        sum_q = sum_k = sum_v = 0.0
        for mask, rest in ((first_low, second_low), (second_low, first_low)):
            q_head, k_head, d_head = q * mask, k * mask, d_numer * mask
            table = ctab[...]
            prob = (mm_nt(q_head, k) * table).astype(bf16)
            d_prob = mm_nt(d_head + turned * rest, v * mask + rest)
            d_score = (d_prob * table).astype(bf16)
            sum_v += mm_tn(prob, d_head)
            sum_q += mm(d_score, k_head)
            sum_k += mm_tn(d_score, q_head)
        dq[:, lanes] = sum_q
        dk[:, lanes] = sum_k
        dv[:, lanes] = sum_v

    state_copy.wait()
    key_copy.wait()

    @pl.loop(0, pairs)
    def _(p):
        lanes = tile_at(p, LANES)
        q, v = rq[:, lanes].astype(f32), vv[:, lanes]
        k = rk[:, lanes].astype(f32)
        d_numer, x = dn[:, lanes], xs[:, lanes]
        sum_q, sum_k, sum_v = dq[:, lanes], dk[:, lanes], dv[:, lanes]
        zblock, dzblock = z[p], dzr[p] * early
        for part, wave in ((0, cosb[...]), (1, sinb[...])):
            state = spread_pair(st[p, part], diag).astype(bf16)
            zmat = (column_of(zblock, part) * diag).astype(bf16)
            sum_q += wave * (mm_nt(d_numer, state) - mm_nt(x, zmat))
            d_state = (spread_pair(drecv[p, part], diag) * early).astype(bf16)
            sum_k += wave * (mm_nt(v, d_state) + dzblock[part : part + 1, :]) * (1.0 / HD)
            sum_v += mm((k * wave * (1.0 / HD)).astype(bf16), d_state)
        sum_q = jnp.where(q > 0, sum_q, 0.0)
        sum_k = jnp.where(k > 0, sum_k, 0.0)
        dql[:, lanes] = sum_q.astype(bf16)
        dkl[:, lanes] = sum_k.astype(bf16)
        dvl[:, lanes] = sum_v.astype(bf16)
        for slot, value in ((6, sum_q), (7, sum_k), (8, sum_v)):
            small_o[slot : slot + 1, lanes] = jnp.sum(value, axis=0, keepdims=True)

    for which, source in enumerate((dql, dkl, dvl)):

        @pl.loop(0, tiles)
        def _(j, which=which, source=source):
            ga_o[tile_at(which * tiles + j, TILE), :] = mm_tn(
                tok[:, tile_at(j, TILE)], source[...]
            ).astype(bf16)

    @pl.loop(0, tiles)
    def _(j):
        cols = tile_at(j, TILE)
        dtok_o[:, cols] = (
            dres[:, cols]
            + mm_nt(dql[...], wq[cols, :])
            + mm_nt(dkl[...], wk[cols, :])
            + mm_nt(dvl[...], wv[cols, :])
        )


def grid_place():
    dp = lax.axis_index("dp")
    core, chip = dp % 2, dp // 2
    return core, chip % 2, chip // 2


def ring_device(spot, depth, core):
    far = spot // depth
    z = far * (2 * depth - 1 - spot) + (1 - far) * spot
    return ((z * 2 + far) * 2 + core, lax.axis_index("tensor"))


def add_rows(target, rows, block):
    target[rows, :] = (target[rows, :].astype(f32) + block.astype(f32)).astype(bf16)


def sum_kernel(
    count, gff, ga, small, ff_o, a_o, small_o,
    cr_ff, cr_a, xr_a, acc_ff, acc_a, rs_ff, rs_a, small_r,
    c_send, c_recv, r_send, r_recv, g_send, g_recv, x_send, x_recv, m_send, m_recv,
):
    depth = count // 2
    half = gff.shape[0] // 2
    quarter = ga.shape[0] // 4
    core, y, z = grid_place()
    rank = lax.axis_index("tensor")
    dp = lax.axis_index("dp")
    spot = y * (2 * depth - 1 - z) + (1 - y) * z
    sibling = (dp + 1 - 2 * core, rank)
    peer = (dp, 1 - rank)
    ahead = ring_device((spot + 1) % count, depth, core)
    behind = ring_device((spot + count - 1) % count, depth, core)
    swaps = [sibling, peer, (dp + 2 - 4 * y, rank)]
    step = 1
    while step < depth:
        bit = (z // step) % 2
        swaps.append((dp + 4 * (step - 2 * step * bit), rank))
        step *= 2
    meet([ahead, behind] + swaps)

    def core_rows(which, size):
        return pl.ds(pl.multiple_of(which * size, size), size)

    core_ff = peer_copy(gff.at[core_rows(1 - core, half), :], cr_ff, (c_send, c_recv), 0, sibling)
    core_a = peer_copy(ga.at[core_rows(1 - core, 2 * quarter), :], cr_a, (c_send, c_recv), 1, sibling)
    core_ff.start()
    core_a.start()

    def small_copy(index):
        return peer_copy(small_o.at[index], small_r.at[index], (m_send, m_recv), index, swaps[index])

    small_o[0] = small[...]
    small_copy(0).start()

    core_a.wait()

    @pl.loop(0, 2 * quarter // 96)
    def _(i):
        rows = tile_at(i, 96)
        at = pl.ds(pl.multiple_of(core * 2 * quarter + i * 96, 96), 96)
        add_rows(cr_a, rows, ga[at, :])

    x_copy = peer_copy(cr_a.at[core_rows(1 - rank, quarter), :], xr_a, (c_send, c_recv), 2, peer)
    x_copy.start()
    core_ff.wait()

    @pl.loop(0, half // 96)
    def _(i):
        rows = tile_at(i, 96)
        at = pl.ds(pl.multiple_of(core * half + i * 96, 96), 96)
        acc_ff[rows, :] = (gff[at, :].astype(f32) + cr_ff[rows, :].astype(f32)).astype(bf16)

    def swap_small(index):
        small_copy(index).wait()
        small_o[index + 1] = small_o[index] + small_r[index]
        if index + 1 < len(swaps):
            small_copy(index + 1).start()

    streams = []
    for kind, (acc, slots, out, base) in enumerate(
        ((acc_ff, rs_ff, ff_o, core * half), (acc_a, rs_a, a_o, (core * 2 + rank) * quarter))
    ):
        size = acc.shape[0] // count // 2
        for way in range(2):
            streams.append((2 * kind + way, way, acc, slots, out, base, size))

    def chunk_at(spot_index, stream, based):
        _, way, _, _, _, base, size = stream
        start = (spot_index % count) * 2 * size + way * size
        return pl.ds(pl.multiple_of(start + base if based else start, size), size)

    def toward(way):
        return behind if way else ahead

    def spread_copy(stream, at, s):
        number, way, acc, slots, _, _, _ = stream
        return pltpu.make_async_remote_copy(
            src_ref=acc.at[chunk_at(at, stream, False), :],
            dst_ref=slots.at[s, way],
            send_sem=r_send.at[number, s],
            recv_sem=r_recv.at[number, s],
            device_id=toward(way),
            device_id_type=MESH,
        )

    def gather_copy(stream, at, s):
        number, way, _, _, out, _, _ = stream
        rows = chunk_at(at, stream, True)
        return pltpu.make_async_remote_copy(
            src_ref=out.at[rows, :],
            dst_ref=out.at[rows, :],
            send_sem=g_send.at[number, s],
            recv_sem=g_recv.at[number, s],
            device_id=toward(way),
            device_id_type=MESH,
        )

    def across_copy(stream, at, s, base):
        _, way, _, _, out, _, size = stream
        start = base + (at % count) * 2 * size + way * size
        rows = pl.ds(pl.multiple_of(start, size), size)
        return pltpu.make_async_remote_copy(
            src_ref=out.at[rows, :],
            dst_ref=out.at[rows, :],
            send_sem=x_send.at[way, s],
            recv_sem=x_recv.at[way, s],
            device_id=peer,
            device_id_type=MESH,
        )

    def sign(stream):
        return -1 if stream[1] else 1

    for stream in streams[:2]:
        spread_copy(stream, spot, 0).start()
    x_copy.wait()

    @pl.loop(0, quarter // 96)
    def _(i):
        rows = tile_at(i, 96)
        at = pl.ds(pl.multiple_of(rank * quarter + i * 96, 96), 96)
        acc_a[rows, :] = (cr_a[at, :].astype(f32) + xr_a[rows, :].astype(f32)).astype(bf16)

    for stream in streams[2:]:
        spread_copy(stream, spot, 0).start()

    def spread_step(s, last):
        for stream in streams:
            number, way, acc, slots, out, base, size = stream
            at = spot + count - sign(stream) * (s + 1)
            spread_copy(stream, at, s).wait_recv()
            rows = chunk_at(at, stream, False)
            total = (acc[rows, :].astype(f32) + slots[s, way].astype(f32)).astype(bf16)
            if last:
                out[chunk_at(at, stream, True), :] = total
                gather_copy(stream, at, 0).start()
                if number >= 2:
                    across_copy(stream, at, 0, base).start()
            else:
                acc[rows, :] = total
                spread_copy(stream, at, s + 1).start()

    def gather_step(s, last):
        for stream in streams:
            number, base = stream[0], stream[5]
            at = spot + 2 * count - sign(stream) * s
            gather_copy(stream, at, s).wait_recv()
            if not last:
                gather_copy(stream, at, s + 1).start()
            if number >= 2:
                across_copy(stream, at, s + 1, base).start()

    for index in range(len(swaps)):
        swap_small(index)

    @pl.loop(0, count - 2)
    def _(s):
        spread_step(s, False)

    spread_step(count - 2, True)

    @pl.loop(0, count - 2)
    def _(s):
        gather_step(s, False)

    gather_step(count - 2, True)

    back_ff = peer_copy(
        ff_o.at[core_rows(core, half), :], ff_o.at[core_rows(core, half), :], (c_send, c_recv), 3, sibling
    )
    back_ff.start()
    other = (core * 2 + 1 - rank) * quarter

    @pl.loop(0, count)
    def _(s):
        for stream in streams[2:]:
            step_sign = sign(stream)
            at = spot + 2 * count + step_sign * (1 - s)
            across_copy(stream, at, s, other).wait_recv()

    back_a = peer_copy(
        a_o.at[core_rows(core, 2 * quarter), :], a_o.at[core_rows(core, 2 * quarter), :],
        (c_send, c_recv), 4, sibling,
    )
    back_a.start()

    @pl.loop(0, count - 1)
    def _(s):
        for stream in streams:
            spread_copy(stream, spot, s).wait_send()
            gather_copy(stream, spot, s).wait_send()

    @pl.loop(0, count)
    def _(s):
        for stream in streams[2:]:
            across_copy(stream, spot, s, stream[5]).wait_send()

    back_ff.wait()
    back_a.wait()


def in_vmem(count):
    return [pl.BlockSpec(memory_space=pltpu.VMEM)] * count


def shaped(*items):
    return tuple(jax.ShapeDtypeStruct(shape, kind) for shape, kind in items)


def pair_device(
    tokens,
    positions,
    span_sizes,
    w_query,
    b_query,
    w_key,
    b_key,
    w_value,
    b_value,
    w_out,
    b_out,
    norm1_gain,
    norm1_bias,
    w_up,
    b_up,
    w_down,
    b_down,
    norm2_gain,
    norm2_bias,
    out_grad,
):
    rank = lax.axis_index("tensor")
    rows, width = tokens.shape
    units = w_up.shape[1]
    pairs = width // LANES
    length = positions.shape[0]
    places = lax.dynamic_slice_in_dim(positions, rank * rows, rows, 0)
    angle = math.pi / 2 * places.astype(f32) / (3 * length)
    line = lax.broadcasted_iota(jnp.int32, (8, rows), 0)
    trig = jnp.where(
        line == 0, jnp.cos(angle)[None], jnp.where(line == 1, jnp.sin(angle)[None], 0.0)
    )
    span = span_sizes.reshape(1, 1)
    vectors = [
        b_query, b_key, b_value, b_out, norm1_gain, norm1_bias, b_down, norm2_gain, norm2_bias, b_up,
    ]
    vec = jnp.concatenate(vectors).astype(f32).reshape(-1, width)
    vec = jnp.pad(vec, ((0, -vec.shape[0] % 8), (0, 0)))
    smalls = 9 + 2 * (units // width)
    smalls += -smalls % 8
    state = (pairs, 2, HD, LANES)
    zrows = (pairs, 8, LANES)
    wide, low, both = ((rows, width), f32), ((rows, width), bf16), (2 * rows, width)
    front_outs = shaped(
        low, ((smalls, width), f32), ((2 * units, width), bf16), low, wide, low, wide, wide,
        low, low, low, wide, ((rows, LANES), f32), (state, bf16), (zrows, f32),
    )
    tables = [
        pltpu.VMEM((rows, rows), f32), pltpu.VMEM((rows, LANES), f32), pltpu.VMEM((rows, LANES), f32),
    ]
    smem = [pl.BlockSpec(memory_space=pltpu.SMEM)]
    (
        result, small, gff, dhs, dho, mixb, mixf, inv, rq, rk, vv, nrm, scl, st, z,
    ) = pl.pallas_call(
        front_kernel,
        out_shape=front_outs,
        in_specs=in_vmem(2) + smem + in_vmem(8),
        out_specs=tuple(in_vmem(len(front_outs))),
        scratch_shapes=[
            pltpu.VMEM(both, bf16),
            pltpu.VMEM((2 * rows, units), bf16),
            pltpu.VMEM((2 * rows, units), f32),
            pltpu.VMEM(both, bf16),
            pltpu.VMEM((2 * rows, units), bf16),
            pltpu.VMEM((rows, width), f32),
            pltpu.VMEM(state, bf16),
            pltpu.VMEM(state, bf16),
            pltpu.VMEM(zrows, f32),
            pltpu.VMEM(zrows, f32),
            pltpu.VMEM((rows, width), bf16),
            pltpu.VMEM((rows, width), bf16),
            pltpu.VMEM((rows, width), f32),
            pltpu.VMEM((rows, width), f32),
            *tables,
            pltpu.VMEM((24, width), f32),
            pltpu.VMEM((8, units), f32),
            pltpu.SemaphoreType.DMA((5,)),
            pltpu.SemaphoreType.DMA((5,)),
        ],
        compiler_params=pltpu.CompilerParams(
            collective_id=0, has_side_effects=True, vmem_limit_bytes=60 << 20
        ),
        name="front",
    )(tokens, trig, span, vec, w_query, w_key, w_value, w_out, w_up, w_down, out_grad)
    back_outs = shaped(wide, ((4 * width, width), bf16), ((smalls, width), f32))
    d_tokens, ga, small = pl.pallas_call(
        back_kernel,
        out_shape=back_outs,
        in_specs=in_vmem(2) + smem + in_vmem(18),
        out_specs=tuple(in_vmem(len(back_outs))),
        scratch_shapes=[
            pltpu.VMEM((rows, width), bf16),
            pltpu.VMEM((rows, width), f32),
            pltpu.VMEM((rows, width), bf16),
            pltpu.VMEM((rows, width), bf16),
            pltpu.VMEM((rows, width), bf16),
            pltpu.VMEM(state, bf16),
            pltpu.VMEM(state, bf16),
            pltpu.VMEM(zrows, f32),
            pltpu.VMEM(zrows, f32),
            pltpu.VMEM((rows, width), f32),
            pltpu.VMEM((rows, width), f32),
            pltpu.VMEM((rows, width), f32),
            pltpu.VMEM((rows, width), bf16),
            pltpu.VMEM((rows, width), bf16),
            pltpu.VMEM((rows, width), bf16),
            *tables,
            pltpu.VMEM((24, width), f32),
            pltpu.SemaphoreType.DMA((3,)),
            pltpu.SemaphoreType.DMA((3,)),
        ],
        compiler_params=pltpu.CompilerParams(
            collective_id=1, has_side_effects=True, vmem_limit_bytes=60 << 20
        ),
        name="back",
    )(
        tokens, trig, span, vec, w_query, w_key, w_value, w_out,
        dhs, dho, mixb, mixf, inv, rq, rk, vv, nrm, scl, st, z, small,
    )
    count = lax.axis_size("dp") // 2
    swaps = 2 + count.bit_length() - 1
    half, quarter = units, width
    ff_part, a_part = half // count // 2, quarter // count // 2
    gff, ga, small = pl.pallas_call(
        functools.partial(sum_kernel, count),
        out_shape=shaped((gff.shape, bf16), (ga.shape, bf16), ((swaps + 1, *small.shape), f32)),
        in_specs=in_vmem(3),
        out_specs=tuple(in_vmem(3)),
        scratch_shapes=[
            pltpu.VMEM((half, width), bf16),
            pltpu.VMEM((2 * quarter, width), bf16),
            pltpu.VMEM((quarter, width), bf16),
            pltpu.VMEM((half, width), bf16),
            pltpu.VMEM((quarter, width), bf16),
            pltpu.VMEM((count - 1, 2, ff_part, width), bf16),
            pltpu.VMEM((count - 1, 2, a_part, width), bf16),
            pltpu.VMEM((swaps, *small.shape), f32),
            pltpu.SemaphoreType.DMA((5,)),
            pltpu.SemaphoreType.DMA((5,)),
            pltpu.SemaphoreType.DMA((4, count - 1)),
            pltpu.SemaphoreType.DMA((4, count - 1)),
            pltpu.SemaphoreType.DMA((4, count - 1)),
            pltpu.SemaphoreType.DMA((4, count - 1)),
            pltpu.SemaphoreType.DMA((2, count)),
            pltpu.SemaphoreType.DMA((2, count)),
            pltpu.SemaphoreType.DMA((swaps,)),
            pltpu.SemaphoreType.DMA((swaps,)),
        ],
        compiler_params=pltpu.CompilerParams(
            collective_id=2, has_side_effects=True, vmem_limit_bytes=60 << 20
        ),
        name="sums",
    )(gff, ga, small)
    small = small[swaps]
    halves = units // width
    g_up = jnp.concatenate(
        [gff[units + h * width : units + (h + 1) * width] for h in range(halves)], axis=1
    )
    g_upbias = lax.dynamic_slice_in_dim(small, 9 + rank * halves, halves, 0).reshape(units)
    return (
        result,
        d_tokens,
        ga[:width].astype(f32),
        small[6],
        ga[width : 2 * width].astype(f32),
        small[7],
        ga[2 * width : 3 * width].astype(f32),
        small[8],
        ga[3 * width :].astype(f32),
        small[2],
        small[0],
        small[1],
        g_up.astype(f32),
        g_upbias,
        gff[:units].astype(f32),
        small[5],
        small[3],
        small[4],
    )


def pick(mesh):
    def per_device(*args):
        tokens, span_sizes, w_up = args[0], args[2], args[13]
        rows, width = tokens.shape
        fits = (
            mesh.shape["tensor"] == 2
            and span_sizes.shape[0] == 1
            and rows % TILE == 0
            and width % TILE == 0
            and w_up.shape[1] % width == 0
            and w_up.shape[1] // width <= 3
            and mesh.shape["dp"] in (8, 16, 32)
            and width % (16 * mesh.shape["dp"]) == 0
        )
        return pair_device(*args) if fits else general_device(*args)

    return per_device


def solution(mesh):
    return jax.shard_map(
        pick(mesh),
        mesh=mesh,
        in_specs=(
            P(("dp", "tensor"), None),
            P("dp"),
            P("dp"),
            P(),
            P(),
            P(),
            P(),
            P(),
            P(),
            P(),
            P(),
            P(),
            P(),
            P(None, "tensor"),
            P("tensor"),
            P("tensor", None),
            P(),
            P(),
            P(),
            P(("dp", "tensor"), None),
        ),
        out_specs=(
            P(("dp", "tensor"), None),
            P(("dp", "tensor"), None),
            P(),
            P(),
            P(),
            P(),
            P(),
            P(),
            P(),
            P(),
            P(),
            P(),
            P(None, "tensor"),
            P("tensor"),
            P("tensor", None),
            P(),
            P(),
            P(),
        ),
        check_vma=False,
    )
```

```python
import functools
import math

import jax
import jax.numpy as jnp
from jax import lax
from jax.experimental import pallas as pl
from jax.experimental.pallas import tpu as pltpu
from jax.sharding import PartitionSpec as P

HEADS = 12
HD = 64
SUBLEN = 32


highest = lax.Precision.HIGHEST
norm_eps = 1e-05


def norm_forward(value, gain, shift):
    mean = jnp.mean(value, axis=-1, keepdims=True)
    centred = value - mean
    scale = lax.rsqrt(jnp.mean(centred * centred, axis=-1, keepdims=True) + norm_eps)
    normal = centred * scale
    return (normal * gain + shift, normal, scale)


def norm_backward(grad, normal, scale, gain):
    along = grad * gain
    inner = (
        along
        - jnp.mean(along, axis=-1, keepdims=True)
        - normal * jnp.mean(along * normal, axis=-1, keepdims=True)
    )
    return (inner * scale, jnp.sum(grad * normal, axis=0), jnp.sum(grad, axis=0))


def gelu_slope(pre):
    normal_cdf = 0.5 * (1.0 + jax.scipy.special.erf(pre * (1.0 / math.sqrt(2.0))))
    return normal_cdf + pre * jnp.exp(-0.5 * pre * pre) * (1.0 / math.sqrt(2.0 * math.pi))


def reach_table(count, span):
    slot_index = jnp.arange(count, dtype=jnp.int32)
    final = (slot_index * SUBLEN // span + 1) * span // SUBLEN - 1
    return (slot_index[None, :] <= final[:, None]).astype(jnp.float32)


def features(rows, w_joint, b_joint, cosine, sine):
    length = rows.shape[0]
    width = rows.shape[1]
    proj = jnp.dot(rows, w_joint, preferred_element_type=jnp.float32) + b_joint
    relu_query = jax.nn.relu(proj[:, :width]).reshape(length, HEADS, HD)
    relu_key = jax.nn.relu(proj[:, width : 2 * width]).reshape(length, HEADS, HD) * (1.0 / HD)
    q_feat = jnp.concatenate([relu_query * cosine, relu_query * sine], axis=-1).astype(jnp.bfloat16)
    k_feat = jnp.concatenate([relu_key * cosine, relu_key * sine], axis=-1).astype(jnp.bfloat16)
    v_low = proj[:, 2 * width :].astype(jnp.bfloat16)
    return (q_feat, k_feat, v_low)


def local_blocks(k_feat, v_low):
    count = k_feat.shape[0] // SUBLEN
    k_sub = k_feat.reshape(count, SUBLEN, HEADS, 2 * HD)
    v_sub = v_low.reshape(count, SUBLEN, HEADS, HD)
    blocks = jnp.einsum("tjhf,tjhd->thfd", k_sub, v_sub, preferred_element_type=jnp.float32)
    k_total = jnp.sum(k_sub.astype(jnp.float32), axis=1)
    return (blocks, k_total)


def attend_core(q_feat, k_feat, v_low, blocks, k_total, reach, extra_blocks, extra_keys):
    count = q_feat.shape[0] // SUBLEN
    q_sub = q_feat.reshape(count, SUBLEN, HEADS, 2 * HD)
    k_sub = k_feat.reshape(count, SUBLEN, HEADS, 2 * HD)
    v_sub = v_low.reshape(count, SUBLEN, HEADS, HD)
    state_low = (
        jnp.einsum("st,thfd->shfd", reach, blocks, precision=highest) + extra_blocks
    ).astype(jnp.bfloat16)
    z_sum = jnp.einsum("st,thf->shf", reach, k_total, precision=highest) + extra_keys
    numer = jnp.einsum("sihf,shfd->sihd", q_sub, state_low, preferred_element_type=jnp.float32)
    denom = jnp.einsum("sihf,shf->sih", q_sub.astype(jnp.float32), z_sum, precision=highest) + 1.0
    return (q_sub, k_sub, v_sub, state_low, z_sum, numer, denom)


def back_first(parts, grad_mixed):
    q_sub, k_sub, v_sub, state_low, z_sum, numer, denom = parts
    count = q_sub.shape[0]
    grad_out = grad_mixed.reshape(count, SUBLEN, HEADS, HD).astype(jnp.float32)
    d_numer = grad_out / denom[..., None]
    d_denom = -jnp.sum(grad_out * numer, axis=-1) / (denom * denom)
    q_wide = q_sub.astype(jnp.float32)
    d_query = jnp.einsum(
        "sihd,shfd->sihf", d_numer, state_low.astype(jnp.float32), precision=highest
    )
    d_query = d_query + d_denom[..., None] * z_sum[:, None]
    d_state = jnp.einsum("sihf,sihd->shfd", q_wide, d_numer, precision=highest)
    d_zsum = jnp.einsum("sihf,sih->shf", q_wide, d_denom, precision=highest)
    return (d_query, d_state, d_zsum)


def back_second(parts, reach, d_state, d_zsum, later_blocks, later_keys):
    q_sub, k_sub, v_sub = (parts[0], parts[1], parts[2])
    d_blocks = jnp.einsum("st,shfd->thfd", reach, d_state, precision=highest) + later_blocks
    d_ktotal = jnp.einsum("st,shf->thf", reach, d_zsum, precision=highest) + later_keys
    d_key = (
        jnp.einsum("thfd,tjhd->tjhf", d_blocks, v_sub.astype(jnp.float32), precision=highest)
        + d_ktotal[:, None]
    )
    d_value = jnp.einsum("thfd,tjhf->tjhd", d_blocks, k_sub.astype(jnp.float32), precision=highest)
    return (d_key, d_value)


def feature_grads(q_feat, k_feat, d_qf, d_kf, d_val, cos_part, sin_part):
    size = q_feat.shape[0]
    d_qf = d_qf.reshape(size, HEADS, 2 * HD)
    d_kf = d_kf.reshape(size, HEADS, 2 * HD)
    d_query = jnp.where(
        q_feat[..., :HD] > 0, d_qf[..., :HD] * cos_part + d_qf[..., HD:] * sin_part, 0.0
    )
    d_key = jnp.where(
        k_feat[..., :HD] > 0,
        (d_kf[..., :HD] * cos_part + d_kf[..., HD:] * sin_part) * (1.0 / HD),
        0.0,
    )
    return jnp.concatenate(
        [
            d_query.reshape(size, HEADS * HD),
            d_key.reshape(size, HEADS * HD),
            d_val.reshape(size, HEADS * HD),
        ],
        axis=1,
    )


def general_device(
    tokens,
    positions,
    span_sizes,
    w_query,
    b_query,
    w_key,
    b_key,
    w_value,
    b_value,
    w_out,
    b_out,
    norm1_gain,
    norm1_bias,
    w_up,
    b_up,
    w_down,
    b_down,
    norm2_gain,
    norm2_bias,
    out_grad,
):
    rank = lax.axis_index("tensor")
    tensor_count = lax.axis_size("tensor")
    own = tokens.shape[0]
    width = tokens.shape[1]
    seqs = span_sizes.shape[0]
    group = own * tensor_count
    length = group // seqs
    start = rank * own
    w_joint = jnp.concatenate([w_query, w_key, w_value], axis=1)
    b_joint = jnp.concatenate([b_query, b_key, b_value]).astype(jnp.float32)
    gain_one = norm1_gain.astype(jnp.float32)
    gain_two = norm2_gain.astype(jnp.float32)
    gathered = lax.all_gather(tokens, "tensor", axis=0, tiled=True)
    angle = math.pi / 2 * positions.astype(jnp.float32) / (3 * length)
    cosine = jnp.cos(angle).reshape(seqs, length, 1, 1)
    sine = jnp.sin(angle).reshape(seqs, length, 1, 1)

    def seq_forward(items):
        rows, cos_part, sin_part, span = items
        q_feat, k_feat, v_low = features(rows, w_joint, b_joint, cos_part, sin_part)
        blocks_seq, ktot_seq = local_blocks(k_feat, v_low)
        parts = attend_core(
            q_feat,
            k_feat,
            v_low,
            blocks_seq,
            ktot_seq,
            reach_table(q_feat.shape[0] // SUBLEN, span),
            0.0,
            0.0,
        )
        mixed_seq = (
            (parts[5] / parts[6][..., None]).reshape(rows.shape[0], width).astype(jnp.bfloat16)
        )
        return (mixed_seq, q_feat, k_feat, v_low)

    mixed, q_all, k_all, v_all = lax.map(
        seq_forward, (gathered.reshape(seqs, length, width), cosine, sine, span_sizes)
    )
    mixed = mixed.reshape(group, width)
    mixed_own = lax.dynamic_slice_in_dim(mixed, start, own, 0)
    resid = (
        tokens.astype(jnp.float32)
        + jnp.dot(mixed_own, w_out, preferred_element_type=jnp.float32)
        + b_out.astype(jnp.float32)
    )
    hidden, normal_one, scale_one = norm_forward(resid, gain_one, norm1_bias.astype(jnp.float32))
    hidden_low = hidden.astype(jnp.bfloat16)
    rows_in = lax.all_gather(hidden_low, "tensor", axis=0, tiled=True)
    pre = jnp.dot(rows_in, w_up, preferred_element_type=jnp.float32) + b_up.astype(jnp.float32)
    act_low = jax.nn.gelu(pre, approximate=False).astype(jnp.bfloat16)
    branch = lax.psum_scatter(
        jnp.dot(act_low, w_down, preferred_element_type=jnp.float32),
        "tensor",
        scatter_dimension=0,
        tiled=True,
    )
    summed = hidden + branch + b_down.astype(jnp.float32)
    result, normal_two, scale_two = norm_forward(summed, gain_two, norm2_bias.astype(jnp.float32))
    d_sum, d_gain_two, d_bias_two = norm_backward(
        out_grad.astype(jnp.float32), normal_two, scale_two, gain_two
    )
    d_bdown = jnp.sum(d_sum, axis=0)
    d_sum_low = d_sum.astype(jnp.bfloat16)
    rows_grad = lax.all_gather(d_sum_low, "tensor", axis=0, tiled=True)
    g_down = jnp.dot(act_low.T, rows_grad, preferred_element_type=jnp.float32)
    d_pre = jnp.dot(rows_grad, w_down.T, preferred_element_type=jnp.float32) * gelu_slope(pre)
    g_upbias = jnp.sum(d_pre, axis=0)
    d_pre_low = d_pre.astype(jnp.bfloat16)
    g_up = jnp.dot(rows_in.T, d_pre_low, preferred_element_type=jnp.float32)
    d_hidden = lax.psum_scatter(
        jnp.dot(d_pre_low, w_up.T, preferred_element_type=jnp.float32),
        "tensor",
        scatter_dimension=0,
        tiled=True,
    )
    g_up, g_upbias, g_down = (
        lax.psum(g_up.astype(jnp.bfloat16), "dp").astype(jnp.float32),
        lax.psum(g_upbias.astype(jnp.bfloat16), "dp").astype(jnp.float32),
        lax.psum(g_down.astype(jnp.bfloat16), "dp").astype(jnp.float32),
    )
    d_hidden = d_hidden + d_sum
    d_resid, d_gain_one, d_bias_one = norm_backward(d_hidden, normal_one, scale_one, gain_one)
    d_bout = jnp.sum(d_resid, axis=0)
    d_gain_one, d_bias_one, d_gain_two, d_bias_two, d_bout, d_bdown = lax.psum(
        (d_gain_one, d_bias_one, d_gain_two, d_bias_two, d_bout, d_bdown), ("dp", "tensor")
    )
    d_resid_low = d_resid.astype(jnp.bfloat16)
    rows_back = lax.all_gather(d_resid_low, "tensor", axis=0, tiled=True)
    g_out = jnp.dot(mixed.T, rows_back, preferred_element_type=jnp.float32)
    d_mixed = jnp.dot(rows_back, w_out.T, preferred_element_type=jnp.float32).astype(jnp.bfloat16)

    def seq_backward(items):
        q_feat, k_feat, v_low, cos_part, sin_part, span, grad_mixed = items
        blocks_seq, ktot_seq = local_blocks(k_feat, v_low)
        reach = reach_table(q_feat.shape[0] // SUBLEN, span)
        parts = attend_core(q_feat, k_feat, v_low, blocks_seq, ktot_seq, reach, 0.0, 0.0)
        d_qf, d_state, d_zsum = back_first(parts, grad_mixed)
        d_kf, d_val = back_second(parts, reach, d_state, d_zsum, 0.0, 0.0)
        joint = feature_grads(q_feat, k_feat, d_qf, d_kf, d_val, cos_part, sin_part)
        return (joint.astype(jnp.bfloat16), jnp.sum(joint, axis=0))

    d_joint, d_jbias = lax.map(
        seq_backward,
        (q_all, k_all, v_all, cosine, sine, span_sizes, d_mixed.reshape(seqs, length, width)),
    )
    d_joint = d_joint.reshape(group, 3 * width)
    d_jbias = jnp.sum(d_jbias, axis=0)
    g_joint = jnp.dot(gathered.T, d_joint, preferred_element_type=jnp.float32)
    d_joint_own = lax.dynamic_slice_in_dim(d_joint, start, own, 0)
    d_tokens = d_resid + jnp.dot(d_joint_own, w_joint.T, preferred_element_type=jnp.float32)
    g_joint, g_out, d_jbias = lax.psum((g_joint, g_out, d_jbias), "dp")
    return (
        result.astype(jnp.bfloat16),
        d_tokens,
        g_joint[:, :width],
        d_jbias[:width],
        g_joint[:, width : 2 * width],
        d_jbias[width : 2 * width],
        g_joint[:, 2 * width :],
        d_jbias[2 * width :],
        g_out,
        d_bout,
        d_gain_one,
        d_bias_one,
        g_up,
        g_upbias,
        g_down,
        d_bdown,
        d_gain_two,
        d_bias_two,
    )


f32 = jnp.float32
bf16 = jnp.bfloat16
MESH = pl.DeviceIdType.MESH
LANES = 2 * HD
TILE = 256
ROWBLOCK = 32
FF_CUTS = 2
A_CUTS = 1


def tile_at(index, size):
    return pl.ds(pl.multiple_of(index * size, size), size)


def contract(left, right, left_dim, right_dim, precision=None):
    return lax.dot_general(
        left,
        right,
        (((left_dim,), (right_dim,)), ((), ())),
        precision=precision,
        preferred_element_type=f32,
    )


def mm(left, right):
    return contract(left, right, 1, 0)


def mm_nt(left, right):
    return contract(left, right, 1, 1)


def mm_tn(left, right):
    return contract(left, right, 0, 0)


def head_masks():
    lane = lax.broadcasted_iota(jnp.int32, (1, LANES), 1)
    first = (lane < HD).astype(f32)
    return first, 1.0 - first


def pair_mask():
    row = lax.broadcasted_iota(jnp.int32, (LANES, LANES), 0)
    col = lax.broadcasted_iota(jnp.int32, (LANES, LANES), 1)
    return ((row < HD) == (col < HD)).astype(f32)


def first_row(block, which):
    row = lax.broadcasted_iota(jnp.int32, block.shape, 0)
    return jnp.where(row == which, block, 0.0)


def column_of(block, which):
    return contract(first_row(block, which), jnp.ones((8, LANES), f32), 0, 0, highest)


def squeeze_pair(square):
    return square[:HD] + square[HD:]


def spread_pair(half, mask):
    return jnp.concatenate([half, half], axis=0).astype(f32) * mask


def fold8(value):
    total = value[0:8]
    for start in range(8, value.shape[0], 8):
        total = total + value[start : start + 8]
    return total


def angle_tables(trig, span, cosb, sinb, ctab):
    rows = cosb.shape[0]
    block = trig[...]
    cosb[...] = column_of(block, 0)
    sinb[...] = column_of(block, 1)
    both = contract(block, block, 0, 0, highest)
    row = lax.broadcasted_iota(jnp.int32, (rows, rows), 0)
    col = lax.broadcasted_iota(jnp.int32, (rows, rows), 1)
    seen = col <= (row | (span[0, 0] - 1))
    ctab[...] = jnp.where(seen, both * (1.0 / HD), 0.0)


def peer_copy(src, dst, sems, slot, device):
    return pltpu.make_async_remote_copy(
        src_ref=src,
        dst_ref=dst,
        send_sem=sems[0].at[slot],
        recv_sem=sems[1].at[slot],
        device_id=device,
        device_id_type=MESH,
    )


def meet(devices):
    barrier = pltpu.get_barrier_semaphore()
    for device in devices:
        pl.semaphore_signal(barrier, inc=1, device_id=device, device_id_type=MESH)
    pl.semaphore_wait(barrier, len(devices))


def front_kernel(
    tok, trig, span, vec, wq, wk, wv, wo, wup, wdn, og,
    res_o, small_o, gff_o, dhs_o, dho_o, mixb, mixf, inv, rq, rk, vv, nrm, scl, st_o, z_o,
    hbuf, act, slope, dbuf, dpre, hid, tsend, trecv, zsend, zrecv, bsend, brecv,
    numer, denom, ctab, cosb, sinb, acc, bup, send, recv,
):
    sems = (send, recv)
    rows, width = tok.shape
    units = wup.shape[1]
    pairs = width // LANES
    tiles = width // TILE
    rank = lax.axis_index("tensor")
    peer = (lax.axis_index("dp"), 1 - rank)
    late = rank.astype(f32)
    own, other = pl.ds(0, rows), pl.ds(rows, rows)
    meet([peer])

    for which, (weight, target) in enumerate(((wq, rq), (wk, rk), (wv, vv))):

        @pl.loop(0, tiles)
        def _(j, which=which, weight=weight, target=target):
            cols = tile_at(j, TILE)
            y = mm(tok[...], weight[:, cols]) + vec[which : which + 1, cols]
            if which < 2:
                y = jnp.maximum(y, 0.0)
            target[:, cols] = y.astype(bf16)

    angle_tables(trig, span, cosb, sinb, ctab)
    diag = pair_mask()
    first, second = head_masks()
    first_low, second_low = first.astype(bf16), second.astype(bf16)

    @pl.loop(0, pairs)
    def _(p):
        lanes = tile_at(p, LANES)
        k = rk[:, lanes].astype(f32) * (1.0 / HD)
        v = vv[:, lanes]
        kc, ks = (k * cosb[...]).astype(bf16), (k * sinb[...]).astype(bf16)
        tsend[p, 0] = squeeze_pair(mm_tn(kc, v) * diag).astype(bf16)
        tsend[p, 1] = squeeze_pair(mm_tn(ks, v) * diag).astype(bf16)
        sum_c = jnp.sum(kc.astype(f32), axis=0, keepdims=True)
        sum_s = jnp.sum(ks.astype(f32), axis=0, keepdims=True)
        row = lax.broadcasted_iota(jnp.int32, (8, LANES), 0)
        zsend[p] = jnp.where(row == 0, sum_c, jnp.where(row == 1, sum_s, 0.0))

    state_copy = peer_copy(tsend, trecv, sems, 0, peer)
    key_copy = peer_copy(zsend, zrecv, sems, 1, peer)
    state_copy.start()
    key_copy.start()

    @pl.loop(0, pairs)
    def _(p):
        lanes = tile_at(p, LANES)
        q, k, v = rq[:, lanes], rk[:, lanes], vv[:, lanes]
        parts = []
        for mask, rest in ((first_low, second_low), (second_low, first_low)):
            score = mm_nt(q * mask, k)
            prob = (score * ctab[...]).astype(bf16)
            parts.append(mm(prob, v * mask + rest))
        numer[:, lanes] = parts[0] * first + parts[1] * second
        denom[:, lanes] = pltpu.roll(parts[0] * second + parts[1] * first, HD, 1)

    state_copy.wait()
    key_copy.wait()

    @pl.loop(0, pairs)
    def _(p):
        lanes = tile_at(p, LANES)
        q = rq[:, lanes].astype(f32)
        qc, qs = (q * cosb[...]).astype(bf16), (q * sinb[...]).astype(bf16)
        st_o[p] = (trecv[p].astype(f32) * late).astype(bf16)
        zblock = zrecv[p] * late
        z_o[p] = zblock
        num, den = numer[:, lanes], denom[:, lanes] + 1.0
        for part, feat in ((0, qc), (1, qs)):
            num += mm(feat, spread_pair(st_o[p, part], diag).astype(bf16))
            den += mm(feat, (column_of(zblock, part) * diag).astype(bf16))
        reciprocal = 1.0 / den
        mix = num * reciprocal
        inv[:, lanes] = reciprocal
        mixf[:, lanes] = mix
        mixb[:, lanes] = mix.astype(bf16)

    @pl.loop(0, tiles)
    def _(j):
        cols = tile_at(j, TILE)
        hid[:, cols] = tok[:, cols].astype(f32) + mm(mixb[...], wo[:, cols]) + vec[3:4, cols]

    @pl.loop(0, rows // ROWBLOCK)
    def _(i):
        at = tile_at(i, ROWBLOCK)
        value = hid[at, :]
        centred = value - jnp.mean(value, axis=-1, keepdims=True)
        scale = lax.rsqrt(jnp.mean(centred * centred, axis=-1, keepdims=True) + norm_eps)
        normal = centred * scale
        hidden = normal * vec[4:5, :] + vec[5:6, :]
        nrm[at, :] = normal
        scl[at, :] = jnp.broadcast_to(scale, (ROWBLOCK, LANES))
        hid[at, :] = hidden
        hbuf[at, :] = hidden.astype(bf16)

    hidden_copy = peer_copy(hbuf.at[own], hbuf.at[other], sems, 2, peer)
    hidden_copy.start()

    def raise_rows(part):
        for half in range(units // width):

            @pl.loop(0, tiles)
            def _(j, half=half):
                cols = tile_at(half * tiles + j, TILE)
                pre = mm(hbuf[part, :], wup[:, cols]) + vec[9 + half : 10 + half, tile_at(j, TILE)]
                cdf = 0.5 * (1.0 + lax.erf(pre * (1.0 / math.sqrt(2.0))))
                act[part, cols] = (pre * cdf).astype(bf16)
                slope[part, cols] = cdf + pre * jnp.exp(-0.5 * pre * pre) * (
                    1.0 / math.sqrt(2.0 * math.pi)
                )

    raise_rows(own)
    hidden_copy.wait()
    raise_rows(other)

    @pl.loop(0, tiles)
    def _(j):
        cols = tile_at(j, TILE)
        bsend[:, cols] = mm(act[other, :], wdn[:, cols]).astype(bf16)

    branch_copy = peer_copy(bsend, brecv, sems, 3, peer)
    branch_copy.start()

    @pl.loop(0, tiles)
    def _(j):
        cols = tile_at(j, TILE)
        hid[:, cols] += mm(act[own, :], wdn[:, cols]) + vec[6:7, cols]

    acc[...] = jnp.zeros_like(acc)
    branch_copy.wait()

    @pl.loop(0, rows // ROWBLOCK)
    def _(i):
        at = tile_at(i, ROWBLOCK)
        value = hid[at, :] + brecv[at, :].astype(f32)
        centred = value - jnp.mean(value, axis=-1, keepdims=True)
        scale = lax.rsqrt(jnp.mean(centred * centred, axis=-1, keepdims=True) + norm_eps)
        normal = centred * scale
        res_o[at, :] = (normal * vec[7:8, :] + vec[8:9, :]).astype(bf16)
        grad = og[at, :].astype(f32)
        along = grad * vec[7:8, :]
        inner = (
            along
            - jnp.mean(along, axis=-1, keepdims=True)
            - normal * jnp.mean(along * normal, axis=-1, keepdims=True)
        ) * scale
        dho_o[at, :] = inner
        dbuf[at, :] = inner.astype(bf16)
        acc[0:8, :] += fold8(grad * normal)
        acc[8:16, :] += fold8(grad)
        acc[16:24, :] += fold8(inner)

    grad_copy = peer_copy(dbuf.at[own], dbuf.at[other], sems, 4, peer)
    grad_copy.start()

    small_o[...] = jnp.zeros_like(small_o)
    for slot in range(3):
        small_o[3 + slot : 4 + slot, :] = jnp.sum(
            acc[8 * slot : 8 * slot + 8, :], axis=0, keepdims=True
        )
    bup[...] = jnp.zeros_like(bup)

    def lower_rows(part):
        @pl.loop(0, units // TILE)
        def _(j):
            cols = tile_at(j, TILE)
            d_pre = mm_nt(dbuf[part, :], wdn[cols, :]) * slope[part, cols]
            bup[:, cols] += fold8(d_pre)
            dpre[part, cols] = d_pre.astype(bf16)

    lower_rows(own)
    grad_copy.wait()
    lower_rows(other)

    @pl.loop(0, tiles)
    def _(j):
        cols = tile_at(j, TILE)
        dhs_o[:, cols] = mm_nt(dpre[other, :], wup[cols, :]).astype(bf16)
        dho_o[:, cols] += mm_nt(dpre[own, :], wup[cols, :])

    for half in range(units // width):
        line = jnp.sum(bup[:, half * width : (half + 1) * width], axis=0, keepdims=True)
        small_o[9 + half : 10 + half, :] = line * (1.0 - late)
        small_o[9 + units // width + half : 10 + units // width + half, :] = line * late

    @pl.loop(0, units // TILE)
    def _(j):
        cols = tile_at(j, TILE)
        gff_o[cols, :] = mm_tn(act[:, cols], dbuf[...]).astype(bf16)

    for half in range(units // width):

        @pl.loop(0, tiles)
        def _(j, half=half):
            gff_o[pl.ds(units + half * width, width), tile_at(j, TILE)] = mm_tn(
                hbuf[...], dpre[:, tile_at(half * tiles + j, TILE)]
            ).astype(bf16)


def grid_place():
    dp = lax.axis_index("dp")
    core, chip = dp % 2, dp // 2
    return core, chip % 2, chip // 2


def ring_device(spot, depth, core):
    far = spot // depth
    z = far * (2 * depth - 1 - spot) + (1 - far) * spot
    return ((z * 2 + far) * 2 + core, lax.axis_index("tensor"))


def add_rows(target, rows, block):
    target[rows, :] = (target[rows, :].astype(f32) + block.astype(f32)).astype(bf16)


def back_kernel(
    count, tok, trig, span, vec, wq, wk, wv, wo,
    dhs, dho, mixb, mixf, inv, rq, rk, vv, nrm, scl, st, z, small_in, gff,
    dtok_o, ff_o, a_o, small_o,
    dhr, dres, dlow, dn, xs, dsend, drecv, dzs, dzr, dq, dk, dv, dql, dkl, dvl,
    ctab, cosb, sinb, acc, ga, small, cr_ff, cr_a, px, xr, acc_ff, acc_a, rs_ff, rs_a, small_r,
    send, recv, r_send, r_recv, g_send, g_recv, x_send, x_recv, y_send, y_recv, m_send, m_recv,
):
    sems = (send, recv)
    rows, width = tok.shape
    pairs = width // LANES
    tiles = width // TILE
    depth = count // 2
    half = gff.shape[0] // 2
    quarter = width
    rank = lax.axis_index("tensor")
    dp = lax.axis_index("dp")
    early = 1.0 - rank.astype(f32)
    core, y, z_place = grid_place()
    spot = y * (2 * depth - 1 - z_place) + (1 - y) * z_place
    sibling = (dp + 1 - 2 * core, rank)
    peer = (dp, 1 - rank)
    ahead = ring_device((spot + 1) % count, depth, core)
    behind = ring_device((spot + count - 1) % count, depth, core)
    swaps = [sibling, peer, (dp + 2 - 4 * y, rank)]
    step = 1
    while step < depth:
        bit = (z_place // step) % 2
        swaps.append((dp + 4 * (step - 2 * step * bit), rank))
        step *= 2
    meet([ahead, behind] + swaps)

    def part_rows(which, size):
        return pl.ds(pl.multiple_of(which * size, size), size)

    core_ff = peer_copy(gff.at[part_rows(1 - core, half), :], cr_ff, sems, 3, sibling)
    core_a = peer_copy(ga.at[part_rows(1 - core, 2 * quarter), :], cr_a, sems, 4, sibling)
    hidden_copy = peer_copy(dhs, dhr, sems, 0, peer)
    hidden_copy.start()
    core_ff.start()

    ff_streams, a_streams = [], []
    for kind, (cuts, group) in enumerate(((FF_CUTS, ff_streams), (A_CUTS, a_streams))):
        own = acc_a if kind else acc_ff
        size = own.shape[0] // count // 2
        first_number = 2 * FF_CUTS * kind
        for way in range(2):
            for cut in range(cuts):
                cols = pl.ds(cut * (width // cuts), width // cuts)
                number = first_number + way * cuts + cut
                group.append((number, kind, way, cols, size))
    slots = (rs_ff, rs_a)
    sums = (acc_ff, acc_a)
    outs = (ff_o, a_o)
    bases = (core * half, (core * 2 + rank) * quarter)

    def chunk_rows(at, stream, base):
        _, _, way, _, size = stream
        return pl.ds(pl.multiple_of(base + (at % count) * 2 * size + way * size, size), size)

    def toward(stream):
        return behind if stream[2] else ahead

    def sign(stream):
        return -1 if stream[2] else 1

    def spread_copy(stream, at, s):
        number, kind, way, cols, _ = stream
        return pltpu.make_async_remote_copy(
            src_ref=sums[kind].at[chunk_rows(at, stream, 0), cols],
            dst_ref=slots[kind].at[s, way, :, cols],
            send_sem=r_send.at[number, s],
            recv_sem=r_recv.at[number, s],
            device_id=toward(stream),
            device_id_type=MESH,
        )

    def gather_copy(stream, at, s):
        number, kind, _, cols, _ = stream
        where = outs[kind].at[chunk_rows(at, stream, bases[kind]), cols]
        return pltpu.make_async_remote_copy(
            src_ref=where,
            dst_ref=where,
            send_sem=g_send.at[number, s],
            recv_sem=g_recv.at[number, s],
            device_id=toward(stream),
            device_id_type=MESH,
        )

    def across_copy(stream, at, s, base):
        number, _, _, cols, _ = stream
        where = a_o.at[chunk_rows(at, stream, base), cols]
        return pltpu.make_async_remote_copy(
            src_ref=where,
            dst_ref=where,
            send_sem=x_send.at[number - 2 * FF_CUTS, s],
            recv_sem=x_recv.at[number - 2 * FF_CUTS, s],
            device_id=peer,
            device_id_type=MESH,
        )

    def fold_copy(stream, s):
        number, _, way, cols, _ = stream
        at = spot + count - sign(stream) * s
        return pltpu.make_async_remote_copy(
            src_ref=px.at[chunk_rows(at, stream, 0), cols],
            dst_ref=xr.at[s, way, :, cols],
            send_sem=y_send.at[number - 2 * FF_CUTS, s],
            recv_sem=y_recv.at[number - 2 * FF_CUTS, s],
            device_id=peer,
            device_id_type=MESH,
        )

    def own_part(stream, at, s):
        _, kind, way, cols, _ = stream
        rows_in = chunk_rows(at, stream, bases[kind])
        if kind == 0:
            return gff[rows_in, cols].astype(f32) + cr_ff[chunk_rows(at, stream, 0), cols].astype(f32)
        fold_copy(stream, s).wait_recv()
        return (
            ga[rows_in, cols].astype(f32)
            + cr_a[chunk_rows(at, stream, rank * quarter), cols].astype(f32)
            + xr[s, way, :, cols].astype(f32)
        )

    def ring_first(streams):
        for stream in streams:
            _, kind, _, cols, _ = stream
            at = spot + count
            sums[kind][chunk_rows(at, stream, 0), cols] = own_part(stream, at, 0).astype(bf16)
            spread_copy(stream, at, 0).start()

    def ring_spread(streams, s, last):
        for stream in streams:
            _, kind, way, cols, _ = stream
            at = spot + count - sign(stream) * (s + 1)
            own = own_part(stream, at, s + 1)
            spread_copy(stream, at, s).wait_recv()
            total = (own + slots[kind][s, way, :, cols].astype(f32)).astype(bf16)
            if last:
                outs[kind][chunk_rows(at, stream, bases[kind]), cols] = total
                gather_copy(stream, at, 0).start()
                if kind:
                    across_copy(stream, at, 0, bases[1]).start()
            else:
                sums[kind][chunk_rows(at, stream, 0), cols] = total
                spread_copy(stream, at, s + 1).start()

    def ring_gather(streams, s, last):
        for stream in streams:
            kind = stream[1]
            at = spot + 2 * count - sign(stream) * s
            gather_copy(stream, at, s).wait_recv()
            if not last:
                gather_copy(stream, at, s + 1).start()
            if kind:
                across_copy(stream, at, s + 1, bases[1]).start()

    angle_tables(trig, span, cosb, sinb, ctab)
    diag = pair_mask()
    first, second = head_masks()
    first_low, second_low = first.astype(bf16), second.astype(bf16)
    diag_low = diag.astype(bf16)
    acc[...] = jnp.zeros_like(acc)
    small[...] = small_in[...]
    core_ff.wait()
    ring_first(ff_streams)
    hidden_copy.wait()
    ring_spread(ff_streams, 0, False)

    @pl.loop(0, rows // ROWBLOCK)
    def _(i):
        at = tile_at(i, ROWBLOCK)
        grad = dho[at, :] + dhr[at, :].astype(f32)
        normal = nrm[at, :]
        along = grad * vec[4:5, :]
        inner = (
            along
            - jnp.mean(along, axis=-1, keepdims=True)
            - normal * jnp.mean(along * normal, axis=-1, keepdims=True)
        ) * scl[at, 0:1]
        dres[at, :] = inner
        dlow[at, :] = inner.astype(bf16)
        acc[0:8, :] += fold8(grad * normal)
        acc[8:16, :] += fold8(grad)
        acc[16:24, :] += fold8(inner)

    for slot in range(3):
        small[slot : slot + 1, :] = jnp.sum(
            acc[8 * slot : 8 * slot + 8, :], axis=0, keepdims=True
        )

    @pl.loop(0, tiles)
    def _(j):
        cols = tile_at(j, TILE)
        d_mixed = mm_nt(dlow[...], wo[cols, :]).astype(bf16).astype(f32)
        d_numer = (d_mixed * inv[:, cols]).astype(bf16)
        dn[:, cols] = d_numer
        xs[:, cols] = (d_numer.astype(f32) * mixf[:, cols]).astype(bf16)

    @pl.loop(0, pairs)
    def _(p):
        lanes = tile_at(p, LANES)
        q = rq[:, lanes].astype(f32)
        qc, qs = (q * cosb[...]).astype(bf16), (q * sinb[...]).astype(bf16)
        d_numer = dn[:, lanes]
        dsend[p, 0] = squeeze_pair(mm_tn(qc, d_numer) * diag).astype(bf16)
        dsend[p, 1] = squeeze_pair(mm_tn(qs, d_numer) * diag).astype(bf16)
        across = mm(xs[:, lanes], diag_low)
        sum_c = jnp.sum(qc.astype(f32) * across, axis=0, keepdims=True)
        sum_s = jnp.sum(qs.astype(f32) * across, axis=0, keepdims=True)
        row = lax.broadcasted_iota(jnp.int32, (8, LANES), 0)
        dzs[p] = -jnp.where(row == 0, sum_c, jnp.where(row == 1, sum_s, 0.0))

    state_copy = peer_copy(dsend, drecv, sems, 1, peer)
    key_copy = peer_copy(dzs, dzr, sems, 2, peer)
    state_copy.start()
    key_copy.start()
    ring_spread(ff_streams, 1, False)

    @pl.loop(0, tiles)
    def _(j):
        cols = tile_at(j, TILE)
        ga[tile_at(3 * tiles + j, TILE), :] = mm_tn(mixb[:, cols], dlow[...]).astype(bf16)

    def inside(p):
        lanes = tile_at(p, LANES)
        q, k, v = rq[:, lanes], rk[:, lanes], vv[:, lanes]
        d_numer = dn[:, lanes]
        turned = -pltpu.roll(xs[:, lanes].astype(f32), HD, 1)
        turned = turned.astype(bf16)
        sum_q = sum_k = sum_v = 0.0
        for mask, rest in ((first_low, second_low), (second_low, first_low)):
            q_head, k_head, d_head = q * mask, k * mask, d_numer * mask
            table = ctab[...]
            prob = (mm_nt(q_head, k) * table).astype(bf16)
            d_prob = mm_nt(d_head + turned * rest, v * mask + rest)
            d_score = (d_prob * table).astype(bf16)
            sum_v += mm_tn(prob, d_head)
            sum_q += mm(d_score, k_head)
            sum_k += mm_tn(d_score, q_head)
        dq[:, lanes] = sum_q
        dk[:, lanes] = sum_k
        dv[:, lanes] = sum_v

    pl.loop(0, pairs // 2)(inside)
    ring_spread(ff_streams, 2, False)
    pl.loop(pairs // 2, pairs)(inside)
    ring_spread(ff_streams, 3, False)
    state_copy.wait()
    key_copy.wait()

    @pl.loop(0, pairs)
    def _(p):
        lanes = tile_at(p, LANES)
        q, v = rq[:, lanes].astype(f32), vv[:, lanes]
        k = rk[:, lanes].astype(f32)
        d_numer, x = dn[:, lanes], xs[:, lanes]
        sum_q, sum_k, sum_v = dq[:, lanes], dk[:, lanes], dv[:, lanes]
        zblock, dzblock = z[p], dzr[p] * early
        for part, wave in ((0, cosb[...]), (1, sinb[...])):
            state = spread_pair(st[p, part], diag).astype(bf16)
            zmat = (column_of(zblock, part) * diag).astype(bf16)
            sum_q += wave * (mm_nt(d_numer, state) - mm_nt(x, zmat))
            d_state = (spread_pair(drecv[p, part], diag) * early).astype(bf16)
            sum_k += wave * (mm_nt(v, d_state) + dzblock[part : part + 1, :]) * (1.0 / HD)
            sum_v += mm((k * wave * (1.0 / HD)).astype(bf16), d_state)
        sum_q = jnp.where(q > 0, sum_q, 0.0)
        sum_k = jnp.where(k > 0, sum_k, 0.0)
        dql[:, lanes] = sum_q.astype(bf16)
        dkl[:, lanes] = sum_k.astype(bf16)
        dvl[:, lanes] = sum_v.astype(bf16)
        for slot, value in ((6, sum_q), (7, sum_k), (8, sum_v)):
            small[slot : slot + 1, lanes] = jnp.sum(value, axis=0, keepdims=True)

    ring_spread(ff_streams, 4, False)

    for which, source in enumerate((dql, dkl, dvl)):

        @pl.loop(0, tiles)
        def _(j, which=which, source=source):
            ga[tile_at(which * tiles + j, TILE), :] = mm_tn(
                tok[:, tile_at(j, TILE)], source[...]
            ).astype(bf16)

    core_a.start()
    ring_spread(ff_streams, 5, False)

    @pl.loop(0, tiles)
    def _(j):
        cols = tile_at(j, TILE)
        dtok_o[:, cols] = (
            dres[:, cols]
            + mm_nt(dql[...], wq[cols, :])
            + mm_nt(dkl[...], wk[cols, :])
            + mm_nt(dvl[...], wv[cols, :])
        )

    def small_copy(index):
        return peer_copy(small_o.at[index], small_r.at[index], (m_send, m_recv), index, swaps[index])

    def swap_small(index):
        small_copy(index).wait()
        small_o[index + 1] = small_o[index] + small_r[index]
        if index + 1 < len(swaps):
            small_copy(index + 1).start()

    small_o[0] = small[...]
    small_copy(0).start()
    core_a.wait()

    @pl.loop(0, quarter // 96)
    def _(i):
        near = pl.ds(pl.multiple_of((core * 2 + 1 - rank) * quarter + i * 96, 96), 96)
        far = pl.ds(pl.multiple_of((1 - rank) * quarter + i * 96, 96), 96)
        px[tile_at(i, 96), :] = (ga[near, :].astype(f32) + cr_a[far, :].astype(f32)).astype(bf16)

    for s in range(3):
        for stream in a_streams:
            fold_copy(stream, s).start()
    ring_spread(ff_streams, count - 2, True)
    swap_small(0)
    ring_first(a_streams)

    @pl.loop(0, count - 2)
    def _(s):
        @pl.when(s + 3 < count)
        def _():
            for stream in a_streams:
                fold_copy(stream, s + 3).start()

        ring_gather(ff_streams, s, False)
        ring_spread(a_streams, s, False)

    ring_gather(ff_streams, count - 2, True)
    back_ff = peer_copy(
        ff_o.at[part_rows(core, half), :], ff_o.at[part_rows(core, half), :], sems, 5, sibling
    )
    back_ff.start()
    ring_spread(a_streams, count - 2, True)
    for index in range(1, len(swaps)):
        swap_small(index)

    @pl.loop(0, count - 2)
    def _(s):
        ring_gather(a_streams, s, False)

    ring_gather(a_streams, count - 2, True)
    other = (core * 2 + 1 - rank) * quarter

    @pl.loop(0, count)
    def _(s):
        for stream in a_streams:
            at = spot + 2 * count + sign(stream) * (1 - s)
            across_copy(stream, at, s, other).wait_recv()

    back_a = peer_copy(
        a_o.at[part_rows(core, 2 * quarter), :], a_o.at[part_rows(core, 2 * quarter), :], sems, 6, sibling
    )
    back_a.start()

    @pl.loop(0, count - 1)
    def _(s):
        for stream in ff_streams + a_streams:
            spread_copy(stream, spot, s).wait_send()
            gather_copy(stream, spot, s).wait_send()

    @pl.loop(0, count)
    def _(s):
        for stream in a_streams:
            across_copy(stream, spot, s, bases[1]).wait_send()
            fold_copy(stream, s).wait_send()

    back_ff.wait()
    back_a.wait()


def in_vmem(count):
    return [pl.BlockSpec(memory_space=pltpu.VMEM)] * count


def shaped(*items):
    return tuple(jax.ShapeDtypeStruct(shape, kind) for shape, kind in items)


def pair_device(
    tokens,
    positions,
    span_sizes,
    w_query,
    b_query,
    w_key,
    b_key,
    w_value,
    b_value,
    w_out,
    b_out,
    norm1_gain,
    norm1_bias,
    w_up,
    b_up,
    w_down,
    b_down,
    norm2_gain,
    norm2_bias,
    out_grad,
):
    rank = lax.axis_index("tensor")
    rows, width = tokens.shape
    units = w_up.shape[1]
    pairs = width // LANES
    length = positions.shape[0]
    places = lax.dynamic_slice_in_dim(positions, rank * rows, rows, 0)
    angle = math.pi / 2 * places.astype(f32) / (3 * length)
    line = lax.broadcasted_iota(jnp.int32, (8, rows), 0)
    trig = jnp.where(
        line == 0, jnp.cos(angle)[None], jnp.where(line == 1, jnp.sin(angle)[None], 0.0)
    )
    span = span_sizes.reshape(1, 1)
    vectors = [
        b_query, b_key, b_value, b_out, norm1_gain, norm1_bias, b_down, norm2_gain, norm2_bias, b_up,
    ]
    vec = jnp.concatenate(vectors).astype(f32).reshape(-1, width)
    vec = jnp.pad(vec, ((0, -vec.shape[0] % 8), (0, 0)))
    smalls = 9 + 2 * (units // width)
    smalls += -smalls % 8
    state = (pairs, 2, HD, LANES)
    zrows = (pairs, 8, LANES)
    wide, low, both = ((rows, width), f32), ((rows, width), bf16), (2 * rows, width)
    front_outs = shaped(
        low, ((smalls, width), f32), ((2 * units, width), bf16), low, wide, low, wide, wide,
        low, low, low, wide, ((rows, LANES), f32), (state, bf16), (zrows, f32),
    )
    tables = [
        pltpu.VMEM((rows, rows), f32), pltpu.VMEM((rows, LANES), f32), pltpu.VMEM((rows, LANES), f32),
    ]
    smem = [pl.BlockSpec(memory_space=pltpu.SMEM)]
    (
        result, small, gff, dhs, dho, mixb, mixf, inv, rq, rk, vv, nrm, scl, st, z,
    ) = pl.pallas_call(
        front_kernel,
        out_shape=front_outs,
        in_specs=in_vmem(2) + smem + in_vmem(8),
        out_specs=tuple(in_vmem(len(front_outs))),
        scratch_shapes=[
            pltpu.VMEM(both, bf16),
            pltpu.VMEM((2 * rows, units), bf16),
            pltpu.VMEM((2 * rows, units), f32),
            pltpu.VMEM(both, bf16),
            pltpu.VMEM((2 * rows, units), bf16),
            pltpu.VMEM((rows, width), f32),
            pltpu.VMEM(state, bf16),
            pltpu.VMEM(state, bf16),
            pltpu.VMEM(zrows, f32),
            pltpu.VMEM(zrows, f32),
            pltpu.VMEM((rows, width), bf16),
            pltpu.VMEM((rows, width), bf16),
            pltpu.VMEM((rows, width), f32),
            pltpu.VMEM((rows, width), f32),
            *tables,
            pltpu.VMEM((24, width), f32),
            pltpu.VMEM((8, units), f32),
            pltpu.SemaphoreType.DMA((5,)),
            pltpu.SemaphoreType.DMA((5,)),
        ],
        compiler_params=pltpu.CompilerParams(
            collective_id=0, has_side_effects=True, vmem_limit_bytes=60 << 20
        ),
        name="front",
    )(tokens, trig, span, vec, w_query, w_key, w_value, w_out, w_up, w_down, out_grad)
    count = lax.axis_size("dp") // 2
    swaps = 2 + count.bit_length() - 1
    half, quarter = units, width
    ff_part, a_part = half // count // 2, quarter // count // 2
    streams = 2 * (FF_CUTS + A_CUTS)
    back_outs = shaped(
        wide, (gff.shape, bf16), ((4 * width, width), bf16), ((swaps + 1, *small.shape), f32)
    )
    d_tokens, gff, ga, small = pl.pallas_call(
        functools.partial(back_kernel, count),
        out_shape=back_outs,
        in_specs=in_vmem(2) + smem + in_vmem(19),
        out_specs=tuple(in_vmem(len(back_outs))),
        scratch_shapes=[
            pltpu.VMEM((rows, width), bf16),
            pltpu.VMEM((rows, width), f32),
            pltpu.VMEM((rows, width), bf16),
            pltpu.VMEM((rows, width), bf16),
            pltpu.VMEM((rows, width), bf16),
            pltpu.VMEM(state, bf16),
            pltpu.VMEM(state, bf16),
            pltpu.VMEM(zrows, f32),
            pltpu.VMEM(zrows, f32),
            pltpu.VMEM((rows, width), f32),
            pltpu.VMEM((rows, width), f32),
            pltpu.VMEM((rows, width), f32),
            pltpu.VMEM((rows, width), bf16),
            pltpu.VMEM((rows, width), bf16),
            pltpu.VMEM((rows, width), bf16),
            *tables,
            pltpu.VMEM((24, width), f32),
            pltpu.VMEM((4 * width, width), bf16),
            pltpu.VMEM(small.shape, f32),
            pltpu.VMEM((half, width), bf16),
            pltpu.VMEM((2 * quarter, width), bf16),
            pltpu.VMEM((quarter, width), bf16),
            pltpu.VMEM((count, 2, a_part, width), bf16),
            pltpu.VMEM((half, width), bf16),
            pltpu.VMEM((quarter, width), bf16),
            pltpu.VMEM((count - 1, 2, ff_part, width), bf16),
            pltpu.VMEM((count - 1, 2, a_part, width), bf16),
            pltpu.VMEM((swaps, *small.shape), f32),
            pltpu.SemaphoreType.DMA((7,)),
            pltpu.SemaphoreType.DMA((7,)),
            pltpu.SemaphoreType.DMA((streams, count - 1)),
            pltpu.SemaphoreType.DMA((streams, count - 1)),
            pltpu.SemaphoreType.DMA((streams, count - 1)),
            pltpu.SemaphoreType.DMA((streams, count - 1)),
            pltpu.SemaphoreType.DMA((2 * A_CUTS, count)),
            pltpu.SemaphoreType.DMA((2 * A_CUTS, count)),
            pltpu.SemaphoreType.DMA((2 * A_CUTS, count)),
            pltpu.SemaphoreType.DMA((2 * A_CUTS, count)),
            pltpu.SemaphoreType.DMA((swaps,)),
            pltpu.SemaphoreType.DMA((swaps,)),
        ],
        compiler_params=pltpu.CompilerParams(
            collective_id=1, has_side_effects=True, vmem_limit_bytes=62 << 20
        ),
        name="back",
    )(
        tokens, trig, span, vec, w_query, w_key, w_value, w_out,
        dhs, dho, mixb, mixf, inv, rq, rk, vv, nrm, scl, st, z, small, gff,
    )
    small = small[swaps]
    halves = units // width
    g_up = jnp.concatenate(
        [gff[units + h * width : units + (h + 1) * width] for h in range(halves)], axis=1
    )
    g_upbias = lax.dynamic_slice_in_dim(small, 9 + rank * halves, halves, 0).reshape(units)
    return (
        result,
        d_tokens,
        ga[:width].astype(f32),
        small[6],
        ga[width : 2 * width].astype(f32),
        small[7],
        ga[2 * width : 3 * width].astype(f32),
        small[8],
        ga[3 * width :].astype(f32),
        small[2],
        small[0],
        small[1],
        g_up.astype(f32),
        g_upbias,
        gff[:units].astype(f32),
        small[5],
        small[3],
        small[4],
    )


def pick(mesh):
    def per_device(*args):
        tokens, span_sizes, w_up = args[0], args[2], args[13]
        rows, width = tokens.shape
        fits = (
            mesh.shape["tensor"] == 2
            and span_sizes.shape[0] == 1
            and rows % TILE == 0
            and width % TILE == 0
            and w_up.shape[1] % width == 0
            and w_up.shape[1] // width <= 3
            and mesh.shape["dp"] == 16
            and width % (16 * mesh.shape["dp"]) == 0
        )
        return pair_device(*args) if fits else general_device(*args)

    return per_device


def solution(mesh):
    return jax.shard_map(
        pick(mesh),
        mesh=mesh,
        in_specs=(
            P(("dp", "tensor"), None),
            P("dp"),
            P("dp"),
            P(),
            P(),
            P(),
            P(),
            P(),
            P(),
            P(),
            P(),
            P(),
            P(),
            P(None, "tensor"),
            P("tensor"),
            P("tensor", None),
            P(),
            P(),
            P(),
            P(("dp", "tensor"), None),
        ),
        out_specs=(
            P(("dp", "tensor"), None),
            P(("dp", "tensor"), None),
            P(),
            P(),
            P(),
            P(),
            P(),
            P(),
            P(),
            P(),
            P(),
            P(),
            P(None, "tensor"),
            P("tensor"),
            P("tensor", None),
            P(),
            P(),
            P(),
        ),
        check_vma=False,
    )
```

```python
import functools
import math

import jax
import jax.numpy as jnp
from jax import lax
from jax.experimental import pallas as pl
from jax.experimental.pallas import tpu as pltpu
from jax.sharding import PartitionSpec as P

HEADS = 12
HD = 64
SUBLEN = 32


highest = lax.Precision.HIGHEST
norm_eps = 1e-05


def norm_forward(value, gain, shift):
    mean = jnp.mean(value, axis=-1, keepdims=True)
    centred = value - mean
    scale = lax.rsqrt(jnp.mean(centred * centred, axis=-1, keepdims=True) + norm_eps)
    normal = centred * scale
    return (normal * gain + shift, normal, scale)


def norm_backward(grad, normal, scale, gain):
    along = grad * gain
    inner = (
        along
        - jnp.mean(along, axis=-1, keepdims=True)
        - normal * jnp.mean(along * normal, axis=-1, keepdims=True)
    )
    return (inner * scale, jnp.sum(grad * normal, axis=0), jnp.sum(grad, axis=0))


def gelu_slope(pre):
    normal_cdf = 0.5 * (1.0 + jax.scipy.special.erf(pre * (1.0 / math.sqrt(2.0))))
    return normal_cdf + pre * jnp.exp(-0.5 * pre * pre) * (1.0 / math.sqrt(2.0 * math.pi))


def reach_table(count, span):
    slot_index = jnp.arange(count, dtype=jnp.int32)
    final = (slot_index * SUBLEN // span + 1) * span // SUBLEN - 1
    return (slot_index[None, :] <= final[:, None]).astype(jnp.float32)


def features(rows, w_joint, b_joint, cosine, sine):
    length = rows.shape[0]
    width = rows.shape[1]
    proj = jnp.dot(rows, w_joint, preferred_element_type=jnp.float32) + b_joint
    relu_query = jax.nn.relu(proj[:, :width]).reshape(length, HEADS, HD)
    relu_key = jax.nn.relu(proj[:, width : 2 * width]).reshape(length, HEADS, HD) * (1.0 / HD)
    q_feat = jnp.concatenate([relu_query * cosine, relu_query * sine], axis=-1).astype(jnp.bfloat16)
    k_feat = jnp.concatenate([relu_key * cosine, relu_key * sine], axis=-1).astype(jnp.bfloat16)
    v_low = proj[:, 2 * width :].astype(jnp.bfloat16)
    return (q_feat, k_feat, v_low)


def local_blocks(k_feat, v_low):
    count = k_feat.shape[0] // SUBLEN
    k_sub = k_feat.reshape(count, SUBLEN, HEADS, 2 * HD)
    v_sub = v_low.reshape(count, SUBLEN, HEADS, HD)
    blocks = jnp.einsum("tjhf,tjhd->thfd", k_sub, v_sub, preferred_element_type=jnp.float32)
    k_total = jnp.sum(k_sub.astype(jnp.float32), axis=1)
    return (blocks, k_total)


def attend_core(q_feat, k_feat, v_low, blocks, k_total, reach, extra_blocks, extra_keys):
    count = q_feat.shape[0] // SUBLEN
    q_sub = q_feat.reshape(count, SUBLEN, HEADS, 2 * HD)
    k_sub = k_feat.reshape(count, SUBLEN, HEADS, 2 * HD)
    v_sub = v_low.reshape(count, SUBLEN, HEADS, HD)
    state_low = (
        jnp.einsum("st,thfd->shfd", reach, blocks, precision=highest) + extra_blocks
    ).astype(jnp.bfloat16)
    z_sum = jnp.einsum("st,thf->shf", reach, k_total, precision=highest) + extra_keys
    numer = jnp.einsum("sihf,shfd->sihd", q_sub, state_low, preferred_element_type=jnp.float32)
    denom = jnp.einsum("sihf,shf->sih", q_sub.astype(jnp.float32), z_sum, precision=highest) + 1.0
    return (q_sub, k_sub, v_sub, state_low, z_sum, numer, denom)


def back_first(parts, grad_mixed):
    q_sub, k_sub, v_sub, state_low, z_sum, numer, denom = parts
    count = q_sub.shape[0]
    grad_out = grad_mixed.reshape(count, SUBLEN, HEADS, HD).astype(jnp.float32)
    d_numer = grad_out / denom[..., None]
    d_denom = -jnp.sum(grad_out * numer, axis=-1) / (denom * denom)
    q_wide = q_sub.astype(jnp.float32)
    d_query = jnp.einsum(
        "sihd,shfd->sihf", d_numer, state_low.astype(jnp.float32), precision=highest
    )
    d_query = d_query + d_denom[..., None] * z_sum[:, None]
    d_state = jnp.einsum("sihf,sihd->shfd", q_wide, d_numer, precision=highest)
    d_zsum = jnp.einsum("sihf,sih->shf", q_wide, d_denom, precision=highest)
    return (d_query, d_state, d_zsum)


def back_second(parts, reach, d_state, d_zsum, later_blocks, later_keys):
    q_sub, k_sub, v_sub = (parts[0], parts[1], parts[2])
    d_blocks = jnp.einsum("st,shfd->thfd", reach, d_state, precision=highest) + later_blocks
    d_ktotal = jnp.einsum("st,shf->thf", reach, d_zsum, precision=highest) + later_keys
    d_key = (
        jnp.einsum("thfd,tjhd->tjhf", d_blocks, v_sub.astype(jnp.float32), precision=highest)
        + d_ktotal[:, None]
    )
    d_value = jnp.einsum("thfd,tjhf->tjhd", d_blocks, k_sub.astype(jnp.float32), precision=highest)
    return (d_key, d_value)


def feature_grads(q_feat, k_feat, d_qf, d_kf, d_val, cos_part, sin_part):
    size = q_feat.shape[0]
    d_qf = d_qf.reshape(size, HEADS, 2 * HD)
    d_kf = d_kf.reshape(size, HEADS, 2 * HD)
    d_query = jnp.where(
        q_feat[..., :HD] > 0, d_qf[..., :HD] * cos_part + d_qf[..., HD:] * sin_part, 0.0
    )
    d_key = jnp.where(
        k_feat[..., :HD] > 0,
        (d_kf[..., :HD] * cos_part + d_kf[..., HD:] * sin_part) * (1.0 / HD),
        0.0,
    )
    return jnp.concatenate(
        [
            d_query.reshape(size, HEADS * HD),
            d_key.reshape(size, HEADS * HD),
            d_val.reshape(size, HEADS * HD),
        ],
        axis=1,
    )


def general_device(
    tokens,
    positions,
    span_sizes,
    w_query,
    b_query,
    w_key,
    b_key,
    w_value,
    b_value,
    w_out,
    b_out,
    norm1_gain,
    norm1_bias,
    w_up,
    b_up,
    w_down,
    b_down,
    norm2_gain,
    norm2_bias,
    out_grad,
):
    rank = lax.axis_index("tensor")
    tensor_count = lax.axis_size("tensor")
    own = tokens.shape[0]
    width = tokens.shape[1]
    seqs = span_sizes.shape[0]
    group = own * tensor_count
    length = group // seqs
    start = rank * own
    w_joint = jnp.concatenate([w_query, w_key, w_value], axis=1)
    b_joint = jnp.concatenate([b_query, b_key, b_value]).astype(jnp.float32)
    gain_one = norm1_gain.astype(jnp.float32)
    gain_two = norm2_gain.astype(jnp.float32)
    gathered = lax.all_gather(tokens, "tensor", axis=0, tiled=True)
    angle = math.pi / 2 * positions.astype(jnp.float32) / (3 * length)
    cosine = jnp.cos(angle).reshape(seqs, length, 1, 1)
    sine = jnp.sin(angle).reshape(seqs, length, 1, 1)

    def seq_forward(items):
        rows, cos_part, sin_part, span = items
        q_feat, k_feat, v_low = features(rows, w_joint, b_joint, cos_part, sin_part)
        blocks_seq, ktot_seq = local_blocks(k_feat, v_low)
        parts = attend_core(
            q_feat,
            k_feat,
            v_low,
            blocks_seq,
            ktot_seq,
            reach_table(q_feat.shape[0] // SUBLEN, span),
            0.0,
            0.0,
        )
        mixed_seq = (
            (parts[5] / parts[6][..., None]).reshape(rows.shape[0], width).astype(jnp.bfloat16)
        )
        return (mixed_seq, q_feat, k_feat, v_low)

    mixed, q_all, k_all, v_all = lax.map(
        seq_forward, (gathered.reshape(seqs, length, width), cosine, sine, span_sizes)
    )
    mixed = mixed.reshape(group, width)
    mixed_own = lax.dynamic_slice_in_dim(mixed, start, own, 0)
    resid = (
        tokens.astype(jnp.float32)
        + jnp.dot(mixed_own, w_out, preferred_element_type=jnp.float32)
        + b_out.astype(jnp.float32)
    )
    hidden, normal_one, scale_one = norm_forward(resid, gain_one, norm1_bias.astype(jnp.float32))
    hidden_low = hidden.astype(jnp.bfloat16)
    rows_in = lax.all_gather(hidden_low, "tensor", axis=0, tiled=True)
    pre = jnp.dot(rows_in, w_up, preferred_element_type=jnp.float32) + b_up.astype(jnp.float32)
    act_low = jax.nn.gelu(pre, approximate=False).astype(jnp.bfloat16)
    branch = lax.psum_scatter(
        jnp.dot(act_low, w_down, preferred_element_type=jnp.float32),
        "tensor",
        scatter_dimension=0,
        tiled=True,
    )
    summed = hidden + branch + b_down.astype(jnp.float32)
    result, normal_two, scale_two = norm_forward(summed, gain_two, norm2_bias.astype(jnp.float32))
    d_sum, d_gain_two, d_bias_two = norm_backward(
        out_grad.astype(jnp.float32), normal_two, scale_two, gain_two
    )
    d_bdown = jnp.sum(d_sum, axis=0)
    d_sum_low = d_sum.astype(jnp.bfloat16)
    rows_grad = lax.all_gather(d_sum_low, "tensor", axis=0, tiled=True)
    g_down = jnp.dot(act_low.T, rows_grad, preferred_element_type=jnp.float32)
    d_pre = jnp.dot(rows_grad, w_down.T, preferred_element_type=jnp.float32) * gelu_slope(pre)
    g_upbias = jnp.sum(d_pre, axis=0)
    d_pre_low = d_pre.astype(jnp.bfloat16)
    g_up = jnp.dot(rows_in.T, d_pre_low, preferred_element_type=jnp.float32)
    d_hidden = lax.psum_scatter(
        jnp.dot(d_pre_low, w_up.T, preferred_element_type=jnp.float32),
        "tensor",
        scatter_dimension=0,
        tiled=True,
    )
    g_up, g_upbias, g_down = (
        lax.psum(g_up.astype(jnp.bfloat16), "dp").astype(jnp.float32),
        lax.psum(g_upbias.astype(jnp.bfloat16), "dp").astype(jnp.float32),
        lax.psum(g_down.astype(jnp.bfloat16), "dp").astype(jnp.float32),
    )
    d_hidden = d_hidden + d_sum
    d_resid, d_gain_one, d_bias_one = norm_backward(d_hidden, normal_one, scale_one, gain_one)
    d_bout = jnp.sum(d_resid, axis=0)
    d_gain_one, d_bias_one, d_gain_two, d_bias_two, d_bout, d_bdown = lax.psum(
        (d_gain_one, d_bias_one, d_gain_two, d_bias_two, d_bout, d_bdown), ("dp", "tensor")
    )
    d_resid_low = d_resid.astype(jnp.bfloat16)
    rows_back = lax.all_gather(d_resid_low, "tensor", axis=0, tiled=True)
    g_out = jnp.dot(mixed.T, rows_back, preferred_element_type=jnp.float32)
    d_mixed = jnp.dot(rows_back, w_out.T, preferred_element_type=jnp.float32).astype(jnp.bfloat16)

    def seq_backward(items):
        q_feat, k_feat, v_low, cos_part, sin_part, span, grad_mixed = items
        blocks_seq, ktot_seq = local_blocks(k_feat, v_low)
        reach = reach_table(q_feat.shape[0] // SUBLEN, span)
        parts = attend_core(q_feat, k_feat, v_low, blocks_seq, ktot_seq, reach, 0.0, 0.0)
        d_qf, d_state, d_zsum = back_first(parts, grad_mixed)
        d_kf, d_val = back_second(parts, reach, d_state, d_zsum, 0.0, 0.0)
        joint = feature_grads(q_feat, k_feat, d_qf, d_kf, d_val, cos_part, sin_part)
        return (joint.astype(jnp.bfloat16), jnp.sum(joint, axis=0))

    d_joint, d_jbias = lax.map(
        seq_backward,
        (q_all, k_all, v_all, cosine, sine, span_sizes, d_mixed.reshape(seqs, length, width)),
    )
    d_joint = d_joint.reshape(group, 3 * width)
    d_jbias = jnp.sum(d_jbias, axis=0)
    g_joint = jnp.dot(gathered.T, d_joint, preferred_element_type=jnp.float32)
    d_joint_own = lax.dynamic_slice_in_dim(d_joint, start, own, 0)
    d_tokens = d_resid + jnp.dot(d_joint_own, w_joint.T, preferred_element_type=jnp.float32)
    g_joint, g_out, d_jbias = lax.psum((g_joint, g_out, d_jbias), "dp")
    return (
        result.astype(jnp.bfloat16),
        d_tokens,
        g_joint[:, :width],
        d_jbias[:width],
        g_joint[:, width : 2 * width],
        d_jbias[width : 2 * width],
        g_joint[:, 2 * width :],
        d_jbias[2 * width :],
        g_out,
        d_bout,
        d_gain_one,
        d_bias_one,
        g_up,
        g_upbias,
        g_down,
        d_bdown,
        d_gain_two,
        d_bias_two,
    )


f32 = jnp.float32
bf16 = jnp.bfloat16
MESH = pl.DeviceIdType.MESH
LANES = 2 * HD
TILE = 256
ROWBLOCK = 32
FF_CUTS = 3
A_CUTS = 3


def tile_at(index, size):
    return pl.ds(pl.multiple_of(index * size, size), size)


def contract(left, right, left_dim, right_dim, precision=None):
    return lax.dot_general(
        left,
        right,
        (((left_dim,), (right_dim,)), ((), ())),
        precision=precision,
        preferred_element_type=f32,
    )


def mm(left, right):
    return contract(left, right, 1, 0)


def mm_nt(left, right):
    return contract(left, right, 1, 1)


def mm_tn(left, right):
    return contract(left, right, 0, 0)


def head_masks():
    lane = lax.broadcasted_iota(jnp.int32, (1, LANES), 1)
    first = (lane < HD).astype(f32)
    return first, 1.0 - first


def pair_mask():
    row = lax.broadcasted_iota(jnp.int32, (LANES, LANES), 0)
    col = lax.broadcasted_iota(jnp.int32, (LANES, LANES), 1)
    return ((row < HD) == (col < HD)).astype(f32)


def column_of(block, which):
    row = lax.broadcasted_iota(jnp.int32, block.shape, 0)
    return contract(jnp.where(row == which, block, 0.0), jnp.ones((8, LANES), f32), 0, 0, highest)


def squeeze_pair(square):
    return square[:HD] + square[HD:]


def spread_pair(part, mask):
    return jnp.concatenate([part, part], axis=0).astype(f32) * mask


def two_rows(top, below):
    row = lax.broadcasted_iota(jnp.int32, (8, LANES), 0)
    return jnp.where(row == 0, top, jnp.where(row == 1, below, 0.0))


def fold8(value):
    total = value[0:8]
    for start in range(8, value.shape[0], 8):
        total = total + value[start : start + 8]
    return total


def angle_tables(places, length, span, cosb, sinb, ctab):
    rows = cosb.shape[0]
    angle = math.pi / 2 * places.astype(f32).reshape(1, rows) / (3 * length)
    line = lax.broadcasted_iota(jnp.int32, (8, rows), 0)
    block = jnp.where(line == 0, jnp.cos(angle), jnp.where(line == 1, jnp.sin(angle), 0.0))
    cosb[...] = column_of(block, 0)
    sinb[...] = column_of(block, 1)
    both = contract(block, block, 0, 0, highest)
    row = lax.broadcasted_iota(jnp.int32, (rows, rows), 0)
    col = lax.broadcasted_iota(jnp.int32, (rows, rows), 1)
    seen = col <= (row | (span[0, 0] - 1))
    ctab[...] = jnp.where(seen, both * (1.0 / HD), 0.0)


def peer_copy(src, dst, sems, slot, device):
    return pltpu.make_async_remote_copy(
        src_ref=src,
        dst_ref=dst,
        send_sem=sems[0].at[slot],
        recv_sem=sems[1].at[slot],
        device_id=device,
        device_id_type=MESH,
    )


def ring_device(spot, depth, core):
    far = spot // depth
    z = far * (2 * depth - 1 - spot) + (1 - far) * spot
    return ((z * 2 + far) * 2 + core, lax.axis_index("tensor"))


def layer_norm(value):
    centred = value - jnp.mean(value, axis=-1, keepdims=True)
    scale = lax.rsqrt(jnp.mean(centred * centred, axis=-1, keepdims=True) + norm_eps)
    return centred * scale, scale


def layer_norm_back(grad, gain, normal, scale):
    along = grad * gain
    return (
        along
        - jnp.mean(along, axis=-1, keepdims=True)
        - normal * jnp.mean(along * normal, axis=-1, keepdims=True)
    ) * scale


def block_kernel(
    count, tok, places, span, bq, bk, bv, bo, g1, b1, bd, g2, b2, bup_in, og,
    wq, wk, wv, wo, wup, wdn,
    res_h, dtok_h, ff_h, a_h, small_h,
    wa, wff, vec, hbuf, act, slope, dbuf, dpre, hid, numer, denom, tsend, trecv, zsend, zrecv,
    bsend, brecv, res, gff, dhs, dhr, dho, mixb, mixf, inv, rq, rk, vv, nrm, scl, st, zst,
    dres, dlow, dn, xs, dsend, drecv, dzs, dzr, dql, dkl, dvl, ctab, cosb, sinb, acc, bup,
    cr_ff, cr_a, px, xr, rs_ff, rs_a, ff_o, a_o, smalls, small_r,
    send, recv, r_send, r_recv, g_send, g_recv, x_send, x_recv, y_send, y_recv, m_send, m_recv,
    w_sem, o_sem,
):
    sems = (send, recv)
    rows, width = tok.shape
    units = wup.shape[1]
    halves = units // width
    pairs = width // LANES
    tiles = width // TILE
    depth = count // 2
    quarter = width
    dq, dk, dv, ga = numer, denom, hid, wff
    dp, rank = lax.axis_index("dp"), lax.axis_index("tensor")
    late = rank.astype(f32)
    early = 1.0 - late
    core, y, z = dp % 2, (dp // 2) % 2, dp // 4
    spot = y * (2 * depth - 1 - z) + (1 - y) * z
    sibling = (dp + 1 - 2 * core, rank)
    peer = (dp, 1 - rank)
    ahead = ring_device((spot + 1) % count, depth, core)
    behind = ring_device((spot + count - 1) % count, depth, core)
    swaps = [sibling, peer, (dp + 2 - 4 * y, rank)]
    step = 1
    while step < depth:
        bit = (z // step) % 2
        swaps.append((dp + 4 * (step - 2 * step * bit), rank))
        step *= 2
    partners = [ahead, behind] + swaps
    barrier = pltpu.get_barrier_semaphore()
    for device in partners:
        pl.semaphore_signal(barrier, inc=1, device_id=device, device_id_type=MESH)

    loads = [
        (wk, wa.at[pl.ds(width, width), :]),
        (wv, wa.at[pl.ds(2 * width, width), :]),
        (wq, wa.at[pl.ds(0, width), :]),
        (wo, wa.at[pl.ds(3 * width, width), :]),
    ]
    for part in range(halves):
        loads.append(
            (wup.at[:, pl.ds(part * width, width)], wff.at[pl.ds(units + part * width, width), :])
        )
    loads.append((wdn, wff.at[pl.ds(0, units), :]))

    def load(index):
        return pltpu.make_async_copy(loads[index][0], loads[index][1], w_sem.at[index])

    for index in range(len(loads)):
        load(index).start()

    def out_copy(source, target, at, slot):
        return pltpu.make_async_copy(source.at[at, :], target.at[at, :], o_sem.at[slot])

    for index, source in enumerate((bq, bk, bv, bo, g1, b1, bd, g2, b2)):
        vec[index : index + 1, :] = source[...].astype(f32).reshape(1, width)
    for part in range(halves):
        piece = bup_in[pl.ds(part * width, width)]
        vec[9 + part : 10 + part, :] = piece.astype(f32).reshape(1, width)
    own, far_rows = pl.ds(0, rows), pl.ds(rows, rows)
    my_places = places[pl.ds(pl.multiple_of(rank * rows, rows), rows)]
    angle_tables(my_places, places.shape[0], span, cosb, sinb, ctab)
    diag = pair_mask()
    first, second = head_masks()
    first_low, second_low = first.astype(bf16), second.astype(bf16)
    diag_low = diag.astype(bf16)
    acc[...] = jnp.zeros_like(acc)
    bup[...] = jnp.zeros_like(bup)
    smalls[0] = jnp.zeros(smalls.shape[1:], f32)

    def add_small(slot, line):
        smalls[0, slot : slot + 1, :] = line

    def project(which, target):
        @pl.loop(0, tiles)
        def _(j):
            cols = tile_at(j, TILE)
            value = mm(tok[...], wa[pl.ds(which * width, width), cols]) + vec[which : which + 1, cols]
            if which < 2:
                value = jnp.maximum(value, 0.0)
            target[:, cols] = value.astype(bf16)

    load(0).wait()
    project(1, rk)
    load(1).wait()
    project(2, vv)

    @pl.loop(0, pairs)
    def _(p):
        lanes = tile_at(p, LANES)
        k = rk[:, lanes].astype(f32) * (1.0 / HD)
        v = vv[:, lanes]
        kc, ks = (k * cosb[...]).astype(bf16), (k * sinb[...]).astype(bf16)
        tsend[p, 0] = squeeze_pair(mm_tn(kc, v) * diag).astype(bf16)
        tsend[p, 1] = squeeze_pair(mm_tn(ks, v) * diag).astype(bf16)
        zsend[p] = two_rows(
            jnp.sum(kc.astype(f32), axis=0, keepdims=True),
            jnp.sum(ks.astype(f32), axis=0, keepdims=True),
        )

    pl.semaphore_wait(barrier, len(partners))
    state_copy = peer_copy(tsend, trecv, sems, 0, peer)
    key_copy = peer_copy(zsend, zrecv, sems, 1, peer)
    state_copy.start()
    key_copy.start()
    load(2).wait()
    project(0, rq)

    @pl.loop(0, pairs)
    def _(p):
        lanes = tile_at(p, LANES)
        q, k, v = rq[:, lanes], rk[:, lanes], vv[:, lanes]
        parts = []
        for mask, rest in ((first_low, second_low), (second_low, first_low)):
            prob = (mm_nt(q * mask, k) * ctab[...]).astype(bf16)
            parts.append(mm(prob, v * mask + rest))
        numer[:, lanes] = parts[0] * first + parts[1] * second
        denom[:, lanes] = pltpu.roll(parts[0] * second + parts[1] * first, HD, 1)

    state_copy.wait()
    key_copy.wait()

    @pl.loop(0, pairs)
    def _(p):
        lanes = tile_at(p, LANES)
        q = rq[:, lanes].astype(f32)
        qc, qs = (q * cosb[...]).astype(bf16), (q * sinb[...]).astype(bf16)
        st[p] = (trecv[p].astype(f32) * late).astype(bf16)
        zblock = zrecv[p] * late
        zst[p] = zblock
        num, den = numer[:, lanes], denom[:, lanes] + 1.0
        for part, feat in ((0, qc), (1, qs)):
            num += mm(feat, spread_pair(st[p, part], diag).astype(bf16))
            den += mm(feat, (column_of(zblock, part) * diag).astype(bf16))
        reciprocal = 1.0 / den
        mix = num * reciprocal
        inv[:, lanes] = reciprocal
        mixf[:, lanes] = mix
        mixb[:, lanes] = mix.astype(bf16)

    load(3).wait()

    @pl.loop(0, tiles)
    def _(j):
        cols = tile_at(j, TILE)
        hid[:, cols] = (
            tok[:, cols].astype(f32) + mm(mixb[...], wa[pl.ds(3 * width, width), cols]) + vec[3:4, cols]
        )

    @pl.loop(0, rows // ROWBLOCK)
    def _(i):
        at = tile_at(i, ROWBLOCK)
        normal, scale = layer_norm(hid[at, :])
        hidden = normal * vec[4:5, :] + vec[5:6, :]
        nrm[at, :] = normal
        scl[at, :] = jnp.broadcast_to(scale, (ROWBLOCK, LANES))
        hid[at, :] = hidden
        hbuf[at, :] = hidden.astype(bf16)

    rows_copy = peer_copy(hbuf.at[own], hbuf.at[far_rows], sems, 2, peer)
    rows_copy.start()
    for index in range(4, len(loads)):
        load(index).wait()

    def raise_rows(part):
        for piece in range(halves):

            @pl.loop(0, tiles)
            def _(j, piece=piece):
                cols, narrow = tile_at(piece * tiles + j, TILE), tile_at(j, TILE)
                weight = wff[pl.ds(units + piece * width, width), narrow]
                pre = mm(hbuf[part, :], weight) + vec[9 + piece : 10 + piece, narrow]
                cdf = 0.5 * (1.0 + lax.erf(pre * (1.0 / math.sqrt(2.0))))
                act[part, cols] = (pre * cdf).astype(bf16)
                slope[part, cols] = cdf + pre * jnp.exp(-0.5 * pre * pre) * (
                    1.0 / math.sqrt(2.0 * math.pi)
                )

    raise_rows(own)
    rows_copy.wait()
    raise_rows(far_rows)

    @pl.loop(0, tiles)
    def _(j):
        cols = tile_at(j, TILE)
        bsend[:, cols] = mm(act[far_rows, :], wff[pl.ds(0, units), cols]).astype(bf16)

    branch_copy = peer_copy(bsend, brecv, sems, 3, peer)
    branch_copy.start()

    @pl.loop(0, tiles)
    def _(j):
        cols = tile_at(j, TILE)
        hid[:, cols] += mm(act[own, :], wff[pl.ds(0, units), cols]) + vec[6:7, cols]

    branch_copy.wait()

    @pl.loop(0, rows // ROWBLOCK)
    def _(i):
        at = tile_at(i, ROWBLOCK)
        normal, scale = layer_norm(hid[at, :] + brecv[at, :].astype(f32))
        res[at, :] = (normal * vec[7:8, :] + vec[8:9, :]).astype(bf16)
        grad = og[at, :].astype(f32)
        inner = layer_norm_back(grad, vec[7:8, :], normal, scale)
        dho[at, :] = inner
        dbuf[at, :] = inner.astype(bf16)
        acc[0:8, :] += fold8(grad * normal)
        acc[8:16, :] += fold8(grad)
        acc[16:24, :] += fold8(inner)

    grad_copy = peer_copy(dbuf.at[own], dbuf.at[far_rows], sems, 4, peer)
    grad_copy.start()
    result_out = pltpu.make_async_copy(res, res_h, o_sem.at[0])
    result_out.start()
    for slot in range(3):
        add_small(3 + slot, jnp.sum(acc[8 * slot : 8 * slot + 8, :], axis=0, keepdims=True))

    def lower_rows(part):
        @pl.loop(0, units // TILE)
        def _(j):
            cols = tile_at(j, TILE)
            d_pre = mm_nt(dbuf[part, :], wff[cols, :]) * slope[part, cols]
            bup[:, cols] += fold8(d_pre)
            dpre[part, cols] = d_pre.astype(bf16)

    def lower_hidden(part, cols, j):
        total = 0.0
        for piece in range(halves):
            weight = wff[pl.ds(pl.multiple_of(units + piece * width + j * TILE, TILE), TILE), :]
            total += mm_nt(dpre[part, piece * width : (piece + 1) * width], weight)
        return total

    lower_rows(own)
    grad_copy.wait()
    lower_rows(far_rows)

    @pl.loop(0, tiles)
    def _(j):
        cols = tile_at(j, TILE)
        dhs[:, cols] = lower_hidden(far_rows, cols, j).astype(bf16)

    hidden_copy = peer_copy(dhs, dhr, sems, 5, peer)
    hidden_copy.start()

    @pl.loop(0, units // TILE)
    def _(j):
        cols = tile_at(j, TILE)
        gff[cols, :] = mm_tn(act[:, cols], dbuf[...]).astype(bf16)

    for piece in range(halves):

        @pl.loop(0, tiles)
        def _(j, piece=piece):
            gff[pl.ds(units + piece * width, width), tile_at(j, TILE)] = mm_tn(
                hbuf[...], dpre[:, tile_at(piece * tiles + j, TILE)]
            ).astype(bf16)

    def part_rows(which, size):
        return pl.ds(pl.multiple_of(which * size, size), size)

    core_ff = peer_copy(gff.at[part_rows(1 - core, units), :], cr_ff, sems, 8, sibling)
    core_a = peer_copy(ga.at[part_rows(1 - core, 2 * quarter), :], cr_a, sems, 9, sibling)
    core_ff.start()

    ff_streams, a_streams = [], []
    for kind, (cuts, group) in enumerate(((FF_CUTS, ff_streams), (A_CUTS, a_streams))):
        size = (quarter if kind else units) // count // 2
        for way in range(2):
            for cut in range(cuts):
                number = 2 * FF_CUTS * kind + way * cuts + cut
                group.append((number, kind, way, pl.ds(cut * (size // cuts), size // cuts), cut, size))
    slots = (rs_ff, rs_a)
    sums = (gff, ga)
    outs = (ff_o, a_o)
    bases = (core * units, (core * 2 + rank) * quarter)

    def chunk_rows(at, stream, base):
        _, _, way, piece, cut, size = stream
        start = base + (at % count) * 2 * size + way * size + cut * piece.size
        return pl.ds(pl.multiple_of(start, piece.size), piece.size)

    def toward(stream):
        return behind if stream[2] else ahead

    def sign(stream):
        return -1 if stream[2] else 1

    def spread_copy(stream, at, s):
        number, kind, way, piece, _, _ = stream
        return pltpu.make_async_remote_copy(
            src_ref=sums[kind].at[chunk_rows(at, stream, bases[kind]), :],
            dst_ref=slots[kind].at[s, way, piece, :],
            send_sem=r_send.at[number, s],
            recv_sem=r_recv.at[number, s],
            device_id=toward(stream),
            device_id_type=MESH,
        )

    def gather_copy(stream, at, s):
        number, kind = stream[:2]
        where = outs[kind].at[chunk_rows(at, stream, bases[kind]), :]
        return pltpu.make_async_remote_copy(
            src_ref=where,
            dst_ref=where,
            send_sem=g_send.at[number, s],
            recv_sem=g_recv.at[number, s],
            device_id=toward(stream),
            device_id_type=MESH,
        )

    def across_copy(stream, at, s, base):
        number = stream[0] - 2 * FF_CUTS
        where = a_o.at[chunk_rows(at, stream, base), :]
        return pltpu.make_async_remote_copy(
            src_ref=where,
            dst_ref=where,
            send_sem=x_send.at[number, s],
            recv_sem=x_recv.at[number, s],
            device_id=peer,
            device_id_type=MESH,
        )

    def fold_copy(stream, s):
        number, _, way, piece, _, _ = stream
        at = spot + count - sign(stream) * s
        return pltpu.make_async_remote_copy(
            src_ref=px.at[chunk_rows(at, stream, 0), :],
            dst_ref=xr.at[s, way, piece, :],
            send_sem=y_send.at[number - 2 * FF_CUTS, s],
            recv_sem=y_recv.at[number - 2 * FF_CUTS, s],
            device_id=peer,
            device_id_type=MESH,
        )

    def own_part(stream, at, s):
        _, kind, way, piece, _, _ = stream
        rows_in = chunk_rows(at, stream, bases[kind])
        if kind == 0:
            return gff[rows_in, :].astype(f32) + cr_ff[chunk_rows(at, stream, 0), :].astype(f32)
        fold_copy(stream, s).wait_recv()
        return (
            ga[rows_in, :].astype(f32)
            + cr_a[chunk_rows(at, stream, rank * quarter), :].astype(f32)
            + xr[s, way, piece, :].astype(f32)
        )

    def ring_first(streams):
        for stream in streams:
            kind, at = stream[1], spot + count
            sums[kind][chunk_rows(at, stream, bases[kind]), :] = own_part(stream, at, 0).astype(bf16)
            spread_copy(stream, at, 0).start()

    def ring_spread(streams, s, last):
        for stream in streams:
            _, kind, way, piece, _, _ = stream
            at = spot + count - sign(stream) * (s + 1)
            target = chunk_rows(at, stream, bases[kind])
            part = own_part(stream, at, s + 1)
            spread_copy(stream, at, s).wait_recv()
            total = (part + slots[kind][s, way, piece, :].astype(f32)).astype(bf16)
            if last:
                outs[kind][target, :] = total
                gather_copy(stream, at, 0).start()
                if kind:
                    across_copy(stream, at, 0, bases[1]).start()
            else:
                sums[kind][target, :] = total
                spread_copy(stream, at, s + 1).start()

    def ring_gather(streams, s, last):
        for stream in streams:
            at = spot + 2 * count - sign(stream) * s
            gather_copy(stream, at, s).wait_recv()
            if not last:
                gather_copy(stream, at, s + 1).start()
            if stream[1]:
                across_copy(stream, at, s + 1, bases[1]).start()

    def small_copy(index):
        return peer_copy(smalls.at[index], small_r.at[index], (m_send, m_recv), index, swaps[index])

    def swap_small(index):
        small_copy(index).wait()
        smalls[index + 1] = smalls[index] + small_r[index]
        if index + 1 < len(swaps):
            small_copy(index + 1).start()

    for piece in range(halves):
        line = jnp.sum(bup[:, piece * width : (piece + 1) * width], axis=0, keepdims=True)
        add_small(9 + piece, line * early)
        add_small(9 + halves + piece, line * late)

    @pl.loop(0, tiles)
    def _(j):
        cols = tile_at(j, TILE)
        dho[:, cols] += lower_hidden(own, cols, j)

    acc[...] = jnp.zeros_like(acc)
    core_ff.wait()
    ring_first(ff_streams)
    hidden_copy.wait()
    ring_spread(ff_streams, 0, False)

    @pl.loop(0, rows // ROWBLOCK)
    def _(i):
        at = tile_at(i, ROWBLOCK)
        grad = dho[at, :] + dhr[at, :].astype(f32)
        normal = nrm[at, :]
        inner = layer_norm_back(grad, vec[4:5, :], normal, scl[at, 0:1])
        dres[at, :] = inner
        dlow[at, :] = inner.astype(bf16)
        acc[0:8, :] += fold8(grad * normal)
        acc[8:16, :] += fold8(grad)
        acc[16:24, :] += fold8(inner)

    for slot in range(3):
        add_small(slot, jnp.sum(acc[8 * slot : 8 * slot + 8, :], axis=0, keepdims=True))

    @pl.loop(0, tiles)
    def _(j):
        cols = tile_at(j, TILE)
        d_mixed = mm_nt(dlow[...], wa[tile_at(3 * tiles + j, TILE), :]).astype(bf16).astype(f32)
        d_numer = (d_mixed * inv[:, cols]).astype(bf16)
        dn[:, cols] = d_numer
        xs[:, cols] = (d_numer.astype(f32) * mixf[:, cols]).astype(bf16)

    ring_spread(ff_streams, 1, False)

    @pl.loop(0, pairs)
    def _(p):
        lanes = tile_at(p, LANES)
        q = rq[:, lanes].astype(f32)
        qc, qs = (q * cosb[...]).astype(bf16), (q * sinb[...]).astype(bf16)
        d_numer = dn[:, lanes]
        dsend[p, 0] = squeeze_pair(mm_tn(qc, d_numer) * diag).astype(bf16)
        dsend[p, 1] = squeeze_pair(mm_tn(qs, d_numer) * diag).astype(bf16)
        across = mm(xs[:, lanes], diag_low)
        dzs[p] = -two_rows(
            jnp.sum(qc.astype(f32) * across, axis=0, keepdims=True),
            jnp.sum(qs.astype(f32) * across, axis=0, keepdims=True),
        )

    turn_copy = peer_copy(dsend, drecv, sems, 6, peer)
    turn_keys = peer_copy(dzs, dzr, sems, 7, peer)
    turn_copy.start()
    turn_keys.start()
    ring_spread(ff_streams, 2, False)

    @pl.loop(0, tiles)
    def _(j):
        cols = tile_at(j, TILE)
        ga[tile_at(3 * tiles + j, TILE), :] = mm_tn(mixb[:, cols], dlow[...]).astype(bf16)

    def inside(p):
        lanes = tile_at(p, LANES)
        q, k, v = rq[:, lanes], rk[:, lanes], vv[:, lanes]
        d_numer = dn[:, lanes]
        turned = (-pltpu.roll(xs[:, lanes].astype(f32), HD, 1)).astype(bf16)
        sum_q = sum_k = sum_v = 0.0
        for mask, rest in ((first_low, second_low), (second_low, first_low)):
            q_head, k_head, d_head = q * mask, k * mask, d_numer * mask
            table = ctab[...]
            prob = (mm_nt(q_head, k) * table).astype(bf16)
            d_prob = mm_nt(d_head + turned * rest, v * mask + rest)
            d_score = (d_prob * table).astype(bf16)
            sum_v += mm_tn(prob, d_head)
            sum_q += mm(d_score, k_head)
            sum_k += mm_tn(d_score, q_head)
        dq[:, lanes] = sum_q
        dk[:, lanes] = sum_k
        dv[:, lanes] = sum_v

    pl.loop(0, pairs // 2)(inside)
    ring_spread(ff_streams, 3, False)
    pl.loop(pairs // 2, pairs)(inside)
    ring_spread(ff_streams, 4, False)
    turn_copy.wait()
    turn_keys.wait()

    @pl.loop(0, pairs)
    def _(p):
        lanes = tile_at(p, LANES)
        q, v = rq[:, lanes].astype(f32), vv[:, lanes]
        k = rk[:, lanes].astype(f32)
        d_numer, x = dn[:, lanes], xs[:, lanes]
        sum_q, sum_k, sum_v = dq[:, lanes], dk[:, lanes], dv[:, lanes]
        zblock, dzblock = zst[p], dzr[p] * early
        for part, wave in ((0, cosb[...]), (1, sinb[...])):
            state = spread_pair(st[p, part], diag).astype(bf16)
            zmat = (column_of(zblock, part) * diag).astype(bf16)
            sum_q += wave * (mm_nt(d_numer, state) - mm_nt(x, zmat))
            d_state = (spread_pair(drecv[p, part], diag) * early).astype(bf16)
            sum_k += wave * (mm_nt(v, d_state) + dzblock[part : part + 1, :]) * (1.0 / HD)
            sum_v += mm((k * wave * (1.0 / HD)).astype(bf16), d_state)
        sum_q = jnp.where(q > 0, sum_q, 0.0)
        sum_k = jnp.where(k > 0, sum_k, 0.0)
        dql[:, lanes] = sum_q.astype(bf16)
        dkl[:, lanes] = sum_k.astype(bf16)
        dvl[:, lanes] = sum_v.astype(bf16)
        for slot, value in ((6, sum_q), (7, sum_k), (8, sum_v)):
            smalls[0, slot : slot + 1, lanes] = jnp.sum(value, axis=0, keepdims=True)

    small_copy(0).start()
    ring_spread(ff_streams, 5, False)

    for which, source in enumerate((dql, dkl, dvl)):

        @pl.loop(0, tiles)
        def _(j, which=which, source=source):
            ga[tile_at(which * tiles + j, TILE), :] = mm_tn(
                tok[:, tile_at(j, TILE)], source[...]
            ).astype(bf16)

    core_a.start()
    ring_spread(ff_streams, count - 2, True)

    @pl.loop(0, tiles)
    def _(j):
        cols = tile_at(j, TILE)
        dres[:, cols] += (
            mm_nt(dql[...], wa[cols, :])
            + mm_nt(dkl[...], wa[tile_at(tiles + j, TILE), :])
            + mm_nt(dvl[...], wa[tile_at(2 * tiles + j, TILE), :])
        )

    token_out = pltpu.make_async_copy(dres, dtok_h, o_sem.at[1])
    token_out.start()
    core_a.wait()

    @pl.loop(0, quarter // 96)
    def _(i):
        near = pl.ds(pl.multiple_of((core * 2 + 1 - rank) * quarter + i * 96, 96), 96)
        far = pl.ds(pl.multiple_of((1 - rank) * quarter + i * 96, 96), 96)
        px[tile_at(i, 96), :] = (ga[near, :].astype(f32) + cr_a[far, :].astype(f32)).astype(bf16)

    for s in range(3):
        for stream in a_streams:
            fold_copy(stream, s).start()
    swap_small(0)
    ring_first(a_streams)

    def both_steps(s):
        @pl.when(s + 3 < count)
        def _():
            for stream in a_streams:
                fold_copy(stream, s + 3).start()

        ring_gather(ff_streams, s, False)
        ring_spread(a_streams, s, False)

    pl.loop(0, 2)(both_steps)
    swap_small(1)
    pl.loop(2, 4)(both_steps)
    swap_small(2)
    pl.loop(4, count - 2)(both_steps)
    swap_small(3)
    ring_gather(ff_streams, count - 2, True)
    own_ff, own_a = part_rows(core, units), part_rows(core, 2 * quarter)
    back_ff = peer_copy(ff_o.at[own_ff, :], ff_o.at[own_ff, :], sems, 10, sibling)
    back_ff.start()
    near_ff = out_copy(ff_o, ff_h, own_ff, 2)
    near_ff.start()
    ring_spread(a_streams, count - 2, True)
    pl.loop(0, 2)(lambda s: ring_gather(a_streams, s, False))
    swap_small(4)
    small_out = pltpu.make_async_copy(smalls.at[len(swaps)], small_h, o_sem.at[6])
    small_out.start()
    back_ff.wait()
    far_ff = out_copy(ff_o, ff_h, part_rows(1 - core, units), 3)
    far_ff.start()
    pl.loop(2, count - 2)(lambda s: ring_gather(a_streams, s, False))
    ring_gather(a_streams, count - 2, True)
    crossed = (core * 2 + 1 - rank) * quarter

    @pl.loop(0, count)
    def _(s):
        for stream in a_streams:
            at = spot + 2 * count + sign(stream) * (1 - s)
            across_copy(stream, at, s, crossed).wait_recv()

    back_a = peer_copy(a_o.at[own_a, :], a_o.at[own_a, :], sems, 11, sibling)
    back_a.start()
    near_a = out_copy(a_o, a_h, own_a, 4)
    near_a.start()

    @pl.loop(0, count - 1)
    def _(s):
        for stream in ff_streams + a_streams:
            spread_copy(stream, spot, s).wait_send()
            gather_copy(stream, spot, s).wait_send()

    @pl.loop(0, count)
    def _(s):
        for stream in a_streams:
            across_copy(stream, spot, s, bases[1]).wait_send()
            fold_copy(stream, s).wait_send()

    back_a.wait()
    far_a = out_copy(a_o, a_h, part_rows(1 - core, 2 * quarter), 5)
    far_a.start()
    for copy in (result_out, token_out, near_ff, far_ff, small_out, near_a, far_a):
        copy.wait()


def finish_kernel(halves, *refs):
    g_out, up, down, small, res, dtok = refs[:4], refs[4 : 4 + halves], *refs[4 + halves : 8 + halves]
    out = refs[8 + halves :]
    late = lax.axis_index("tensor") > 0
    for source, where in zip(g_out, (2, 4, 6, 8)):
        out[where][...] = source[...].astype(f32)
    width = res.shape[1]
    for piece in range(halves):
        out[12][:, piece * width : (piece + 1) * width] = up[piece][...].astype(f32)
    out[14][...] = down[...].astype(f32)

    @pl.when(pl.program_id(0) == 0)
    def _():
        out[0][...] = res[...]
        out[1][...] = dtok[...]
        for where, row in ((3, 6), (5, 7), (7, 8), (9, 2), (10, 0), (11, 1), (15, 5), (16, 3), (17, 4)):
            out[where][...] = small[row : row + 1, :].reshape(width)
        for piece in range(halves):
            line = jnp.where(
                late,
                small[9 + halves + piece : 10 + halves + piece, :],
                small[9 + piece : 10 + piece, :],
            )
            out[13][pl.ds(piece * width, width)] = line.reshape(width)


def finish(rows, width, units, res, dtok, ff, a, small):
    halves, steps = units // width, width // LANES
    low = (LANES, width)
    down_rows = units // steps

    def whole(shape):
        return pl.BlockSpec(shape, lambda i: (0,) * len(shape))

    def at_block(shape, start):
        return pl.BlockSpec(shape, lambda i: (start + i, 0))

    in_specs = [at_block(low, which * steps) for which in range(4)]
    in_specs += [at_block(low, units // LANES + piece * steps) for piece in range(halves)]
    in_specs += [at_block((down_rows, width), 0), whole(small.shape), whole(res.shape), whole(dtok.shape)]
    matrix, line = (width, width), (width,)
    shapes = [
        (res.shape, bf16), (dtok.shape, f32), (matrix, f32), (line, f32), (matrix, f32), (line, f32),
        (matrix, f32), (line, f32), (matrix, f32), (line, f32), (line, f32), (line, f32),
        ((width, units), f32), ((units,), f32), ((units, width), f32), (line, f32), (line, f32), (line, f32),
    ]
    special = {
        2: at_block(low, 0), 4: at_block(low, 0), 6: at_block(low, 0), 8: at_block(low, 0),
        12: at_block((LANES, units), 0), 14: at_block((down_rows, width), 0),
    }
    return pl.pallas_call(
        functools.partial(finish_kernel, halves),
        grid=(steps,),
        out_shape=shaped(*shapes),
        in_specs=in_specs,
        out_specs=tuple(special.get(i, whole(shape)) for i, (shape, _) in enumerate(shapes)),
        compiler_params=pltpu.CompilerParams(vmem_limit_bytes=62 << 20),
        name="finish",
    )(*([a] * 4), *([ff] * (halves + 1)), small, res, dtok)


def shaped(*items):
    return tuple(jax.ShapeDtypeStruct(shape, kind) for shape, kind in items)


def pair_device(
    tokens,
    positions,
    span_sizes,
    w_query,
    b_query,
    w_key,
    b_key,
    w_value,
    b_value,
    w_out,
    b_out,
    norm1_gain,
    norm1_bias,
    w_up,
    b_up,
    w_down,
    b_down,
    norm2_gain,
    norm2_bias,
    out_grad,
):
    rows, width = tokens.shape
    units = w_up.shape[1]
    pairs = width // LANES
    halves = units // width
    count = lax.axis_size("dp") // 2
    swaps = 2 + count.bit_length() - 1
    streams = 2 * (FF_CUTS + A_CUTS)
    ff_part, a_part = units // count // 2, width // count // 2
    lines = 9 + 2 * halves
    lines += -lines % 8

    def low(*shape):
        return pltpu.VMEM(shape, bf16)

    def wide(*shape):
        return pltpu.VMEM(shape, f32)

    def sem(*shape):
        return pltpu.SemaphoreType.DMA(shape)

    state, zrows = (pairs, 2, HD, LANES), (pairs, 8, LANES)
    own, pair = (rows, width), (2 * rows, width)
    scratch = dict(
        wa=low(4 * width, width), wff=low(2 * units, width), vec=wide(9 + halves + -(9 + halves) % 8, width),
        hbuf=low(*pair), act=low(2 * rows, units), slope=wide(2 * rows, units), dbuf=low(*pair),
        dpre=low(2 * rows, units), hid=wide(*own), numer=wide(*own), denom=wide(*own),
        tsend=low(*state), trecv=low(*state), zsend=wide(*zrows), zrecv=wide(*zrows),
        bsend=low(*own), brecv=low(*own), res=low(*own), gff=low(2 * units, width),
        dhs=low(*own), dhr=low(*own), dho=wide(*own), mixb=low(*own), mixf=wide(*own), inv=wide(*own),
        rq=low(*own), rk=low(*own), vv=low(*own), nrm=wide(*own), scl=wide(rows, LANES),
        st=low(*state), zst=wide(*zrows), dres=wide(*own), dlow=low(*own), dn=low(*own), xs=low(*own),
        dsend=low(*state), drecv=low(*state), dzs=wide(*zrows), dzr=wide(*zrows),
        dql=low(*own), dkl=low(*own), dvl=low(*own),
        ctab=wide(rows, rows), cosb=wide(rows, LANES), sinb=wide(rows, LANES),
        acc=wide(24, width), bup=wide(8, units),
        cr_ff=low(units, width), cr_a=low(2 * width, width), px=low(width, width),
        xr=low(count, 2, a_part, width), rs_ff=low(count - 1, 2, ff_part, width),
        rs_a=low(count - 1, 2, a_part, width), ff_o=low(2 * units, width), a_o=low(4 * width, width),
        smalls=wide(swaps + 1, lines, width), small_r=wide(swaps, lines, width),
        send=sem(12), recv=sem(12), r_send=sem(streams, count - 1), r_recv=sem(streams, count - 1),
        g_send=sem(streams, count - 1), g_recv=sem(streams, count - 1),
        x_send=sem(2 * A_CUTS, count), x_recv=sem(2 * A_CUTS, count),
        y_send=sem(2 * A_CUTS, count), y_recv=sem(2 * A_CUTS, count),
        m_send=sem(swaps), m_recv=sem(swaps), w_sem=sem(5 + halves), o_sem=sem(7),
    )
    vmem, anywhere = pl.BlockSpec(memory_space=pltpu.VMEM), pl.BlockSpec(memory_space=pl.ANY)
    outs = shaped(
        (own, bf16), (own, f32), ((2 * units, width), bf16), ((4 * width, width), bf16),
        ((lines, width), f32),
    )
    res, dtok, ff, a, small = pl.pallas_call(
        functools.partial(block_kernel, count),
        out_shape=outs,
        in_specs=[vmem] * 2 + [pl.BlockSpec(memory_space=pltpu.SMEM)] + [vmem] * 11 + [anywhere] * 6,
        out_specs=tuple([anywhere] * len(outs)),
        scratch_shapes=list(scratch.values()),
        compiler_params=pltpu.CompilerParams(
            collective_id=0, has_side_effects=True, vmem_limit_bytes=62 << 20
        ),
        name="block",
    )(
        tokens, positions, span_sizes.reshape(1, 1), b_query, b_key, b_value, b_out, norm1_gain,
        norm1_bias, b_down, norm2_gain, norm2_bias, b_up, out_grad,
        w_query, w_key, w_value, w_out, w_up, w_down,
    )
    return finish(rows, width, units, res, dtok, ff, a, small)


def pick(mesh):
    def per_device(*args):
        tokens, span_sizes, w_up = args[0], args[2], args[13]
        rows, width = tokens.shape
        units = w_up.shape[1]
        fits = (
            mesh.shape["tensor"] == 2
            and mesh.shape["dp"] == 16
            and span_sizes.shape[0] == 1
            and rows % TILE == 0
            and width == HEADS * HD
            and width % TILE == 0
            and units == 2 * width
        )
        return pair_device(*args) if fits else general_device(*args)

    return per_device


def solution(mesh):
    return jax.shard_map(
        pick(mesh),
        mesh=mesh,
        in_specs=(
            P(("dp", "tensor"), None),
            P("dp"),
            P("dp"),
            P(),
            P(),
            P(),
            P(),
            P(),
            P(),
            P(),
            P(),
            P(),
            P(),
            P(None, "tensor"),
            P("tensor"),
            P("tensor", None),
            P(),
            P(),
            P(),
            P(("dp", "tensor"), None),
        ),
        out_specs=(
            P(("dp", "tensor"), None),
            P(("dp", "tensor"), None),
            P(),
            P(),
            P(),
            P(),
            P(),
            P(),
            P(),
            P(),
            P(),
            P(),
            P(None, "tensor"),
            P("tensor"),
            P("tensor", None),
            P(),
            P(),
            P(),
        ),
        check_vma=False,
    )
```

```python
import functools
import math

import jax
import jax.numpy as jnp
from jax import lax
from jax.experimental import pallas as pl
from jax.experimental.pallas import tpu as pltpu
from jax.sharding import PartitionSpec as P

HEADS = 12
HD = 64
SUBLEN = 32


highest = lax.Precision.HIGHEST
norm_eps = 1e-05


def norm_forward(value, gain, shift):
    mean = jnp.mean(value, axis=-1, keepdims=True)
    centred = value - mean
    scale = lax.rsqrt(jnp.mean(centred * centred, axis=-1, keepdims=True) + norm_eps)
    normal = centred * scale
    return (normal * gain + shift, normal, scale)


def norm_backward(grad, normal, scale, gain):
    along = grad * gain
    inner = (
        along
        - jnp.mean(along, axis=-1, keepdims=True)
        - normal * jnp.mean(along * normal, axis=-1, keepdims=True)
    )
    return (inner * scale, jnp.sum(grad * normal, axis=0), jnp.sum(grad, axis=0))


def gelu_slope(pre):
    normal_cdf = 0.5 * (1.0 + jax.scipy.special.erf(pre * (1.0 / math.sqrt(2.0))))
    return normal_cdf + pre * jnp.exp(-0.5 * pre * pre) * (1.0 / math.sqrt(2.0 * math.pi))


def reach_table(count, span):
    slot_index = jnp.arange(count, dtype=jnp.int32)
    final = (slot_index * SUBLEN // span + 1) * span // SUBLEN - 1
    return (slot_index[None, :] <= final[:, None]).astype(jnp.float32)


def features(rows, w_joint, b_joint, cosine, sine):
    length = rows.shape[0]
    width = rows.shape[1]
    proj = jnp.dot(rows, w_joint, preferred_element_type=jnp.float32) + b_joint
    relu_query = jax.nn.relu(proj[:, :width]).reshape(length, HEADS, HD)
    relu_key = jax.nn.relu(proj[:, width : 2 * width]).reshape(length, HEADS, HD) * (1.0 / HD)
    q_feat = jnp.concatenate([relu_query * cosine, relu_query * sine], axis=-1).astype(jnp.bfloat16)
    k_feat = jnp.concatenate([relu_key * cosine, relu_key * sine], axis=-1).astype(jnp.bfloat16)
    v_low = proj[:, 2 * width :].astype(jnp.bfloat16)
    return (q_feat, k_feat, v_low)


def local_blocks(k_feat, v_low):
    count = k_feat.shape[0] // SUBLEN
    k_sub = k_feat.reshape(count, SUBLEN, HEADS, 2 * HD)
    v_sub = v_low.reshape(count, SUBLEN, HEADS, HD)
    blocks = jnp.einsum("tjhf,tjhd->thfd", k_sub, v_sub, preferred_element_type=jnp.float32)
    k_total = jnp.sum(k_sub.astype(jnp.float32), axis=1)
    return (blocks, k_total)


def attend_core(q_feat, k_feat, v_low, blocks, k_total, reach, extra_blocks, extra_keys):
    count = q_feat.shape[0] // SUBLEN
    q_sub = q_feat.reshape(count, SUBLEN, HEADS, 2 * HD)
    k_sub = k_feat.reshape(count, SUBLEN, HEADS, 2 * HD)
    v_sub = v_low.reshape(count, SUBLEN, HEADS, HD)
    state_low = (
        jnp.einsum("st,thfd->shfd", reach, blocks, precision=highest) + extra_blocks
    ).astype(jnp.bfloat16)
    z_sum = jnp.einsum("st,thf->shf", reach, k_total, precision=highest) + extra_keys
    numer = jnp.einsum("sihf,shfd->sihd", q_sub, state_low, preferred_element_type=jnp.float32)
    denom = jnp.einsum("sihf,shf->sih", q_sub.astype(jnp.float32), z_sum, precision=highest) + 1.0
    return (q_sub, k_sub, v_sub, state_low, z_sum, numer, denom)


def back_first(parts, grad_mixed):
    q_sub, k_sub, v_sub, state_low, z_sum, numer, denom = parts
    count = q_sub.shape[0]
    grad_out = grad_mixed.reshape(count, SUBLEN, HEADS, HD).astype(jnp.float32)
    d_numer = grad_out / denom[..., None]
    d_denom = -jnp.sum(grad_out * numer, axis=-1) / (denom * denom)
    q_wide = q_sub.astype(jnp.float32)
    d_query = jnp.einsum(
        "sihd,shfd->sihf", d_numer, state_low.astype(jnp.float32), precision=highest
    )
    d_query = d_query + d_denom[..., None] * z_sum[:, None]
    d_state = jnp.einsum("sihf,sihd->shfd", q_wide, d_numer, precision=highest)
    d_zsum = jnp.einsum("sihf,sih->shf", q_wide, d_denom, precision=highest)
    return (d_query, d_state, d_zsum)


def back_second(parts, reach, d_state, d_zsum, later_blocks, later_keys):
    q_sub, k_sub, v_sub = (parts[0], parts[1], parts[2])
    d_blocks = jnp.einsum("st,shfd->thfd", reach, d_state, precision=highest) + later_blocks
    d_ktotal = jnp.einsum("st,shf->thf", reach, d_zsum, precision=highest) + later_keys
    d_key = (
        jnp.einsum("thfd,tjhd->tjhf", d_blocks, v_sub.astype(jnp.float32), precision=highest)
        + d_ktotal[:, None]
    )
    d_value = jnp.einsum("thfd,tjhf->tjhd", d_blocks, k_sub.astype(jnp.float32), precision=highest)
    return (d_key, d_value)


def feature_grads(q_feat, k_feat, d_qf, d_kf, d_val, cos_part, sin_part):
    size = q_feat.shape[0]
    d_qf = d_qf.reshape(size, HEADS, 2 * HD)
    d_kf = d_kf.reshape(size, HEADS, 2 * HD)
    d_query = jnp.where(
        q_feat[..., :HD] > 0, d_qf[..., :HD] * cos_part + d_qf[..., HD:] * sin_part, 0.0
    )
    d_key = jnp.where(
        k_feat[..., :HD] > 0,
        (d_kf[..., :HD] * cos_part + d_kf[..., HD:] * sin_part) * (1.0 / HD),
        0.0,
    )
    return jnp.concatenate(
        [
            d_query.reshape(size, HEADS * HD),
            d_key.reshape(size, HEADS * HD),
            d_val.reshape(size, HEADS * HD),
        ],
        axis=1,
    )


def general_device(
    tokens,
    positions,
    span_sizes,
    w_query,
    b_query,
    w_key,
    b_key,
    w_value,
    b_value,
    w_out,
    b_out,
    norm1_gain,
    norm1_bias,
    w_up,
    b_up,
    w_down,
    b_down,
    norm2_gain,
    norm2_bias,
    out_grad,
):
    rank = lax.axis_index("tensor")
    tensor_count = lax.axis_size("tensor")
    own = tokens.shape[0]
    width = tokens.shape[1]
    seqs = span_sizes.shape[0]
    group = own * tensor_count
    length = group // seqs
    start = rank * own
    w_joint = jnp.concatenate([w_query, w_key, w_value], axis=1)
    b_joint = jnp.concatenate([b_query, b_key, b_value]).astype(jnp.float32)
    gain_one = norm1_gain.astype(jnp.float32)
    gain_two = norm2_gain.astype(jnp.float32)
    gathered = lax.all_gather(tokens, "tensor", axis=0, tiled=True)
    angle = math.pi / 2 * positions.astype(jnp.float32) / (3 * length)
    cosine = jnp.cos(angle).reshape(seqs, length, 1, 1)
    sine = jnp.sin(angle).reshape(seqs, length, 1, 1)

    def seq_forward(items):
        rows, cos_part, sin_part, span = items
        q_feat, k_feat, v_low = features(rows, w_joint, b_joint, cos_part, sin_part)
        blocks_seq, ktot_seq = local_blocks(k_feat, v_low)
        parts = attend_core(
            q_feat,
            k_feat,
            v_low,
            blocks_seq,
            ktot_seq,
            reach_table(q_feat.shape[0] // SUBLEN, span),
            0.0,
            0.0,
        )
        mixed_seq = (
            (parts[5] / parts[6][..., None]).reshape(rows.shape[0], width).astype(jnp.bfloat16)
        )
        return (mixed_seq, q_feat, k_feat, v_low)

    mixed, q_all, k_all, v_all = lax.map(
        seq_forward, (gathered.reshape(seqs, length, width), cosine, sine, span_sizes)
    )
    mixed = mixed.reshape(group, width)
    mixed_own = lax.dynamic_slice_in_dim(mixed, start, own, 0)
    resid = (
        tokens.astype(jnp.float32)
        + jnp.dot(mixed_own, w_out, preferred_element_type=jnp.float32)
        + b_out.astype(jnp.float32)
    )
    hidden, normal_one, scale_one = norm_forward(resid, gain_one, norm1_bias.astype(jnp.float32))
    hidden_low = hidden.astype(jnp.bfloat16)
    rows_in = lax.all_gather(hidden_low, "tensor", axis=0, tiled=True)
    pre = jnp.dot(rows_in, w_up, preferred_element_type=jnp.float32) + b_up.astype(jnp.float32)
    act_low = jax.nn.gelu(pre, approximate=False).astype(jnp.bfloat16)
    branch = lax.psum_scatter(
        jnp.dot(act_low, w_down, preferred_element_type=jnp.float32),
        "tensor",
        scatter_dimension=0,
        tiled=True,
    )
    summed = hidden + branch + b_down.astype(jnp.float32)
    result, normal_two, scale_two = norm_forward(summed, gain_two, norm2_bias.astype(jnp.float32))
    d_sum, d_gain_two, d_bias_two = norm_backward(
        out_grad.astype(jnp.float32), normal_two, scale_two, gain_two
    )
    d_bdown = jnp.sum(d_sum, axis=0)
    d_sum_low = d_sum.astype(jnp.bfloat16)
    rows_grad = lax.all_gather(d_sum_low, "tensor", axis=0, tiled=True)
    g_down = jnp.dot(act_low.T, rows_grad, preferred_element_type=jnp.float32)
    d_pre = jnp.dot(rows_grad, w_down.T, preferred_element_type=jnp.float32) * gelu_slope(pre)
    g_upbias = jnp.sum(d_pre, axis=0)
    d_pre_low = d_pre.astype(jnp.bfloat16)
    g_up = jnp.dot(rows_in.T, d_pre_low, preferred_element_type=jnp.float32)
    d_hidden = lax.psum_scatter(
        jnp.dot(d_pre_low, w_up.T, preferred_element_type=jnp.float32),
        "tensor",
        scatter_dimension=0,
        tiled=True,
    )
    g_up, g_upbias, g_down = (
        lax.psum(g_up.astype(jnp.bfloat16), "dp").astype(jnp.float32),
        lax.psum(g_upbias.astype(jnp.bfloat16), "dp").astype(jnp.float32),
        lax.psum(g_down.astype(jnp.bfloat16), "dp").astype(jnp.float32),
    )
    d_hidden = d_hidden + d_sum
    d_resid, d_gain_one, d_bias_one = norm_backward(d_hidden, normal_one, scale_one, gain_one)
    d_bout = jnp.sum(d_resid, axis=0)
    d_gain_one, d_bias_one, d_gain_two, d_bias_two, d_bout, d_bdown = lax.psum(
        (d_gain_one, d_bias_one, d_gain_two, d_bias_two, d_bout, d_bdown), ("dp", "tensor")
    )
    d_resid_low = d_resid.astype(jnp.bfloat16)
    rows_back = lax.all_gather(d_resid_low, "tensor", axis=0, tiled=True)
    g_out = jnp.dot(mixed.T, rows_back, preferred_element_type=jnp.float32)
    d_mixed = jnp.dot(rows_back, w_out.T, preferred_element_type=jnp.float32).astype(jnp.bfloat16)

    def seq_backward(items):
        q_feat, k_feat, v_low, cos_part, sin_part, span, grad_mixed = items
        blocks_seq, ktot_seq = local_blocks(k_feat, v_low)
        reach = reach_table(q_feat.shape[0] // SUBLEN, span)
        parts = attend_core(q_feat, k_feat, v_low, blocks_seq, ktot_seq, reach, 0.0, 0.0)
        d_qf, d_state, d_zsum = back_first(parts, grad_mixed)
        d_kf, d_val = back_second(parts, reach, d_state, d_zsum, 0.0, 0.0)
        joint = feature_grads(q_feat, k_feat, d_qf, d_kf, d_val, cos_part, sin_part)
        return (joint.astype(jnp.bfloat16), jnp.sum(joint, axis=0))

    d_joint, d_jbias = lax.map(
        seq_backward,
        (q_all, k_all, v_all, cosine, sine, span_sizes, d_mixed.reshape(seqs, length, width)),
    )
    d_joint = d_joint.reshape(group, 3 * width)
    d_jbias = jnp.sum(d_jbias, axis=0)
    g_joint = jnp.dot(gathered.T, d_joint, preferred_element_type=jnp.float32)
    d_joint_own = lax.dynamic_slice_in_dim(d_joint, start, own, 0)
    d_tokens = d_resid + jnp.dot(d_joint_own, w_joint.T, preferred_element_type=jnp.float32)
    g_joint, g_out, d_jbias = lax.psum((g_joint, g_out, d_jbias), "dp")
    return (
        result.astype(jnp.bfloat16),
        d_tokens,
        g_joint[:, :width],
        d_jbias[:width],
        g_joint[:, width : 2 * width],
        d_jbias[width : 2 * width],
        g_joint[:, 2 * width :],
        d_jbias[2 * width :],
        g_out,
        d_bout,
        d_gain_one,
        d_bias_one,
        g_up,
        g_upbias,
        g_down,
        d_bdown,
        d_gain_two,
        d_bias_two,
    )


f32 = jnp.float32
bf16 = jnp.bfloat16
MESH = pl.DeviceIdType.MESH
LANES = 2 * HD
TILE = 256
ROWBLOCK = 32
FF_CUTS = 3
A_CUTS = 3
LINES = tuple("l" + str(index) for index in range(9))


def tile_at(index, size):
    return pl.ds(pl.multiple_of(index * size, size), size)


def contract(left, right, left_dim, right_dim, precision=None):
    return lax.dot_general(
        left,
        right,
        (((left_dim,), (right_dim,)), ((), ())),
        precision=precision,
        preferred_element_type=f32,
    )


def mm(left, right):
    return contract(left, right, 1, 0)


def mm_nt(left, right):
    return contract(left, right, 1, 1)


def mm_tn(left, right):
    return contract(left, right, 0, 0)


def head_masks():
    lane = lax.broadcasted_iota(jnp.int32, (1, LANES), 1)
    first = (lane < HD).astype(f32)
    return first, 1.0 - first


def pair_mask():
    row = lax.broadcasted_iota(jnp.int32, (LANES, LANES), 0)
    col = lax.broadcasted_iota(jnp.int32, (LANES, LANES), 1)
    return ((row < HD) == (col < HD)).astype(f32)


def column_of(block, which):
    row = lax.broadcasted_iota(jnp.int32, block.shape, 0)
    return contract(jnp.where(row == which, block, 0.0), jnp.ones((8, LANES), f32), 0, 0, highest)


def squeeze_pair(square):
    return square[:HD] + square[HD:]


def spread_pair(part, mask):
    return jnp.concatenate([part, part], axis=0).astype(f32) * mask


def two_rows(top, below):
    row = lax.broadcasted_iota(jnp.int32, (8, LANES), 0)
    return jnp.where(row == 0, top, jnp.where(row == 1, below, 0.0))


def fold8(value):
    total = value[0:8]
    for start in range(8, value.shape[0], 8):
        total = total + value[start : start + 8]
    return total


def angle_tables(places, length, span, cosb, sinb, ctab):
    rows = cosb.shape[0]
    angle = math.pi / 2 * places.astype(f32).reshape(1, rows) / (3 * length)
    line = lax.broadcasted_iota(jnp.int32, (8, rows), 0)
    block = jnp.where(line == 0, jnp.cos(angle), jnp.where(line == 1, jnp.sin(angle), 0.0))
    cosb[...] = column_of(block, 0)
    sinb[...] = column_of(block, 1)
    both = contract(block, block, 0, 0, highest)
    row = lax.broadcasted_iota(jnp.int32, (rows, rows), 0)
    col = lax.broadcasted_iota(jnp.int32, (rows, rows), 1)
    seen = col <= (row | (span[0, 0] - 1))
    ctab[...] = jnp.where(seen, both * (1.0 / HD), 0.0)


def peer_copy(src, dst, sems, slot, device):
    return pltpu.make_async_remote_copy(
        src_ref=src,
        dst_ref=dst,
        send_sem=sems[0].at[slot],
        recv_sem=sems[1].at[slot],
        device_id=device,
        device_id_type=MESH,
    )


def ring_device(spot, depth, core):
    far = spot // depth
    z = far * (2 * depth - 1 - spot) + (1 - far) * spot
    return ((z * 2 + far) * 2 + core, lax.axis_index("tensor"))


def layer_norm(value):
    centred = value - jnp.mean(value, axis=-1, keepdims=True)
    scale = lax.rsqrt(jnp.mean(centred * centred, axis=-1, keepdims=True) + norm_eps)
    return centred * scale, scale


def layer_norm_back(grad, gain, normal, scale):
    along = grad * gain
    return (
        along
        - jnp.mean(along, axis=-1, keepdims=True)
        - normal * jnp.mean(along * normal, axis=-1, keepdims=True)
    ) * scale


def block_kernel(
    count, tok_h, places_h, span_h, bq, bk, bv, bo, g1, b1, bd, g2, b2, bup_in, og_h,
    wq, wk, wv, wo, wup, wdn,
    res_h, dtok_h, ff_h, a_h, small_h,
    tok, places, span, og, l0, l1, l2, l3, l4, l5, l6, l7, l8, bup_line, wa, wff, vec, hbuf, act, slope, dbuf, dpre, hid, numer, denom, tsend, trecv, zsend, zrecv,
    bsend, brecv, res, gff, dhs, dhr, dho, mixb, mixf, inv, rq, rk, vv, nrm, scl, st, zst,
    dres, dlow, dn, xs, dsend, drecv, dzs, dzr, dql, dkl, dvl, ctab, cosb, sinb, acc, bup,
    cr_ff, cr_a, px, xr, rs_ff, rs_a, ff_o, a_o, smalls, small_r,
    send, recv, r_send, r_recv, g_send, g_recv, x_send, x_recv, s_recv, y_recv, m_send, m_recv,
    w_sem, o_sem, l_sem,
):
    sems = (send, recv)
    rows, width = tok.shape
    units = wup.shape[1]
    halves = units // width
    pairs = width // LANES
    tiles = width // TILE
    depth = count // 2
    quarter = width
    dq, dk, dv, ga = numer, denom, hid, wff
    dp, rank = lax.axis_index("dp"), lax.axis_index("tensor")
    late = rank.astype(f32)
    early = 1.0 - late
    core, y, z = dp % 2, (dp // 2) % 2, dp // 4
    spot = y * (2 * depth - 1 - z) + (1 - y) * z
    sibling = (dp + 1 - 2 * core, rank)
    peer = (dp, 1 - rank)
    ahead = ring_device((spot + 1) % count, depth, core)
    behind = ring_device((spot + count - 1) % count, depth, core)
    swaps = [sibling, peer, (dp + 2 - 4 * y, rank)]
    step = 1
    while step < depth:
        bit = (z // step) % 2
        swaps.append((dp + 4 * (step - 2 * step * bit), rank))
        step *= 2
    partners = [ahead, behind] + swaps
    barrier = pltpu.get_barrier_semaphore()
    for device in partners:
        pl.semaphore_signal(barrier, inc=1, device_id=device, device_id_type=MESH)

    loads = [
        (wk, wa.at[pl.ds(width, width), :]),
        (wv, wa.at[pl.ds(2 * width, width), :]),
        (wq, wa.at[pl.ds(0, width), :]),
        (wo, wa.at[pl.ds(3 * width, width), :]),
    ]
    for part in range(halves):
        loads.append(
            (wup.at[:, pl.ds(part * width, width)], wff.at[pl.ds(units + part * width, width), :])
        )
    loads.append((wdn, wff.at[pl.ds(0, units), :]))

    def load(index):
        return pltpu.make_async_copy(loads[index][0], loads[index][1], w_sem.at[index])

    small_loads = [(tok_h, tok), (places_h, places), (span_h, span)]
    vectors = (bq, bk, bv, bo, g1, b1, bd, g2, b2)
    lines = (l0, l1, l2, l3, l4, l5, l6, l7, l8)
    small_loads += [pair for pair in zip(vectors, lines)]
    small_loads += [(bup_in, bup_line), (og_h, og)]

    def fetch(index):
        return pltpu.make_async_copy(*small_loads[index], l_sem.at[index])

    fetch(0).start()
    for index in range(3):
        load(index).start()
    for index in range(1, len(small_loads)):
        fetch(index).start()
    for index in range(1, len(small_loads) - 1):
        fetch(index).wait()

    def out_copy(source, target, at, slot):
        return pltpu.make_async_copy(source.at[at, :], target.at[at, :], o_sem.at[slot])

    for index in range(len(vectors)):
        vec[index : index + 1, :] = lines[index][...].astype(f32).reshape(1, width)
    for part in range(halves):
        piece = bup_line[pl.ds(part * width, width)]
        vec[9 + part : 10 + part, :] = piece.astype(f32).reshape(1, width)
    own, far_rows = pl.ds(0, rows), pl.ds(rows, rows)
    my_places = places[pl.ds(pl.multiple_of(rank * rows, rows), rows)]
    angle_tables(my_places, places.shape[0], span, cosb, sinb, ctab)
    diag = pair_mask()
    first, second = head_masks()
    first_low, second_low = first.astype(bf16), second.astype(bf16)
    diag_low = diag.astype(bf16)
    acc[...] = jnp.zeros_like(acc)
    bup[...] = jnp.zeros_like(bup)
    smalls[0] = jnp.zeros(smalls.shape[1:], f32)

    def add_small(slot, line):
        smalls[0, slot : slot + 1, :] = line

    def project(which, target):
        @pl.loop(0, tiles)
        def _(j):
            cols = tile_at(j, TILE)
            value = mm(tok[...], wa[pl.ds(which * width, width), cols]) + vec[which : which + 1, cols]
            if which < 2:
                value = jnp.maximum(value, 0.0)
            target[:, cols] = value.astype(bf16)

    fetch(0).wait()
    load(0).wait()
    project(1, rk)
    load(1).wait()
    project(2, vv)
    for index in range(3, len(loads)):
        load(index).start()

    @pl.loop(0, pairs)
    def _(p):
        lanes = tile_at(p, LANES)
        k = rk[:, lanes].astype(f32) * (1.0 / HD)
        v = vv[:, lanes]
        kc, ks = (k * cosb[...]).astype(bf16), (k * sinb[...]).astype(bf16)
        tsend[p, 0] = squeeze_pair(mm_tn(kc, v) * diag).astype(bf16)
        tsend[p, 1] = squeeze_pair(mm_tn(ks, v) * diag).astype(bf16)
        zsend[p] = two_rows(
            jnp.sum(kc.astype(f32), axis=0, keepdims=True),
            jnp.sum(ks.astype(f32), axis=0, keepdims=True),
        )

    pl.semaphore_wait(barrier, len(partners))
    state_copy = peer_copy(tsend, trecv, sems, 0, peer)
    key_copy = peer_copy(zsend, zrecv, sems, 1, peer)
    state_copy.start()
    key_copy.start()
    load(2).wait()
    project(0, rq)

    @pl.loop(0, pairs)
    def _(p):
        lanes = tile_at(p, LANES)
        q, k, v = rq[:, lanes], rk[:, lanes], vv[:, lanes]
        parts = []
        for mask, rest in ((first_low, second_low), (second_low, first_low)):
            prob = (mm_nt(q * mask, k) * ctab[...]).astype(bf16)
            parts.append(mm(prob, v * mask + rest))
        numer[:, lanes] = parts[0] * first + parts[1] * second
        denom[:, lanes] = pltpu.roll(parts[0] * second + parts[1] * first, HD, 1)

    state_copy.wait()
    key_copy.wait()

    @pl.loop(0, pairs)
    def _(p):
        lanes = tile_at(p, LANES)
        q = rq[:, lanes].astype(f32)
        qc, qs = (q * cosb[...]).astype(bf16), (q * sinb[...]).astype(bf16)
        st[p] = (trecv[p].astype(f32) * late).astype(bf16)
        zblock = zrecv[p] * late
        zst[p] = zblock
        weighted = qc.astype(f32) * zblock[0:1, :] + qs.astype(f32) * zblock[1:2, :]
        num, den = numer[:, lanes], denom[:, lanes] + 1.0 + mm(weighted.astype(bf16), diag_low)
        for part, feat in ((0, qc), (1, qs)):
            num += mm(feat, spread_pair(st[p, part], diag).astype(bf16))
        reciprocal = 1.0 / den
        mix = num * reciprocal
        inv[:, lanes] = reciprocal
        mixf[:, lanes] = mix
        mixb[:, lanes] = mix.astype(bf16)

    load(3).wait()

    @pl.loop(0, tiles)
    def _(j):
        cols = tile_at(j, TILE)
        hid[:, cols] = (
            tok[:, cols].astype(f32) + mm(mixb[...], wa[pl.ds(3 * width, width), cols]) + vec[3:4, cols]
        )

    span_rows = rows // 2
    near = [pl.ds(k * span_rows, span_rows) for k in range(2)]
    away = [pl.ds(rows + k * span_rows, span_rows) for k in range(2)]
    blocks = span_rows // ROWBLOCK

    def norm_rows(i):
        at = tile_at(i, ROWBLOCK)
        normal, scale = layer_norm(hid[at, :])
        hidden = normal * vec[4:5, :] + vec[5:6, :]
        nrm[at, :] = normal
        scl[at, :] = jnp.broadcast_to(scale, (ROWBLOCK, LANES))
        hid[at, :] = hidden
        hbuf[at, :] = hidden.astype(bf16)

    def rows_copy(k):
        return peer_copy(hbuf.at[near[k]], hbuf.at[away[k]], sems, 12 + k, peer)

    def branch_copy(k):
        return peer_copy(bsend.at[near[k]], brecv.at[near[k]], sems, 14 + k, peer)

    def grad_copy(k):
        return peer_copy(dbuf.at[near[k]], dbuf.at[away[k]], sems, 16 + k, peer)

    def hidden_copy(k):
        return peer_copy(dhs.at[near[k]], dhr.at[near[k]], sems, 18 + k, peer)

    for k in range(2):
        pl.loop(k * blocks, (k + 1) * blocks)(norm_rows)
        rows_copy(k).start()
    for index in range(4, len(loads)):
        load(index).wait()
    fetch(len(small_loads) - 1).wait()

    def raise_rows(part):
        for piece in range(halves):

            @pl.loop(0, tiles)
            def _(j, piece=piece):
                cols, narrow = tile_at(piece * tiles + j, TILE), tile_at(j, TILE)
                weight = wff[pl.ds(units + piece * width, width), narrow]
                pre = mm(hbuf[part, :], weight) + vec[9 + piece : 10 + piece, narrow]
                cdf = 0.5 * (1.0 + lax.erf(pre * (1.0 / math.sqrt(2.0))))
                act[part, cols] = (pre * cdf).astype(bf16)
                slope[part, cols] = cdf + pre * jnp.exp(-0.5 * pre * pre) * (
                    1.0 / math.sqrt(2.0 * math.pi)
                )

    raise_rows(own)
    for k in range(2):
        rows_copy(k).wait()
        raise_rows(away[k])

        @pl.loop(0, tiles)
        def _(j, k=k):
            cols = tile_at(j, TILE)
            bsend[near[k], cols] = mm(act[away[k], :], wff[pl.ds(0, units), cols]).astype(bf16)

        branch_copy(k).start()

    @pl.loop(0, tiles)
    def _(j):
        cols = tile_at(j, TILE)
        hid[:, cols] += mm(act[own, :], wff[pl.ds(0, units), cols]) + vec[6:7, cols]

    def finish_rows(i):
        at = tile_at(i, ROWBLOCK)
        normal, scale = layer_norm(hid[at, :] + brecv[at, :].astype(f32))
        res[at, :] = (normal * vec[7:8, :] + vec[8:9, :]).astype(bf16)
        grad = og[at, :].astype(f32)
        inner = layer_norm_back(grad, vec[7:8, :], normal, scale)
        dho[at, :] = inner
        dbuf[at, :] = inner.astype(bf16)
        acc[0:8, :] += fold8(grad * normal)
        acc[8:16, :] += fold8(grad)
        acc[16:24, :] += fold8(inner)

    for k in range(2):
        branch_copy(k).wait()
        pl.loop(k * blocks, (k + 1) * blocks)(finish_rows)
        grad_copy(k).start()
    result_out = pltpu.make_async_copy(res, res_h, o_sem.at[0])
    result_out.start()
    for slot in range(3):
        add_small(3 + slot, jnp.sum(acc[8 * slot : 8 * slot + 8, :], axis=0, keepdims=True))

    def lower_rows(part):
        @pl.loop(0, units // TILE)
        def _(j):
            cols = tile_at(j, TILE)
            d_pre = mm_nt(dbuf[part, :], wff[cols, :]) * slope[part, cols]
            bup[:, cols] += fold8(d_pre)
            dpre[part, cols] = d_pre.astype(bf16)

    def lower_hidden(part, cols, j):
        total = 0.0
        for piece in range(halves):
            weight = wff[pl.ds(pl.multiple_of(units + piece * width + j * TILE, TILE), TILE), :]
            total += mm_nt(dpre[part, piece * width : (piece + 1) * width], weight)
        return total

    lower_rows(own)
    for k in range(2):
        grad_copy(k).wait()
        lower_rows(away[k])

        @pl.loop(0, tiles)
        def _(j, k=k):
            cols = tile_at(j, TILE)
            dhs[near[k], cols] = lower_hidden(away[k], cols, j).astype(bf16)

        hidden_copy(k).start()

    def make_down():
        @pl.loop(0, units // TILE)
        def _(j):
            cols = tile_at(j, TILE)
            gff[cols, :] = mm_tn(act[:, cols], dbuf[...]).astype(bf16)

    def make_up():
        for piece in range(halves):

            @pl.loop(0, tiles)
            def _(j, piece=piece):
                gff[pl.ds(units + piece * width, width), tile_at(j, TILE)] = mm_tn(
                    hbuf[...], dpre[:, tile_at(piece * tiles + j, TILE)]
                ).astype(bf16)

    def part_rows(which, size):
        return pl.ds(pl.multiple_of(which * size, size), size)

    core_ff = peer_copy(gff.at[part_rows(1 - core, units), :], cr_ff, sems, 8, sibling)
    pl.when(core == 0)(make_up)
    pl.when(core == 1)(make_down)
    core_ff.start()
    pl.when(core == 0)(make_down)
    pl.when(core == 1)(make_up)

    band, per = width // 4, count // 4
    ff_streams, a_streams = [], []
    for kind, (cuts, group) in enumerate(((FF_CUTS, ff_streams), (A_CUTS, a_streams))):
        size = (quarter if kind else units) // count // 2
        for way in range(2):
            for cut in range(cuts):
                number = 2 * FF_CUTS * kind + way * cuts + cut
                piece = size // cuts
                group.append((number, kind, way, cut * piece, piece))
    slots, sums, outs = (rs_ff, rs_a), (gff, ga), (ff_o, a_o)
    ff_size, a_size = units // count // 2, quarter // count // 2
    mine, theirs = core * 2 + rank, core * 2 + 1 - rank

    def ff_rows(at, way, offset, length, base):
        start = base + (at % count) * 2 * ff_size + way * ff_size + offset
        return pl.ds(pl.multiple_of(start, 16), length)

    def a_rows(at, way, offset, length, owner):
        chunk = at % count
        start = (chunk // per) * width + owner * band + (chunk % per) * 2 * a_size
        return pl.ds(pl.multiple_of(start + way * a_size + offset, 16), length)

    def line_rows(at, way, offset, length):
        start = (at % count) * 2 * a_size + way * a_size + offset
        return pl.ds(pl.multiple_of(start, 16), length)

    def core_rows(at, way, offset, length):
        chunk = at % count
        start = (chunk // per) * 2 * band + rank * band + (chunk % per) * 2 * a_size
        return pl.ds(pl.multiple_of(start + way * a_size + offset, 16), length)

    def stream_rows(stream, at):
        _, kind, way, offset, length = stream
        if kind:
            return a_rows(at, way, offset, length, mine)
        return ff_rows(at, way, offset, length, core * units)

    def toward(way):
        return behind if way else ahead

    def turn(way):
        return -1 if way else 1

    def remote(source, target, send_sem, recv_sem, device):
        return pltpu.make_async_remote_copy(
            src_ref=source,
            dst_ref=target,
            send_sem=send_sem,
            recv_sem=recv_sem,
            device_id=device,
            device_id_type=MESH,
        )

    def spread_copy(stream, at, s):
        number, kind, way, offset, length = stream
        return remote(
            sums[kind].at[stream_rows(stream, at), :],
            slots[kind].at[s, way, pl.ds(offset, length), :],
            r_send.at[kind],
            r_recv.at[number, s],
            toward(way),
        )

    def gather_copy(stream, at, s):
        number, kind, way, _, _ = stream
        where = outs[kind].at[stream_rows(stream, at), :]
        return remote(where, where, g_send.at[kind], g_recv.at[number, s], toward(way))

    def across_copy(way, s, owner):
        at = spot + 2 * count + turn(way) * (1 - s)
        where = a_o.at[a_rows(at, way, 0, a_size, owner), :]
        return remote(where, where, x_send.at[0], x_recv.at[way, s], peer)

    def side_copy(way, s, owner, lane):
        at = spot + 2 * count + turn(way) * (1 - s)
        where = a_o.at[a_rows(at, way, 0, a_size, owner), :]
        return remote(where, where, x_send.at[1], s_recv.at[2 * lane + way, s], sibling)

    def fold_copy(way, s):
        at = spot + count - turn(way) * s
        return remote(
            px.at[line_rows(at, way, 0, a_size), :],
            xr.at[s, way],
            x_send.at[2],
            y_recv.at[way, s],
            peer,
        )

    def start_folds(s):
        for way in range(2):
            fold_copy(way, s).start()

    def own_part(stream, at, s):
        _, kind, way, offset, length = stream
        value = sums[kind][stream_rows(stream, at), :].astype(f32)
        if kind == 0:
            return value + cr_ff[ff_rows(at, way, offset, length, 0), :].astype(f32)
        if offset == 0:
            fold_copy(way, s).wait_recv()
        return (
            value
            + cr_a[core_rows(at, way, offset, length), :].astype(f32)
            + xr[s, way, pl.ds(offset, length), :].astype(f32)
        )

    def ring_first(streams):
        for stream in streams:
            at = spot + count
            sums[stream[1]][stream_rows(stream, at), :] = own_part(stream, at, 0).astype(bf16)
            spread_copy(stream, at, 0).start()

    def pass_on(stream, s):
        _, kind, way, offset, length = stream
        if kind and offset + length == a_size:
            across_copy(way, s, mine).start()
            side_copy(way, s, mine, 0).start()

    def ring_spread(streams, s, last=False):
        for stream in streams:
            _, kind, way, offset, length = stream
            at = spot + count - turn(way) * (s + 1)
            target = stream_rows(stream, at)
            part = own_part(stream, at, s + 1)
            spread_copy(stream, at, s).wait_recv()
            arrived = slots[kind][s, way, pl.ds(offset, length), :].astype(f32)
            total = (part + arrived).astype(bf16)
            if last:
                outs[kind][target, :] = total
                gather_copy(stream, at, 0).start()
                pass_on(stream, 0)
            else:
                sums[kind][target, :] = total
                spread_copy(stream, at, s + 1).start()

    def ring_gather(streams, s, last=False):
        for stream in streams:
            at = spot + 2 * count - turn(stream[2]) * s
            gather_copy(stream, at, s).wait_recv()
            if not last:
                gather_copy(stream, at, s + 1).start()
            pass_on(stream, s + 1)

    def cross_over(s):
        for way in range(2):
            across_copy(way, s, theirs).wait_recv()
            side_copy(way, s, theirs, 1).start()

    def small_copy(index):
        return peer_copy(smalls.at[index], small_r.at[index], (m_send, m_recv), index, swaps[index])

    def swap_small(index):
        small_copy(index).wait()
        smalls[index + 1] = smalls[index] + small_r[index]
        if index + 1 < len(swaps):
            small_copy(index + 1).start()

    for piece in range(halves):
        line = jnp.sum(bup[:, piece * width : (piece + 1) * width], axis=0, keepdims=True)
        add_small(9 + piece, line * early)
        add_small(9 + halves + piece, line * late)

    @pl.loop(0, tiles)
    def _(j):
        cols = tile_at(j, TILE)
        dho[:, cols] += lower_hidden(own, cols, j)

    acc[...] = jnp.zeros_like(acc)
    core_ff.wait()
    ring_first(ff_streams)
    hidden_copy(0).wait()
    hidden_copy(1).wait()
    ring_spread(ff_streams, 0)

    @pl.loop(0, rows // ROWBLOCK)
    def _(i):
        at = tile_at(i, ROWBLOCK)
        grad = dho[at, :] + dhr[at, :].astype(f32)
        normal = nrm[at, :]
        inner = layer_norm_back(grad, vec[4:5, :], normal, scl[at, 0:1])
        dres[at, :] = inner
        dlow[at, :] = inner.astype(bf16)
        acc[0:8, :] += fold8(grad * normal)
        acc[8:16, :] += fold8(grad)
        acc[16:24, :] += fold8(inner)

    for slot in range(3):
        add_small(slot, jnp.sum(acc[8 * slot : 8 * slot + 8, :], axis=0, keepdims=True))

    @pl.loop(0, tiles)
    def _(j):
        cols = tile_at(j, TILE)
        d_mixed = mm_nt(dlow[...], wa[tile_at(3 * tiles + j, TILE), :]).astype(bf16).astype(f32)
        d_numer = (d_mixed * inv[:, cols]).astype(bf16)
        dn[:, cols] = d_numer
        xs[:, cols] = (d_numer.astype(f32) * mixf[:, cols]).astype(bf16)

    ring_spread(ff_streams, 1)

    @pl.loop(0, pairs)
    def _(p):
        lanes = tile_at(p, LANES)
        q = rq[:, lanes].astype(f32)
        qc, qs = (q * cosb[...]).astype(bf16), (q * sinb[...]).astype(bf16)
        d_numer = dn[:, lanes]
        dsend[p, 0] = squeeze_pair(mm_tn(qc, d_numer) * diag).astype(bf16)
        dsend[p, 1] = squeeze_pair(mm_tn(qs, d_numer) * diag).astype(bf16)
        across = mm(xs[:, lanes], diag_low)
        dzs[p] = -two_rows(
            jnp.sum(qc.astype(f32) * across, axis=0, keepdims=True),
            jnp.sum(qs.astype(f32) * across, axis=0, keepdims=True),
        )

    turn_copy = peer_copy(dsend, drecv, sems, 6, peer)
    turn_keys = peer_copy(dzs, dzr, sems, 7, peer)
    turn_copy.start()
    turn_keys.start()

    @pl.loop(0, tiles)
    def _(j):
        cols = tile_at(j, TILE)
        ga[tile_at(3 * tiles + j, TILE), :] = mm_tn(mixb[:, cols], dlow[...]).astype(bf16)

    def core_a(m):
        there = pl.ds(pl.multiple_of(m * width + (1 - core) * 2 * band, 2 * band), 2 * band)
        here = pl.ds(m * 2 * band, 2 * band)
        return peer_copy(ga.at[there, :], cr_a.at[here, :], sems, (9, 11, 20, 21)[m], sibling)

    def fill_px(m):
        core_a(m).wait()
        there = pl.ds(pl.multiple_of(m * width + theirs * band, band), band)
        here = pl.ds(pl.multiple_of(m * 2 * band + (1 - rank) * band, band), band)
        px[m * band : (m + 1) * band, :] = (
            ga[there, :].astype(f32) + cr_a[here, :].astype(f32)
        ).astype(bf16)

    core_a(3).start()
    ring_spread(ff_streams, 2)

    def inside(p):
        lanes = tile_at(p, LANES)
        q, k, v = rq[:, lanes], rk[:, lanes], vv[:, lanes]
        d_numer = dn[:, lanes]
        turned = (-pltpu.roll(xs[:, lanes].astype(f32), HD, 1)).astype(bf16)
        sum_q = sum_k = sum_v = 0.0
        for mask, rest in ((first_low, second_low), (second_low, first_low)):
            q_head, k_head, d_head = q * mask, k * mask, d_numer * mask
            table = ctab[...]
            prob = (mm_nt(q_head, k) * table).astype(bf16)
            d_prob = mm_nt(d_head + turned * rest, v * mask + rest)
            d_score = (d_prob * table).astype(bf16)
            sum_v += mm_tn(prob, d_head)
            sum_q += mm(d_score, k_head)
            sum_k += mm_tn(d_score, q_head)
        dq[:, lanes] = sum_q
        dk[:, lanes] = sum_k
        dv[:, lanes] = sum_v

    pl.loop(0, pairs // 2)(inside)
    ring_spread(ff_streams, 3)
    pl.loop(pairs // 2, pairs)(inside)
    turn_copy.wait()
    turn_keys.wait()

    @pl.loop(0, pairs)
    def _(p):
        lanes = tile_at(p, LANES)
        q, v = rq[:, lanes].astype(f32), vv[:, lanes]
        k = rk[:, lanes].astype(f32)
        d_numer, x = dn[:, lanes], xs[:, lanes]
        sum_q, sum_k, sum_v = dq[:, lanes], dk[:, lanes], dv[:, lanes]
        zblock, dzblock = zst[p], dzr[p] * early
        along = mm(x, diag_low)
        for part, wave in ((0, cosb[...]), (1, sinb[...])):
            state = spread_pair(st[p, part], diag).astype(bf16)
            sum_q += wave * (mm_nt(d_numer, state) - along * zblock[part : part + 1, :])
            d_state = (spread_pair(drecv[p, part], diag) * early).astype(bf16)
            sum_k += wave * (mm_nt(v, d_state) + dzblock[part : part + 1, :]) * (1.0 / HD)
            sum_v += mm((k * wave * (1.0 / HD)).astype(bf16), d_state)
        sum_q = jnp.where(q > 0, sum_q, 0.0)
        sum_k = jnp.where(k > 0, sum_k, 0.0)
        dql[:, lanes] = sum_q.astype(bf16)
        dkl[:, lanes] = sum_k.astype(bf16)
        dvl[:, lanes] = sum_v.astype(bf16)
        for slot, value in ((6, sum_q), (7, sum_k), (8, sum_v)):
            smalls[0, slot : slot + 1, lanes] = jnp.sum(value, axis=0, keepdims=True)

    small_copy(0).start()

    def make_grad(which, source):
        @pl.loop(0, tiles)
        def _(j):
            ga[tile_at(which * tiles + j, TILE), :] = mm_tn(
                tok[:, tile_at(j, TILE)], source[...]
            ).astype(bf16)

        core_a(which).start()

    make_grad(2, dvl)
    make_grad(0, dql)
    fill_px(3)
    make_grad(1, dkl)
    fill_px(2)
    fill_px(0)
    fill_px(1)
    for s in range(3):
        start_folds(s)

    @pl.loop(0, tiles)
    def _(j):
        cols = tile_at(j, TILE)
        dres[:, cols] += (
            mm_nt(dql[...], wa[cols, :])
            + mm_nt(dkl[...], wa[tile_at(tiles + j, TILE), :])
            + mm_nt(dvl[...], wa[tile_at(2 * tiles + j, TILE), :])
        )

    token_out = pltpu.make_async_copy(dres, dtok_h, o_sem.at[1])
    token_out.start()
    ring_first(a_streams)
    swap_small(0)

    def spread_both(s):
        start_folds(s + 3)
        ring_spread(a_streams, s)
        ring_spread(ff_streams, s + 4)

    def spread_gather(s):
        ring_spread(a_streams, s)
        ring_gather(ff_streams, s - 3)

    def gather_both(s):
        ring_gather(a_streams, s)
        ring_gather(ff_streams, s + 4)
        cross_over(s)

    def gather_one(s):
        ring_gather(a_streams, s)
        cross_over(s)

    pl.loop(0, 2)(spread_both)
    swap_small(1)
    start_folds(5)
    ring_spread(a_streams, 2)
    ring_spread(ff_streams, 6, True)
    start_folds(6)
    start_folds(7)
    swap_small(2)
    pl.loop(3, 6)(spread_gather)
    swap_small(3)
    ring_spread(a_streams, 6, True)
    ring_gather(ff_streams, 3)
    pl.loop(0, 2)(gather_both)
    swap_small(4)
    small_out = pltpu.make_async_copy(smalls.at[len(swaps)], small_h, o_sem.at[6])
    small_out.start()
    ring_gather(a_streams, 2)
    ring_gather(ff_streams, 6, True)
    own_ff = part_rows(core, units)
    back_ff = peer_copy(ff_o.at[own_ff, :], ff_o.at[own_ff, :], sems, 10, sibling)
    back_ff.start()
    near_ff = out_copy(ff_o, ff_h, own_ff, 2)
    near_ff.start()
    cross_over(2)
    gather_one(3)
    back_ff.wait()
    far_ff = out_copy(ff_o, ff_h, part_rows(1 - core, units), 3)
    far_ff.start()
    pl.loop(4, 6)(gather_one)
    ring_gather(a_streams, 6, True)
    cross_over(6)
    cross_over(7)

    def drain(kind, source, total, sem):
        where = source.at[pl.ds(0, total), :]
        remote(where, where, sem, x_recv.at[0, 0], peer).wait_send()

    for kind, size in ((0, ff_size), (1, a_size)):
        drain(kind, sums[kind], 2 * (count - 1) * size, r_send.at[kind])
        drain(kind, outs[kind], 2 * (count - 1) * size, g_send.at[kind])
    drain(1, px, 2 * count * a_size, x_send.at[2])

    @pl.loop(0, count)
    def _(s):
        for way in range(2):
            for lane, owner in ((0, (1 - core) * 2 + rank), (1, (1 - core) * 2 + 1 - rank)):
                side_copy(way, s, owner, lane).wait_recv()

    whole_a = pltpu.make_async_copy(a_o, a_h, o_sem.at[4])
    whole_a.start()
    drain(1, a_o, 2 * count * a_size, x_send.at[0])
    drain(1, a_o, 4 * count * a_size, x_send.at[1])
    for copy in (result_out, token_out, near_ff, far_ff, small_out, whole_a):
        copy.wait()


def finish_kernel(halves, *refs):
    g_out, up, down, small, res, dtok = refs[:4], refs[4 : 4 + halves], *refs[4 + halves : 8 + halves]
    out = refs[8 + halves :]
    late = lax.axis_index("tensor") > 0
    for source, where in zip(g_out, (2, 4, 6, 8)):
        out[where][...] = source[...].astype(f32)
    width = res.shape[1]
    for piece in range(halves):
        out[12][:, piece * width : (piece + 1) * width] = up[piece][...].astype(f32)
    out[14][...] = down[...].astype(f32)

    @pl.when(pl.program_id(0) == 0)
    def _():
        out[0][...] = res[...]
        out[1][...] = dtok[...]
        for where, row in ((3, 6), (5, 7), (7, 8), (9, 2), (10, 0), (11, 1), (15, 5), (16, 3), (17, 4)):
            out[where][...] = small[row : row + 1, :].reshape(width)
        for piece in range(halves):
            line = jnp.where(
                late,
                small[9 + halves + piece : 10 + halves + piece, :],
                small[9 + piece : 10 + piece, :],
            )
            out[13][pl.ds(piece * width, width)] = line.reshape(width)


def finish(rows, width, units, res, dtok, ff, a, small):
    halves, steps = units // width, width // LANES
    low = (LANES, width)
    down_rows = units // steps

    def whole(shape):
        return pl.BlockSpec(shape, lambda i: (0,) * len(shape))

    def at_block(shape, start):
        return pl.BlockSpec(shape, lambda i: (start + i, 0))

    in_specs = [at_block(low, which * steps) for which in range(4)]
    in_specs += [at_block(low, units // LANES + piece * steps) for piece in range(halves)]
    in_specs += [at_block((down_rows, width), 0), whole(small.shape), whole(res.shape), whole(dtok.shape)]
    matrix, line = (width, width), (width,)
    shapes = [
        (res.shape, bf16), (dtok.shape, f32), (matrix, f32), (line, f32), (matrix, f32), (line, f32),
        (matrix, f32), (line, f32), (matrix, f32), (line, f32), (line, f32), (line, f32),
        ((width, units), f32), ((units,), f32), ((units, width), f32), (line, f32), (line, f32), (line, f32),
    ]
    special = {
        2: at_block(low, 0), 4: at_block(low, 0), 6: at_block(low, 0), 8: at_block(low, 0),
        12: at_block((LANES, units), 0), 14: at_block((down_rows, width), 0),
    }
    return pl.pallas_call(
        functools.partial(finish_kernel, halves),
        grid=(steps,),
        out_shape=shaped(*shapes),
        in_specs=in_specs,
        out_specs=tuple(special.get(i, whole(shape)) for i, (shape, _) in enumerate(shapes)),
        compiler_params=pltpu.CompilerParams(vmem_limit_bytes=62 << 20),
        name="finish",
    )(*([a] * 4), *([ff] * (halves + 1)), small, res, dtok)


def shaped(*items):
    return tuple(jax.ShapeDtypeStruct(shape, kind) for shape, kind in items)


def pair_device(
    tokens,
    positions,
    span_sizes,
    w_query,
    b_query,
    w_key,
    b_key,
    w_value,
    b_value,
    w_out,
    b_out,
    norm1_gain,
    norm1_bias,
    w_up,
    b_up,
    w_down,
    b_down,
    norm2_gain,
    norm2_bias,
    out_grad,
):
    rows, width = tokens.shape
    units = w_up.shape[1]
    pairs = width // LANES
    halves = units // width
    count = lax.axis_size("dp") // 2
    swaps = 2 + count.bit_length() - 1
    streams = 2 * (FF_CUTS + A_CUTS)
    ff_part, a_part = units // count // 2, width // count // 2
    lines = 9 + 2 * halves
    lines += -lines % 8

    def low(*shape):
        return pltpu.VMEM(shape, bf16)

    def wide(*shape):
        return pltpu.VMEM(shape, f32)

    def sem(*shape):
        return pltpu.SemaphoreType.DMA(shape)

    state, zrows = (pairs, 2, HD, LANES), (pairs, 8, LANES)
    own, pair = (rows, width), (2 * rows, width)
    scratch = dict(
        tok=low(*own), places=pltpu.VMEM(positions.shape, jnp.int32), span=pltpu.SMEM((1, 1), jnp.int32),
        og=low(*own), **{name: low(width) for name in LINES}, bup_line=low(units),
        wa=low(4 * width, width), wff=low(2 * units, width), vec=wide(9 + halves + -(9 + halves) % 8, width),
        hbuf=low(*pair), act=low(2 * rows, units), slope=wide(2 * rows, units), dbuf=low(*pair),
        dpre=low(2 * rows, units), hid=wide(*own), numer=wide(*own), denom=wide(*own),
        tsend=low(*state), trecv=low(*state), zsend=wide(*zrows), zrecv=wide(*zrows),
        bsend=low(*own), brecv=low(*own), res=low(*own), gff=low(2 * units, width),
        dhs=low(*own), dhr=low(*own), dho=wide(*own), mixb=low(*own), mixf=wide(*own), inv=wide(*own),
        rq=low(*own), rk=low(*own), vv=low(*own), nrm=wide(*own), scl=wide(rows, LANES),
        st=low(*state), zst=wide(*zrows), dres=wide(*own), dlow=low(*own), dn=low(*own), xs=low(*own),
        dsend=low(*state), drecv=low(*state), dzs=wide(*zrows), dzr=wide(*zrows),
        dql=low(*own), dkl=low(*own), dvl=low(*own),
        ctab=wide(rows, rows), cosb=wide(rows, LANES), sinb=wide(rows, LANES),
        acc=wide(24, width), bup=wide(8, units),
        cr_ff=low(units, width), cr_a=low(2 * width, width), px=low(width, width),
        xr=low(count, 2, a_part, width), rs_ff=low(count - 1, 2, ff_part, width),
        rs_a=low(count - 1, 2, a_part, width), ff_o=low(2 * units, width), a_o=low(4 * width, width),
        smalls=wide(swaps + 1, lines, width), small_r=wide(swaps, lines, width),
        send=sem(22), recv=sem(22), r_send=sem(2), r_recv=sem(streams, count - 1),
        g_send=sem(2), g_recv=sem(streams, count - 1), x_send=sem(3), x_recv=sem(2, count),
        s_recv=sem(4, count), y_recv=sem(2, count),
        m_send=sem(swaps), m_recv=sem(swaps), w_sem=sem(5 + halves), o_sem=sem(7), l_sem=sem(14),
    )
    anywhere = pl.BlockSpec(memory_space=pl.ANY)
    outs = shaped(
        (own, bf16), (own, f32), ((2 * units, width), bf16), ((4 * width, width), bf16),
        ((lines, width), f32),
    )
    res, dtok, ff, a, small = pl.pallas_call(
        functools.partial(block_kernel, count),
        out_shape=outs,
        in_specs=[anywhere] * 20,
        out_specs=tuple([anywhere] * len(outs)),
        scratch_shapes=list(scratch.values()),
        compiler_params=pltpu.CompilerParams(
            collective_id=0, has_side_effects=True, vmem_limit_bytes=62 << 20
        ),
        name="block",
    )(
        tokens, positions, span_sizes.reshape(1, 1), b_query, b_key, b_value, b_out, norm1_gain,
        norm1_bias, b_down, norm2_gain, norm2_bias, b_up, out_grad,
        w_query, w_key, w_value, w_out, w_up, w_down,
    )
    return finish(rows, width, units, res, dtok, ff, a, small)


def pick(mesh):
    def per_device(*args):
        tokens, span_sizes, w_up = args[0], args[2], args[13]
        rows, width = tokens.shape
        units = w_up.shape[1]
        fits = (
            mesh.shape["tensor"] == 2
            and mesh.shape["dp"] == 16
            and span_sizes.shape[0] == 1
            and rows % TILE == 0
            and width == HEADS * HD
            and width % TILE == 0
            and units == 2 * width
        )
        return pair_device(*args) if fits else general_device(*args)

    return per_device


def solution(mesh):
    return jax.shard_map(
        pick(mesh),
        mesh=mesh,
        in_specs=(
            P(("dp", "tensor"), None),
            P("dp"),
            P("dp"),
            P(),
            P(),
            P(),
            P(),
            P(),
            P(),
            P(),
            P(),
            P(),
            P(),
            P(None, "tensor"),
            P("tensor"),
            P("tensor", None),
            P(),
            P(),
            P(),
            P(("dp", "tensor"), None),
        ),
        out_specs=(
            P(("dp", "tensor"), None),
            P(("dp", "tensor"), None),
            P(),
            P(),
            P(),
            P(),
            P(),
            P(),
            P(),
            P(),
            P(),
            P(),
            P(None, "tensor"),
            P("tensor"),
            P("tensor", None),
            P(),
            P(),
            P(),
        ),
        check_vma=False,
    )
```

```python
import functools
import math

import jax
import jax.numpy as jnp
from jax import lax
from jax.experimental import pallas as pl
from jax.experimental.pallas import tpu as pltpu
from jax.sharding import PartitionSpec as P

HEADS = 12
HD = 64
SUBLEN = 32


highest = lax.Precision.HIGHEST
norm_eps = 1e-05


def norm_forward(value, gain, shift):
    mean = jnp.mean(value, axis=-1, keepdims=True)
    centred = value - mean
    scale = lax.rsqrt(jnp.mean(centred * centred, axis=-1, keepdims=True) + norm_eps)
    normal = centred * scale
    return (normal * gain + shift, normal, scale)


def norm_backward(grad, normal, scale, gain):
    along = grad * gain
    inner = (
        along
        - jnp.mean(along, axis=-1, keepdims=True)
        - normal * jnp.mean(along * normal, axis=-1, keepdims=True)
    )
    return (inner * scale, jnp.sum(grad * normal, axis=0), jnp.sum(grad, axis=0))


def gelu_slope(pre):
    normal_cdf = 0.5 * (1.0 + jax.scipy.special.erf(pre * (1.0 / math.sqrt(2.0))))
    return normal_cdf + pre * jnp.exp(-0.5 * pre * pre) * (1.0 / math.sqrt(2.0 * math.pi))


def reach_table(count, span):
    slot_index = jnp.arange(count, dtype=jnp.int32)
    final = (slot_index * SUBLEN // span + 1) * span // SUBLEN - 1
    return (slot_index[None, :] <= final[:, None]).astype(jnp.float32)


def features(rows, w_joint, b_joint, cosine, sine):
    length = rows.shape[0]
    width = rows.shape[1]
    proj = jnp.dot(rows, w_joint, preferred_element_type=jnp.float32) + b_joint
    relu_query = jax.nn.relu(proj[:, :width]).reshape(length, HEADS, HD)
    relu_key = jax.nn.relu(proj[:, width : 2 * width]).reshape(length, HEADS, HD) * (1.0 / HD)
    q_feat = jnp.concatenate([relu_query * cosine, relu_query * sine], axis=-1).astype(jnp.bfloat16)
    k_feat = jnp.concatenate([relu_key * cosine, relu_key * sine], axis=-1).astype(jnp.bfloat16)
    v_low = proj[:, 2 * width :].astype(jnp.bfloat16)
    return (q_feat, k_feat, v_low)


def local_blocks(k_feat, v_low):
    count = k_feat.shape[0] // SUBLEN
    k_sub = k_feat.reshape(count, SUBLEN, HEADS, 2 * HD)
    v_sub = v_low.reshape(count, SUBLEN, HEADS, HD)
    blocks = jnp.einsum("tjhf,tjhd->thfd", k_sub, v_sub, preferred_element_type=jnp.float32)
    k_total = jnp.sum(k_sub.astype(jnp.float32), axis=1)
    return (blocks, k_total)


def attend_core(q_feat, k_feat, v_low, blocks, k_total, reach, extra_blocks, extra_keys):
    count = q_feat.shape[0] // SUBLEN
    q_sub = q_feat.reshape(count, SUBLEN, HEADS, 2 * HD)
    k_sub = k_feat.reshape(count, SUBLEN, HEADS, 2 * HD)
    v_sub = v_low.reshape(count, SUBLEN, HEADS, HD)
    state_low = (
        jnp.einsum("st,thfd->shfd", reach, blocks, precision=highest) + extra_blocks
    ).astype(jnp.bfloat16)
    z_sum = jnp.einsum("st,thf->shf", reach, k_total, precision=highest) + extra_keys
    numer = jnp.einsum("sihf,shfd->sihd", q_sub, state_low, preferred_element_type=jnp.float32)
    denom = jnp.einsum("sihf,shf->sih", q_sub.astype(jnp.float32), z_sum, precision=highest) + 1.0
    return (q_sub, k_sub, v_sub, state_low, z_sum, numer, denom)


def back_first(parts, grad_mixed):
    q_sub, k_sub, v_sub, state_low, z_sum, numer, denom = parts
    count = q_sub.shape[0]
    grad_out = grad_mixed.reshape(count, SUBLEN, HEADS, HD).astype(jnp.float32)
    d_numer = grad_out / denom[..., None]
    d_denom = -jnp.sum(grad_out * numer, axis=-1) / (denom * denom)
    q_wide = q_sub.astype(jnp.float32)
    d_query = jnp.einsum(
        "sihd,shfd->sihf", d_numer, state_low.astype(jnp.float32), precision=highest
    )
    d_query = d_query + d_denom[..., None] * z_sum[:, None]
    d_state = jnp.einsum("sihf,sihd->shfd", q_wide, d_numer, precision=highest)
    d_zsum = jnp.einsum("sihf,sih->shf", q_wide, d_denom, precision=highest)
    return (d_query, d_state, d_zsum)


def back_second(parts, reach, d_state, d_zsum, later_blocks, later_keys):
    q_sub, k_sub, v_sub = (parts[0], parts[1], parts[2])
    d_blocks = jnp.einsum("st,shfd->thfd", reach, d_state, precision=highest) + later_blocks
    d_ktotal = jnp.einsum("st,shf->thf", reach, d_zsum, precision=highest) + later_keys
    d_key = (
        jnp.einsum("thfd,tjhd->tjhf", d_blocks, v_sub.astype(jnp.float32), precision=highest)
        + d_ktotal[:, None]
    )
    d_value = jnp.einsum("thfd,tjhf->tjhd", d_blocks, k_sub.astype(jnp.float32), precision=highest)
    return (d_key, d_value)


def feature_grads(q_feat, k_feat, d_qf, d_kf, d_val, cos_part, sin_part):
    size = q_feat.shape[0]
    d_qf = d_qf.reshape(size, HEADS, 2 * HD)
    d_kf = d_kf.reshape(size, HEADS, 2 * HD)
    d_query = jnp.where(
        q_feat[..., :HD] > 0, d_qf[..., :HD] * cos_part + d_qf[..., HD:] * sin_part, 0.0
    )
    d_key = jnp.where(
        k_feat[..., :HD] > 0,
        (d_kf[..., :HD] * cos_part + d_kf[..., HD:] * sin_part) * (1.0 / HD),
        0.0,
    )
    return jnp.concatenate(
        [
            d_query.reshape(size, HEADS * HD),
            d_key.reshape(size, HEADS * HD),
            d_val.reshape(size, HEADS * HD),
        ],
        axis=1,
    )


def general_device(
    tokens,
    positions,
    span_sizes,
    w_query,
    b_query,
    w_key,
    b_key,
    w_value,
    b_value,
    w_out,
    b_out,
    norm1_gain,
    norm1_bias,
    w_up,
    b_up,
    w_down,
    b_down,
    norm2_gain,
    norm2_bias,
    out_grad,
):
    rank = lax.axis_index("tensor")
    tensor_count = lax.axis_size("tensor")
    own = tokens.shape[0]
    width = tokens.shape[1]
    seqs = span_sizes.shape[0]
    group = own * tensor_count
    length = group // seqs
    start = rank * own
    w_joint = jnp.concatenate([w_query, w_key, w_value], axis=1)
    b_joint = jnp.concatenate([b_query, b_key, b_value]).astype(jnp.float32)
    gain_one = norm1_gain.astype(jnp.float32)
    gain_two = norm2_gain.astype(jnp.float32)
    gathered = lax.all_gather(tokens, "tensor", axis=0, tiled=True)
    angle = math.pi / 2 * positions.astype(jnp.float32) / (3 * length)
    cosine = jnp.cos(angle).reshape(seqs, length, 1, 1)
    sine = jnp.sin(angle).reshape(seqs, length, 1, 1)

    def seq_forward(items):
        rows, cos_part, sin_part, span = items
        q_feat, k_feat, v_low = features(rows, w_joint, b_joint, cos_part, sin_part)
        blocks_seq, ktot_seq = local_blocks(k_feat, v_low)
        parts = attend_core(
            q_feat,
            k_feat,
            v_low,
            blocks_seq,
            ktot_seq,
            reach_table(q_feat.shape[0] // SUBLEN, span),
            0.0,
            0.0,
        )
        mixed_seq = (
            (parts[5] / parts[6][..., None]).reshape(rows.shape[0], width).astype(jnp.bfloat16)
        )
        return (mixed_seq, q_feat, k_feat, v_low)

    mixed, q_all, k_all, v_all = lax.map(
        seq_forward, (gathered.reshape(seqs, length, width), cosine, sine, span_sizes)
    )
    mixed = mixed.reshape(group, width)
    mixed_own = lax.dynamic_slice_in_dim(mixed, start, own, 0)
    resid = (
        tokens.astype(jnp.float32)
        + jnp.dot(mixed_own, w_out, preferred_element_type=jnp.float32)
        + b_out.astype(jnp.float32)
    )
    hidden, normal_one, scale_one = norm_forward(resid, gain_one, norm1_bias.astype(jnp.float32))
    hidden_low = hidden.astype(jnp.bfloat16)
    rows_in = lax.all_gather(hidden_low, "tensor", axis=0, tiled=True)
    pre = jnp.dot(rows_in, w_up, preferred_element_type=jnp.float32) + b_up.astype(jnp.float32)
    act_low = jax.nn.gelu(pre, approximate=False).astype(jnp.bfloat16)
    branch = lax.psum_scatter(
        jnp.dot(act_low, w_down, preferred_element_type=jnp.float32),
        "tensor",
        scatter_dimension=0,
        tiled=True,
    )
    summed = hidden + branch + b_down.astype(jnp.float32)
    result, normal_two, scale_two = norm_forward(summed, gain_two, norm2_bias.astype(jnp.float32))
    d_sum, d_gain_two, d_bias_two = norm_backward(
        out_grad.astype(jnp.float32), normal_two, scale_two, gain_two
    )
    d_bdown = jnp.sum(d_sum, axis=0)
    d_sum_low = d_sum.astype(jnp.bfloat16)
    rows_grad = lax.all_gather(d_sum_low, "tensor", axis=0, tiled=True)
    g_down = jnp.dot(act_low.T, rows_grad, preferred_element_type=jnp.float32)
    d_pre = jnp.dot(rows_grad, w_down.T, preferred_element_type=jnp.float32) * gelu_slope(pre)
    g_upbias = jnp.sum(d_pre, axis=0)
    d_pre_low = d_pre.astype(jnp.bfloat16)
    g_up = jnp.dot(rows_in.T, d_pre_low, preferred_element_type=jnp.float32)
    d_hidden = lax.psum_scatter(
        jnp.dot(d_pre_low, w_up.T, preferred_element_type=jnp.float32),
        "tensor",
        scatter_dimension=0,
        tiled=True,
    )
    g_up, g_upbias, g_down = (
        lax.psum(g_up.astype(jnp.bfloat16), "dp").astype(jnp.float32),
        lax.psum(g_upbias.astype(jnp.bfloat16), "dp").astype(jnp.float32),
        lax.psum(g_down.astype(jnp.bfloat16), "dp").astype(jnp.float32),
    )
    d_hidden = d_hidden + d_sum
    d_resid, d_gain_one, d_bias_one = norm_backward(d_hidden, normal_one, scale_one, gain_one)
    d_bout = jnp.sum(d_resid, axis=0)
    d_gain_one, d_bias_one, d_gain_two, d_bias_two, d_bout, d_bdown = lax.psum(
        (d_gain_one, d_bias_one, d_gain_two, d_bias_two, d_bout, d_bdown), ("dp", "tensor")
    )
    d_resid_low = d_resid.astype(jnp.bfloat16)
    rows_back = lax.all_gather(d_resid_low, "tensor", axis=0, tiled=True)
    g_out = jnp.dot(mixed.T, rows_back, preferred_element_type=jnp.float32)
    d_mixed = jnp.dot(rows_back, w_out.T, preferred_element_type=jnp.float32).astype(jnp.bfloat16)

    def seq_backward(items):
        q_feat, k_feat, v_low, cos_part, sin_part, span, grad_mixed = items
        blocks_seq, ktot_seq = local_blocks(k_feat, v_low)
        reach = reach_table(q_feat.shape[0] // SUBLEN, span)
        parts = attend_core(q_feat, k_feat, v_low, blocks_seq, ktot_seq, reach, 0.0, 0.0)
        d_qf, d_state, d_zsum = back_first(parts, grad_mixed)
        d_kf, d_val = back_second(parts, reach, d_state, d_zsum, 0.0, 0.0)
        joint = feature_grads(q_feat, k_feat, d_qf, d_kf, d_val, cos_part, sin_part)
        return (joint.astype(jnp.bfloat16), jnp.sum(joint, axis=0))

    d_joint, d_jbias = lax.map(
        seq_backward,
        (q_all, k_all, v_all, cosine, sine, span_sizes, d_mixed.reshape(seqs, length, width)),
    )
    d_joint = d_joint.reshape(group, 3 * width)
    d_jbias = jnp.sum(d_jbias, axis=0)
    g_joint = jnp.dot(gathered.T, d_joint, preferred_element_type=jnp.float32)
    d_joint_own = lax.dynamic_slice_in_dim(d_joint, start, own, 0)
    d_tokens = d_resid + jnp.dot(d_joint_own, w_joint.T, preferred_element_type=jnp.float32)
    g_joint, g_out, d_jbias = lax.psum((g_joint, g_out, d_jbias), "dp")
    return (
        result.astype(jnp.bfloat16),
        d_tokens,
        g_joint[:, :width],
        d_jbias[:width],
        g_joint[:, width : 2 * width],
        d_jbias[width : 2 * width],
        g_joint[:, 2 * width :],
        d_jbias[2 * width :],
        g_out,
        d_bout,
        d_gain_one,
        d_bias_one,
        g_up,
        g_upbias,
        g_down,
        d_bdown,
        d_gain_two,
        d_bias_two,
    )


f32 = jnp.float32
bf16 = jnp.bfloat16
MESH = pl.DeviceIdType.MESH
LANES = 2 * HD
TILE = 256
ROWBLOCK = 32
FINISH = 256
FF_CUTS = 3
A_CUTS = 3
LINES = tuple("l" + str(index) for index in range(9))


def tile_at(index, size):
    return pl.ds(pl.multiple_of(index * size, size), size)


def contract(left, right, left_dim, right_dim, precision=None):
    return lax.dot_general(
        left,
        right,
        (((left_dim,), (right_dim,)), ((), ())),
        precision=precision,
        preferred_element_type=f32,
    )


def mm(left, right):
    return contract(left, right, 1, 0)


def mm_nt(left, right):
    return contract(left, right, 1, 1)


def mm_tn(left, right):
    return contract(left, right, 0, 0)


def head_masks():
    lane = lax.broadcasted_iota(jnp.int32, (1, LANES), 1)
    first = (lane < HD).astype(f32)
    return first, 1.0 - first


def pair_mask():
    row = lax.broadcasted_iota(jnp.int32, (LANES, LANES), 0)
    col = lax.broadcasted_iota(jnp.int32, (LANES, LANES), 1)
    return ((row < HD) == (col < HD)).astype(f32)


def column_of(block, which):
    row = lax.broadcasted_iota(jnp.int32, block.shape, 0)
    return contract(jnp.where(row == which, block, 0.0), jnp.ones((8, LANES), f32), 0, 0, highest)


def squeeze_pair(square):
    return square[:HD] + square[HD:]


def spread_pair(part, mask):
    return jnp.concatenate([part, part], axis=0).astype(f32) * mask


def two_rows(top, below):
    row = lax.broadcasted_iota(jnp.int32, (8, LANES), 0)
    return jnp.where(row == 0, top, jnp.where(row == 1, below, 0.0))


def fold8(value):
    total = value[0:8]
    for start in range(8, value.shape[0], 8):
        total = total + value[start : start + 8]
    return total


def angle_tables(places, length, span, cosb, sinb, ctab):
    rows = cosb.shape[0]
    angle = math.pi / 2 * places.astype(f32).reshape(1, rows) / (3 * length)
    line = lax.broadcasted_iota(jnp.int32, (8, rows), 0)
    block = jnp.where(line == 0, jnp.cos(angle), jnp.where(line == 1, jnp.sin(angle), 0.0))
    cosb[...] = column_of(block, 0)
    sinb[...] = column_of(block, 1)
    both = contract(block, block, 0, 0, highest)
    row = lax.broadcasted_iota(jnp.int32, (rows, rows), 0)
    col = lax.broadcasted_iota(jnp.int32, (rows, rows), 1)
    seen = col <= (row | (span[0, 0] - 1))
    ctab[...] = jnp.where(seen, both * (1.0 / HD), 0.0)


def peer_copy(src, dst, sems, slot, device):
    return pltpu.make_async_remote_copy(
        src_ref=src,
        dst_ref=dst,
        send_sem=sems[0].at[slot],
        recv_sem=sems[1].at[slot],
        device_id=device,
        device_id_type=MESH,
    )


def ring_device(spot, depth, core):
    far = spot // depth
    z = far * (2 * depth - 1 - spot) + (1 - far) * spot
    return ((z * 2 + far) * 2 + core, lax.axis_index("tensor"))


def layer_norm(value):
    centred = value - jnp.mean(value, axis=-1, keepdims=True)
    scale = lax.rsqrt(jnp.mean(centred * centred, axis=-1, keepdims=True) + norm_eps)
    return centred * scale, scale


def layer_norm_back(grad, gain, normal, scale):
    along = grad * gain
    return (
        along
        - jnp.mean(along, axis=-1, keepdims=True)
        - normal * jnp.mean(along * normal, axis=-1, keepdims=True)
    ) * scale


def block_kernel(
    count, tok_h, places_h, span_h, bq, bk, bv, bo, g1, b1, bd, g2, b2, bup_in, og_h,
    wq, wk, wv, wo, wup, wdn,
    res_h, dtok_h, ff_h, a_h, small_h,
    tok, places, span, og, l0, l1, l2, l3, l4, l5, l6, l7, l8, bup_line, wa, wff, vec, hbuf, act, slope, dbuf, dpre, hid, numer, denom, tsend, trecv, zsend, zrecv,
    bsend, brecv, res, gff, dhs, dhr, dho, mixb, mixf, inv, rq, rk, vv, nrm, scl, st, zst,
    dres, dlow, dn, xs, dsend, drecv, dzs, dzr, dql, dkl, dvl, ctab, cosb, sinb, acc, bup,
    cr_ff, cr_a, px, xr, rs_ff, rs_a, ff_o, a_o, smalls, small_r,
    send, recv, r_send, r_recv, g_send, g_recv, x_send, x_recv, s_recv, y_recv, m_send, m_recv,
    w_sem, o_sem, l_sem,
):
    sems = (send, recv)
    rows, width = tok.shape
    units = wup.shape[1]
    halves = units // width
    pairs = width // LANES
    tiles = width // TILE
    depth = count // 2
    quarter = width
    dq, dk, dv, ga = numer, denom, hid, wff
    dp, rank = lax.axis_index("dp"), lax.axis_index("tensor")
    late = rank.astype(f32)
    early = 1.0 - late
    core, y, z = dp % 2, (dp // 2) % 2, dp // 4
    spot = y * (2 * depth - 1 - z) + (1 - y) * z
    sibling = (dp + 1 - 2 * core, rank)
    peer = (dp, 1 - rank)
    ahead = ring_device((spot + 1) % count, depth, core)
    behind = ring_device((spot + count - 1) % count, depth, core)
    swaps = [sibling, peer, (dp + 2 - 4 * y, rank)]
    step = 1
    while step < depth:
        bit = (z // step) % 2
        swaps.append((dp + 4 * (step - 2 * step * bit), rank))
        step *= 2
    partners = [ahead, behind] + swaps
    barrier = pltpu.get_barrier_semaphore()
    for device in partners:
        pl.semaphore_signal(barrier, inc=1, device_id=device, device_id_type=MESH)

    loads = [
        (wk, wa.at[pl.ds(width, width), :]),
        (wv, wa.at[pl.ds(2 * width, width), :]),
        (wq, wa.at[pl.ds(0, width), :]),
        (wo, wa.at[pl.ds(3 * width, width), :]),
    ]
    for part in range(halves):
        loads.append(
            (wup.at[:, pl.ds(part * width, width)], wff.at[pl.ds(units + part * width, width), :])
        )
    loads.append((wdn, wff.at[pl.ds(0, units), :]))

    def load(index):
        return pltpu.make_async_copy(loads[index][0], loads[index][1], w_sem.at[index])

    small_loads = [(tok_h, tok), (places_h, places), (span_h, span)]
    vectors = (bq, bk, bv, bo, g1, b1, bd, g2, b2)
    lines = (l0, l1, l2, l3, l4, l5, l6, l7, l8)
    small_loads += [pair for pair in zip(vectors, lines)]
    small_loads += [(bup_in, bup_line), (og_h, og)]

    def fetch(index):
        return pltpu.make_async_copy(*small_loads[index], l_sem.at[index])

    fetch(0).start()
    for index in range(3):
        load(index).start()
    for index in range(1, len(small_loads)):
        fetch(index).start()
    for index in range(1, len(small_loads) - 1):
        fetch(index).wait()

    def out_copy(source, target, at, slot):
        return pltpu.make_async_copy(source.at[at, :], target.at[at, :], o_sem.at[slot])

    for index in range(len(vectors)):
        vec[index : index + 1, :] = lines[index][...].astype(f32).reshape(1, width)
    for part in range(halves):
        piece = bup_line[pl.ds(part * width, width)]
        vec[9 + part : 10 + part, :] = piece.astype(f32).reshape(1, width)
    own, far_rows = pl.ds(0, rows), pl.ds(rows, rows)
    my_places = places[pl.ds(pl.multiple_of(rank * rows, rows), rows)]
    angle_tables(my_places, places.shape[0], span, cosb, sinb, ctab)
    diag = pair_mask()
    first, second = head_masks()
    first_low, second_low = first.astype(bf16), second.astype(bf16)
    diag_low = diag.astype(bf16)
    acc[...] = jnp.zeros_like(acc)
    bup[...] = jnp.zeros_like(bup)
    smalls[0] = jnp.zeros(smalls.shape[1:], f32)

    def add_small(slot, line):
        smalls[0, slot : slot + 1, :] = line

    def project(which, target):
        @pl.loop(0, tiles)
        def _(j):
            cols = tile_at(j, TILE)
            value = mm(tok[...], wa[pl.ds(which * width, width), cols]) + vec[which : which + 1, cols]
            if which < 2:
                value = jnp.maximum(value, 0.0)
            target[:, cols] = value.astype(bf16)

    fetch(0).wait()
    load(0).wait()
    project(1, rk)
    load(1).wait()
    project(2, vv)
    for index in range(3, len(loads)):
        load(index).start()

    @pl.loop(0, pairs)
    def _(p):
        lanes = tile_at(p, LANES)
        k = rk[:, lanes].astype(f32) * (1.0 / HD)
        v = vv[:, lanes]
        kc, ks = (k * cosb[...]).astype(bf16), (k * sinb[...]).astype(bf16)
        tsend[p, 0] = squeeze_pair(mm_tn(kc, v) * diag).astype(bf16)
        tsend[p, 1] = squeeze_pair(mm_tn(ks, v) * diag).astype(bf16)
        zsend[p] = two_rows(
            jnp.sum(kc.astype(f32), axis=0, keepdims=True),
            jnp.sum(ks.astype(f32), axis=0, keepdims=True),
        )

    pl.semaphore_wait(barrier, len(partners))
    state_copy = peer_copy(tsend, trecv, sems, 0, peer)
    key_copy = peer_copy(zsend, zrecv, sems, 1, peer)
    state_copy.start()
    key_copy.start()
    load(2).wait()
    project(0, rq)

    @pl.loop(0, pairs)
    def _(p):
        lanes = tile_at(p, LANES)
        q, k, v = rq[:, lanes], rk[:, lanes], vv[:, lanes]
        parts = []
        for mask, rest in ((first_low, second_low), (second_low, first_low)):
            prob = (mm_nt(q * mask, k) * ctab[...]).astype(bf16)
            parts.append(mm(prob, v * mask + rest))
        numer[:, lanes] = parts[0] * first + parts[1] * second
        denom[:, lanes] = pltpu.roll(parts[0] * second + parts[1] * first, HD, 1)

    state_copy.wait()
    key_copy.wait()

    @pl.loop(0, pairs)
    def _(p):
        lanes = tile_at(p, LANES)
        q = rq[:, lanes].astype(f32)
        qc, qs = (q * cosb[...]).astype(bf16), (q * sinb[...]).astype(bf16)
        st[p] = (trecv[p].astype(f32) * late).astype(bf16)
        zblock = zrecv[p] * late
        zst[p] = zblock
        weighted = qc.astype(f32) * zblock[0:1, :] + qs.astype(f32) * zblock[1:2, :]
        num, den = numer[:, lanes], denom[:, lanes] + 1.0 + mm(weighted.astype(bf16), diag_low)
        for part, feat in ((0, qc), (1, qs)):
            num += mm(feat, spread_pair(st[p, part], diag).astype(bf16))
        reciprocal = 1.0 / den
        mix = num * reciprocal
        inv[:, lanes] = reciprocal
        mixf[:, lanes] = mix
        mixb[:, lanes] = mix.astype(bf16)

    load(3).wait()

    @pl.loop(0, tiles)
    def _(j):
        cols = tile_at(j, TILE)
        hid[:, cols] = (
            tok[:, cols].astype(f32) + mm(mixb[...], wa[pl.ds(3 * width, width), cols]) + vec[3:4, cols]
        )

    span_rows = rows // 2
    near = [pl.ds(k * span_rows, span_rows) for k in range(2)]
    away = [pl.ds(rows + k * span_rows, span_rows) for k in range(2)]
    blocks = span_rows // ROWBLOCK

    def norm_rows(i):
        at = tile_at(i, ROWBLOCK)
        normal, scale = layer_norm(hid[at, :])
        hidden = normal * vec[4:5, :] + vec[5:6, :]
        nrm[at, :] = normal
        scl[at, :] = jnp.broadcast_to(scale, (ROWBLOCK, LANES))
        hid[at, :] = hidden
        hbuf[at, :] = hidden.astype(bf16)

    def rows_copy(k):
        return peer_copy(hbuf.at[near[k]], hbuf.at[away[k]], sems, 12 + k, peer)

    def branch_copy(k):
        return peer_copy(bsend.at[near[k]], brecv.at[near[k]], sems, 14 + k, peer)

    def grad_copy(k):
        return peer_copy(dbuf.at[near[k]], dbuf.at[away[k]], sems, 16 + k, peer)

    def hidden_copy(k):
        return peer_copy(dhs.at[near[k]], dhr.at[near[k]], sems, 18 + k, peer)

    for k in range(2):
        pl.loop(k * blocks, (k + 1) * blocks)(norm_rows)
        rows_copy(k).start()
    for index in range(4, len(loads)):
        load(index).wait()
    fetch(len(small_loads) - 1).wait()

    def raise_rows(part):
        for piece in range(halves):

            @pl.loop(0, tiles)
            def _(j, piece=piece):
                cols, narrow = tile_at(piece * tiles + j, TILE), tile_at(j, TILE)
                weight = wff[pl.ds(units + piece * width, width), narrow]
                pre = mm(hbuf[part, :], weight) + vec[9 + piece : 10 + piece, narrow]
                cdf = 0.5 * (1.0 + lax.erf(pre * (1.0 / math.sqrt(2.0))))
                act[part, cols] = (pre * cdf).astype(bf16)
                slope[part, cols] = cdf + pre * jnp.exp(-0.5 * pre * pre) * (
                    1.0 / math.sqrt(2.0 * math.pi)
                )

    raise_rows(own)
    for k in range(2):
        rows_copy(k).wait()
        raise_rows(away[k])

        @pl.loop(0, tiles)
        def _(j, k=k):
            cols = tile_at(j, TILE)
            bsend[near[k], cols] = mm(act[away[k], :], wff[pl.ds(0, units), cols]).astype(bf16)

        branch_copy(k).start()

    @pl.loop(0, tiles)
    def _(j):
        cols = tile_at(j, TILE)
        hid[:, cols] += mm(act[own, :], wff[pl.ds(0, units), cols]) + vec[6:7, cols]

    def finish_rows(i):
        at = tile_at(i, ROWBLOCK)
        normal, scale = layer_norm(hid[at, :] + brecv[at, :].astype(f32))
        res[at, :] = (normal * vec[7:8, :] + vec[8:9, :]).astype(bf16)
        grad = og[at, :].astype(f32)
        inner = layer_norm_back(grad, vec[7:8, :], normal, scale)
        dho[at, :] = inner
        dbuf[at, :] = inner.astype(bf16)
        acc[0:8, :] += fold8(grad * normal)
        acc[8:16, :] += fold8(grad)
        acc[16:24, :] += fold8(inner)

    for k in range(2):
        branch_copy(k).wait()
        pl.loop(k * blocks, (k + 1) * blocks)(finish_rows)
        grad_copy(k).start()
    result_out = pltpu.make_async_copy(res, res_h, o_sem.at[0])
    result_out.start()
    for slot in range(3):
        add_small(3 + slot, jnp.sum(acc[8 * slot : 8 * slot + 8, :], axis=0, keepdims=True))

    def lower_rows(part):
        @pl.loop(0, units // TILE)
        def _(j):
            cols = tile_at(j, TILE)
            d_pre = mm_nt(dbuf[part, :], wff[cols, :]) * slope[part, cols]
            bup[:, cols] += fold8(d_pre)
            dpre[part, cols] = d_pre.astype(bf16)

    def lower_hidden(part, cols, j):
        total = 0.0
        for piece in range(halves):
            weight = wff[pl.ds(pl.multiple_of(units + piece * width + j * TILE, TILE), TILE), :]
            total += mm_nt(dpre[part, piece * width : (piece + 1) * width], weight)
        return total

    lower_rows(own)
    for k in range(2):
        grad_copy(k).wait()
        lower_rows(away[k])

        @pl.loop(0, tiles)
        def _(j, k=k):
            cols = tile_at(j, TILE)
            dhs[near[k], cols] = lower_hidden(away[k], cols, j).astype(bf16)

        hidden_copy(k).start()

    def make_down():
        @pl.loop(0, units // TILE)
        def _(j):
            cols = tile_at(j, TILE)
            gff[cols, :] = mm_tn(act[:, cols], dbuf[...]).astype(bf16)

    def make_up():
        for piece in range(halves):

            @pl.loop(0, tiles)
            def _(j, piece=piece):
                gff[pl.ds(units + piece * width, width), tile_at(j, TILE)] = mm_tn(
                    hbuf[...], dpre[:, tile_at(piece * tiles + j, TILE)]
                ).astype(bf16)

    def part_rows(which, size):
        return pl.ds(pl.multiple_of(which * size, size), size)

    core_ff = peer_copy(gff.at[part_rows(1 - core, units), :], cr_ff, sems, 8, sibling)
    pl.when(core == 0)(make_up)
    pl.when(core == 1)(make_down)
    core_ff.start()
    pl.when(core == 0)(make_down)
    pl.when(core == 1)(make_up)

    band, per = width // 4, count // 4
    ff_streams, a_streams = [], []
    for kind, (cuts, group) in enumerate(((FF_CUTS, ff_streams), (A_CUTS, a_streams))):
        size = (quarter if kind else units) // count // 2
        for way in range(2):
            for cut in range(cuts):
                number = 2 * FF_CUTS * kind + way * cuts + cut
                piece = size // cuts
                group.append((number, kind, way, cut * piece, piece))
    slots, sums, outs = (rs_ff, rs_a), (gff, ga), (ff_o, a_o)
    ff_size, a_size = units // count // 2, quarter // count // 2
    mine, theirs = core * 2 + rank, core * 2 + 1 - rank

    def ff_rows(at, way, offset, length, base):
        start = base + (at % count) * 2 * ff_size + way * ff_size + offset
        return pl.ds(pl.multiple_of(start, 16), length)

    def a_rows(at, way, offset, length, owner):
        chunk = at % count
        start = (chunk // per) * width + owner * band + (chunk % per) * 2 * a_size
        return pl.ds(pl.multiple_of(start + way * a_size + offset, 16), length)

    def line_rows(at, way, offset, length):
        start = (at % count) * 2 * a_size + way * a_size + offset
        return pl.ds(pl.multiple_of(start, 16), length)

    def core_rows(at, way, offset, length):
        chunk = at % count
        start = (chunk // per) * 2 * band + rank * band + (chunk % per) * 2 * a_size
        return pl.ds(pl.multiple_of(start + way * a_size + offset, 16), length)

    def stream_rows(stream, at):
        _, kind, way, offset, length = stream
        if kind:
            return a_rows(at, way, offset, length, mine)
        return ff_rows(at, way, offset, length, core * units)

    def toward(way):
        return behind if way else ahead

    def turn(way):
        return -1 if way else 1

    def remote(source, target, send_sem, recv_sem, device):
        return pltpu.make_async_remote_copy(
            src_ref=source,
            dst_ref=target,
            send_sem=send_sem,
            recv_sem=recv_sem,
            device_id=device,
            device_id_type=MESH,
        )

    def spread_copy(stream, at, s):
        number, kind, way, offset, length = stream
        return remote(
            sums[kind].at[stream_rows(stream, at), :],
            slots[kind].at[s, way, pl.ds(offset, length), :],
            r_send.at[kind],
            r_recv.at[number, s],
            toward(way),
        )

    def gather_copy(stream, at, s):
        number, kind, way, _, _ = stream
        where = outs[kind].at[stream_rows(stream, at), :]
        return remote(where, where, g_send.at[kind], g_recv.at[number, s], toward(way))

    def across_copy(way, s, owner):
        at = spot + 2 * count + turn(way) * (1 - s)
        where = a_o.at[a_rows(at, way, 0, a_size, owner), :]
        return remote(where, where, x_send.at[0], x_recv.at[way, s], peer)

    def side_copy(way, s, owner, lane):
        at = spot + 2 * count + turn(way) * (1 - s)
        where = a_o.at[a_rows(at, way, 0, a_size, owner), :]
        return remote(where, where, x_send.at[1], s_recv.at[2 * lane + way, s], sibling)

    def fold_copy(way, s):
        at = spot + count - turn(way) * s
        return remote(
            px.at[line_rows(at, way, 0, a_size), :],
            xr.at[s, way],
            x_send.at[2],
            y_recv.at[way, s],
            peer,
        )

    def start_folds(s):
        for way in range(2):
            fold_copy(way, s).start()

    def own_part(stream, at, s):
        _, kind, way, offset, length = stream
        value = sums[kind][stream_rows(stream, at), :].astype(f32)
        if kind == 0:
            return value + cr_ff[ff_rows(at, way, offset, length, 0), :].astype(f32)
        if offset == 0:
            fold_copy(way, s).wait_recv()
        return (
            value
            + cr_a[core_rows(at, way, offset, length), :].astype(f32)
            + xr[s, way, pl.ds(offset, length), :].astype(f32)
        )

    def ring_first(streams):
        for stream in streams:
            at = spot + count
            sums[stream[1]][stream_rows(stream, at), :] = own_part(stream, at, 0).astype(bf16)
            spread_copy(stream, at, 0).start()

    def store_chunk(way, s, owner):
        rows_at = a_rows(spot + 2 * count + turn(way) * (1 - s), way, 0, a_size, owner)
        pltpu.make_async_copy(a_o.at[rows_at, :], a_h.at[rows_at, :], o_sem.at[4]).start()

    def pass_on(stream, s):
        _, kind, way, offset, length = stream
        if kind and offset + length == a_size:
            across_copy(way, s, mine).start()
            side_copy(way, s, mine, 0).start()
            store_chunk(way, s, mine)

    def ring_spread(streams, s, last=False):
        for stream in streams:
            _, kind, way, offset, length = stream
            at = spot + count - turn(way) * (s + 1)
            target = stream_rows(stream, at)
            part = own_part(stream, at, s + 1)
            spread_copy(stream, at, s).wait_recv()
            arrived = slots[kind][s, way, pl.ds(offset, length), :].astype(f32)
            total = (part + arrived).astype(bf16)
            if last:
                outs[kind][target, :] = total
                gather_copy(stream, at, 0).start()
                pass_on(stream, 0)
            else:
                sums[kind][target, :] = total
                spread_copy(stream, at, s + 1).start()

    def ring_gather(streams, s, last=False):
        for stream in streams:
            at = spot + 2 * count - turn(stream[2]) * s
            gather_copy(stream, at, s).wait_recv()
            if not last:
                gather_copy(stream, at, s + 1).start()
            pass_on(stream, s + 1)

    def cross_over(s):
        for way in range(2):
            across_copy(way, s, theirs).wait_recv()
            side_copy(way, s, theirs, 1).start()
            store_chunk(way, s, theirs)

    def side_done(lane, s):
        owner = (1 - core) * 2 + (1 - rank if lane else rank)
        for way in range(2):
            side_copy(way, s, owner, lane).wait_recv()
            store_chunk(way, s, owner)

    def small_copy(index):
        return peer_copy(smalls.at[index], small_r.at[index], (m_send, m_recv), index, swaps[index])

    def swap_small(index):
        small_copy(index).wait()
        smalls[index + 1] = smalls[index] + small_r[index]
        if index + 1 < len(swaps):
            small_copy(index + 1).start()

    for piece in range(halves):
        line = jnp.sum(bup[:, piece * width : (piece + 1) * width], axis=0, keepdims=True)
        add_small(9 + piece, line * early)
        add_small(9 + halves + piece, line * late)

    @pl.loop(0, tiles)
    def _(j):
        cols = tile_at(j, TILE)
        dho[:, cols] += lower_hidden(own, cols, j)

    acc[...] = jnp.zeros_like(acc)
    core_ff.wait()
    ring_first(ff_streams)
    hidden_copy(0).wait()
    hidden_copy(1).wait()

    @pl.loop(0, rows // ROWBLOCK)
    def _(i):
        at = tile_at(i, ROWBLOCK)
        grad = dho[at, :] + dhr[at, :].astype(f32)
        normal = nrm[at, :]
        inner = layer_norm_back(grad, vec[4:5, :], normal, scl[at, 0:1])
        dres[at, :] = inner
        dlow[at, :] = inner.astype(bf16)
        acc[0:8, :] += fold8(grad * normal)
        acc[8:16, :] += fold8(grad)
        acc[16:24, :] += fold8(inner)

    for slot in range(3):
        add_small(slot, jnp.sum(acc[8 * slot : 8 * slot + 8, :], axis=0, keepdims=True))

    @pl.loop(0, tiles)
    def _(j):
        cols = tile_at(j, TILE)
        d_mixed = mm_nt(dlow[...], wa[tile_at(3 * tiles + j, TILE), :]).astype(bf16).astype(f32)
        d_numer = (d_mixed * inv[:, cols]).astype(bf16)
        dn[:, cols] = d_numer
        xs[:, cols] = (d_numer.astype(f32) * mixf[:, cols]).astype(bf16)


    @pl.loop(0, pairs)
    def _(p):
        lanes = tile_at(p, LANES)
        q = rq[:, lanes].astype(f32)
        qc, qs = (q * cosb[...]).astype(bf16), (q * sinb[...]).astype(bf16)
        d_numer = dn[:, lanes]
        dsend[p, 0] = squeeze_pair(mm_tn(qc, d_numer) * diag).astype(bf16)
        dsend[p, 1] = squeeze_pair(mm_tn(qs, d_numer) * diag).astype(bf16)
        across = mm(xs[:, lanes], diag_low)
        dzs[p] = -two_rows(
            jnp.sum(qc.astype(f32) * across, axis=0, keepdims=True),
            jnp.sum(qs.astype(f32) * across, axis=0, keepdims=True),
        )

    turn_copy = peer_copy(dsend, drecv, sems, 6, peer)
    turn_keys = peer_copy(dzs, dzr, sems, 7, peer)
    turn_copy.start()
    turn_keys.start()
    ring_spread(ff_streams, 0)

    @pl.loop(0, tiles)
    def _(j):
        cols = tile_at(j, TILE)
        ga[tile_at(3 * tiles + j, TILE), :] = mm_tn(mixb[:, cols], dlow[...]).astype(bf16)

    def core_a(m):
        there = pl.ds(pl.multiple_of(m * width + (1 - core) * 2 * band, 2 * band), 2 * band)
        here = pl.ds(m * 2 * band, 2 * band)
        return peer_copy(ga.at[there, :], cr_a.at[here, :], sems, (9, 11, 20, 21)[m], sibling)

    def fill_px(m):
        core_a(m).wait()
        there = pl.ds(pl.multiple_of(m * width + theirs * band, band), band)
        here = pl.ds(pl.multiple_of(m * 2 * band + (1 - rank) * band, band), band)
        px[m * band : (m + 1) * band, :] = (
            ga[there, :].astype(f32) + cr_a[here, :].astype(f32)
        ).astype(bf16)

    core_a(3).start()

    def inside(p):
        lanes = tile_at(p, LANES)
        q, k, v = rq[:, lanes], rk[:, lanes], vv[:, lanes]
        d_numer = dn[:, lanes]
        turned = (-pltpu.roll(xs[:, lanes].astype(f32), HD, 1)).astype(bf16)
        sum_q = sum_k = sum_v = 0.0
        for mask, rest in ((first_low, second_low), (second_low, first_low)):
            q_head, k_head, d_head = q * mask, k * mask, d_numer * mask
            table = ctab[...]
            prob = (mm_nt(q_head, k) * table).astype(bf16)
            d_prob = mm_nt(d_head + turned * rest, v * mask + rest)
            d_score = (d_prob * table).astype(bf16)
            sum_v += mm_tn(prob, d_head)
            sum_q += mm(d_score, k_head)
            sum_k += mm_tn(d_score, q_head)
        dq[:, lanes] = sum_q
        dk[:, lanes] = sum_k
        dv[:, lanes] = sum_v

    pl.loop(0, pairs // 2)(inside)
    ring_spread(ff_streams, 1)
    pl.loop(pairs // 2, pairs)(inside)
    ring_spread(ff_streams, 2)
    turn_copy.wait()
    turn_keys.wait()

    @pl.loop(0, pairs)
    def _(p):
        lanes = tile_at(p, LANES)
        q, v = rq[:, lanes].astype(f32), vv[:, lanes]
        k = rk[:, lanes].astype(f32)
        d_numer, x = dn[:, lanes], xs[:, lanes]
        sum_q, sum_k, sum_v = dq[:, lanes], dk[:, lanes], dv[:, lanes]
        zblock, dzblock = zst[p], dzr[p] * early
        along = mm(x, diag_low)
        for part, wave in ((0, cosb[...]), (1, sinb[...])):
            state = spread_pair(st[p, part], diag).astype(bf16)
            sum_q += wave * (mm_nt(d_numer, state) - along * zblock[part : part + 1, :])
            d_state = (spread_pair(drecv[p, part], diag) * early).astype(bf16)
            sum_k += wave * (mm_nt(v, d_state) + dzblock[part : part + 1, :]) * (1.0 / HD)
            sum_v += mm((k * wave * (1.0 / HD)).astype(bf16), d_state)
        sum_q = jnp.where(q > 0, sum_q, 0.0)
        sum_k = jnp.where(k > 0, sum_k, 0.0)
        dql[:, lanes] = sum_q.astype(bf16)
        dkl[:, lanes] = sum_k.astype(bf16)
        dvl[:, lanes] = sum_v.astype(bf16)
        for slot, value in ((6, sum_q), (7, sum_k), (8, sum_v)):
            smalls[0, slot : slot + 1, lanes] = jnp.sum(value, axis=0, keepdims=True)

    small_copy(0).start()

    def make_grad(which, source):
        @pl.loop(0, tiles)
        def _(j):
            ga[tile_at(which * tiles + j, TILE), :] = mm_tn(
                tok[:, tile_at(j, TILE)], source[...]
            ).astype(bf16)

        core_a(which).start()

    make_grad(2, dvl)
    ring_spread(ff_streams, 3)
    make_grad(0, dql)
    make_grad(1, dkl)
    for m in (3, 2, 0):
        fill_px(m)
    ring_spread(ff_streams, 4)
    fill_px(1)
    for s in range(3):
        start_folds(s)

    @pl.loop(0, tiles)
    def _(j):
        cols = tile_at(j, TILE)
        dres[:, cols] += (
            mm_nt(dql[...], wa[cols, :])
            + mm_nt(dkl[...], wa[tile_at(tiles + j, TILE), :])
            + mm_nt(dvl[...], wa[tile_at(2 * tiles + j, TILE), :])
        )

    token_out = pltpu.make_async_copy(dres, dtok_h, o_sem.at[1])
    token_out.start()
    ring_spread(ff_streams, 5)
    ring_first(a_streams)
    swap_small(0)

    def spread_gather(s):
        ring_spread(a_streams, s)
        ring_gather(ff_streams, s - 1)

    start_folds(3)
    ring_spread(a_streams, 0)
    ring_spread(ff_streams, 6, True)
    swap_small(1)

    @pl.loop(1, 3)
    def _(s):
        start_folds(s + 3)
        spread_gather(s)

    swap_small(2)
    start_folds(6)
    start_folds(7)
    pl.loop(3, 6)(spread_gather)
    swap_small(3)
    ring_spread(a_streams, 6, True)
    ring_gather(ff_streams, 5)
    ring_gather(a_streams, 0)
    ring_gather(ff_streams, 6, True)
    own_ff = part_rows(core, units)
    back_ff = peer_copy(ff_o.at[own_ff, :], ff_o.at[own_ff, :], sems, 10, sibling)
    back_ff.start()
    near_ff = out_copy(ff_o, ff_h, own_ff, 2)
    near_ff.start()
    cross_over(0)
    side_done(0, 0)
    swap_small(4)
    small_out = pltpu.make_async_copy(smalls.at[len(swaps)], small_h, o_sem.at[6])
    small_out.start()

    def gather_one(s):
        ring_gather(a_streams, s)
        cross_over(s)
        side_done(0, s)
        side_done(1, s - 1)

    gather_one(1)
    back_ff.wait()
    far_ff = out_copy(ff_o, ff_h, part_rows(1 - core, units), 3)
    far_ff.start()
    pl.loop(2, 6)(gather_one)
    ring_gather(a_streams, 6, True)
    cross_over(6)
    side_done(0, 6)
    side_done(1, 5)
    cross_over(7)
    side_done(0, 7)
    side_done(1, 6)

    def drain(kind, source, total, sem):
        where = source.at[pl.ds(0, total), :]
        remote(where, where, sem, x_recv.at[0, 0], peer).wait_send()

    for kind, size in ((0, ff_size), (1, a_size)):
        drain(kind, sums[kind], 2 * (count - 1) * size, r_send.at[kind])
        drain(kind, outs[kind], 2 * (count - 1) * size, g_send.at[kind])
    drain(1, px, 2 * count * a_size, x_send.at[2])

    drain(1, a_o, 2 * count * a_size, x_send.at[0])
    side_done(1, 7)
    drain(1, a_o, 4 * count * a_size, x_send.at[1])
    whole_a = pltpu.make_async_copy(a_o, a_h, o_sem.at[4])
    for copy in (result_out, token_out, near_ff, far_ff, small_out, whole_a):
        copy.wait()


def finish_kernel(halves, *refs):
    g_out, up, down, small, res, dtok = refs[:4], refs[4 : 4 + halves], *refs[4 + halves : 8 + halves]
    out = refs[8 + halves :]
    late = lax.axis_index("tensor") > 0
    for source, where in zip(g_out, (2, 4, 6, 8)):
        out[where][...] = source[...].astype(f32)
    width = res.shape[1]
    for piece in range(halves):
        out[12][:, piece * width : (piece + 1) * width] = up[piece][...].astype(f32)
    out[14][...] = down[...].astype(f32)

    @pl.when(pl.program_id(0) == 0)
    def _():
        out[0][...] = res[...]
        out[1][...] = dtok[...]
        for where, row in ((3, 6), (5, 7), (7, 8), (9, 2), (10, 0), (11, 1), (15, 5), (16, 3), (17, 4)):
            out[where][...] = small[row : row + 1, :].reshape(width)
        for piece in range(halves):
            line = jnp.where(
                late,
                small[9 + halves + piece : 10 + halves + piece, :],
                small[9 + piece : 10 + piece, :],
            )
            out[13][pl.ds(piece * width, width)] = line.reshape(width)


def finish(rows, width, units, res, dtok, ff, a, small):
    halves, steps = units // width, width // FINISH
    low = (FINISH, width)
    down_rows = units // steps

    def whole(shape):
        return pl.BlockSpec(shape, lambda i: (0,) * len(shape))

    def at_block(shape, start):
        return pl.BlockSpec(shape, lambda i: (start + i, 0))

    in_specs = [at_block(low, which * steps) for which in range(4)]
    in_specs += [at_block(low, units // FINISH + piece * steps) for piece in range(halves)]
    in_specs += [at_block((down_rows, width), 0), whole(small.shape), whole(res.shape), whole(dtok.shape)]
    matrix, line = (width, width), (width,)
    shapes = [
        (res.shape, bf16), (dtok.shape, f32), (matrix, f32), (line, f32), (matrix, f32), (line, f32),
        (matrix, f32), (line, f32), (matrix, f32), (line, f32), (line, f32), (line, f32),
        ((width, units), f32), ((units,), f32), ((units, width), f32), (line, f32), (line, f32), (line, f32),
    ]
    special = {
        2: at_block(low, 0), 4: at_block(low, 0), 6: at_block(low, 0), 8: at_block(low, 0),
        12: at_block((FINISH, units), 0), 14: at_block((down_rows, width), 0),
    }
    return pl.pallas_call(
        functools.partial(finish_kernel, halves),
        grid=(steps,),
        out_shape=shaped(*shapes),
        in_specs=in_specs,
        out_specs=tuple(special.get(i, whole(shape)) for i, (shape, _) in enumerate(shapes)),
        compiler_params=pltpu.CompilerParams(vmem_limit_bytes=62 << 20),
        name="finish",
    )(*([a] * 4), *([ff] * (halves + 1)), small, res, dtok)


def shaped(*items):
    return tuple(jax.ShapeDtypeStruct(shape, kind) for shape, kind in items)


def pair_device(
    tokens,
    positions,
    span_sizes,
    w_query,
    b_query,
    w_key,
    b_key,
    w_value,
    b_value,
    w_out,
    b_out,
    norm1_gain,
    norm1_bias,
    w_up,
    b_up,
    w_down,
    b_down,
    norm2_gain,
    norm2_bias,
    out_grad,
):
    rows, width = tokens.shape
    units = w_up.shape[1]
    pairs = width // LANES
    halves = units // width
    count = lax.axis_size("dp") // 2
    swaps = 2 + count.bit_length() - 1
    streams = 2 * (FF_CUTS + A_CUTS)
    ff_part, a_part = units // count // 2, width // count // 2
    lines = 9 + 2 * halves
    lines += -lines % 8

    def low(*shape):
        return pltpu.VMEM(shape, bf16)

    def wide(*shape):
        return pltpu.VMEM(shape, f32)

    def sem(*shape):
        return pltpu.SemaphoreType.DMA(shape)

    state, zrows = (pairs, 2, HD, LANES), (pairs, 8, LANES)
    own, pair = (rows, width), (2 * rows, width)
    scratch = dict(
        tok=low(*own), places=pltpu.VMEM(positions.shape, jnp.int32), span=pltpu.SMEM((1, 1), jnp.int32),
        og=low(*own), **{name: low(width) for name in LINES}, bup_line=low(units),
        wa=low(4 * width, width), wff=low(2 * units, width), vec=wide(9 + halves + -(9 + halves) % 8, width),
        hbuf=low(*pair), act=low(2 * rows, units), slope=wide(2 * rows, units), dbuf=low(*pair),
        dpre=low(2 * rows, units), hid=wide(*own), numer=wide(*own), denom=wide(*own),
        tsend=low(*state), trecv=low(*state), zsend=wide(*zrows), zrecv=wide(*zrows),
        bsend=low(*own), brecv=low(*own), res=low(*own), gff=low(2 * units, width),
        dhs=low(*own), dhr=low(*own), dho=wide(*own), mixb=low(*own), mixf=wide(*own), inv=wide(*own),
        rq=low(*own), rk=low(*own), vv=low(*own), nrm=wide(*own), scl=wide(rows, LANES),
        st=low(*state), zst=wide(*zrows), dres=wide(*own), dlow=low(*own), dn=low(*own), xs=low(*own),
        dsend=low(*state), drecv=low(*state), dzs=wide(*zrows), dzr=wide(*zrows),
        dql=low(*own), dkl=low(*own), dvl=low(*own),
        ctab=wide(rows, rows), cosb=wide(rows, LANES), sinb=wide(rows, LANES),
        acc=wide(24, width), bup=wide(8, units),
        cr_ff=low(units, width), cr_a=low(2 * width, width), px=low(width, width),
        xr=low(count, 2, a_part, width), rs_ff=low(count - 1, 2, ff_part, width),
        rs_a=low(count - 1, 2, a_part, width), ff_o=low(2 * units, width), a_o=low(4 * width, width),
        smalls=wide(swaps + 1, lines, width), small_r=wide(swaps, lines, width),
        send=sem(22), recv=sem(22), r_send=sem(2), r_recv=sem(streams, count - 1),
        g_send=sem(2), g_recv=sem(streams, count - 1), x_send=sem(3), x_recv=sem(2, count),
        s_recv=sem(4, count), y_recv=sem(2, count),
        m_send=sem(swaps), m_recv=sem(swaps), w_sem=sem(5 + halves), o_sem=sem(7), l_sem=sem(14),
    )
    anywhere = pl.BlockSpec(memory_space=pl.ANY)
    outs = shaped(
        (own, bf16), (own, f32), ((2 * units, width), bf16), ((4 * width, width), bf16),
        ((lines, width), f32),
    )
    res, dtok, ff, a, small = pl.pallas_call(
        functools.partial(block_kernel, count),
        out_shape=outs,
        in_specs=[anywhere] * 20,
        out_specs=tuple([anywhere] * len(outs)),
        scratch_shapes=list(scratch.values()),
        compiler_params=pltpu.CompilerParams(
            collective_id=0, has_side_effects=True, vmem_limit_bytes=62 << 20
        ),
        name="block",
    )(
        tokens, positions, span_sizes.reshape(1, 1), b_query, b_key, b_value, b_out, norm1_gain,
        norm1_bias, b_down, norm2_gain, norm2_bias, b_up, out_grad,
        w_query, w_key, w_value, w_out, w_up, w_down,
    )
    return finish(rows, width, units, res, dtok, ff, a, small)


def pick(mesh):
    def per_device(*args):
        tokens, span_sizes, w_up = args[0], args[2], args[13]
        rows, width = tokens.shape
        units = w_up.shape[1]
        fits = (
            mesh.shape["tensor"] == 2
            and mesh.shape["dp"] == 16
            and span_sizes.shape[0] == 1
            and rows % TILE == 0
            and width == HEADS * HD
            and width % TILE == 0
            and units == 2 * width
        )
        return pair_device(*args) if fits else general_device(*args)

    return per_device


def solution(mesh):
    return jax.shard_map(
        pick(mesh),
        mesh=mesh,
        in_specs=(
            P(("dp", "tensor"), None),
            P("dp"),
            P("dp"),
            P(),
            P(),
            P(),
            P(),
            P(),
            P(),
            P(),
            P(),
            P(),
            P(),
            P(None, "tensor"),
            P("tensor"),
            P("tensor", None),
            P(),
            P(),
            P(),
            P(("dp", "tensor"), None),
        ),
        out_specs=(
            P(("dp", "tensor"), None),
            P(("dp", "tensor"), None),
            P(),
            P(),
            P(),
            P(),
            P(),
            P(),
            P(),
            P(),
            P(),
            P(),
            P(None, "tensor"),
            P("tensor"),
            P("tensor", None),
            P(),
            P(),
            P(),
        ),
        check_vma=False,
    )
```

```python
import functools
import math

import jax
import jax.numpy as jnp
from jax import lax
from jax.experimental import pallas as pl
from jax.experimental.pallas import tpu as pltpu
from jax.sharding import PartitionSpec as P

HEADS = 12
HD = 64
SUBLEN = 32


highest = lax.Precision.HIGHEST
norm_eps = 1e-05


def norm_forward(value, gain, shift):
    mean = jnp.mean(value, axis=-1, keepdims=True)
    centred = value - mean
    scale = lax.rsqrt(jnp.mean(centred * centred, axis=-1, keepdims=True) + norm_eps)
    normal = centred * scale
    return (normal * gain + shift, normal, scale)


def norm_backward(grad, normal, scale, gain):
    along = grad * gain
    inner = (
        along
        - jnp.mean(along, axis=-1, keepdims=True)
        - normal * jnp.mean(along * normal, axis=-1, keepdims=True)
    )
    return (inner * scale, jnp.sum(grad * normal, axis=0), jnp.sum(grad, axis=0))


def gelu_slope(pre):
    normal_cdf = 0.5 * (1.0 + jax.scipy.special.erf(pre * (1.0 / math.sqrt(2.0))))
    return normal_cdf + pre * jnp.exp(-0.5 * pre * pre) * (1.0 / math.sqrt(2.0 * math.pi))


def reach_table(count, span):
    slot_index = jnp.arange(count, dtype=jnp.int32)
    final = (slot_index * SUBLEN // span + 1) * span // SUBLEN - 1
    return (slot_index[None, :] <= final[:, None]).astype(jnp.float32)


def features(rows, w_joint, b_joint, cosine, sine):
    length = rows.shape[0]
    width = rows.shape[1]
    proj = jnp.dot(rows, w_joint, preferred_element_type=jnp.float32) + b_joint
    relu_query = jax.nn.relu(proj[:, :width]).reshape(length, HEADS, HD)
    relu_key = jax.nn.relu(proj[:, width : 2 * width]).reshape(length, HEADS, HD) * (1.0 / HD)
    q_feat = jnp.concatenate([relu_query * cosine, relu_query * sine], axis=-1).astype(jnp.bfloat16)
    k_feat = jnp.concatenate([relu_key * cosine, relu_key * sine], axis=-1).astype(jnp.bfloat16)
    v_low = proj[:, 2 * width :].astype(jnp.bfloat16)
    return (q_feat, k_feat, v_low)


def local_blocks(k_feat, v_low):
    count = k_feat.shape[0] // SUBLEN
    k_sub = k_feat.reshape(count, SUBLEN, HEADS, 2 * HD)
    v_sub = v_low.reshape(count, SUBLEN, HEADS, HD)
    blocks = jnp.einsum("tjhf,tjhd->thfd", k_sub, v_sub, preferred_element_type=jnp.float32)
    k_total = jnp.sum(k_sub.astype(jnp.float32), axis=1)
    return (blocks, k_total)


def attend_core(q_feat, k_feat, v_low, blocks, k_total, reach, extra_blocks, extra_keys):
    count = q_feat.shape[0] // SUBLEN
    q_sub = q_feat.reshape(count, SUBLEN, HEADS, 2 * HD)
    k_sub = k_feat.reshape(count, SUBLEN, HEADS, 2 * HD)
    v_sub = v_low.reshape(count, SUBLEN, HEADS, HD)
    state_low = (
        jnp.einsum("st,thfd->shfd", reach, blocks, precision=highest) + extra_blocks
    ).astype(jnp.bfloat16)
    z_sum = jnp.einsum("st,thf->shf", reach, k_total, precision=highest) + extra_keys
    numer = jnp.einsum("sihf,shfd->sihd", q_sub, state_low, preferred_element_type=jnp.float32)
    denom = jnp.einsum("sihf,shf->sih", q_sub.astype(jnp.float32), z_sum, precision=highest) + 1.0
    return (q_sub, k_sub, v_sub, state_low, z_sum, numer, denom)


def back_first(parts, grad_mixed):
    q_sub, k_sub, v_sub, state_low, z_sum, numer, denom = parts
    count = q_sub.shape[0]
    grad_out = grad_mixed.reshape(count, SUBLEN, HEADS, HD).astype(jnp.float32)
    d_numer = grad_out / denom[..., None]
    d_denom = -jnp.sum(grad_out * numer, axis=-1) / (denom * denom)
    q_wide = q_sub.astype(jnp.float32)
    d_query = jnp.einsum(
        "sihd,shfd->sihf", d_numer, state_low.astype(jnp.float32), precision=highest
    )
    d_query = d_query + d_denom[..., None] * z_sum[:, None]
    d_state = jnp.einsum("sihf,sihd->shfd", q_wide, d_numer, precision=highest)
    d_zsum = jnp.einsum("sihf,sih->shf", q_wide, d_denom, precision=highest)
    return (d_query, d_state, d_zsum)


def back_second(parts, reach, d_state, d_zsum, later_blocks, later_keys):
    q_sub, k_sub, v_sub = (parts[0], parts[1], parts[2])
    d_blocks = jnp.einsum("st,shfd->thfd", reach, d_state, precision=highest) + later_blocks
    d_ktotal = jnp.einsum("st,shf->thf", reach, d_zsum, precision=highest) + later_keys
    d_key = (
        jnp.einsum("thfd,tjhd->tjhf", d_blocks, v_sub.astype(jnp.float32), precision=highest)
        + d_ktotal[:, None]
    )
    d_value = jnp.einsum("thfd,tjhf->tjhd", d_blocks, k_sub.astype(jnp.float32), precision=highest)
    return (d_key, d_value)


def feature_grads(q_feat, k_feat, d_qf, d_kf, d_val, cos_part, sin_part):
    size = q_feat.shape[0]
    d_qf = d_qf.reshape(size, HEADS, 2 * HD)
    d_kf = d_kf.reshape(size, HEADS, 2 * HD)
    d_query = jnp.where(
        q_feat[..., :HD] > 0, d_qf[..., :HD] * cos_part + d_qf[..., HD:] * sin_part, 0.0
    )
    d_key = jnp.where(
        k_feat[..., :HD] > 0,
        (d_kf[..., :HD] * cos_part + d_kf[..., HD:] * sin_part) * (1.0 / HD),
        0.0,
    )
    return jnp.concatenate(
        [
            d_query.reshape(size, HEADS * HD),
            d_key.reshape(size, HEADS * HD),
            d_val.reshape(size, HEADS * HD),
        ],
        axis=1,
    )


def general_device(
    tokens,
    positions,
    span_sizes,
    w_query,
    b_query,
    w_key,
    b_key,
    w_value,
    b_value,
    w_out,
    b_out,
    norm1_gain,
    norm1_bias,
    w_up,
    b_up,
    w_down,
    b_down,
    norm2_gain,
    norm2_bias,
    out_grad,
):
    rank = lax.axis_index("tensor")
    tensor_count = lax.axis_size("tensor")
    own = tokens.shape[0]
    width = tokens.shape[1]
    seqs = span_sizes.shape[0]
    group = own * tensor_count
    length = group // seqs
    start = rank * own
    w_joint = jnp.concatenate([w_query, w_key, w_value], axis=1)
    b_joint = jnp.concatenate([b_query, b_key, b_value]).astype(jnp.float32)
    gain_one = norm1_gain.astype(jnp.float32)
    gain_two = norm2_gain.astype(jnp.float32)
    gathered = lax.all_gather(tokens, "tensor", axis=0, tiled=True)
    angle = math.pi / 2 * positions.astype(jnp.float32) / (3 * length)
    cosine = jnp.cos(angle).reshape(seqs, length, 1, 1)
    sine = jnp.sin(angle).reshape(seqs, length, 1, 1)

    def seq_forward(items):
        rows, cos_part, sin_part, span = items
        q_feat, k_feat, v_low = features(rows, w_joint, b_joint, cos_part, sin_part)
        blocks_seq, ktot_seq = local_blocks(k_feat, v_low)
        parts = attend_core(
            q_feat,
            k_feat,
            v_low,
            blocks_seq,
            ktot_seq,
            reach_table(q_feat.shape[0] // SUBLEN, span),
            0.0,
            0.0,
        )
        mixed_seq = (
            (parts[5] / parts[6][..., None]).reshape(rows.shape[0], width).astype(jnp.bfloat16)
        )
        return (mixed_seq, q_feat, k_feat, v_low)

    mixed, q_all, k_all, v_all = lax.map(
        seq_forward, (gathered.reshape(seqs, length, width), cosine, sine, span_sizes)
    )
    mixed = mixed.reshape(group, width)
    mixed_own = lax.dynamic_slice_in_dim(mixed, start, own, 0)
    resid = (
        tokens.astype(jnp.float32)
        + jnp.dot(mixed_own, w_out, preferred_element_type=jnp.float32)
        + b_out.astype(jnp.float32)
    )
    hidden, normal_one, scale_one = norm_forward(resid, gain_one, norm1_bias.astype(jnp.float32))
    hidden_low = hidden.astype(jnp.bfloat16)
    rows_in = lax.all_gather(hidden_low, "tensor", axis=0, tiled=True)
    pre = jnp.dot(rows_in, w_up, preferred_element_type=jnp.float32) + b_up.astype(jnp.float32)
    act_low = jax.nn.gelu(pre, approximate=False).astype(jnp.bfloat16)
    branch = lax.psum_scatter(
        jnp.dot(act_low, w_down, preferred_element_type=jnp.float32),
        "tensor",
        scatter_dimension=0,
        tiled=True,
    )
    summed = hidden + branch + b_down.astype(jnp.float32)
    result, normal_two, scale_two = norm_forward(summed, gain_two, norm2_bias.astype(jnp.float32))
    d_sum, d_gain_two, d_bias_two = norm_backward(
        out_grad.astype(jnp.float32), normal_two, scale_two, gain_two
    )
    d_bdown = jnp.sum(d_sum, axis=0)
    d_sum_low = d_sum.astype(jnp.bfloat16)
    rows_grad = lax.all_gather(d_sum_low, "tensor", axis=0, tiled=True)
    g_down = jnp.dot(act_low.T, rows_grad, preferred_element_type=jnp.float32)
    d_pre = jnp.dot(rows_grad, w_down.T, preferred_element_type=jnp.float32) * gelu_slope(pre)
    g_upbias = jnp.sum(d_pre, axis=0)
    d_pre_low = d_pre.astype(jnp.bfloat16)
    g_up = jnp.dot(rows_in.T, d_pre_low, preferred_element_type=jnp.float32)
    d_hidden = lax.psum_scatter(
        jnp.dot(d_pre_low, w_up.T, preferred_element_type=jnp.float32),
        "tensor",
        scatter_dimension=0,
        tiled=True,
    )
    g_up, g_upbias, g_down = (
        lax.psum(g_up.astype(jnp.bfloat16), "dp").astype(jnp.float32),
        lax.psum(g_upbias.astype(jnp.bfloat16), "dp").astype(jnp.float32),
        lax.psum(g_down.astype(jnp.bfloat16), "dp").astype(jnp.float32),
    )
    d_hidden = d_hidden + d_sum
    d_resid, d_gain_one, d_bias_one = norm_backward(d_hidden, normal_one, scale_one, gain_one)
    d_bout = jnp.sum(d_resid, axis=0)
    d_gain_one, d_bias_one, d_gain_two, d_bias_two, d_bout, d_bdown = lax.psum(
        (d_gain_one, d_bias_one, d_gain_two, d_bias_two, d_bout, d_bdown), ("dp", "tensor")
    )
    d_resid_low = d_resid.astype(jnp.bfloat16)
    rows_back = lax.all_gather(d_resid_low, "tensor", axis=0, tiled=True)
    g_out = jnp.dot(mixed.T, rows_back, preferred_element_type=jnp.float32)
    d_mixed = jnp.dot(rows_back, w_out.T, preferred_element_type=jnp.float32).astype(jnp.bfloat16)

    def seq_backward(items):
        q_feat, k_feat, v_low, cos_part, sin_part, span, grad_mixed = items
        blocks_seq, ktot_seq = local_blocks(k_feat, v_low)
        reach = reach_table(q_feat.shape[0] // SUBLEN, span)
        parts = attend_core(q_feat, k_feat, v_low, blocks_seq, ktot_seq, reach, 0.0, 0.0)
        d_qf, d_state, d_zsum = back_first(parts, grad_mixed)
        d_kf, d_val = back_second(parts, reach, d_state, d_zsum, 0.0, 0.0)
        joint = feature_grads(q_feat, k_feat, d_qf, d_kf, d_val, cos_part, sin_part)
        return (joint.astype(jnp.bfloat16), jnp.sum(joint, axis=0))

    d_joint, d_jbias = lax.map(
        seq_backward,
        (q_all, k_all, v_all, cosine, sine, span_sizes, d_mixed.reshape(seqs, length, width)),
    )
    d_joint = d_joint.reshape(group, 3 * width)
    d_jbias = jnp.sum(d_jbias, axis=0)
    g_joint = jnp.dot(gathered.T, d_joint, preferred_element_type=jnp.float32)
    d_joint_own = lax.dynamic_slice_in_dim(d_joint, start, own, 0)
    d_tokens = d_resid + jnp.dot(d_joint_own, w_joint.T, preferred_element_type=jnp.float32)
    g_joint, g_out, d_jbias = lax.psum((g_joint, g_out, d_jbias), "dp")
    return (
        result.astype(jnp.bfloat16),
        d_tokens,
        g_joint[:, :width],
        d_jbias[:width],
        g_joint[:, width : 2 * width],
        d_jbias[width : 2 * width],
        g_joint[:, 2 * width :],
        d_jbias[2 * width :],
        g_out,
        d_bout,
        d_gain_one,
        d_bias_one,
        g_up,
        g_upbias,
        g_down,
        d_bdown,
        d_gain_two,
        d_bias_two,
    )


f32 = jnp.float32
bf16 = jnp.bfloat16
MESH = pl.DeviceIdType.MESH
LANES = 2 * HD
TILE = 256
ROWBLOCK = 32
FINISH = 256
FF_CUTS = 3
A_CUTS = 3
RING_ROWS = 16
LINES = tuple("l" + str(index) for index in range(9))


def tile_at(index, size):
    return pl.ds(pl.multiple_of(index * size, size), size)


def contract(left, right, left_dim, right_dim, precision=None):
    return lax.dot_general(
        left,
        right,
        (((left_dim,), (right_dim,)), ((), ())),
        precision=precision,
        preferred_element_type=f32,
    )


def mm(left, right):
    return contract(left, right, 1, 0)


def mm_nt(left, right):
    return contract(left, right, 1, 1)


def mm_tn(left, right):
    return contract(left, right, 0, 0)


def head_masks():
    lane = lax.broadcasted_iota(jnp.int32, (1, LANES), 1)
    first = (lane < HD).astype(f32)
    return first, 1.0 - first


def pair_mask():
    row = lax.broadcasted_iota(jnp.int32, (LANES, LANES), 0)
    col = lax.broadcasted_iota(jnp.int32, (LANES, LANES), 1)
    return ((row < HD) == (col < HD)).astype(f32)


def column_of(block, which):
    row = lax.broadcasted_iota(jnp.int32, block.shape, 0)
    return contract(jnp.where(row == which, block, 0.0), jnp.ones((8, LANES), f32), 0, 0, highest)


def squeeze_pair(square):
    return square[:HD] + square[HD:]


def spread_pair(part, mask):
    return jnp.concatenate([part, part], axis=0).astype(f32) * mask


def two_rows(top, below):
    row = lax.broadcasted_iota(jnp.int32, (8, LANES), 0)
    return jnp.where(row == 0, top, jnp.where(row == 1, below, 0.0))


def fold8(value):
    total = value[0:8]
    for start in range(8, value.shape[0], 8):
        total = total + value[start : start + 8]
    return total


def angle_tables(places, length, span, cosb, sinb, ctab):
    rows = cosb.shape[0]
    angle = math.pi / 2 * places.astype(f32).reshape(1, rows) / (3 * length)
    line = lax.broadcasted_iota(jnp.int32, (8, rows), 0)
    block = jnp.where(line == 0, jnp.cos(angle), jnp.where(line == 1, jnp.sin(angle), 0.0))
    cosb[...] = column_of(block, 0)
    sinb[...] = column_of(block, 1)
    both = contract(block, block, 0, 0, highest)
    row = lax.broadcasted_iota(jnp.int32, (rows, rows), 0)
    col = lax.broadcasted_iota(jnp.int32, (rows, rows), 1)
    seen = col <= (row | (span[0, 0] - 1))
    ctab[...] = jnp.where(seen, both * (1.0 / HD), 0.0)


def peer_copy(src, dst, sems, slot, device):
    return pltpu.make_async_remote_copy(
        src_ref=src,
        dst_ref=dst,
        send_sem=sems[0].at[slot],
        recv_sem=sems[1].at[slot],
        device_id=device,
        device_id_type=MESH,
    )


def ring_device(spot, depth, core):
    far = spot // depth
    z = far * (2 * depth - 1 - spot) + (1 - far) * spot
    return ((z * 2 + far) * 2 + core, lax.axis_index("tensor"))


def layer_norm(value):
    centred = value - jnp.mean(value, axis=-1, keepdims=True)
    scale = lax.rsqrt(jnp.mean(centred * centred, axis=-1, keepdims=True) + norm_eps)
    return centred * scale, scale


def layer_norm_back(grad, gain, normal, scale):
    along = grad * gain
    return (
        along
        - jnp.mean(along, axis=-1, keepdims=True)
        - normal * jnp.mean(along * normal, axis=-1, keepdims=True)
    ) * scale


def block_kernel(
    count, tok_h, places_h, span_h, bq, bk, bv, bo, g1, b1, bd, g2, b2, bup_in, og_h,
    wq, wk, wv, wo, wup, wdn,
    res_h, dtok_h, ff_h, a_h, small_h,
    tok, places, span, og, l0, l1, l2, l3, l4, l5, l6, l7, l8, bup_line, wa, wff, vec, hbuf, act, slope, dbuf, dpre, hid, numer, denom, tsend, trecv, zsend, zrecv,
    bsend, brecv, res, gff, dhs, dhr, dho, mixb, mixf, inv, rq, rk, vv, nrm, scl, st, zst,
    dres, dlow, dn, xs, dsend, drecv, dzs, dzr, dql, dkl, dvl, ctab, cosb, sinb, acc, bup,
    cr_ff, cr_a, px, xr, rs_ff, rs_a, ff_o, a_o, smalls, small_r,
    send, recv, r_send, r_recv, g_send, g_recv, x_send, x_recv, t_recv, s_recv, y_recv, m_send, m_recv,
    w_sem, o_sem, l_sem,
):
    sems = (send, recv)
    rows, width = tok.shape
    units = wup.shape[1]
    halves = units // width
    pairs = width // LANES
    tiles = width // TILE
    depth = count // 2
    quarter = width
    dq, dk, dv, ga = numer, denom, hid, wff
    dp, rank = lax.axis_index("dp"), lax.axis_index("tensor")
    late = rank.astype(f32)
    early = 1.0 - late
    core, y, z = dp % 2, (dp // 2) % 2, dp // 4
    spot = y * (2 * depth - 1 - z) + (1 - y) * z
    sibling = (dp + 1 - 2 * core, rank)
    peer = (dp, 1 - rank)
    ahead = ring_device((spot + 1) % count, depth, core)
    behind = ring_device((spot + count - 1) % count, depth, core)
    swaps = [sibling, peer, (dp + 2 - 4 * y, rank)]
    step = 1
    while step < depth:
        bit = (z // step) % 2
        swaps.append((dp + 4 * (step - 2 * step * bit), rank))
        step *= 2
    partners = [ahead, behind] + swaps
    barrier = pltpu.get_barrier_semaphore()
    for device in partners:
        pl.semaphore_signal(barrier, inc=1, device_id=device, device_id_type=MESH)

    loads = [
        (wk, wa.at[pl.ds(width, width), :]),
        (wv, wa.at[pl.ds(2 * width, width), :]),
        (wq, wa.at[pl.ds(0, width), :]),
        (wo, wa.at[pl.ds(3 * width, width), :]),
    ]
    for part in range(halves):
        loads.append(
            (wup.at[:, pl.ds(part * width, width)], wff.at[pl.ds(units + part * width, width), :])
        )
    loads.append((wdn, wff.at[pl.ds(0, units), :]))

    def load(index):
        return pltpu.make_async_copy(loads[index][0], loads[index][1], w_sem.at[index])

    small_loads = [(tok_h, tok), (places_h, places), (span_h, span)]
    vectors = (bq, bk, bv, bo, g1, b1, bd, g2, b2)
    lines = (l0, l1, l2, l3, l4, l5, l6, l7, l8)
    small_loads += [pair for pair in zip(vectors, lines)]
    small_loads += [(bup_in, bup_line), (og_h, og)]

    def fetch(index):
        return pltpu.make_async_copy(*small_loads[index], l_sem.at[index])

    fetch(0).start()
    for index in range(3):
        load(index).start()
    for index in range(1, len(small_loads)):
        fetch(index).start()
    for index in range(1, len(small_loads) - 1):
        fetch(index).wait()

    def out_copy(source, target, at, slot):
        return pltpu.make_async_copy(source.at[at, :], target.at[at, :], o_sem.at[slot])

    for index in range(len(vectors)):
        vec[index : index + 1, :] = lines[index][...].astype(f32).reshape(1, width)
    for part in range(halves):
        piece = bup_line[pl.ds(part * width, width)]
        vec[9 + part : 10 + part, :] = piece.astype(f32).reshape(1, width)
    own, far_rows = pl.ds(0, rows), pl.ds(rows, rows)
    my_places = places[pl.ds(pl.multiple_of(rank * rows, rows), rows)]
    angle_tables(my_places, places.shape[0], span, cosb, sinb, ctab)
    diag = pair_mask()
    first, second = head_masks()
    first_low, second_low = first.astype(bf16), second.astype(bf16)
    diag_low = diag.astype(bf16)
    acc[...] = jnp.zeros_like(acc)
    bup[...] = jnp.zeros_like(bup)
    smalls[0] = jnp.zeros(smalls.shape[1:], f32)

    def add_small(slot, line):
        smalls[0, slot : slot + 1, :] = line

    def project(which, target):
        @pl.loop(0, tiles)
        def _(j):
            cols = tile_at(j, TILE)
            value = mm(tok[...], wa[pl.ds(which * width, width), cols]) + vec[which : which + 1, cols]
            if which < 2:
                value = jnp.maximum(value, 0.0)
            target[:, cols] = value.astype(bf16)

    fetch(0).wait()
    load(0).wait()
    project(1, rk)
    load(1).wait()
    project(2, vv)
    for index in range(3, len(loads)):
        load(index).start()

    @pl.loop(0, pairs)
    def _(p):
        lanes = tile_at(p, LANES)
        k = rk[:, lanes].astype(f32) * (1.0 / HD)
        v = vv[:, lanes]
        kc, ks = (k * cosb[...]).astype(bf16), (k * sinb[...]).astype(bf16)
        tsend[p, 0] = squeeze_pair(mm_tn(kc, v) * diag).astype(bf16)
        tsend[p, 1] = squeeze_pair(mm_tn(ks, v) * diag).astype(bf16)
        zsend[p] = two_rows(
            jnp.sum(kc.astype(f32), axis=0, keepdims=True),
            jnp.sum(ks.astype(f32), axis=0, keepdims=True),
        )

    pl.semaphore_wait(barrier, len(partners))
    state_copy = peer_copy(tsend, trecv, sems, 0, peer)
    key_copy = peer_copy(zsend, zrecv, sems, 1, peer)
    state_copy.start()
    key_copy.start()
    load(2).wait()
    project(0, rq)

    @pl.loop(0, pairs)
    def _(p):
        lanes = tile_at(p, LANES)
        q, k, v = rq[:, lanes], rk[:, lanes], vv[:, lanes]
        parts = []
        for mask, rest in ((first_low, second_low), (second_low, first_low)):
            prob = (mm_nt(q * mask, k) * ctab[...]).astype(bf16)
            parts.append(mm(prob, v * mask + rest))
        numer[:, lanes] = parts[0] * first + parts[1] * second
        denom[:, lanes] = pltpu.roll(parts[0] * second + parts[1] * first, HD, 1)

    state_copy.wait()
    key_copy.wait()

    @pl.loop(0, pairs)
    def _(p):
        lanes = tile_at(p, LANES)
        q = rq[:, lanes].astype(f32)
        qc, qs = (q * cosb[...]).astype(bf16), (q * sinb[...]).astype(bf16)
        st[p] = (trecv[p].astype(f32) * late).astype(bf16)
        zblock = zrecv[p] * late
        zst[p] = zblock
        weighted = qc.astype(f32) * zblock[0:1, :] + qs.astype(f32) * zblock[1:2, :]
        num, den = numer[:, lanes], denom[:, lanes] + 1.0 + mm(weighted.astype(bf16), diag_low)
        for part, feat in ((0, qc), (1, qs)):
            num += mm(feat, spread_pair(st[p, part], diag).astype(bf16))
        reciprocal = 1.0 / den
        mix = num * reciprocal
        inv[:, lanes] = reciprocal
        mixf[:, lanes] = mix
        mixb[:, lanes] = mix.astype(bf16)

    load(3).wait()

    @pl.loop(0, tiles)
    def _(j):
        cols = tile_at(j, TILE)
        hid[:, cols] = (
            tok[:, cols].astype(f32) + mm(mixb[...], wa[pl.ds(3 * width, width), cols]) + vec[3:4, cols]
        )

    span_rows = rows // 2
    near = [pl.ds(k * span_rows, span_rows) for k in range(2)]
    away = [pl.ds(rows + k * span_rows, span_rows) for k in range(2)]
    blocks = span_rows // ROWBLOCK

    def norm_rows(i):
        at = tile_at(i, ROWBLOCK)
        normal, scale = layer_norm(hid[at, :])
        hidden = normal * vec[4:5, :] + vec[5:6, :]
        nrm[at, :] = normal
        scl[at, :] = jnp.broadcast_to(scale, (ROWBLOCK, LANES))
        hid[at, :] = hidden
        hbuf[at, :] = hidden.astype(bf16)

    def rows_copy(k):
        return peer_copy(hbuf.at[near[k]], hbuf.at[away[k]], sems, 12 + k, peer)

    def branch_copy(k):
        return peer_copy(bsend.at[near[k]], brecv.at[near[k]], sems, 14 + k, peer)

    def grad_copy(k):
        return peer_copy(dbuf.at[near[k]], dbuf.at[away[k]], sems, 16 + k, peer)

    def hidden_copy(k):
        return peer_copy(dhs.at[near[k]], dhr.at[near[k]], sems, 18 + k, peer)

    for k in range(2):
        pl.loop(k * blocks, (k + 1) * blocks)(norm_rows)
        rows_copy(k).start()
    for index in range(4, len(loads)):
        load(index).wait()
    fetch(len(small_loads) - 1).wait()

    def raise_rows(part):
        for piece in range(halves):

            @pl.loop(0, tiles)
            def _(j, piece=piece):
                cols, narrow = tile_at(piece * tiles + j, TILE), tile_at(j, TILE)
                weight = wff[pl.ds(units + piece * width, width), narrow]
                pre = mm(hbuf[part, :], weight) + vec[9 + piece : 10 + piece, narrow]
                cdf = 0.5 * (1.0 + lax.erf(pre * (1.0 / math.sqrt(2.0))))
                act[part, cols] = (pre * cdf).astype(bf16)
                slope[part, cols] = cdf + pre * jnp.exp(-0.5 * pre * pre) * (
                    1.0 / math.sqrt(2.0 * math.pi)
                )

    raise_rows(own)
    for k in range(2):
        rows_copy(k).wait()
        raise_rows(away[k])

        @pl.loop(0, tiles)
        def _(j, k=k):
            cols = tile_at(j, TILE)
            bsend[near[k], cols] = mm(act[away[k], :], wff[pl.ds(0, units), cols]).astype(bf16)

        branch_copy(k).start()

    @pl.loop(0, tiles)
    def _(j):
        cols = tile_at(j, TILE)
        hid[:, cols] += mm(act[own, :], wff[pl.ds(0, units), cols]) + vec[6:7, cols]

    def finish_rows(i):
        at = tile_at(i, ROWBLOCK)
        normal, scale = layer_norm(hid[at, :] + brecv[at, :].astype(f32))
        res[at, :] = (normal * vec[7:8, :] + vec[8:9, :]).astype(bf16)
        grad = og[at, :].astype(f32)
        inner = layer_norm_back(grad, vec[7:8, :], normal, scale)
        dho[at, :] = inner
        dbuf[at, :] = inner.astype(bf16)
        acc[0:8, :] += fold8(grad * normal)
        acc[8:16, :] += fold8(grad)
        acc[16:24, :] += fold8(inner)

    for k in range(2):
        branch_copy(k).wait()
        pl.loop(k * blocks, (k + 1) * blocks)(finish_rows)
        grad_copy(k).start()
    result_out = pltpu.make_async_copy(res, res_h, o_sem.at[0])
    result_out.start()
    for slot in range(3):
        add_small(3 + slot, jnp.sum(acc[8 * slot : 8 * slot + 8, :], axis=0, keepdims=True))

    def lower_rows(part):
        @pl.loop(0, units // TILE)
        def _(j):
            cols = tile_at(j, TILE)
            d_pre = mm_nt(dbuf[part, :], wff[cols, :]) * slope[part, cols]
            bup[:, cols] += fold8(d_pre)
            dpre[part, cols] = d_pre.astype(bf16)

    def lower_hidden(part, cols, j):
        total = 0.0
        for piece in range(halves):
            weight = wff[pl.ds(pl.multiple_of(units + piece * width + j * TILE, TILE), TILE), :]
            total += mm_nt(dpre[part, piece * width : (piece + 1) * width], weight)
        return total

    lower_rows(own)
    def send_hidden(k):
        @pl.loop(0, tiles)
        def _(j):
            cols = tile_at(j, TILE)
            dhs[near[k], cols] = lower_hidden(away[k], cols, j).astype(bf16)

        hidden_copy(k).start()

    grad_copy(0).wait()
    lower_rows(away[0])
    send_hidden(0)
    grad_copy(1).wait()
    lower_rows(away[1])

    def make_down(part):
        @pl.loop(part * tiles, (part + 1) * tiles)
        def _(j):
            cols = tile_at(j, TILE)
            gff[cols, :] = mm_tn(act[:, cols], dbuf[...]).astype(bf16)

    def make_up(part):
        @pl.loop(0, tiles)
        def _(j):
            gff[pl.ds(units + part * width, width), tile_at(j, TILE)] = mm_tn(
                hbuf[...], dpre[:, tile_at(part * tiles + j, TILE)]
            ).astype(bf16)

    def part_rows(which, size):
        return pl.ds(pl.multiple_of(which * size, size), size)

    def core_ff(part):
        start = pl.multiple_of((1 - core) * units + part * width, width)
        return peer_copy(
            gff.at[pl.ds(start, width), :],
            cr_ff.at[pl.ds(part * width, width), :],
            sems, (8, 22, 23)[part], sibling,
        )

    for part in range(halves):
        pl.when(core == 0)(functools.partial(make_up, part))
        pl.when(core == 1)(functools.partial(make_down, part))
        core_ff(part).start()
    send_hidden(1)
    for part in range(halves):
        pl.when(core == 0)(functools.partial(make_down, part))
        pl.when(core == 1)(functools.partial(make_up, part))

    band, per = width // 4, count // 4
    ff_streams, a_streams = [], []
    for kind, (cuts, group) in enumerate(((FF_CUTS, ff_streams), (A_CUTS, a_streams))):
        size = (quarter if kind else units) // count // 2
        for way in range(2):
            for cut in range(cuts):
                number = 2 * FF_CUTS * kind + way * cuts + cut
                piece = size // cuts
                group.append((number, kind, way, cut * piece, piece))
    slots, sums, outs = (rs_ff, rs_a), (gff, ga), (ff_o, a_o)
    ff_size, a_size = units // count // 2, quarter // count // 2
    mine, theirs = core * 2 + rank, core * 2 + 1 - rank

    def ff_rows(at, way, offset, length, base):
        start = base + (at % count) * 2 * ff_size + way * ff_size + offset
        return pl.ds(pl.multiple_of(start, 16), length)

    def a_rows(at, way, offset, length, owner):
        chunk = at % count
        start = (chunk // per) * width + owner * band + (chunk % per) * 2 * a_size
        return pl.ds(pl.multiple_of(start + way * a_size + offset, 16), length)

    def line_rows(at, way, offset, length):
        start = (at % count) * 2 * a_size + way * a_size + offset
        return pl.ds(pl.multiple_of(start, 16), length)

    def core_rows(at, way, offset, length):
        chunk = at % count
        start = (chunk // per) * 2 * band + rank * band + (chunk % per) * 2 * a_size
        return pl.ds(pl.multiple_of(start + way * a_size + offset, 16), length)

    def stream_rows(stream, at):
        _, kind, way, offset, length = stream
        if kind:
            return a_rows(at, way, offset, length, mine)
        return ff_rows(at, way, offset, length, core * units)

    def toward(way):
        return behind if way else ahead

    def turn(way):
        return -1 if way else 1

    def remote(source, target, send_sem, recv_sem, device):
        return pltpu.make_async_remote_copy(
            src_ref=source,
            dst_ref=target,
            send_sem=send_sem,
            recv_sem=recv_sem,
            device_id=device,
            device_id_type=MESH,
        )

    def spread_copy(stream, at, s):
        number, kind, way, offset, length = stream
        return remote(
            sums[kind].at[stream_rows(stream, at), :],
            slots[kind].at[s, way, pl.ds(offset, length), :],
            r_send.at[kind],
            r_recv.at[number, s],
            toward(way),
        )

    def gather_copy(stream, at, s):
        number, kind, way, _, _ = stream
        where = outs[kind].at[stream_rows(stream, at), :]
        return remote(where, where, g_send.at[kind], g_recv.at[number, s], toward(way))

    def across_copy(way, s, owner, first):
        at, skip = spot + 2 * count + turn(way) * (1 - s), 0 if first else RING_ROWS
        where = a_o.at[a_rows(at, way, skip, a_size - skip, owner), :]
        return remote(where, where, x_send.at[0], x_recv.at[way, s], peer)

    def round_copy(way, s):
        at = spot + 2 * count + turn(way) * (1 - s)
        where = a_o.at[a_rows(at, way, 0, RING_ROWS, theirs), :]
        return remote(where, where, x_send.at[3], t_recv.at[way, s], toward(way))

    def side_copy(way, s, owner, lane):
        at = spot + 2 * count + turn(way) * (1 - s)
        where = a_o.at[a_rows(at, way, 0, a_size, owner), :]
        return remote(where, where, x_send.at[1], s_recv.at[2 * lane + way, s], sibling)

    def fold_copy(way, s):
        at = spot + count - turn(way) * s
        return remote(
            px.at[line_rows(at, way, 0, a_size), :],
            xr.at[s, way],
            x_send.at[2],
            y_recv.at[way, s],
            peer,
        )

    def start_folds(s):
        for way in range(2):
            fold_copy(way, s).start()

    def own_part(stream, at, s):
        _, kind, way, offset, length = stream
        value = sums[kind][stream_rows(stream, at), :].astype(f32)
        if kind == 0:
            return value + cr_ff[ff_rows(at, way, offset, length, 0), :].astype(f32)
        if offset == 0:
            fold_copy(way, s).wait_recv()
        return (
            value
            + cr_a[core_rows(at, way, offset, length), :].astype(f32)
            + xr[s, way, pl.ds(offset, length), :].astype(f32)
        )

    def ring_first(streams):
        for stream in streams:
            at = spot + count
            sums[stream[1]][stream_rows(stream, at), :] = own_part(stream, at, 0).astype(bf16)
            spread_copy(stream, at, 0).start()

    def store_chunk(way, s, owner):
        rows_at = a_rows(spot + 2 * count + turn(way) * (1 - s), way, 0, a_size, owner)
        pltpu.make_async_copy(a_o.at[rows_at, :], a_h.at[rows_at, :], o_sem.at[4]).start()

    def pass_on(stream, s, first=False):
        _, kind, way, offset, length = stream
        if kind and offset + length == a_size:
            across_copy(way, s, mine, first).start()
            side_copy(way, s, mine, 0).start()
            store_chunk(way, s, mine)

    def ring_spread(streams, s, last=False):
        for stream in streams:
            _, kind, way, offset, length = stream
            at = spot + count - turn(way) * (s + 1)
            target = stream_rows(stream, at)
            part = own_part(stream, at, s + 1)
            spread_copy(stream, at, s).wait_recv()
            arrived = slots[kind][s, way, pl.ds(offset, length), :].astype(f32)
            total = (part + arrived).astype(bf16)
            if last:
                outs[kind][target, :] = total
                gather_copy(stream, at, 0).start()
                pass_on(stream, 0, True)
            else:
                sums[kind][target, :] = total
                spread_copy(stream, at, s + 1).start()

    def ring_gather(streams, s, last=False):
        for stream in streams:
            at = spot + 2 * count - turn(stream[2]) * s
            gather_copy(stream, at, s).wait_recv()
            if not last:
                gather_copy(stream, at, s + 1).start()
        for stream in streams:
            pass_on(stream, s + 1)

    def cross_over(s, first=False, last=False):
        for way in range(2):
            across_copy(way, s, theirs, first).wait_recv()
            if not first:
                round_copy(way, s - 1).wait_recv()
            if not last:
                round_copy(way, s).start()
        for way in range(2):
            side_copy(way, s, theirs, 1).start()
            store_chunk(way, s, theirs)

    def side_done(lane, s):
        owner = (1 - core) * 2 + (1 - rank if lane else rank)
        for way in range(2):
            side_copy(way, s, owner, lane).wait_recv()
            store_chunk(way, s, owner)

    def ff_part(q):
        s, cut = q // FF_CUTS, q % FF_CUTS
        piece = ff_size // FF_CUTS
        ring_spread([(way * FF_CUTS + cut, 0, way, cut * piece, piece) for way in range(2)], s)

    def small_copy(index):
        return peer_copy(smalls.at[index], small_r.at[index], (m_send, m_recv), index, swaps[index])

    def swap_small(index):
        small_copy(index).wait()
        smalls[index + 1] = smalls[index] + small_r[index]
        if index + 1 < len(swaps):
            small_copy(index + 1).start()

    for piece in range(halves):
        line = jnp.sum(bup[:, piece * width : (piece + 1) * width], axis=0, keepdims=True)
        add_small(9 + piece, line * early)
        add_small(9 + halves + piece, line * late)

    @pl.loop(0, tiles)
    def _(j):
        cols = tile_at(j, TILE)
        dho[:, cols] += lower_hidden(own, cols, j)

    acc[...] = jnp.zeros_like(acc)
    for part in range(halves):
        core_ff(part).wait()
    ring_first(ff_streams)
    hidden_copy(0).wait()
    hidden_copy(1).wait()

    @pl.loop(0, rows // ROWBLOCK)
    def _(i):
        at = tile_at(i, ROWBLOCK)
        grad = dho[at, :] + dhr[at, :].astype(f32)
        normal = nrm[at, :]
        inner = layer_norm_back(grad, vec[4:5, :], normal, scl[at, 0:1])
        dres[at, :] = inner
        dlow[at, :] = inner.astype(bf16)
        acc[0:8, :] += fold8(grad * normal)
        acc[8:16, :] += fold8(grad)
        acc[16:24, :] += fold8(inner)

    for slot in range(3):
        add_small(slot, jnp.sum(acc[8 * slot : 8 * slot + 8, :], axis=0, keepdims=True))

    ff_part(0)

    @pl.loop(0, tiles)
    def _(j):
        cols = tile_at(j, TILE)
        d_mixed = mm_nt(dlow[...], wa[tile_at(3 * tiles + j, TILE), :]).astype(bf16).astype(f32)
        d_numer = (d_mixed * inv[:, cols]).astype(bf16)
        dn[:, cols] = d_numer
        xs[:, cols] = (d_numer.astype(f32) * mixf[:, cols]).astype(bf16)

    ff_part(1)


    @pl.loop(0, pairs)
    def _(p):
        lanes = tile_at(p, LANES)
        q = rq[:, lanes].astype(f32)
        qc, qs = (q * cosb[...]).astype(bf16), (q * sinb[...]).astype(bf16)
        d_numer = dn[:, lanes]
        dsend[p, 0] = squeeze_pair(mm_tn(qc, d_numer) * diag).astype(bf16)
        dsend[p, 1] = squeeze_pair(mm_tn(qs, d_numer) * diag).astype(bf16)
        across = mm(xs[:, lanes], diag_low)
        dzs[p] = -two_rows(
            jnp.sum(qc.astype(f32) * across, axis=0, keepdims=True),
            jnp.sum(qs.astype(f32) * across, axis=0, keepdims=True),
        )

    turn_copy = peer_copy(dsend, drecv, sems, 6, peer)
    turn_keys = peer_copy(dzs, dzr, sems, 7, peer)
    turn_copy.start()
    turn_keys.start()
    ff_part(2)

    @pl.loop(0, tiles)
    def _(j):
        cols = tile_at(j, TILE)
        ga[tile_at(3 * tiles + j, TILE), :] = mm_tn(mixb[:, cols], dlow[...]).astype(bf16)

    def core_a(m):
        there = pl.ds(pl.multiple_of(m * width + (1 - core) * 2 * band, 2 * band), 2 * band)
        here = pl.ds(m * 2 * band, 2 * band)
        return peer_copy(ga.at[there, :], cr_a.at[here, :], sems, (9, 11, 20, 21)[m], sibling)

    def fill_px(m):
        core_a(m).wait()
        there = pl.ds(pl.multiple_of(m * width + theirs * band, band), band)
        here = pl.ds(pl.multiple_of(m * 2 * band + (1 - rank) * band, band), band)
        px[m * band : (m + 1) * band, :] = (
            ga[there, :].astype(f32) + cr_a[here, :].astype(f32)
        ).astype(bf16)

    core_a(3).start()
    ff_part(3)

    def inside(p):
        lanes = tile_at(p, LANES)
        q, k, v = rq[:, lanes], rk[:, lanes], vv[:, lanes]
        d_numer = dn[:, lanes]
        turned = (-pltpu.roll(xs[:, lanes].astype(f32), HD, 1)).astype(bf16)
        sum_q = sum_k = sum_v = 0.0
        for mask, rest in ((first_low, second_low), (second_low, first_low)):
            q_head, k_head, d_head = q * mask, k * mask, d_numer * mask
            table = ctab[...]
            prob = (mm_nt(q_head, k) * table).astype(bf16)
            d_prob = mm_nt(d_head + turned * rest, v * mask + rest)
            d_score = (d_prob * table).astype(bf16)
            sum_v += mm_tn(prob, d_head)
            sum_q += mm(d_score, k_head)
            sum_k += mm_tn(d_score, q_head)
        dq[:, lanes] = sum_q
        dk[:, lanes] = sum_k
        dv[:, lanes] = sum_v

    @pl.loop(0, pairs)
    def _(p):
        inside(p)
        ff_part(4 + p)

    turn_copy.wait()
    turn_keys.wait()

    @pl.loop(0, pairs)
    def _(p):
        lanes = tile_at(p, LANES)
        q, v = rq[:, lanes].astype(f32), vv[:, lanes]
        k = rk[:, lanes].astype(f32)
        d_numer, x = dn[:, lanes], xs[:, lanes]
        sum_q, sum_k, sum_v = dq[:, lanes], dk[:, lanes], dv[:, lanes]
        zblock, dzblock = zst[p], dzr[p] * early
        along = mm(x, diag_low)
        for part, wave in ((0, cosb[...]), (1, sinb[...])):
            state = spread_pair(st[p, part], diag).astype(bf16)
            sum_q += wave * (mm_nt(d_numer, state) - along * zblock[part : part + 1, :])
            d_state = (spread_pair(drecv[p, part], diag) * early).astype(bf16)
            sum_k += wave * (mm_nt(v, d_state) + dzblock[part : part + 1, :]) * (1.0 / HD)
            sum_v += mm((k * wave * (1.0 / HD)).astype(bf16), d_state)
        sum_q = jnp.where(q > 0, sum_q, 0.0)
        sum_k = jnp.where(k > 0, sum_k, 0.0)
        dql[:, lanes] = sum_q.astype(bf16)
        dkl[:, lanes] = sum_k.astype(bf16)
        dvl[:, lanes] = sum_v.astype(bf16)
        for slot, value in ((6, sum_q), (7, sum_k), (8, sum_v)):
            smalls[0, slot : slot + 1, lanes] = jnp.sum(value, axis=0, keepdims=True)

    small_copy(0).start()
    ff_part(10)

    def make_grad(which, source):
        @pl.loop(0, tiles)
        def _(j):
            ga[tile_at(which * tiles + j, TILE), :] = mm_tn(
                tok[:, tile_at(j, TILE)], source[...]
            ).astype(bf16)

        core_a(which).start()

    make_grad(2, dvl)
    ff_part(11)
    make_grad(0, dql)
    ff_part(12)
    make_grad(1, dkl)
    ff_part(13)
    for m in (3, 2, 0, 1):
        fill_px(m)
    start_folds(0)
    ff_part(14)

    @pl.loop(0, tiles)
    def _(j):
        cols = tile_at(j, TILE)
        dres[:, cols] += (
            mm_nt(dql[...], wa[cols, :])
            + mm_nt(dkl[...], wa[tile_at(tiles + j, TILE), :])
            + mm_nt(dvl[...], wa[tile_at(2 * tiles + j, TILE), :])
        )

    token_out = pltpu.make_async_copy(dres, dtok_h, o_sem.at[1])
    token_out.start()
    start_folds(1)
    ring_spread(ff_streams, 5)
    ring_first(a_streams)
    swap_small(0)

    def spread_gather(s):
        ring_spread(a_streams, s)
        ring_gather(ff_streams, s - 1)

    start_folds(2)
    ring_spread(a_streams, 0)
    ring_spread(ff_streams, 6, True)
    swap_small(1)

    def spread_fold(s):
        start_folds(s + 2)
        spread_gather(s)

    pl.loop(1, 3)(spread_fold)
    swap_small(2)
    pl.loop(3, 6)(spread_fold)
    swap_small(3)
    ring_spread(a_streams, 6, True)
    ring_gather(ff_streams, 5)
    ring_gather(a_streams, 0)
    ring_gather(ff_streams, 6, True)
    own_ff = part_rows(core, units)
    back_ff = peer_copy(ff_o.at[own_ff, :], ff_o.at[own_ff, :], sems, 10, sibling)
    back_ff.start()
    near_ff = out_copy(ff_o, ff_h, own_ff, 2)
    near_ff.start()
    cross_over(0, first=True)
    side_done(0, 0)
    swap_small(4)
    small_out = pltpu.make_async_copy(smalls.at[len(swaps)], small_h, o_sem.at[6])
    small_out.start()

    def gather_one(s):
        ring_gather(a_streams, s)
        cross_over(s)
        side_done(0, s)
        side_done(1, s - 1)

    gather_one(1)
    back_ff.wait()
    far_ff = out_copy(ff_o, ff_h, part_rows(1 - core, units), 3)
    far_ff.start()
    pl.loop(2, 6)(gather_one)
    ring_gather(a_streams, 6, True)
    cross_over(6)
    side_done(0, 6)
    side_done(1, 5)
    cross_over(7, last=True)
    side_done(0, 7)
    side_done(1, 6)

    def drain(kind, source, total, sem):
        where = source.at[pl.ds(0, total), :]
        remote(where, where, sem, x_recv.at[0, 0], peer).wait_send()

    for kind, size in ((0, ff_size), (1, a_size)):
        drain(kind, sums[kind], 2 * (count - 1) * size, r_send.at[kind])
        drain(kind, outs[kind], 2 * (count - 1) * size, g_send.at[kind])
    drain(1, px, 2 * count * a_size, x_send.at[2])

    drain(1, a_o, 2 * count * a_size - 2 * (count - 1) * RING_ROWS, x_send.at[0])
    drain(1, a_o, 2 * (count - 1) * RING_ROWS, x_send.at[3])
    side_done(1, 7)
    drain(1, a_o, 4 * count * a_size, x_send.at[1])
    whole_a = pltpu.make_async_copy(a_o, a_h, o_sem.at[4])
    for copy in (result_out, token_out, near_ff, far_ff, small_out, whole_a):
        copy.wait()


def finish_kernel(halves, *refs):
    g_out, up, down, small, res, dtok = refs[:4], refs[4 : 4 + halves], *refs[4 + halves : 8 + halves]
    out = refs[8 + halves :]
    late = lax.axis_index("tensor") > 0
    for source, where in zip(g_out, (2, 4, 6, 8)):
        out[where][...] = source[...].astype(f32)
    width = res.shape[1]
    for piece in range(halves):
        out[12][:, piece * width : (piece + 1) * width] = up[piece][...].astype(f32)
    out[14][...] = down[...].astype(f32)

    @pl.when(pl.program_id(0) == 0)
    def _():
        out[0][...] = res[...]
        out[1][...] = dtok[...]
        for where, row in ((3, 6), (5, 7), (7, 8), (9, 2), (10, 0), (11, 1), (15, 5), (16, 3), (17, 4)):
            out[where][...] = small[row : row + 1, :].reshape(width)
        for piece in range(halves):
            line = jnp.where(
                late,
                small[9 + halves + piece : 10 + halves + piece, :],
                small[9 + piece : 10 + piece, :],
            )
            out[13][pl.ds(piece * width, width)] = line.reshape(width)


def finish(rows, width, units, res, dtok, ff, a, small):
    halves, steps = units // width, width // FINISH
    low = (FINISH, width)
    down_rows = units // steps

    def whole(shape):
        return pl.BlockSpec(shape, lambda i: (0,) * len(shape))

    def at_block(shape, start):
        return pl.BlockSpec(shape, lambda i: (start + i, 0))

    in_specs = [at_block(low, which * steps) for which in range(4)]
    in_specs += [at_block(low, units // FINISH + piece * steps) for piece in range(halves)]
    in_specs += [at_block((down_rows, width), 0), whole(small.shape), whole(res.shape), whole(dtok.shape)]
    matrix, line = (width, width), (width,)
    shapes = [
        (res.shape, bf16), (dtok.shape, f32), (matrix, f32), (line, f32), (matrix, f32), (line, f32),
        (matrix, f32), (line, f32), (matrix, f32), (line, f32), (line, f32), (line, f32),
        ((width, units), f32), ((units,), f32), ((units, width), f32), (line, f32), (line, f32), (line, f32),
    ]
    special = {
        2: at_block(low, 0), 4: at_block(low, 0), 6: at_block(low, 0), 8: at_block(low, 0),
        12: at_block((FINISH, units), 0), 14: at_block((down_rows, width), 0),
    }
    return pl.pallas_call(
        functools.partial(finish_kernel, halves),
        grid=(steps,),
        out_shape=shaped(*shapes),
        in_specs=in_specs,
        out_specs=tuple(special.get(i, whole(shape)) for i, (shape, _) in enumerate(shapes)),
        compiler_params=pltpu.CompilerParams(vmem_limit_bytes=62 << 20),
        name="finish",
    )(*([a] * 4), *([ff] * (halves + 1)), small, res, dtok)


def shaped(*items):
    return tuple(jax.ShapeDtypeStruct(shape, kind) for shape, kind in items)


def pair_device(
    tokens,
    positions,
    span_sizes,
    w_query,
    b_query,
    w_key,
    b_key,
    w_value,
    b_value,
    w_out,
    b_out,
    norm1_gain,
    norm1_bias,
    w_up,
    b_up,
    w_down,
    b_down,
    norm2_gain,
    norm2_bias,
    out_grad,
):
    rows, width = tokens.shape
    units = w_up.shape[1]
    pairs = width // LANES
    halves = units // width
    count = lax.axis_size("dp") // 2
    swaps = 2 + count.bit_length() - 1
    streams = 2 * (FF_CUTS + A_CUTS)
    ff_part, a_part = units // count // 2, width // count // 2
    lines = 9 + 2 * halves
    lines += -lines % 8

    def low(*shape):
        return pltpu.VMEM(shape, bf16)

    def wide(*shape):
        return pltpu.VMEM(shape, f32)

    def sem(*shape):
        return pltpu.SemaphoreType.DMA(shape)

    state, zrows = (pairs, 2, HD, LANES), (pairs, 8, LANES)
    own, pair = (rows, width), (2 * rows, width)
    scratch = dict(
        tok=low(*own), places=pltpu.VMEM(positions.shape, jnp.int32), span=pltpu.SMEM((1, 1), jnp.int32),
        og=low(*own), **{name: low(width) for name in LINES}, bup_line=low(units),
        wa=low(4 * width, width), wff=low(2 * units, width), vec=wide(9 + halves + -(9 + halves) % 8, width),
        hbuf=low(*pair), act=low(2 * rows, units), slope=wide(2 * rows, units), dbuf=low(*pair),
        dpre=low(2 * rows, units), hid=wide(*own), numer=wide(*own), denom=wide(*own),
        tsend=low(*state), trecv=low(*state), zsend=wide(*zrows), zrecv=wide(*zrows),
        bsend=low(*own), brecv=low(*own), res=low(*own), gff=low(2 * units, width),
        dhs=low(*own), dhr=low(*own), dho=wide(*own), mixb=low(*own), mixf=wide(*own), inv=wide(*own),
        rq=low(*own), rk=low(*own), vv=low(*own), nrm=wide(*own), scl=wide(rows, LANES),
        st=low(*state), zst=wide(*zrows), dres=wide(*own), dlow=low(*own), dn=low(*own), xs=low(*own),
        dsend=low(*state), drecv=low(*state), dzs=wide(*zrows), dzr=wide(*zrows),
        dql=low(*own), dkl=low(*own), dvl=low(*own),
        ctab=wide(rows, rows), cosb=wide(rows, LANES), sinb=wide(rows, LANES),
        acc=wide(24, width), bup=wide(8, units),
        cr_ff=low(units, width), cr_a=low(2 * width, width), px=low(width, width),
        xr=low(count, 2, a_part, width), rs_ff=low(count - 1, 2, ff_part, width),
        rs_a=low(count - 1, 2, a_part, width), ff_o=low(2 * units, width), a_o=low(4 * width, width),
        smalls=wide(swaps + 1, lines, width), small_r=wide(swaps, lines, width),
        send=sem(24), recv=sem(24), r_send=sem(2), r_recv=sem(streams, count - 1),
        g_send=sem(2), g_recv=sem(streams, count - 1), x_send=sem(4), x_recv=sem(2, count),
        t_recv=sem(2, count - 1),
        s_recv=sem(4, count), y_recv=sem(2, count),
        m_send=sem(swaps), m_recv=sem(swaps), w_sem=sem(5 + halves), o_sem=sem(7), l_sem=sem(14),
    )
    anywhere = pl.BlockSpec(memory_space=pl.ANY)
    outs = shaped(
        (own, bf16), (own, f32), ((2 * units, width), bf16), ((4 * width, width), bf16),
        ((lines, width), f32),
    )
    res, dtok, ff, a, small = pl.pallas_call(
        functools.partial(block_kernel, count),
        out_shape=outs,
        in_specs=[anywhere] * 20,
        out_specs=tuple([anywhere] * len(outs)),
        scratch_shapes=list(scratch.values()),
        compiler_params=pltpu.CompilerParams(
            collective_id=0, has_side_effects=True, vmem_limit_bytes=62 << 20
        ),
        name="block",
    )(
        tokens, positions, span_sizes.reshape(1, 1), b_query, b_key, b_value, b_out, norm1_gain,
        norm1_bias, b_down, norm2_gain, norm2_bias, b_up, out_grad,
        w_query, w_key, w_value, w_out, w_up, w_down,
    )
    return finish(rows, width, units, res, dtok, ff, a, small)


def pick(mesh):
    def per_device(*args):
        tokens, span_sizes, w_up = args[0], args[2], args[13]
        rows, width = tokens.shape
        units = w_up.shape[1]
        fits = (
            mesh.shape["tensor"] == 2
            and mesh.shape["dp"] == 16
            and span_sizes.shape[0] == 1
            and rows % TILE == 0
            and width == HEADS * HD
            and width % TILE == 0
            and units == 2 * width
        )
        return pair_device(*args) if fits else general_device(*args)

    return per_device


def solution(mesh):
    return jax.shard_map(
        pick(mesh),
        mesh=mesh,
        in_specs=(
            P(("dp", "tensor"), None),
            P("dp"),
            P("dp"),
            P(),
            P(),
            P(),
            P(),
            P(),
            P(),
            P(),
            P(),
            P(),
            P(),
            P(None, "tensor"),
            P("tensor"),
            P("tensor", None),
            P(),
            P(),
            P(),
            P(("dp", "tensor"), None),
        ),
        out_specs=(
            P(("dp", "tensor"), None),
            P(("dp", "tensor"), None),
            P(),
            P(),
            P(),
            P(),
            P(),
            P(),
            P(),
            P(),
            P(),
            P(),
            P(None, "tensor"),
            P("tensor"),
            P("tensor", None),
            P(),
            P(),
            P(),
        ),
        check_vma=False,
    )
```

```python
import functools
import math

import jax
import jax.numpy as jnp
from jax import lax
from jax.experimental import pallas as pl
from jax.experimental.pallas import tpu as pltpu
from jax.sharding import PartitionSpec as P

HEADS = 12
HD = 64
SUBLEN = 32


highest = lax.Precision.HIGHEST
norm_eps = 1e-05


def norm_forward(value, gain, shift):
    mean = jnp.mean(value, axis=-1, keepdims=True)
    centred = value - mean
    scale = lax.rsqrt(jnp.mean(centred * centred, axis=-1, keepdims=True) + norm_eps)
    normal = centred * scale
    return (normal * gain + shift, normal, scale)


def norm_backward(grad, normal, scale, gain):
    along = grad * gain
    inner = (
        along
        - jnp.mean(along, axis=-1, keepdims=True)
        - normal * jnp.mean(along * normal, axis=-1, keepdims=True)
    )
    return (inner * scale, jnp.sum(grad * normal, axis=0), jnp.sum(grad, axis=0))


def gelu_slope(pre):
    normal_cdf = 0.5 * (1.0 + jax.scipy.special.erf(pre * (1.0 / math.sqrt(2.0))))
    return normal_cdf + pre * jnp.exp(-0.5 * pre * pre) * (1.0 / math.sqrt(2.0 * math.pi))


def reach_table(count, span):
    slot_index = jnp.arange(count, dtype=jnp.int32)
    final = (slot_index * SUBLEN // span + 1) * span // SUBLEN - 1
    return (slot_index[None, :] <= final[:, None]).astype(jnp.float32)


def features(rows, w_joint, b_joint, cosine, sine):
    length = rows.shape[0]
    width = rows.shape[1]
    proj = jnp.dot(rows, w_joint, preferred_element_type=jnp.float32) + b_joint
    relu_query = jax.nn.relu(proj[:, :width]).reshape(length, HEADS, HD)
    relu_key = jax.nn.relu(proj[:, width : 2 * width]).reshape(length, HEADS, HD) * (1.0 / HD)
    q_feat = jnp.concatenate([relu_query * cosine, relu_query * sine], axis=-1).astype(jnp.bfloat16)
    k_feat = jnp.concatenate([relu_key * cosine, relu_key * sine], axis=-1).astype(jnp.bfloat16)
    v_low = proj[:, 2 * width :].astype(jnp.bfloat16)
    return (q_feat, k_feat, v_low)


def local_blocks(k_feat, v_low):
    count = k_feat.shape[0] // SUBLEN
    k_sub = k_feat.reshape(count, SUBLEN, HEADS, 2 * HD)
    v_sub = v_low.reshape(count, SUBLEN, HEADS, HD)
    blocks = jnp.einsum("tjhf,tjhd->thfd", k_sub, v_sub, preferred_element_type=jnp.float32)
    k_total = jnp.sum(k_sub.astype(jnp.float32), axis=1)
    return (blocks, k_total)


def attend_core(q_feat, k_feat, v_low, blocks, k_total, reach, extra_blocks, extra_keys):
    count = q_feat.shape[0] // SUBLEN
    q_sub = q_feat.reshape(count, SUBLEN, HEADS, 2 * HD)
    k_sub = k_feat.reshape(count, SUBLEN, HEADS, 2 * HD)
    v_sub = v_low.reshape(count, SUBLEN, HEADS, HD)
    state_low = (
        jnp.einsum("st,thfd->shfd", reach, blocks, precision=highest) + extra_blocks
    ).astype(jnp.bfloat16)
    z_sum = jnp.einsum("st,thf->shf", reach, k_total, precision=highest) + extra_keys
    numer = jnp.einsum("sihf,shfd->sihd", q_sub, state_low, preferred_element_type=jnp.float32)
    denom = jnp.einsum("sihf,shf->sih", q_sub.astype(jnp.float32), z_sum, precision=highest) + 1.0
    return (q_sub, k_sub, v_sub, state_low, z_sum, numer, denom)


def back_first(parts, grad_mixed):
    q_sub, k_sub, v_sub, state_low, z_sum, numer, denom = parts
    count = q_sub.shape[0]
    grad_out = grad_mixed.reshape(count, SUBLEN, HEADS, HD).astype(jnp.float32)
    d_numer = grad_out / denom[..., None]
    d_denom = -jnp.sum(grad_out * numer, axis=-1) / (denom * denom)
    q_wide = q_sub.astype(jnp.float32)
    d_query = jnp.einsum(
        "sihd,shfd->sihf", d_numer, state_low.astype(jnp.float32), precision=highest
    )
    d_query = d_query + d_denom[..., None] * z_sum[:, None]
    d_state = jnp.einsum("sihf,sihd->shfd", q_wide, d_numer, precision=highest)
    d_zsum = jnp.einsum("sihf,sih->shf", q_wide, d_denom, precision=highest)
    return (d_query, d_state, d_zsum)


def back_second(parts, reach, d_state, d_zsum, later_blocks, later_keys):
    q_sub, k_sub, v_sub = (parts[0], parts[1], parts[2])
    d_blocks = jnp.einsum("st,shfd->thfd", reach, d_state, precision=highest) + later_blocks
    d_ktotal = jnp.einsum("st,shf->thf", reach, d_zsum, precision=highest) + later_keys
    d_key = (
        jnp.einsum("thfd,tjhd->tjhf", d_blocks, v_sub.astype(jnp.float32), precision=highest)
        + d_ktotal[:, None]
    )
    d_value = jnp.einsum("thfd,tjhf->tjhd", d_blocks, k_sub.astype(jnp.float32), precision=highest)
    return (d_key, d_value)


def feature_grads(q_feat, k_feat, d_qf, d_kf, d_val, cos_part, sin_part):
    size = q_feat.shape[0]
    d_qf = d_qf.reshape(size, HEADS, 2 * HD)
    d_kf = d_kf.reshape(size, HEADS, 2 * HD)
    d_query = jnp.where(
        q_feat[..., :HD] > 0, d_qf[..., :HD] * cos_part + d_qf[..., HD:] * sin_part, 0.0
    )
    d_key = jnp.where(
        k_feat[..., :HD] > 0,
        (d_kf[..., :HD] * cos_part + d_kf[..., HD:] * sin_part) * (1.0 / HD),
        0.0,
    )
    return jnp.concatenate(
        [
            d_query.reshape(size, HEADS * HD),
            d_key.reshape(size, HEADS * HD),
            d_val.reshape(size, HEADS * HD),
        ],
        axis=1,
    )


def general_device(
    tokens,
    positions,
    span_sizes,
    w_query,
    b_query,
    w_key,
    b_key,
    w_value,
    b_value,
    w_out,
    b_out,
    norm1_gain,
    norm1_bias,
    w_up,
    b_up,
    w_down,
    b_down,
    norm2_gain,
    norm2_bias,
    out_grad,
):
    rank = lax.axis_index("tensor")
    tensor_count = lax.axis_size("tensor")
    own = tokens.shape[0]
    width = tokens.shape[1]
    seqs = span_sizes.shape[0]
    group = own * tensor_count
    length = group // seqs
    start = rank * own
    w_joint = jnp.concatenate([w_query, w_key, w_value], axis=1)
    b_joint = jnp.concatenate([b_query, b_key, b_value]).astype(jnp.float32)
    gain_one = norm1_gain.astype(jnp.float32)
    gain_two = norm2_gain.astype(jnp.float32)
    gathered = lax.all_gather(tokens, "tensor", axis=0, tiled=True)
    angle = math.pi / 2 * positions.astype(jnp.float32) / (3 * length)
    cosine = jnp.cos(angle).reshape(seqs, length, 1, 1)
    sine = jnp.sin(angle).reshape(seqs, length, 1, 1)

    def seq_forward(items):
        rows, cos_part, sin_part, span = items
        q_feat, k_feat, v_low = features(rows, w_joint, b_joint, cos_part, sin_part)
        blocks_seq, ktot_seq = local_blocks(k_feat, v_low)
        parts = attend_core(
            q_feat,
            k_feat,
            v_low,
            blocks_seq,
            ktot_seq,
            reach_table(q_feat.shape[0] // SUBLEN, span),
            0.0,
            0.0,
        )
        mixed_seq = (
            (parts[5] / parts[6][..., None]).reshape(rows.shape[0], width).astype(jnp.bfloat16)
        )
        return (mixed_seq, q_feat, k_feat, v_low)

    mixed, q_all, k_all, v_all = lax.map(
        seq_forward, (gathered.reshape(seqs, length, width), cosine, sine, span_sizes)
    )
    mixed = mixed.reshape(group, width)
    mixed_own = lax.dynamic_slice_in_dim(mixed, start, own, 0)
    resid = (
        tokens.astype(jnp.float32)
        + jnp.dot(mixed_own, w_out, preferred_element_type=jnp.float32)
        + b_out.astype(jnp.float32)
    )
    hidden, normal_one, scale_one = norm_forward(resid, gain_one, norm1_bias.astype(jnp.float32))
    hidden_low = hidden.astype(jnp.bfloat16)
    rows_in = lax.all_gather(hidden_low, "tensor", axis=0, tiled=True)
    pre = jnp.dot(rows_in, w_up, preferred_element_type=jnp.float32) + b_up.astype(jnp.float32)
    act_low = jax.nn.gelu(pre, approximate=False).astype(jnp.bfloat16)
    branch = lax.psum_scatter(
        jnp.dot(act_low, w_down, preferred_element_type=jnp.float32),
        "tensor",
        scatter_dimension=0,
        tiled=True,
    )
    summed = hidden + branch + b_down.astype(jnp.float32)
    result, normal_two, scale_two = norm_forward(summed, gain_two, norm2_bias.astype(jnp.float32))
    d_sum, d_gain_two, d_bias_two = norm_backward(
        out_grad.astype(jnp.float32), normal_two, scale_two, gain_two
    )
    d_bdown = jnp.sum(d_sum, axis=0)
    d_sum_low = d_sum.astype(jnp.bfloat16)
    rows_grad = lax.all_gather(d_sum_low, "tensor", axis=0, tiled=True)
    g_down = jnp.dot(act_low.T, rows_grad, preferred_element_type=jnp.float32)
    d_pre = jnp.dot(rows_grad, w_down.T, preferred_element_type=jnp.float32) * gelu_slope(pre)
    g_upbias = jnp.sum(d_pre, axis=0)
    d_pre_low = d_pre.astype(jnp.bfloat16)
    g_up = jnp.dot(rows_in.T, d_pre_low, preferred_element_type=jnp.float32)
    d_hidden = lax.psum_scatter(
        jnp.dot(d_pre_low, w_up.T, preferred_element_type=jnp.float32),
        "tensor",
        scatter_dimension=0,
        tiled=True,
    )
    g_up, g_upbias, g_down = (
        lax.psum(g_up.astype(jnp.bfloat16), "dp").astype(jnp.float32),
        lax.psum(g_upbias.astype(jnp.bfloat16), "dp").astype(jnp.float32),
        lax.psum(g_down.astype(jnp.bfloat16), "dp").astype(jnp.float32),
    )
    d_hidden = d_hidden + d_sum
    d_resid, d_gain_one, d_bias_one = norm_backward(d_hidden, normal_one, scale_one, gain_one)
    d_bout = jnp.sum(d_resid, axis=0)
    d_gain_one, d_bias_one, d_gain_two, d_bias_two, d_bout, d_bdown = lax.psum(
        (d_gain_one, d_bias_one, d_gain_two, d_bias_two, d_bout, d_bdown), ("dp", "tensor")
    )
    d_resid_low = d_resid.astype(jnp.bfloat16)
    rows_back = lax.all_gather(d_resid_low, "tensor", axis=0, tiled=True)
    g_out = jnp.dot(mixed.T, rows_back, preferred_element_type=jnp.float32)
    d_mixed = jnp.dot(rows_back, w_out.T, preferred_element_type=jnp.float32).astype(jnp.bfloat16)

    def seq_backward(items):
        q_feat, k_feat, v_low, cos_part, sin_part, span, grad_mixed = items
        blocks_seq, ktot_seq = local_blocks(k_feat, v_low)
        reach = reach_table(q_feat.shape[0] // SUBLEN, span)
        parts = attend_core(q_feat, k_feat, v_low, blocks_seq, ktot_seq, reach, 0.0, 0.0)
        d_qf, d_state, d_zsum = back_first(parts, grad_mixed)
        d_kf, d_val = back_second(parts, reach, d_state, d_zsum, 0.0, 0.0)
        joint = feature_grads(q_feat, k_feat, d_qf, d_kf, d_val, cos_part, sin_part)
        return (joint.astype(jnp.bfloat16), jnp.sum(joint, axis=0))

    d_joint, d_jbias = lax.map(
        seq_backward,
        (q_all, k_all, v_all, cosine, sine, span_sizes, d_mixed.reshape(seqs, length, width)),
    )
    d_joint = d_joint.reshape(group, 3 * width)
    d_jbias = jnp.sum(d_jbias, axis=0)
    g_joint = jnp.dot(gathered.T, d_joint, preferred_element_type=jnp.float32)
    d_joint_own = lax.dynamic_slice_in_dim(d_joint, start, own, 0)
    d_tokens = d_resid + jnp.dot(d_joint_own, w_joint.T, preferred_element_type=jnp.float32)
    g_joint, g_out, d_jbias = lax.psum((g_joint, g_out, d_jbias), "dp")
    return (
        result.astype(jnp.bfloat16),
        d_tokens,
        g_joint[:, :width],
        d_jbias[:width],
        g_joint[:, width : 2 * width],
        d_jbias[width : 2 * width],
        g_joint[:, 2 * width :],
        d_jbias[2 * width :],
        g_out,
        d_bout,
        d_gain_one,
        d_bias_one,
        g_up,
        g_upbias,
        g_down,
        d_bdown,
        d_gain_two,
        d_bias_two,
    )


f32 = jnp.float32
bf16 = jnp.bfloat16
MESH = pl.DeviceIdType.MESH
LANES = 2 * HD
TILE = 256
ROWBLOCK = 32
FINISH = 256
FF_CUTS = 3
A_CUTS = 3
RING_ROWS = 16
LINES = tuple("l" + str(index) for index in range(9))


def tile_at(index, size):
    return pl.ds(pl.multiple_of(index * size, size), size)


def contract(left, right, left_dim, right_dim, precision=None):
    return lax.dot_general(
        left,
        right,
        (((left_dim,), (right_dim,)), ((), ())),
        precision=precision,
        preferred_element_type=f32,
    )


def mm(left, right):
    return contract(left, right, 1, 0)


def mm_nt(left, right):
    return contract(left, right, 1, 1)


def mm_tn(left, right):
    return contract(left, right, 0, 0)


def head_masks():
    lane = lax.broadcasted_iota(jnp.int32, (1, LANES), 1)
    first = (lane < HD).astype(f32)
    return first, 1.0 - first


def pair_mask():
    row = lax.broadcasted_iota(jnp.int32, (LANES, LANES), 0)
    col = lax.broadcasted_iota(jnp.int32, (LANES, LANES), 1)
    return ((row < HD) == (col < HD)).astype(f32)


def column_of(block, which):
    row = lax.broadcasted_iota(jnp.int32, block.shape, 0)
    return contract(jnp.where(row == which, block, 0.0), jnp.ones((8, LANES), f32), 0, 0, highest)


def squeeze_pair(square):
    return square[:HD] + square[HD:]


def spread_pair(part, mask):
    return jnp.concatenate([part, part], axis=0).astype(f32) * mask


def two_rows(top, below):
    row = lax.broadcasted_iota(jnp.int32, (8, LANES), 0)
    return jnp.where(row == 0, top, jnp.where(row == 1, below, 0.0))


def fold8(value):
    total = value[0:8]
    for start in range(8, value.shape[0], 8):
        total = total + value[start : start + 8]
    return total


def angle_lines(places, length):
    rows = places.shape[0]
    angle = math.pi / 2 * places.astype(f32).reshape(1, rows) / (3 * length)
    line = lax.broadcasted_iota(jnp.int32, (8, rows), 0)
    return jnp.where(line == 0, jnp.cos(angle), jnp.where(line == 1, jnp.sin(angle), 0.0))


def angle_products(block, span, ctab):
    rows = ctab.shape[0]
    both = contract(block, block, 0, 0, highest)
    row = lax.broadcasted_iota(jnp.int32, (rows, rows), 0)
    col = lax.broadcasted_iota(jnp.int32, (rows, rows), 1)
    seen = col <= (row | (span[0, 0] - 1))
    ctab[...] = jnp.where(seen, both * (1.0 / HD), 0.0)


def peer_copy(src, dst, sems, slot, device):
    return pltpu.make_async_remote_copy(
        src_ref=src,
        dst_ref=dst,
        send_sem=sems[0].at[slot],
        recv_sem=sems[1].at[slot],
        device_id=device,
        device_id_type=MESH,
    )


def ring_device(spot, depth, core):
    far = spot // depth
    z = far * (2 * depth - 1 - spot) + (1 - far) * spot
    return ((z * 2 + far) * 2 + core, lax.axis_index("tensor"))


def layer_norm(value):
    centred = value - jnp.mean(value, axis=-1, keepdims=True)
    scale = lax.rsqrt(jnp.mean(centred * centred, axis=-1, keepdims=True) + norm_eps)
    return centred * scale, scale


def layer_norm_back(grad, gain, normal, scale):
    along = grad * gain
    return (
        along
        - jnp.mean(along, axis=-1, keepdims=True)
        - normal * jnp.mean(along * normal, axis=-1, keepdims=True)
    ) * scale


def block_kernel(
    count, tok_h, places_h, span_h, bq, bk, bv, bo, g1, b1, bd, g2, b2, bup_in, og_h,
    wq, wk, wv, wo, wup, wdn,
    res_h, dtok_h, ff_h, a_h, small_h,
    tok, places, span, og, l0, l1, l2, l3, l4, l5, l6, l7, l8, bup_line, wa, wff, vec, hbuf, act, slope, dbuf, dpre, hid, numer, denom, tsend, trecv, zsend, zrecv,
    bsend, brecv, res, gff, dhs, dhr, dho, mixb, mixf, inv, rq, rk, vv, nrm, scl, st, zst,
    dres, dlow, dn, xs, dsend, drecv, dzs, dzr, dql, dkl, dvl, ctab, cosb, sinb, acc, bup,
    cr_ff, cr_a, px, xr, rs_ff, rs_a, ff_o, a_o, smalls, small_r,
    send, recv, r_send, r_recv, g_send, g_recv, x_send, x_recv, t_recv, s_recv, y_recv, m_send, m_recv,
    w_sem, o_sem, l_sem,
):
    sems = (send, recv)
    rows, width = tok.shape
    units = wup.shape[1]
    halves = units // width
    pairs = width // LANES
    tiles = width // TILE
    depth = count // 2
    quarter = width
    dq, dk, dv, ga = numer, denom, hid, wff
    dp, rank = lax.axis_index("dp"), lax.axis_index("tensor")
    late = rank.astype(f32)
    early = 1.0 - late
    core, y, z = dp % 2, (dp // 2) % 2, dp // 4
    spot = y * (2 * depth - 1 - z) + (1 - y) * z
    sibling = (dp + 1 - 2 * core, rank)
    peer = (dp, 1 - rank)
    ahead = ring_device((spot + 1) % count, depth, core)
    behind = ring_device((spot + count - 1) % count, depth, core)
    swaps = [sibling, peer, (dp + 2 - 4 * y, rank)]
    step = 1
    while step < depth:
        bit = (z // step) % 2
        swaps.append((dp + 4 * (step - 2 * step * bit), rank))
        step *= 2
    partners = [ahead, behind] + swaps
    barrier = pltpu.get_barrier_semaphore()
    for device in partners:
        pl.semaphore_signal(barrier, inc=1, device_id=device, device_id_type=MESH)

    loads = [
        (wk, wa.at[pl.ds(width, width), :]),
        (wv, wa.at[pl.ds(2 * width, width), :]),
        (wq, wa.at[pl.ds(0, width), :]),
        (wo, wa.at[pl.ds(3 * width, width), :]),
    ]
    for part in range(halves):
        loads.append(
            (wup.at[:, pl.ds(part * width, width)], wff.at[pl.ds(units + part * width, width), :])
        )
    loads.append((wdn, wff.at[pl.ds(0, units), :]))

    def load(index):
        return pltpu.make_async_copy(loads[index][0], loads[index][1], w_sem.at[index])

    small_loads = [(tok_h, tok), (places_h, places), (span_h, span)]
    vectors = (bq, bk, bv, bo, g1, b1, bd, g2, b2)
    lines = (l0, l1, l2, l3, l4, l5, l6, l7, l8)
    small_loads += [pair for pair in zip(vectors, lines)]
    small_loads += [(bup_in, bup_line), (og_h, og)]

    def fetch(index):
        return pltpu.make_async_copy(*small_loads[index], l_sem.at[index])

    fetch(0).start()
    for index in range(3):
        load(index).start()
    for index in range(1, len(small_loads)):
        fetch(index).start()
    for index in range(1, len(small_loads) - 1):
        fetch(index).wait()

    def out_copy(source, target, at, slot):
        return pltpu.make_async_copy(source.at[at, :], target.at[at, :], o_sem.at[slot])

    for index in range(len(vectors)):
        vec[index : index + 1, :] = lines[index][...].astype(f32).reshape(1, width)
    for part in range(halves):
        piece = bup_line[pl.ds(part * width, width)]
        vec[9 + part : 10 + part, :] = piece.astype(f32).reshape(1, width)
    own, far_rows = pl.ds(0, rows), pl.ds(rows, rows)
    my_places = places[pl.ds(pl.multiple_of(rank * rows, rows), rows)]
    angles = angle_lines(my_places, places.shape[0])
    cosb[...] = column_of(angles, 0)
    sinb[...] = column_of(angles, 1)
    diag = pair_mask()
    first, second = head_masks()
    first_low, second_low = first.astype(bf16), second.astype(bf16)
    diag_low = diag.astype(bf16)
    acc[...] = jnp.zeros_like(acc)
    bup[...] = jnp.zeros_like(bup)
    smalls[0] = jnp.zeros(smalls.shape[1:], f32)

    def add_small(slot, line):
        smalls[0, slot : slot + 1, :] = line

    def project(which, target, j):
        cols = tile_at(j, TILE)
        value = mm(tok[...], wa[pl.ds(which * width, width), cols]) + vec[which : which + 1, cols]
        if which < 2:
            value = jnp.maximum(value, 0.0)
        target[:, cols] = value.astype(bf16)

    def make_state(p):
        lanes = tile_at(p, LANES)
        k = rk[:, lanes].astype(f32) * (1.0 / HD)
        v = vv[:, lanes]
        kc, ks = (k * cosb[...]).astype(bf16), (k * sinb[...]).astype(bf16)
        tsend[p, 0] = squeeze_pair(mm_tn(kc, v) * diag).astype(bf16)
        tsend[p, 1] = squeeze_pair(mm_tn(ks, v) * diag).astype(bf16)
        zsend[p] = two_rows(
            jnp.sum(kc.astype(f32), axis=0, keepdims=True),
            jnp.sum(ks.astype(f32), axis=0, keepdims=True),
        )

    together = TILE // LANES

    def state_copy(j):
        where = pl.ds(j * together, together)
        return peer_copy(tsend.at[where], trecv.at[where], sems, (0, 24, 25)[j], peer)

    key_copy = peer_copy(zsend, zrecv, sems, 1, peer)
    fetch(0).wait()
    load(0).wait()
    load(1).wait()
    for index in range(3, len(loads)):
        load(index).start()
    for j in range(tiles):
        project(1, rk, j)
        project(2, vv, j)
        pl.loop(j * together, (j + 1) * together)(make_state)
        if j == 0:
            pl.semaphore_wait(barrier, len(partners))
        state_copy(j).start()
    key_copy.start()
    angle_products(angles, span, ctab)
    load(2).wait()
    pl.loop(0, tiles)(functools.partial(project, 0, rq))

    @pl.loop(0, pairs)
    def _(p):
        lanes = tile_at(p, LANES)
        q, k, v = rq[:, lanes], rk[:, lanes], vv[:, lanes]
        parts = []
        for mask, rest in ((first_low, second_low), (second_low, first_low)):
            prob = (mm_nt(q * mask, k) * ctab[...]).astype(bf16)
            parts.append(mm(prob, v * mask + rest))
        numer[:, lanes] = parts[0] * first + parts[1] * second
        denom[:, lanes] = pltpu.roll(parts[0] * second + parts[1] * first, HD, 1)

    for j in range(tiles):
        state_copy(j).wait()
    key_copy.wait()

    @pl.loop(0, pairs)
    def _(p):
        lanes = tile_at(p, LANES)
        q = rq[:, lanes].astype(f32)
        qc, qs = (q * cosb[...]).astype(bf16), (q * sinb[...]).astype(bf16)
        st[p] = (trecv[p].astype(f32) * late).astype(bf16)
        zblock = zrecv[p] * late
        zst[p] = zblock
        weighted = qc.astype(f32) * zblock[0:1, :] + qs.astype(f32) * zblock[1:2, :]
        num, den = numer[:, lanes], denom[:, lanes] + 1.0 + mm(weighted.astype(bf16), diag_low)
        for part, feat in ((0, qc), (1, qs)):
            num += mm(feat, spread_pair(st[p, part], diag).astype(bf16))
        reciprocal = 1.0 / den
        mix = num * reciprocal
        inv[:, lanes] = reciprocal
        mixf[:, lanes] = mix
        mixb[:, lanes] = mix.astype(bf16)

    load(3).wait()

    @pl.loop(0, tiles)
    def _(j):
        cols = tile_at(j, TILE)
        hid[:, cols] = (
            tok[:, cols].astype(f32) + mm(mixb[...], wa[pl.ds(3 * width, width), cols]) + vec[3:4, cols]
        )

    span_rows = rows // 2
    near = [pl.ds(k * span_rows, span_rows) for k in range(2)]
    away = [pl.ds(rows + k * span_rows, span_rows) for k in range(2)]
    blocks = span_rows // ROWBLOCK

    def norm_rows(i):
        at = tile_at(i, ROWBLOCK)
        normal, scale = layer_norm(hid[at, :])
        hidden = normal * vec[4:5, :] + vec[5:6, :]
        nrm[at, :] = normal
        scl[at, :] = jnp.broadcast_to(scale, (ROWBLOCK, LANES))
        hid[at, :] = hidden
        hbuf[at, :] = hidden.astype(bf16)

    def rows_copy(k):
        return peer_copy(hbuf.at[near[k]], hbuf.at[away[k]], sems, 12 + k, peer)

    def branch_copy(k):
        return peer_copy(bsend.at[near[k]], brecv.at[near[k]], sems, 14 + k, peer)

    def grad_copy(k):
        return peer_copy(dbuf.at[near[k]], dbuf.at[away[k]], sems, 16 + k, peer)

    def hidden_copy(k):
        return peer_copy(dhs.at[near[k]], dhr.at[near[k]], sems, 18 + k, peer)

    for k in range(2):
        pl.loop(k * blocks, (k + 1) * blocks)(norm_rows)
        rows_copy(k).start()
    for index in range(4, len(loads)):
        load(index).wait()
    fetch(len(small_loads) - 1).wait()

    def raise_rows(part):
        for piece in range(halves):

            @pl.loop(0, tiles)
            def _(j, piece=piece):
                cols, narrow = tile_at(piece * tiles + j, TILE), tile_at(j, TILE)
                weight = wff[pl.ds(units + piece * width, width), narrow]
                pre = mm(hbuf[part, :], weight) + vec[9 + piece : 10 + piece, narrow]
                cdf = 0.5 * (1.0 + lax.erf(pre * (1.0 / math.sqrt(2.0))))
                act[part, cols] = (pre * cdf).astype(bf16)
                slope[part, cols] = cdf + pre * jnp.exp(-0.5 * pre * pre) * (
                    1.0 / math.sqrt(2.0 * math.pi)
                )

    raise_rows(own)
    for k in range(2):
        rows_copy(k).wait()
        raise_rows(away[k])

        @pl.loop(0, tiles)
        def _(j, k=k):
            cols = tile_at(j, TILE)
            bsend[near[k], cols] = mm(act[away[k], :], wff[pl.ds(0, units), cols]).astype(bf16)

        branch_copy(k).start()

    @pl.loop(0, tiles)
    def _(j):
        cols = tile_at(j, TILE)
        hid[:, cols] += mm(act[own, :], wff[pl.ds(0, units), cols]) + vec[6:7, cols]

    def finish_rows(i):
        at = tile_at(i, ROWBLOCK)
        normal, scale = layer_norm(hid[at, :] + brecv[at, :].astype(f32))
        res[at, :] = (normal * vec[7:8, :] + vec[8:9, :]).astype(bf16)
        grad = og[at, :].astype(f32)
        inner = layer_norm_back(grad, vec[7:8, :], normal, scale)
        dho[at, :] = inner
        dbuf[at, :] = inner.astype(bf16)
        acc[0:8, :] += fold8(grad * normal)
        acc[8:16, :] += fold8(grad)
        acc[16:24, :] += fold8(inner)

    for k in range(2):
        branch_copy(k).wait()
        pl.loop(k * blocks, (k + 1) * blocks)(finish_rows)
        grad_copy(k).start()
    result_out = pltpu.make_async_copy(res, res_h, o_sem.at[0])
    result_out.start()
    for slot in range(3):
        add_small(3 + slot, jnp.sum(acc[8 * slot : 8 * slot + 8, :], axis=0, keepdims=True))

    def lower_rows(part):
        @pl.loop(0, units // TILE)
        def _(j):
            cols = tile_at(j, TILE)
            d_pre = mm_nt(dbuf[part, :], wff[cols, :]) * slope[part, cols]
            bup[:, cols] += fold8(d_pre)
            dpre[part, cols] = d_pre.astype(bf16)

    def lower_hidden(part, cols, j):
        total = 0.0
        for piece in range(halves):
            weight = wff[pl.ds(pl.multiple_of(units + piece * width + j * TILE, TILE), TILE), :]
            total += mm_nt(dpre[part, piece * width : (piece + 1) * width], weight)
        return total

    lower_rows(own)
    def send_hidden(k):
        @pl.loop(0, tiles)
        def _(j):
            cols = tile_at(j, TILE)
            dhs[near[k], cols] = lower_hidden(away[k], cols, j).astype(bf16)

        hidden_copy(k).start()

    grad_copy(0).wait()
    lower_rows(away[0])
    send_hidden(0)
    grad_copy(1).wait()
    lower_rows(away[1])

    def make_down(part):
        @pl.loop(part * tiles, (part + 1) * tiles)
        def _(j):
            cols = tile_at(j, TILE)
            gff[cols, :] = mm_tn(act[:, cols], dbuf[...]).astype(bf16)

    def make_up(part):
        @pl.loop(0, tiles)
        def _(j):
            gff[pl.ds(units + part * width, width), tile_at(j, TILE)] = mm_tn(
                hbuf[...], dpre[:, tile_at(part * tiles + j, TILE)]
            ).astype(bf16)

    def part_rows(which, size):
        return pl.ds(pl.multiple_of(which * size, size), size)

    def core_ff(part):
        start = pl.multiple_of((1 - core) * units + part * width, width)
        return peer_copy(
            gff.at[pl.ds(start, width), :],
            cr_ff.at[pl.ds(part * width, width), :],
            sems, (8, 22, 23)[part], sibling,
        )

    for part in range(halves):
        pl.when(core == 0)(functools.partial(make_up, part))
        pl.when(core == 1)(functools.partial(make_down, part))
        core_ff(part).start()
    send_hidden(1)
    for part in range(halves):
        pl.when(core == 0)(functools.partial(make_down, part))
        pl.when(core == 1)(functools.partial(make_up, part))

    band, per = width // 4, count // 4
    ff_streams, a_streams = [], []
    for kind, (cuts, group) in enumerate(((FF_CUTS, ff_streams), (A_CUTS, a_streams))):
        size = (quarter if kind else units) // count // 2
        for way in range(2):
            for cut in range(cuts):
                number = 2 * FF_CUTS * kind + way * cuts + cut
                piece = size // cuts
                group.append((number, kind, way, cut * piece, piece))
    slots, sums, outs = (rs_ff, rs_a), (gff, ga), (ff_o, a_o)
    ff_size, a_size = units // count // 2, quarter // count // 2
    mine, theirs = core * 2 + rank, core * 2 + 1 - rank

    def ff_rows(at, way, offset, length, base):
        start = base + (at % count) * 2 * ff_size + way * ff_size + offset
        return pl.ds(pl.multiple_of(start, 16), length)

    def a_rows(at, way, offset, length, owner):
        chunk = at % count
        start = (chunk // per) * width + owner * band + (chunk % per) * 2 * a_size
        return pl.ds(pl.multiple_of(start + way * a_size + offset, 16), length)

    def line_rows(at, way, offset, length):
        start = (at % count) * 2 * a_size + way * a_size + offset
        return pl.ds(pl.multiple_of(start, 16), length)

    def core_rows(at, way, offset, length):
        chunk = at % count
        start = (chunk // per) * 2 * band + rank * band + (chunk % per) * 2 * a_size
        return pl.ds(pl.multiple_of(start + way * a_size + offset, 16), length)

    def stream_rows(stream, at):
        _, kind, way, offset, length = stream
        if kind:
            return a_rows(at, way, offset, length, mine)
        return ff_rows(at, way, offset, length, core * units)

    def toward(way):
        return behind if way else ahead

    def turn(way):
        return -1 if way else 1

    def remote(source, target, send_sem, recv_sem, device):
        return pltpu.make_async_remote_copy(
            src_ref=source,
            dst_ref=target,
            send_sem=send_sem,
            recv_sem=recv_sem,
            device_id=device,
            device_id_type=MESH,
        )

    def spread_copy(stream, at, s):
        number, kind, way, offset, length = stream
        return remote(
            sums[kind].at[stream_rows(stream, at), :],
            slots[kind].at[s, way, pl.ds(offset, length), :],
            r_send.at[kind],
            r_recv.at[number, s],
            toward(way),
        )

    def gather_copy(stream, at, s):
        number, kind, way, _, _ = stream
        where = outs[kind].at[stream_rows(stream, at), :]
        return remote(where, where, g_send.at[kind], g_recv.at[number, s], toward(way))

    def across_copy(way, s, owner, first):
        at, skip = spot + 2 * count + turn(way) * (1 - s), 0 if first else RING_ROWS
        where = a_o.at[a_rows(at, way, skip, a_size - skip, owner), :]
        return remote(where, where, x_send.at[0], x_recv.at[way, s], peer)

    def round_copy(way, s):
        at = spot + 2 * count + turn(way) * (1 - s)
        where = a_o.at[a_rows(at, way, 0, RING_ROWS, theirs), :]
        return remote(where, where, x_send.at[3], t_recv.at[way, s], toward(way))

    def side_copy(way, s, owner, lane):
        at = spot + 2 * count + turn(way) * (1 - s)
        where = a_o.at[a_rows(at, way, 0, a_size, owner), :]
        return remote(where, where, x_send.at[1], s_recv.at[2 * lane + way, s], sibling)

    def fold_copy(way, s):
        at = spot + count - turn(way) * s
        return remote(
            px.at[line_rows(at, way, 0, a_size), :],
            xr.at[s, way],
            x_send.at[2],
            y_recv.at[way, s],
            peer,
        )

    def start_folds(s):
        for way in range(2):
            fold_copy(way, s).start()

    def own_part(stream, at, s):
        _, kind, way, offset, length = stream
        value = sums[kind][stream_rows(stream, at), :].astype(f32)
        if kind == 0:
            return value + cr_ff[ff_rows(at, way, offset, length, 0), :].astype(f32)
        if offset == 0:
            fold_copy(way, s).wait_recv()
        return (
            value
            + cr_a[core_rows(at, way, offset, length), :].astype(f32)
            + xr[s, way, pl.ds(offset, length), :].astype(f32)
        )

    def ring_first(streams):
        for stream in streams:
            at = spot + count
            sums[stream[1]][stream_rows(stream, at), :] = own_part(stream, at, 0).astype(bf16)
            spread_copy(stream, at, 0).start()

    def store_chunk(way, s, owner):
        rows_at = a_rows(spot + 2 * count + turn(way) * (1 - s), way, 0, a_size, owner)
        pltpu.make_async_copy(a_o.at[rows_at, :], a_h.at[rows_at, :], o_sem.at[4]).start()

    def pass_on(stream, s, first=False):
        _, kind, way, offset, length = stream
        if kind and offset + length == a_size:
            across_copy(way, s, mine, first).start()
            side_copy(way, s, mine, 0).start()
            store_chunk(way, s, mine)

    def ring_spread(streams, s, last=False):
        for stream in streams:
            _, kind, way, offset, length = stream
            at = spot + count - turn(way) * (s + 1)
            target = stream_rows(stream, at)
            part = own_part(stream, at, s + 1)
            spread_copy(stream, at, s).wait_recv()
            arrived = slots[kind][s, way, pl.ds(offset, length), :].astype(f32)
            total = (part + arrived).astype(bf16)
            if last:
                outs[kind][target, :] = total
                gather_copy(stream, at, 0).start()
                pass_on(stream, 0, True)
            else:
                sums[kind][target, :] = total
                spread_copy(stream, at, s + 1).start()

    def ring_gather(streams, s, last=False):
        for stream in streams:
            at = spot + 2 * count - turn(stream[2]) * s
            gather_copy(stream, at, s).wait_recv()
            if not last:
                gather_copy(stream, at, s + 1).start()
        for stream in streams:
            pass_on(stream, s + 1)

    def cross_over(s, first=False, last=False):
        for way in range(2):
            across_copy(way, s, theirs, first).wait_recv()
            if not first:
                round_copy(way, s - 1).wait_recv()
            if not last:
                round_copy(way, s).start()
        for way in range(2):
            side_copy(way, s, theirs, 1).start()
            store_chunk(way, s, theirs)

    def side_done(lane, s):
        owner = (1 - core) * 2 + (1 - rank if lane else rank)
        for way in range(2):
            side_copy(way, s, owner, lane).wait_recv()
            store_chunk(way, s, owner)

    def ff_part(q):
        s, cut = q // FF_CUTS, q % FF_CUTS
        piece = ff_size // FF_CUTS
        ring_spread([(way * FF_CUTS + cut, 0, way, cut * piece, piece) for way in range(2)], s)

    def small_copy(index):
        return peer_copy(smalls.at[index], small_r.at[index], (m_send, m_recv), index, swaps[index])

    def swap_small(index):
        small_copy(index).wait()
        smalls[index + 1] = smalls[index] + small_r[index]
        if index + 1 < len(swaps):
            small_copy(index + 1).start()

    for piece in range(halves):
        line = jnp.sum(bup[:, piece * width : (piece + 1) * width], axis=0, keepdims=True)
        add_small(9 + piece, line * early)
        add_small(9 + halves + piece, line * late)

    @pl.loop(0, tiles)
    def _(j):
        cols = tile_at(j, TILE)
        dho[:, cols] += lower_hidden(own, cols, j)

    acc[...] = jnp.zeros_like(acc)
    for part in range(halves):
        core_ff(part).wait()
    ring_first(ff_streams)
    hidden_copy(0).wait()
    hidden_copy(1).wait()

    @pl.loop(0, rows // ROWBLOCK)
    def _(i):
        at = tile_at(i, ROWBLOCK)
        grad = dho[at, :] + dhr[at, :].astype(f32)
        normal = nrm[at, :]
        inner = layer_norm_back(grad, vec[4:5, :], normal, scl[at, 0:1])
        dres[at, :] = inner
        dlow[at, :] = inner.astype(bf16)
        acc[0:8, :] += fold8(grad * normal)
        acc[8:16, :] += fold8(grad)
        acc[16:24, :] += fold8(inner)

    for slot in range(3):
        add_small(slot, jnp.sum(acc[8 * slot : 8 * slot + 8, :], axis=0, keepdims=True))

    ff_part(0)

    @pl.loop(0, tiles)
    def _(j):
        cols = tile_at(j, TILE)
        d_mixed = mm_nt(dlow[...], wa[tile_at(3 * tiles + j, TILE), :]).astype(bf16).astype(f32)
        d_numer = (d_mixed * inv[:, cols]).astype(bf16)
        dn[:, cols] = d_numer
        xs[:, cols] = (d_numer.astype(f32) * mixf[:, cols]).astype(bf16)

    ff_part(1)


    @pl.loop(0, pairs)
    def _(p):
        lanes = tile_at(p, LANES)
        q = rq[:, lanes].astype(f32)
        qc, qs = (q * cosb[...]).astype(bf16), (q * sinb[...]).astype(bf16)
        d_numer = dn[:, lanes]
        dsend[p, 0] = squeeze_pair(mm_tn(qc, d_numer) * diag).astype(bf16)
        dsend[p, 1] = squeeze_pair(mm_tn(qs, d_numer) * diag).astype(bf16)
        across = mm(xs[:, lanes], diag_low)
        dzs[p] = -two_rows(
            jnp.sum(qc.astype(f32) * across, axis=0, keepdims=True),
            jnp.sum(qs.astype(f32) * across, axis=0, keepdims=True),
        )

    turn_copy = peer_copy(dsend, drecv, sems, 6, peer)
    turn_keys = peer_copy(dzs, dzr, sems, 7, peer)
    turn_copy.start()
    turn_keys.start()
    ff_part(2)

    @pl.loop(0, tiles)
    def _(j):
        cols = tile_at(j, TILE)
        ga[tile_at(3 * tiles + j, TILE), :] = mm_tn(mixb[:, cols], dlow[...]).astype(bf16)

    def core_a(m):
        there = pl.ds(pl.multiple_of(m * width + (1 - core) * 2 * band, 2 * band), 2 * band)
        here = pl.ds(m * 2 * band, 2 * band)
        return peer_copy(ga.at[there, :], cr_a.at[here, :], sems, (9, 11, 20, 21)[m], sibling)

    def fill_px(m):
        core_a(m).wait()
        there = pl.ds(pl.multiple_of(m * width + theirs * band, band), band)
        here = pl.ds(pl.multiple_of(m * 2 * band + (1 - rank) * band, band), band)
        px[m * band : (m + 1) * band, :] = (
            ga[there, :].astype(f32) + cr_a[here, :].astype(f32)
        ).astype(bf16)

    core_a(3).start()
    ff_part(3)

    def inside(p):
        lanes = tile_at(p, LANES)
        q, k, v = rq[:, lanes], rk[:, lanes], vv[:, lanes]
        d_numer = dn[:, lanes]
        turned = (-pltpu.roll(xs[:, lanes].astype(f32), HD, 1)).astype(bf16)
        sum_q = sum_k = sum_v = 0.0
        for mask, rest in ((first_low, second_low), (second_low, first_low)):
            q_head, k_head, d_head = q * mask, k * mask, d_numer * mask
            table = ctab[...]
            prob = (mm_nt(q_head, k) * table).astype(bf16)
            d_prob = mm_nt(d_head + turned * rest, v * mask + rest)
            d_score = (d_prob * table).astype(bf16)
            sum_v += mm_tn(prob, d_head)
            sum_q += mm(d_score, k_head)
            sum_k += mm_tn(d_score, q_head)
        dq[:, lanes] = sum_q
        dk[:, lanes] = sum_k
        dv[:, lanes] = sum_v

    @pl.loop(0, pairs)
    def _(p):
        inside(p)
        ff_part(4 + p)

    turn_copy.wait()
    turn_keys.wait()

    @pl.loop(0, pairs)
    def _(p):
        lanes = tile_at(p, LANES)
        q, v = rq[:, lanes].astype(f32), vv[:, lanes]
        k = rk[:, lanes].astype(f32)
        d_numer, x = dn[:, lanes], xs[:, lanes]
        sum_q, sum_k, sum_v = dq[:, lanes], dk[:, lanes], dv[:, lanes]
        zblock, dzblock = zst[p], dzr[p] * early
        along = mm(x, diag_low)
        for part, wave in ((0, cosb[...]), (1, sinb[...])):
            state = spread_pair(st[p, part], diag).astype(bf16)
            sum_q += wave * (mm_nt(d_numer, state) - along * zblock[part : part + 1, :])
            d_state = (spread_pair(drecv[p, part], diag) * early).astype(bf16)
            sum_k += wave * (mm_nt(v, d_state) + dzblock[part : part + 1, :]) * (1.0 / HD)
            sum_v += mm((k * wave * (1.0 / HD)).astype(bf16), d_state)
        sum_q = jnp.where(q > 0, sum_q, 0.0)
        sum_k = jnp.where(k > 0, sum_k, 0.0)
        dql[:, lanes] = sum_q.astype(bf16)
        dkl[:, lanes] = sum_k.astype(bf16)
        dvl[:, lanes] = sum_v.astype(bf16)
        for slot, value in ((6, sum_q), (7, sum_k), (8, sum_v)):
            smalls[0, slot : slot + 1, lanes] = jnp.sum(value, axis=0, keepdims=True)

    small_copy(0).start()
    ff_part(10)

    def make_grad(which, source):
        @pl.loop(0, tiles)
        def _(j):
            ga[tile_at(which * tiles + j, TILE), :] = mm_tn(
                tok[:, tile_at(j, TILE)], source[...]
            ).astype(bf16)

        core_a(which).start()

    make_grad(2, dvl)
    ff_part(11)
    make_grad(0, dql)
    ff_part(12)
    make_grad(1, dkl)
    ff_part(13)
    for m in (3, 2, 0, 1):
        fill_px(m)
    start_folds(0)
    ff_part(14)

    @pl.loop(0, tiles)
    def _(j):
        cols = tile_at(j, TILE)
        dres[:, cols] += (
            mm_nt(dql[...], wa[cols, :])
            + mm_nt(dkl[...], wa[tile_at(tiles + j, TILE), :])
            + mm_nt(dvl[...], wa[tile_at(2 * tiles + j, TILE), :])
        )

    token_out = pltpu.make_async_copy(dres, dtok_h, o_sem.at[1])
    token_out.start()
    start_folds(1)
    ring_spread(ff_streams, 5)
    ring_first(a_streams)
    swap_small(0)

    def spread_gather(s):
        for cut in range(FF_CUTS):
            ring_spread(a_streams[cut::A_CUTS], s)
            ring_gather(ff_streams[cut::FF_CUTS], s - 1)

    start_folds(2)
    ring_spread(a_streams, 0)
    ring_spread(ff_streams, 6, True)
    swap_small(1)

    def spread_fold(s):
        start_folds(s + 2)
        spread_gather(s)

    pl.loop(1, 3)(spread_fold)
    swap_small(2)
    pl.loop(3, 6)(spread_fold)
    swap_small(3)
    ring_spread(a_streams, 6, True)
    ring_gather(ff_streams, 5)
    ring_gather(a_streams, 0)
    ring_gather(ff_streams, 6, True)
    own_ff = part_rows(core, units)
    back_ff = peer_copy(ff_o.at[own_ff, :], ff_o.at[own_ff, :], sems, 10, sibling)
    back_ff.start()
    near_ff = out_copy(ff_o, ff_h, own_ff, 2)
    near_ff.start()
    cross_over(0, first=True)
    side_done(0, 0)
    swap_small(4)
    small_out = pltpu.make_async_copy(smalls.at[len(swaps)], small_h, o_sem.at[6])
    small_out.start()

    def gather_one(s):
        ring_gather(a_streams, s)
        cross_over(s)
        side_done(0, s)
        side_done(1, s - 1)

    gather_one(1)
    back_ff.wait()
    far_ff = out_copy(ff_o, ff_h, part_rows(1 - core, units), 3)
    far_ff.start()
    pl.loop(2, 6)(gather_one)
    ring_gather(a_streams, 6, True)
    cross_over(6)
    side_done(0, 6)
    side_done(1, 5)
    cross_over(7, last=True)
    side_done(0, 7)
    side_done(1, 6)

    def drain(kind, source, total, sem):
        where = source.at[pl.ds(0, total), :]
        remote(where, where, sem, x_recv.at[0, 0], peer).wait_send()

    for kind, size in ((0, ff_size), (1, a_size)):
        drain(kind, sums[kind], 2 * (count - 1) * size, r_send.at[kind])
        drain(kind, outs[kind], 2 * (count - 1) * size, g_send.at[kind])
    drain(1, px, 2 * count * a_size, x_send.at[2])

    drain(1, a_o, 2 * count * a_size - 2 * (count - 1) * RING_ROWS, x_send.at[0])
    drain(1, a_o, 2 * (count - 1) * RING_ROWS, x_send.at[3])
    side_done(1, 7)
    drain(1, a_o, 4 * count * a_size, x_send.at[1])
    whole_a = pltpu.make_async_copy(a_o, a_h, o_sem.at[4])
    for copy in (result_out, token_out, near_ff, far_ff, small_out, whole_a):
        copy.wait()


def finish_kernel(halves, *refs):
    g_out, up, down, small, res, dtok = refs[:4], refs[4 : 4 + halves], *refs[4 + halves : 8 + halves]
    out = refs[8 + halves :]
    late = lax.axis_index("tensor") > 0
    for source, where in zip(g_out, (2, 4, 6, 8)):
        out[where][...] = source[...].astype(f32)
    width = res.shape[1]
    for piece in range(halves):
        out[12][:, piece * width : (piece + 1) * width] = up[piece][...].astype(f32)
    out[14][...] = down[...].astype(f32)

    @pl.when(pl.program_id(0) == 0)
    def _():
        out[0][...] = res[...]
        out[1][...] = dtok[...]
        for where, row in ((3, 6), (5, 7), (7, 8), (9, 2), (10, 0), (11, 1), (15, 5), (16, 3), (17, 4)):
            out[where][...] = small[row : row + 1, :].reshape(width)
        for piece in range(halves):
            line = jnp.where(
                late,
                small[9 + halves + piece : 10 + halves + piece, :],
                small[9 + piece : 10 + piece, :],
            )
            out[13][pl.ds(piece * width, width)] = line.reshape(width)


def finish(rows, width, units, res, dtok, ff, a, small):
    halves, steps = units // width, width // FINISH
    low = (FINISH, width)
    down_rows = units // steps

    def whole(shape):
        return pl.BlockSpec(shape, lambda i: (0,) * len(shape))

    def at_block(shape, start):
        return pl.BlockSpec(shape, lambda i: (start + i, 0))

    in_specs = [at_block(low, which * steps) for which in range(4)]
    in_specs += [at_block(low, units // FINISH + piece * steps) for piece in range(halves)]
    in_specs += [at_block((down_rows, width), 0), whole(small.shape), whole(res.shape), whole(dtok.shape)]
    matrix, line = (width, width), (width,)
    shapes = [
        (res.shape, bf16), (dtok.shape, f32), (matrix, f32), (line, f32), (matrix, f32), (line, f32),
        (matrix, f32), (line, f32), (matrix, f32), (line, f32), (line, f32), (line, f32),
        ((width, units), f32), ((units,), f32), ((units, width), f32), (line, f32), (line, f32), (line, f32),
    ]
    special = {
        2: at_block(low, 0), 4: at_block(low, 0), 6: at_block(low, 0), 8: at_block(low, 0),
        12: at_block((FINISH, units), 0), 14: at_block((down_rows, width), 0),
    }
    return pl.pallas_call(
        functools.partial(finish_kernel, halves),
        grid=(steps,),
        out_shape=shaped(*shapes),
        in_specs=in_specs,
        out_specs=tuple(special.get(i, whole(shape)) for i, (shape, _) in enumerate(shapes)),
        compiler_params=pltpu.CompilerParams(vmem_limit_bytes=62 << 20),
        name="finish",
    )(*([a] * 4), *([ff] * (halves + 1)), small, res, dtok)


def shaped(*items):
    return tuple(jax.ShapeDtypeStruct(shape, kind) for shape, kind in items)


def pair_device(
    tokens,
    positions,
    span_sizes,
    w_query,
    b_query,
    w_key,
    b_key,
    w_value,
    b_value,
    w_out,
    b_out,
    norm1_gain,
    norm1_bias,
    w_up,
    b_up,
    w_down,
    b_down,
    norm2_gain,
    norm2_bias,
    out_grad,
):
    rows, width = tokens.shape
    units = w_up.shape[1]
    pairs = width // LANES
    halves = units // width
    count = lax.axis_size("dp") // 2
    swaps = 2 + count.bit_length() - 1
    streams = 2 * (FF_CUTS + A_CUTS)
    ff_part, a_part = units // count // 2, width // count // 2
    lines = 9 + 2 * halves
    lines += -lines % 8

    def low(*shape):
        return pltpu.VMEM(shape, bf16)

    def wide(*shape):
        return pltpu.VMEM(shape, f32)

    def sem(*shape):
        return pltpu.SemaphoreType.DMA(shape)

    state, zrows = (pairs, 2, HD, LANES), (pairs, 8, LANES)
    own, pair = (rows, width), (2 * rows, width)
    scratch = dict(
        tok=low(*own), places=pltpu.VMEM(positions.shape, jnp.int32), span=pltpu.SMEM((1, 1), jnp.int32),
        og=low(*own), **{name: low(width) for name in LINES}, bup_line=low(units),
        wa=low(4 * width, width), wff=low(2 * units, width), vec=wide(9 + halves + -(9 + halves) % 8, width),
        hbuf=low(*pair), act=low(2 * rows, units), slope=wide(2 * rows, units), dbuf=low(*pair),
        dpre=low(2 * rows, units), hid=wide(*own), numer=wide(*own), denom=wide(*own),
        tsend=low(*state), trecv=low(*state), zsend=wide(*zrows), zrecv=wide(*zrows),
        bsend=low(*own), brecv=low(*own), res=low(*own), gff=low(2 * units, width),
        dhs=low(*own), dhr=low(*own), dho=wide(*own), mixb=low(*own), mixf=wide(*own), inv=wide(*own),
        rq=low(*own), rk=low(*own), vv=low(*own), nrm=wide(*own), scl=wide(rows, LANES),
        st=low(*state), zst=wide(*zrows), dres=wide(*own), dlow=low(*own), dn=low(*own), xs=low(*own),
        dsend=low(*state), drecv=low(*state), dzs=wide(*zrows), dzr=wide(*zrows),
        dql=low(*own), dkl=low(*own), dvl=low(*own),
        ctab=wide(rows, rows), cosb=wide(rows, LANES), sinb=wide(rows, LANES),
        acc=wide(24, width), bup=wide(8, units),
        cr_ff=low(units, width), cr_a=low(2 * width, width), px=low(width, width),
        xr=low(count, 2, a_part, width), rs_ff=low(count - 1, 2, ff_part, width),
        rs_a=low(count - 1, 2, a_part, width), ff_o=low(2 * units, width), a_o=low(4 * width, width),
        smalls=wide(swaps + 1, lines, width), small_r=wide(swaps, lines, width),
        send=sem(26), recv=sem(26), r_send=sem(2), r_recv=sem(streams, count - 1),
        g_send=sem(2), g_recv=sem(streams, count - 1), x_send=sem(4), x_recv=sem(2, count),
        t_recv=sem(2, count - 1),
        s_recv=sem(4, count), y_recv=sem(2, count),
        m_send=sem(swaps), m_recv=sem(swaps), w_sem=sem(5 + halves), o_sem=sem(7), l_sem=sem(14),
    )
    anywhere = pl.BlockSpec(memory_space=pl.ANY)
    outs = shaped(
        (own, bf16), (own, f32), ((2 * units, width), bf16), ((4 * width, width), bf16),
        ((lines, width), f32),
    )
    res, dtok, ff, a, small = pl.pallas_call(
        functools.partial(block_kernel, count),
        out_shape=outs,
        in_specs=[anywhere] * 20,
        out_specs=tuple([anywhere] * len(outs)),
        scratch_shapes=list(scratch.values()),
        compiler_params=pltpu.CompilerParams(
            collective_id=0, has_side_effects=True, vmem_limit_bytes=62 << 20
        ),
        name="block",
    )(
        tokens, positions, span_sizes.reshape(1, 1), b_query, b_key, b_value, b_out, norm1_gain,
        norm1_bias, b_down, norm2_gain, norm2_bias, b_up, out_grad,
        w_query, w_key, w_value, w_out, w_up, w_down,
    )
    return finish(rows, width, units, res, dtok, ff, a, small)


def pick(mesh):
    def per_device(*args):
        tokens, span_sizes, w_up = args[0], args[2], args[13]
        rows, width = tokens.shape
        units = w_up.shape[1]
        fits = (
            mesh.shape["tensor"] == 2
            and mesh.shape["dp"] == 16
            and span_sizes.shape[0] == 1
            and rows % TILE == 0
            and width == HEADS * HD
            and width % TILE == 0
            and units == 2 * width
        )
        return pair_device(*args) if fits else general_device(*args)

    return per_device


def solution(mesh):
    return jax.shard_map(
        pick(mesh),
        mesh=mesh,
        in_specs=(
            P(("dp", "tensor"), None),
            P("dp"),
            P("dp"),
            P(),
            P(),
            P(),
            P(),
            P(),
            P(),
            P(),
            P(),
            P(),
            P(),
            P(None, "tensor"),
            P("tensor"),
            P("tensor", None),
            P(),
            P(),
            P(),
            P(("dp", "tensor"), None),
        ),
        out_specs=(
            P(("dp", "tensor"), None),
            P(("dp", "tensor"), None),
            P(),
            P(),
            P(),
            P(),
            P(),
            P(),
            P(),
            P(),
            P(),
            P(),
            P(None, "tensor"),
            P("tensor"),
            P("tensor", None),
            P(),
            P(),
            P(),
        ),
        check_vma=False,
    )
```

```python
import functools
import math

import jax
import jax.numpy as jnp
from jax import lax
from jax.experimental import pallas as pl
from jax.experimental.pallas import tpu as pltpu
from jax.sharding import PartitionSpec as P

HEADS = 12
HD = 64
SUBLEN = 32


highest = lax.Precision.HIGHEST
norm_eps = 1e-05


def norm_forward(value, gain, shift):
    mean = jnp.mean(value, axis=-1, keepdims=True)
    centred = value - mean
    scale = lax.rsqrt(jnp.mean(centred * centred, axis=-1, keepdims=True) + norm_eps)
    normal = centred * scale
    return (normal * gain + shift, normal, scale)


def norm_backward(grad, normal, scale, gain):
    along = grad * gain
    inner = (
        along
        - jnp.mean(along, axis=-1, keepdims=True)
        - normal * jnp.mean(along * normal, axis=-1, keepdims=True)
    )
    return (inner * scale, jnp.sum(grad * normal, axis=0), jnp.sum(grad, axis=0))


def gelu_slope(pre):
    normal_cdf = 0.5 * (1.0 + jax.scipy.special.erf(pre * (1.0 / math.sqrt(2.0))))
    return normal_cdf + pre * jnp.exp(-0.5 * pre * pre) * (1.0 / math.sqrt(2.0 * math.pi))


def reach_table(count, span):
    slot_index = jnp.arange(count, dtype=jnp.int32)
    final = (slot_index * SUBLEN // span + 1) * span // SUBLEN - 1
    return (slot_index[None, :] <= final[:, None]).astype(jnp.float32)


def features(rows, w_joint, b_joint, cosine, sine):
    length = rows.shape[0]
    width = rows.shape[1]
    proj = jnp.dot(rows, w_joint, preferred_element_type=jnp.float32) + b_joint
    relu_query = jax.nn.relu(proj[:, :width]).reshape(length, HEADS, HD)
    relu_key = jax.nn.relu(proj[:, width : 2 * width]).reshape(length, HEADS, HD) * (1.0 / HD)
    q_feat = jnp.concatenate([relu_query * cosine, relu_query * sine], axis=-1).astype(jnp.bfloat16)
    k_feat = jnp.concatenate([relu_key * cosine, relu_key * sine], axis=-1).astype(jnp.bfloat16)
    v_low = proj[:, 2 * width :].astype(jnp.bfloat16)
    return (q_feat, k_feat, v_low)


def local_blocks(k_feat, v_low):
    count = k_feat.shape[0] // SUBLEN
    k_sub = k_feat.reshape(count, SUBLEN, HEADS, 2 * HD)
    v_sub = v_low.reshape(count, SUBLEN, HEADS, HD)
    blocks = jnp.einsum("tjhf,tjhd->thfd", k_sub, v_sub, preferred_element_type=jnp.float32)
    k_total = jnp.sum(k_sub.astype(jnp.float32), axis=1)
    return (blocks, k_total)


def attend_core(q_feat, k_feat, v_low, blocks, k_total, reach, extra_blocks, extra_keys):
    count = q_feat.shape[0] // SUBLEN
    q_sub = q_feat.reshape(count, SUBLEN, HEADS, 2 * HD)
    k_sub = k_feat.reshape(count, SUBLEN, HEADS, 2 * HD)
    v_sub = v_low.reshape(count, SUBLEN, HEADS, HD)
    state_low = (
        jnp.einsum("st,thfd->shfd", reach, blocks, precision=highest) + extra_blocks
    ).astype(jnp.bfloat16)
    z_sum = jnp.einsum("st,thf->shf", reach, k_total, precision=highest) + extra_keys
    numer = jnp.einsum("sihf,shfd->sihd", q_sub, state_low, preferred_element_type=jnp.float32)
    denom = jnp.einsum("sihf,shf->sih", q_sub.astype(jnp.float32), z_sum, precision=highest) + 1.0
    return (q_sub, k_sub, v_sub, state_low, z_sum, numer, denom)


def back_first(parts, grad_mixed):
    q_sub, k_sub, v_sub, state_low, z_sum, numer, denom = parts
    count = q_sub.shape[0]
    grad_out = grad_mixed.reshape(count, SUBLEN, HEADS, HD).astype(jnp.float32)
    d_numer = grad_out / denom[..., None]
    d_denom = -jnp.sum(grad_out * numer, axis=-1) / (denom * denom)
    q_wide = q_sub.astype(jnp.float32)
    d_query = jnp.einsum(
        "sihd,shfd->sihf", d_numer, state_low.astype(jnp.float32), precision=highest
    )
    d_query = d_query + d_denom[..., None] * z_sum[:, None]
    d_state = jnp.einsum("sihf,sihd->shfd", q_wide, d_numer, precision=highest)
    d_zsum = jnp.einsum("sihf,sih->shf", q_wide, d_denom, precision=highest)
    return (d_query, d_state, d_zsum)


def back_second(parts, reach, d_state, d_zsum, later_blocks, later_keys):
    q_sub, k_sub, v_sub = (parts[0], parts[1], parts[2])
    d_blocks = jnp.einsum("st,shfd->thfd", reach, d_state, precision=highest) + later_blocks
    d_ktotal = jnp.einsum("st,shf->thf", reach, d_zsum, precision=highest) + later_keys
    d_key = (
        jnp.einsum("thfd,tjhd->tjhf", d_blocks, v_sub.astype(jnp.float32), precision=highest)
        + d_ktotal[:, None]
    )
    d_value = jnp.einsum("thfd,tjhf->tjhd", d_blocks, k_sub.astype(jnp.float32), precision=highest)
    return (d_key, d_value)


def feature_grads(q_feat, k_feat, d_qf, d_kf, d_val, cos_part, sin_part):
    size = q_feat.shape[0]
    d_qf = d_qf.reshape(size, HEADS, 2 * HD)
    d_kf = d_kf.reshape(size, HEADS, 2 * HD)
    d_query = jnp.where(
        q_feat[..., :HD] > 0, d_qf[..., :HD] * cos_part + d_qf[..., HD:] * sin_part, 0.0
    )
    d_key = jnp.where(
        k_feat[..., :HD] > 0,
        (d_kf[..., :HD] * cos_part + d_kf[..., HD:] * sin_part) * (1.0 / HD),
        0.0,
    )
    return jnp.concatenate(
        [
            d_query.reshape(size, HEADS * HD),
            d_key.reshape(size, HEADS * HD),
            d_val.reshape(size, HEADS * HD),
        ],
        axis=1,
    )


def general_device(
    tokens,
    positions,
    span_sizes,
    w_query,
    b_query,
    w_key,
    b_key,
    w_value,
    b_value,
    w_out,
    b_out,
    norm1_gain,
    norm1_bias,
    w_up,
    b_up,
    w_down,
    b_down,
    norm2_gain,
    norm2_bias,
    out_grad,
):
    rank = lax.axis_index("tensor")
    tensor_count = lax.axis_size("tensor")
    own = tokens.shape[0]
    width = tokens.shape[1]
    seqs = span_sizes.shape[0]
    group = own * tensor_count
    length = group // seqs
    start = rank * own
    w_joint = jnp.concatenate([w_query, w_key, w_value], axis=1)
    b_joint = jnp.concatenate([b_query, b_key, b_value]).astype(jnp.float32)
    gain_one = norm1_gain.astype(jnp.float32)
    gain_two = norm2_gain.astype(jnp.float32)
    gathered = lax.all_gather(tokens, "tensor", axis=0, tiled=True)
    angle = math.pi / 2 * positions.astype(jnp.float32) / (3 * length)
    cosine = jnp.cos(angle).reshape(seqs, length, 1, 1)
    sine = jnp.sin(angle).reshape(seqs, length, 1, 1)

    def seq_forward(items):
        rows, cos_part, sin_part, span = items
        q_feat, k_feat, v_low = features(rows, w_joint, b_joint, cos_part, sin_part)
        blocks_seq, ktot_seq = local_blocks(k_feat, v_low)
        parts = attend_core(
            q_feat,
            k_feat,
            v_low,
            blocks_seq,
            ktot_seq,
            reach_table(q_feat.shape[0] // SUBLEN, span),
            0.0,
            0.0,
        )
        mixed_seq = (
            (parts[5] / parts[6][..., None]).reshape(rows.shape[0], width).astype(jnp.bfloat16)
        )
        return (mixed_seq, q_feat, k_feat, v_low)

    mixed, q_all, k_all, v_all = lax.map(
        seq_forward, (gathered.reshape(seqs, length, width), cosine, sine, span_sizes)
    )
    mixed = mixed.reshape(group, width)
    mixed_own = lax.dynamic_slice_in_dim(mixed, start, own, 0)
    resid = (
        tokens.astype(jnp.float32)
        + jnp.dot(mixed_own, w_out, preferred_element_type=jnp.float32)
        + b_out.astype(jnp.float32)
    )
    hidden, normal_one, scale_one = norm_forward(resid, gain_one, norm1_bias.astype(jnp.float32))
    hidden_low = hidden.astype(jnp.bfloat16)
    rows_in = lax.all_gather(hidden_low, "tensor", axis=0, tiled=True)
    pre = jnp.dot(rows_in, w_up, preferred_element_type=jnp.float32) + b_up.astype(jnp.float32)
    act_low = jax.nn.gelu(pre, approximate=False).astype(jnp.bfloat16)
    branch = lax.psum_scatter(
        jnp.dot(act_low, w_down, preferred_element_type=jnp.float32),
        "tensor",
        scatter_dimension=0,
        tiled=True,
    )
    summed = hidden + branch + b_down.astype(jnp.float32)
    result, normal_two, scale_two = norm_forward(summed, gain_two, norm2_bias.astype(jnp.float32))
    d_sum, d_gain_two, d_bias_two = norm_backward(
        out_grad.astype(jnp.float32), normal_two, scale_two, gain_two
    )
    d_bdown = jnp.sum(d_sum, axis=0)
    d_sum_low = d_sum.astype(jnp.bfloat16)
    rows_grad = lax.all_gather(d_sum_low, "tensor", axis=0, tiled=True)
    g_down = jnp.dot(act_low.T, rows_grad, preferred_element_type=jnp.float32)
    d_pre = jnp.dot(rows_grad, w_down.T, preferred_element_type=jnp.float32) * gelu_slope(pre)
    g_upbias = jnp.sum(d_pre, axis=0)
    d_pre_low = d_pre.astype(jnp.bfloat16)
    g_up = jnp.dot(rows_in.T, d_pre_low, preferred_element_type=jnp.float32)
    d_hidden = lax.psum_scatter(
        jnp.dot(d_pre_low, w_up.T, preferred_element_type=jnp.float32),
        "tensor",
        scatter_dimension=0,
        tiled=True,
    )
    g_up, g_upbias, g_down = (
        lax.psum(g_up.astype(jnp.bfloat16), "dp").astype(jnp.float32),
        lax.psum(g_upbias.astype(jnp.bfloat16), "dp").astype(jnp.float32),
        lax.psum(g_down.astype(jnp.bfloat16), "dp").astype(jnp.float32),
    )
    d_hidden = d_hidden + d_sum
    d_resid, d_gain_one, d_bias_one = norm_backward(d_hidden, normal_one, scale_one, gain_one)
    d_bout = jnp.sum(d_resid, axis=0)
    d_gain_one, d_bias_one, d_gain_two, d_bias_two, d_bout, d_bdown = lax.psum(
        (d_gain_one, d_bias_one, d_gain_two, d_bias_two, d_bout, d_bdown), ("dp", "tensor")
    )
    d_resid_low = d_resid.astype(jnp.bfloat16)
    rows_back = lax.all_gather(d_resid_low, "tensor", axis=0, tiled=True)
    g_out = jnp.dot(mixed.T, rows_back, preferred_element_type=jnp.float32)
    d_mixed = jnp.dot(rows_back, w_out.T, preferred_element_type=jnp.float32).astype(jnp.bfloat16)

    def seq_backward(items):
        q_feat, k_feat, v_low, cos_part, sin_part, span, grad_mixed = items
        blocks_seq, ktot_seq = local_blocks(k_feat, v_low)
        reach = reach_table(q_feat.shape[0] // SUBLEN, span)
        parts = attend_core(q_feat, k_feat, v_low, blocks_seq, ktot_seq, reach, 0.0, 0.0)
        d_qf, d_state, d_zsum = back_first(parts, grad_mixed)
        d_kf, d_val = back_second(parts, reach, d_state, d_zsum, 0.0, 0.0)
        joint = feature_grads(q_feat, k_feat, d_qf, d_kf, d_val, cos_part, sin_part)
        return (joint.astype(jnp.bfloat16), jnp.sum(joint, axis=0))

    d_joint, d_jbias = lax.map(
        seq_backward,
        (q_all, k_all, v_all, cosine, sine, span_sizes, d_mixed.reshape(seqs, length, width)),
    )
    d_joint = d_joint.reshape(group, 3 * width)
    d_jbias = jnp.sum(d_jbias, axis=0)
    g_joint = jnp.dot(gathered.T, d_joint, preferred_element_type=jnp.float32)
    d_joint_own = lax.dynamic_slice_in_dim(d_joint, start, own, 0)
    d_tokens = d_resid + jnp.dot(d_joint_own, w_joint.T, preferred_element_type=jnp.float32)
    g_joint, g_out, d_jbias = lax.psum((g_joint, g_out, d_jbias), "dp")
    return (
        result.astype(jnp.bfloat16),
        d_tokens,
        g_joint[:, :width],
        d_jbias[:width],
        g_joint[:, width : 2 * width],
        d_jbias[width : 2 * width],
        g_joint[:, 2 * width :],
        d_jbias[2 * width :],
        g_out,
        d_bout,
        d_gain_one,
        d_bias_one,
        g_up,
        g_upbias,
        g_down,
        d_bdown,
        d_gain_two,
        d_bias_two,
    )


f32 = jnp.float32
bf16 = jnp.bfloat16
MESH = pl.DeviceIdType.MESH
LANES = 2 * HD
TILE = 256
ROWBLOCK = 64
FINISH = 256
FF_CUTS = 3
A_CUTS = 3
RING_ROWS = 16
LINES = tuple("l" + str(index) for index in range(9))


def tile_at(index, size):
    return pl.ds(pl.multiple_of(index * size, size), size)


def contract(left, right, left_dim, right_dim, precision=None):
    return lax.dot_general(
        left,
        right,
        (((left_dim,), (right_dim,)), ((), ())),
        precision=precision,
        preferred_element_type=f32,
    )


def mm(left, right):
    return contract(left, right, 1, 0)


def mm_nt(left, right):
    return contract(left, right, 1, 1)


def mm_tn(left, right):
    return contract(left, right, 0, 0)


def head_masks():
    lane = lax.broadcasted_iota(jnp.int32, (1, LANES), 1)
    first = (lane < HD).astype(f32)
    return first, 1.0 - first


def pair_mask():
    row = lax.broadcasted_iota(jnp.int32, (LANES, LANES), 0)
    col = lax.broadcasted_iota(jnp.int32, (LANES, LANES), 1)
    return ((row < HD) == (col < HD)).astype(f32)


def column_of(block, which):
    row = lax.broadcasted_iota(jnp.int32, block.shape, 0)
    return contract(jnp.where(row == which, block, 0.0), jnp.ones((8, LANES), f32), 0, 0, highest)


def squeeze_pair(square):
    return square[:HD] + square[HD:]


def spread_pair(part, mask):
    return jnp.concatenate([part, part], axis=0).astype(f32) * mask


def two_rows(top, below):
    row = lax.broadcasted_iota(jnp.int32, (8, LANES), 0)
    return jnp.where(row == 0, top, jnp.where(row == 1, below, 0.0))


def fold8(value):
    total = value[0:8]
    for start in range(8, value.shape[0], 8):
        total = total + value[start : start + 8]
    return total


def angle_lines(places, length):
    rows = places.shape[0]
    angle = math.pi / 2 * places.astype(f32).reshape(1, rows) / (3 * length)
    line = lax.broadcasted_iota(jnp.int32, (8, rows), 0)
    return jnp.where(line == 0, jnp.cos(angle), jnp.where(line == 1, jnp.sin(angle), 0.0))


def angle_products(block, span, ctab):
    rows = ctab.shape[0]
    both = contract(block, block, 0, 0, highest)
    row = lax.broadcasted_iota(jnp.int32, (rows, rows), 0)
    col = lax.broadcasted_iota(jnp.int32, (rows, rows), 1)
    seen = col <= (row | (span[0, 0] - 1))
    ctab[...] = jnp.where(seen, both * (1.0 / HD), 0.0)


def peer_copy(src, dst, sems, slot, device):
    return pltpu.make_async_remote_copy(
        src_ref=src,
        dst_ref=dst,
        send_sem=sems[0].at[slot],
        recv_sem=sems[1].at[slot],
        device_id=device,
        device_id_type=MESH,
    )


def ring_device(spot, depth, core):
    far = spot // depth
    z = far * (2 * depth - 1 - spot) + (1 - far) * spot
    return ((z * 2 + far) * 2 + core, lax.axis_index("tensor"))


def layer_norm(value):
    centred = value - jnp.mean(value, axis=-1, keepdims=True)
    scale = lax.rsqrt(jnp.mean(centred * centred, axis=-1, keepdims=True) + norm_eps)
    return centred * scale, scale


def layer_norm_back(grad, gain, normal, scale):
    along = grad * gain
    return (
        along
        - jnp.mean(along, axis=-1, keepdims=True)
        - normal * jnp.mean(along * normal, axis=-1, keepdims=True)
    ) * scale


def block_kernel(
    count, tok_h, places_h, span_h, bq, bk, bv, bo, g1, b1, bd, g2, b2, bup_in, og_h,
    wq, wk, wv, wo, wup, wdn,
    res_h, dtok_h, ff_h, a_h, small_h,
    tok, places, span, og, l0, l1, l2, l3, l4, l5, l6, l7, l8, bup_line, wa, wff, vec, hbuf, act, slope, dbuf, dpre, hid, numer, denom, tsend, trecv, zsend, zrecv,
    bsend, brecv, res, gff, dhs, dhr, dho, mixb, mixf, inv, rq, rk, vv, nrm, scl, st, zst,
    dres, dlow, dn, xs, dsend, drecv, dzs, dzr, dql, dkl, dvl, ctab, cosb, sinb, acc, bup,
    cr_ff, cr_a, px, xr, rs_ff, rs_a, ff_o, a_o, smalls, small_r,
    send, recv, r_send, r_recv, g_send, g_recv, x_send, x_recv, t_recv, s_recv, y_recv, m_send, m_recv,
    w_sem, o_sem, l_sem,
):
    sems = (send, recv)
    rows, width = tok.shape
    units = wup.shape[1]
    halves = units // width
    pairs = width // LANES
    tiles = width // TILE
    depth = count // 2
    quarter = width
    dq, dk, dv, ga = numer, denom, hid, wff
    dp, rank = lax.axis_index("dp"), lax.axis_index("tensor")
    late = rank.astype(f32)
    early = 1.0 - late
    core, y, z = dp % 2, (dp // 2) % 2, dp // 4
    spot = y * (2 * depth - 1 - z) + (1 - y) * z
    sibling = (dp + 1 - 2 * core, rank)
    peer = (dp, 1 - rank)
    ahead = ring_device((spot + 1) % count, depth, core)
    behind = ring_device((spot + count - 1) % count, depth, core)
    swaps = [sibling, peer, (dp + 2 - 4 * y, rank)]
    step = 1
    while step < depth:
        bit = (z // step) % 2
        swaps.append((dp + 4 * (step - 2 * step * bit), rank))
        step *= 2
    partners = [ahead, behind] + swaps
    barrier = pltpu.get_barrier_semaphore()
    for device in partners:
        pl.semaphore_signal(barrier, inc=1, device_id=device, device_id_type=MESH)

    loads = [
        (wk, wa.at[pl.ds(width, width), :]),
        (wv, wa.at[pl.ds(2 * width, width), :]),
        (wq, wa.at[pl.ds(0, width), :]),
        (wo, wa.at[pl.ds(3 * width, width), :]),
    ]
    for part in range(halves):
        loads.append(
            (wup.at[:, pl.ds(part * width, width)], wff.at[pl.ds(units + part * width, width), :])
        )
    loads.append((wdn, wff.at[pl.ds(0, units), :]))

    def load(index):
        return pltpu.make_async_copy(loads[index][0], loads[index][1], w_sem.at[index])

    small_loads = [(tok_h, tok), (places_h, places), (span_h, span)]
    vectors = (bq, bk, bv, bo, g1, b1, bd, g2, b2)
    lines = (l0, l1, l2, l3, l4, l5, l6, l7, l8)
    small_loads += [pair for pair in zip(vectors, lines)]
    small_loads += [(bup_in, bup_line), (og_h, og)]

    def fetch(index):
        return pltpu.make_async_copy(*small_loads[index], l_sem.at[index])

    fetch(0).start()
    for index in range(3):
        load(index).start()
    for index in range(1, len(small_loads)):
        fetch(index).start()
    for index in range(1, len(small_loads) - 1):
        fetch(index).wait()

    def out_copy(source, target, at, slot):
        return pltpu.make_async_copy(source.at[at, :], target.at[at, :], o_sem.at[slot])

    for index in range(len(vectors)):
        vec[index : index + 1, :] = lines[index][...].astype(f32).reshape(1, width)
    for part in range(halves):
        piece = bup_line[pl.ds(part * width, width)]
        vec[9 + part : 10 + part, :] = piece.astype(f32).reshape(1, width)
    own, far_rows = pl.ds(0, rows), pl.ds(rows, rows)
    my_places = places[pl.ds(pl.multiple_of(rank * rows, rows), rows)]
    angles = angle_lines(my_places, places.shape[0])
    cosb[...] = column_of(angles, 0)
    sinb[...] = column_of(angles, 1)
    diag = pair_mask()
    first, second = head_masks()
    first_low, second_low = first.astype(bf16), second.astype(bf16)
    diag_low = diag.astype(bf16)
    acc[...] = jnp.zeros_like(acc)
    bup[...] = jnp.zeros_like(bup)
    smalls[0] = jnp.zeros(smalls.shape[1:], f32)

    def add_small(slot, line):
        smalls[0, slot : slot + 1, :] = line

    def project(which, target, j):
        cols = tile_at(j, TILE)
        value = mm(tok[...], wa[pl.ds(which * width, width), cols]) + vec[which : which + 1, cols]
        if which < 2:
            value = jnp.maximum(value, 0.0)
        target[:, cols] = value.astype(bf16)

    def make_state(p):
        lanes = tile_at(p, LANES)
        k = rk[:, lanes].astype(f32) * (1.0 / HD)
        v = vv[:, lanes]
        kc, ks = (k * cosb[...]).astype(bf16), (k * sinb[...]).astype(bf16)
        tsend[p, 0] = squeeze_pair(mm_tn(kc, v) * diag).astype(bf16)
        tsend[p, 1] = squeeze_pair(mm_tn(ks, v) * diag).astype(bf16)
        zsend[p] = two_rows(
            jnp.sum(kc.astype(f32), axis=0, keepdims=True),
            jnp.sum(ks.astype(f32), axis=0, keepdims=True),
        )

    together = TILE // LANES

    def state_copy(j):
        where = pl.ds(j * together, together)
        return peer_copy(tsend.at[where], trecv.at[where], sems, (0, 24, 25)[j], peer)

    key_copy = peer_copy(zsend, zrecv, sems, 1, peer)
    fetch(0).wait()
    load(0).wait()
    load(1).wait()
    for index in range(3, len(loads)):
        load(index).start()
    for j in range(tiles):
        project(1, rk, j)
        project(2, vv, j)
        pl.loop(j * together, (j + 1) * together)(make_state)
        if j == 0:
            pl.semaphore_wait(barrier, len(partners))
        state_copy(j).start()
    key_copy.start()
    angle_products(angles, span, ctab)
    load(2).wait()
    pl.loop(0, tiles)(functools.partial(project, 0, rq))

    @pl.loop(0, pairs)
    def _(p):
        lanes = tile_at(p, LANES)
        q, k, v = rq[:, lanes], rk[:, lanes], vv[:, lanes]
        parts = []
        for mask, rest in ((first_low, second_low), (second_low, first_low)):
            prob = (mm_nt(q * mask, k) * ctab[...]).astype(bf16)
            parts.append(mm(prob, v * mask + rest))
        numer[:, lanes] = parts[0] * first + parts[1] * second
        denom[:, lanes] = pltpu.roll(parts[0] * second + parts[1] * first, HD, 1)

    for j in range(tiles):
        state_copy(j).wait()
    key_copy.wait()

    @pl.loop(0, pairs)
    def _(p):
        lanes = tile_at(p, LANES)
        q = rq[:, lanes].astype(f32)
        qc, qs = (q * cosb[...]).astype(bf16), (q * sinb[...]).astype(bf16)
        st[p] = (trecv[p].astype(f32) * late).astype(bf16)
        zblock = zrecv[p] * late
        zst[p] = zblock
        weighted = qc.astype(f32) * zblock[0:1, :] + qs.astype(f32) * zblock[1:2, :]
        num, den = numer[:, lanes], denom[:, lanes] + 1.0 + mm(weighted.astype(bf16), diag_low)
        for part, feat in ((0, qc), (1, qs)):
            num += mm(feat, spread_pair(st[p, part], diag).astype(bf16))
        reciprocal = 1.0 / den
        mix = num * reciprocal
        inv[:, lanes] = reciprocal
        mixf[:, lanes] = mix
        mixb[:, lanes] = mix.astype(bf16)

    load(3).wait()

    @pl.loop(0, tiles)
    def _(j):
        cols = tile_at(j, TILE)
        hid[:, cols] = (
            tok[:, cols].astype(f32) + mm(mixb[...], wa[pl.ds(3 * width, width), cols]) + vec[3:4, cols]
        )

    span_rows = rows // 2
    near = [pl.ds(k * span_rows, span_rows) for k in range(2)]
    away = [pl.ds(rows + k * span_rows, span_rows) for k in range(2)]
    blocks = span_rows // ROWBLOCK

    def norm_rows(i):
        at = tile_at(i, ROWBLOCK)
        normal, scale = layer_norm(hid[at, :])
        hidden = normal * vec[4:5, :] + vec[5:6, :]
        nrm[at, :] = normal
        scl[at, :] = jnp.broadcast_to(scale, (ROWBLOCK, LANES))
        hid[at, :] = hidden
        hbuf[at, :] = hidden.astype(bf16)

    def rows_copy(k):
        return peer_copy(hbuf.at[near[k]], hbuf.at[away[k]], sems, 12 + k, peer)

    def branch_copy(k):
        return peer_copy(bsend.at[near[k]], brecv.at[near[k]], sems, 14 + k, peer)

    def grad_copy(k):
        return peer_copy(dbuf.at[near[k]], dbuf.at[away[k]], sems, 16 + k, peer)

    def hidden_copy(k):
        return peer_copy(dhs.at[near[k]], dhr.at[near[k]], sems, 18 + k, peer)

    for k in range(2):
        pl.loop(k * blocks, (k + 1) * blocks)(norm_rows)
        rows_copy(k).start()
    for index in range(4, len(loads)):
        load(index).wait()
    fetch(len(small_loads) - 1).wait()

    def raise_rows(part):
        for piece in range(halves):

            @pl.loop(0, tiles)
            def _(j, piece=piece):
                cols, narrow = tile_at(piece * tiles + j, TILE), tile_at(j, TILE)
                weight = wff[pl.ds(units + piece * width, width), narrow]
                pre = mm(hbuf[part, :], weight) + vec[9 + piece : 10 + piece, narrow]
                cdf = 0.5 * (1.0 + lax.erf(pre * (1.0 / math.sqrt(2.0))))
                act[part, cols] = (pre * cdf).astype(bf16)
                slope[part, cols] = cdf + pre * jnp.exp(-0.5 * pre * pre) * (
                    1.0 / math.sqrt(2.0 * math.pi)
                )

    raise_rows(own)
    for k in range(2):
        rows_copy(k).wait()
        raise_rows(away[k])

        @pl.loop(0, tiles)
        def _(j, k=k):
            cols = tile_at(j, TILE)
            bsend[near[k], cols] = mm(act[away[k], :], wff[pl.ds(0, units), cols]).astype(bf16)

        branch_copy(k).start()

    @pl.loop(0, tiles)
    def _(j):
        cols = tile_at(j, TILE)
        hid[:, cols] += mm(act[own, :], wff[pl.ds(0, units), cols]) + vec[6:7, cols]

    def finish_rows(i):
        at = tile_at(i, ROWBLOCK)
        normal, scale = layer_norm(hid[at, :] + brecv[at, :].astype(f32))
        res[at, :] = (normal * vec[7:8, :] + vec[8:9, :]).astype(bf16)
        grad = og[at, :].astype(f32)
        inner = layer_norm_back(grad, vec[7:8, :], normal, scale)
        dho[at, :] = inner
        dbuf[at, :] = inner.astype(bf16)
        acc[0:8, :] += fold8(grad * normal)
        acc[8:16, :] += fold8(grad)
        acc[16:24, :] += fold8(inner)

    for k in range(2):
        branch_copy(k).wait()
        pl.loop(k * blocks, (k + 1) * blocks)(finish_rows)
        grad_copy(k).start()
    result_out = pltpu.make_async_copy(res, res_h, o_sem.at[0])
    result_out.start()
    for slot in range(3):
        add_small(3 + slot, jnp.sum(acc[8 * slot : 8 * slot + 8, :], axis=0, keepdims=True))

    def lower_rows(part):
        @pl.loop(0, units // TILE)
        def _(j):
            cols = tile_at(j, TILE)
            d_pre = mm_nt(dbuf[part, :], wff[cols, :]) * slope[part, cols]
            bup[:, cols] += fold8(d_pre)
            dpre[part, cols] = d_pre.astype(bf16)

    def lower_hidden(part, cols, j):
        total = 0.0
        for piece in range(halves):
            weight = wff[pl.ds(pl.multiple_of(units + piece * width + j * TILE, TILE), TILE), :]
            total += mm_nt(dpre[part, piece * width : (piece + 1) * width], weight)
        return total

    lower_rows(own)
    def send_hidden(k):
        @pl.loop(0, tiles)
        def _(j):
            cols = tile_at(j, TILE)
            dhs[near[k], cols] = lower_hidden(away[k], cols, j).astype(bf16)

        hidden_copy(k).start()

    grad_copy(0).wait()
    lower_rows(away[0])
    send_hidden(0)
    grad_copy(1).wait()
    lower_rows(away[1])

    def make_down(part):
        @pl.loop(part * tiles, (part + 1) * tiles)
        def _(j):
            cols = tile_at(j, TILE)
            gff[cols, :] = mm_tn(act[:, cols], dbuf[...]).astype(bf16)

    def make_up(part):
        @pl.loop(0, tiles)
        def _(j):
            gff[pl.ds(units + part * width, width), tile_at(j, TILE)] = mm_tn(
                hbuf[...], dpre[:, tile_at(part * tiles + j, TILE)]
            ).astype(bf16)

    def part_rows(which, size):
        return pl.ds(pl.multiple_of(which * size, size), size)

    def core_ff(part):
        start = pl.multiple_of((1 - core) * units + part * width, width)
        return peer_copy(
            gff.at[pl.ds(start, width), :],
            cr_ff.at[pl.ds(part * width, width), :],
            sems, (8, 22, 23)[part], sibling,
        )

    for part in range(halves):
        pl.when(core == 0)(functools.partial(make_up, part))
        pl.when(core == 1)(functools.partial(make_down, part))
        core_ff(part).start()
    send_hidden(1)
    for part in range(halves):
        pl.when(core == 0)(functools.partial(make_down, part))
        pl.when(core == 1)(functools.partial(make_up, part))

    band, per = width // 4, count // 4
    ff_streams, a_streams = [], []
    for kind, (cuts, group) in enumerate(((FF_CUTS, ff_streams), (A_CUTS, a_streams))):
        size = (quarter if kind else units) // count // 2
        for way in range(2):
            for cut in range(cuts):
                number = 2 * FF_CUTS * kind + way * cuts + cut
                piece = size // cuts
                group.append((number, kind, way, cut * piece, piece))
    slots, sums, outs = (rs_ff, rs_a), (gff, ga), (ff_o, a_o)
    ff_size, a_size = units // count // 2, quarter // count // 2
    mine, theirs = core * 2 + rank, core * 2 + 1 - rank

    def ff_rows(at, way, offset, length, base):
        start = base + (at % count) * 2 * ff_size + way * ff_size + offset
        return pl.ds(pl.multiple_of(start, 16), length)

    def a_rows(at, way, offset, length, owner):
        chunk = at % count
        start = (chunk // per) * width + owner * band + (chunk % per) * 2 * a_size
        return pl.ds(pl.multiple_of(start + way * a_size + offset, 16), length)

    def line_rows(at, way, offset, length):
        start = (at % count) * 2 * a_size + way * a_size + offset
        return pl.ds(pl.multiple_of(start, 16), length)

    def core_rows(at, way, offset, length):
        chunk = at % count
        start = (chunk // per) * 2 * band + rank * band + (chunk % per) * 2 * a_size
        return pl.ds(pl.multiple_of(start + way * a_size + offset, 16), length)

    def stream_rows(stream, at):
        _, kind, way, offset, length = stream
        if kind:
            return a_rows(at, way, offset, length, mine)
        return ff_rows(at, way, offset, length, core * units)

    def toward(way):
        return behind if way else ahead

    def turn(way):
        return -1 if way else 1

    def remote(source, target, send_sem, recv_sem, device):
        return pltpu.make_async_remote_copy(
            src_ref=source,
            dst_ref=target,
            send_sem=send_sem,
            recv_sem=recv_sem,
            device_id=device,
            device_id_type=MESH,
        )

    def spread_copy(stream, at, s):
        number, kind, way, offset, length = stream
        return remote(
            sums[kind].at[stream_rows(stream, at), :],
            slots[kind].at[s, way, pl.ds(offset, length), :],
            r_send.at[kind],
            r_recv.at[number, s],
            toward(way),
        )

    def gather_copy(stream, at, s):
        number, kind, way, _, _ = stream
        where = outs[kind].at[stream_rows(stream, at), :]
        return remote(where, where, g_send.at[kind], g_recv.at[number, s], toward(way))

    def across_copy(way, s, owner, first):
        at, skip = spot + 2 * count + turn(way) * (1 - s), 0 if first else RING_ROWS
        where = a_o.at[a_rows(at, way, skip, a_size - skip, owner), :]
        return remote(where, where, x_send.at[0], x_recv.at[way, s], peer)

    def round_copy(way, s):
        at = spot + 2 * count + turn(way) * (1 - s)
        where = a_o.at[a_rows(at, way, 0, RING_ROWS, theirs), :]
        return remote(where, where, x_send.at[3], t_recv.at[way, s], toward(way))

    def side_copy(way, s, owner, lane):
        at = spot + 2 * count + turn(way) * (1 - s)
        where = a_o.at[a_rows(at, way, 0, a_size, owner), :]
        return remote(where, where, x_send.at[1], s_recv.at[2 * lane + way, s], sibling)

    def fold_copy(way, s):
        at = spot + count - turn(way) * s
        return remote(
            px.at[line_rows(at, way, 0, a_size), :],
            xr.at[s, way],
            x_send.at[2],
            y_recv.at[way, s],
            peer,
        )

    def start_folds(s):
        for way in range(2):
            fold_copy(way, s).start()

    def own_part(stream, at, s):
        _, kind, way, offset, length = stream
        value = sums[kind][stream_rows(stream, at), :].astype(f32)
        if kind == 0:
            return value + cr_ff[ff_rows(at, way, offset, length, 0), :].astype(f32)
        if offset == 0:
            fold_copy(way, s).wait_recv()
        return (
            value
            + cr_a[core_rows(at, way, offset, length), :].astype(f32)
            + xr[s, way, pl.ds(offset, length), :].astype(f32)
        )

    def ring_first(streams):
        for stream in streams:
            at = spot + count
            sums[stream[1]][stream_rows(stream, at), :] = own_part(stream, at, 0).astype(bf16)
            spread_copy(stream, at, 0).start()

    def store_chunk(way, s, owner):
        rows_at = a_rows(spot + 2 * count + turn(way) * (1 - s), way, 0, a_size, owner)
        pltpu.make_async_copy(a_o.at[rows_at, :], a_h.at[rows_at, :], o_sem.at[4]).start()

    def pass_on(stream, s, first=False):
        _, kind, way, offset, length = stream
        if kind and offset + length == a_size:
            across_copy(way, s, mine, first).start()
            side_copy(way, s, mine, 0).start()
            store_chunk(way, s, mine)

    def ring_spread(streams, s, last=False):
        for stream in streams:
            _, kind, way, offset, length = stream
            at = spot + count - turn(way) * (s + 1)
            target = stream_rows(stream, at)
            part = own_part(stream, at, s + 1)
            spread_copy(stream, at, s).wait_recv()
            arrived = slots[kind][s, way, pl.ds(offset, length), :].astype(f32)
            total = (part + arrived).astype(bf16)
            if last:
                outs[kind][target, :] = total
                gather_copy(stream, at, 0).start()
                pass_on(stream, 0, True)
            else:
                sums[kind][target, :] = total
                spread_copy(stream, at, s + 1).start()

    def ring_gather(streams, s, last=False):
        for stream in streams:
            at = spot + 2 * count - turn(stream[2]) * s
            gather_copy(stream, at, s).wait_recv()
            if not last:
                gather_copy(stream, at, s + 1).start()
        for stream in streams:
            pass_on(stream, s + 1)

    def cross_over(s, first=False, last=False):
        for way in range(2):
            across_copy(way, s, theirs, first).wait_recv()
            if not first:
                round_copy(way, s - 1).wait_recv()
            if not last:
                round_copy(way, s).start()
        for way in range(2):
            side_copy(way, s, theirs, 1).start()
            store_chunk(way, s, theirs)

    def side_done(lane, s):
        owner = (1 - core) * 2 + (1 - rank if lane else rank)
        for way in range(2):
            side_copy(way, s, owner, lane).wait_recv()
            store_chunk(way, s, owner)

    def ff_part(q):
        s, cut = q // FF_CUTS, q % FF_CUTS
        piece = ff_size // FF_CUTS
        ring_spread([(way * FF_CUTS + cut, 0, way, cut * piece, piece) for way in range(2)], s)

    def small_copy(index):
        return peer_copy(smalls.at[index], small_r.at[index], (m_send, m_recv), index, swaps[index])

    def swap_small(index):
        small_copy(index).wait()
        smalls[index + 1] = smalls[index] + small_r[index]
        if index + 1 < len(swaps):
            small_copy(index + 1).start()

    for piece in range(halves):
        line = jnp.sum(bup[:, piece * width : (piece + 1) * width], axis=0, keepdims=True)
        add_small(9 + piece, line * early)
        add_small(9 + halves + piece, line * late)

    @pl.loop(0, tiles)
    def _(j):
        cols = tile_at(j, TILE)
        dho[:, cols] += lower_hidden(own, cols, j)

    acc[...] = jnp.zeros_like(acc)
    for part in range(halves):
        core_ff(part).wait()
    ring_first(ff_streams)
    hidden_copy(0).wait()
    hidden_copy(1).wait()

    @pl.loop(0, rows // ROWBLOCK)
    def _(i):
        at = tile_at(i, ROWBLOCK)
        grad = dho[at, :] + dhr[at, :].astype(f32)
        normal = nrm[at, :]
        inner = layer_norm_back(grad, vec[4:5, :], normal, scl[at, 0:1])
        dres[at, :] = inner
        dlow[at, :] = inner.astype(bf16)
        acc[0:8, :] += fold8(grad * normal)
        acc[8:16, :] += fold8(grad)
        acc[16:24, :] += fold8(inner)

    for slot in range(3):
        add_small(slot, jnp.sum(acc[8 * slot : 8 * slot + 8, :], axis=0, keepdims=True))

    ff_part(0)

    @pl.loop(0, tiles)
    def _(j):
        cols = tile_at(j, TILE)
        d_mixed = mm_nt(dlow[...], wa[tile_at(3 * tiles + j, TILE), :]).astype(bf16).astype(f32)
        d_numer = (d_mixed * inv[:, cols]).astype(bf16)
        dn[:, cols] = d_numer
        xs[:, cols] = (d_numer.astype(f32) * mixf[:, cols]).astype(bf16)

    ff_part(1)


    @pl.loop(0, pairs)
    def _(p):
        lanes = tile_at(p, LANES)
        q = rq[:, lanes].astype(f32)
        qc, qs = (q * cosb[...]).astype(bf16), (q * sinb[...]).astype(bf16)
        d_numer = dn[:, lanes]
        dsend[p, 0] = squeeze_pair(mm_tn(qc, d_numer) * diag).astype(bf16)
        dsend[p, 1] = squeeze_pair(mm_tn(qs, d_numer) * diag).astype(bf16)
        across = mm(xs[:, lanes], diag_low)
        dzs[p] = -two_rows(
            jnp.sum(qc.astype(f32) * across, axis=0, keepdims=True),
            jnp.sum(qs.astype(f32) * across, axis=0, keepdims=True),
        )

    turn_copy = peer_copy(dsend, drecv, sems, 6, peer)
    turn_keys = peer_copy(dzs, dzr, sems, 7, peer)
    turn_copy.start()
    turn_keys.start()
    ff_part(2)

    @pl.loop(0, tiles)
    def _(j):
        cols = tile_at(j, TILE)
        ga[tile_at(3 * tiles + j, TILE), :] = mm_tn(mixb[:, cols], dlow[...]).astype(bf16)

    def core_a(m):
        there = pl.ds(pl.multiple_of(m * width + (1 - core) * 2 * band, 2 * band), 2 * band)
        here = pl.ds(m * 2 * band, 2 * band)
        return peer_copy(ga.at[there, :], cr_a.at[here, :], sems, (9, 11, 20, 21)[m], sibling)

    def fill_px(m):
        core_a(m).wait()
        there = pl.ds(pl.multiple_of(m * width + theirs * band, band), band)
        here = pl.ds(pl.multiple_of(m * 2 * band + (1 - rank) * band, band), band)
        px[m * band : (m + 1) * band, :] = (
            ga[there, :].astype(f32) + cr_a[here, :].astype(f32)
        ).astype(bf16)

    core_a(3).start()
    ff_part(3)

    def inside(p):
        lanes = tile_at(p, LANES)
        q, k, v = rq[:, lanes], rk[:, lanes], vv[:, lanes]
        d_numer = dn[:, lanes]
        turned = (-pltpu.roll(xs[:, lanes].astype(f32), HD, 1)).astype(bf16)
        sum_q = sum_k = sum_v = 0.0
        for mask, rest in ((first_low, second_low), (second_low, first_low)):
            q_head, k_head, d_head = q * mask, k * mask, d_numer * mask
            table = ctab[...]
            prob = (mm_nt(q_head, k) * table).astype(bf16)
            d_prob = mm_nt(d_head + turned * rest, v * mask + rest)
            d_score = (d_prob * table).astype(bf16)
            sum_v += mm_tn(prob, d_head)
            sum_q += mm(d_score, k_head)
            sum_k += mm_tn(d_score, q_head)
        dq[:, lanes] = sum_q
        dk[:, lanes] = sum_k
        dv[:, lanes] = sum_v

    @pl.loop(0, pairs)
    def _(p):
        inside(p)
        ff_part(4 + p)

    turn_copy.wait()
    turn_keys.wait()

    @pl.loop(0, pairs)
    def _(p):
        lanes = tile_at(p, LANES)
        q, v = rq[:, lanes].astype(f32), vv[:, lanes]
        k = rk[:, lanes].astype(f32)
        d_numer, x = dn[:, lanes], xs[:, lanes]
        sum_q, sum_k, sum_v = dq[:, lanes], dk[:, lanes], dv[:, lanes]
        zblock, dzblock = zst[p], dzr[p] * early
        along = mm(x, diag_low)
        for part, wave in ((0, cosb[...]), (1, sinb[...])):
            state = spread_pair(st[p, part], diag).astype(bf16)
            sum_q += wave * (mm_nt(d_numer, state) - along * zblock[part : part + 1, :])
            d_state = (spread_pair(drecv[p, part], diag) * early).astype(bf16)
            sum_k += wave * (mm_nt(v, d_state) + dzblock[part : part + 1, :]) * (1.0 / HD)
            sum_v += mm((k * wave * (1.0 / HD)).astype(bf16), d_state)
        sum_q = jnp.where(q > 0, sum_q, 0.0)
        sum_k = jnp.where(k > 0, sum_k, 0.0)
        dql[:, lanes] = sum_q.astype(bf16)
        dkl[:, lanes] = sum_k.astype(bf16)
        dvl[:, lanes] = sum_v.astype(bf16)
        for slot, value in ((6, sum_q), (7, sum_k), (8, sum_v)):
            smalls[0, slot : slot + 1, lanes] = jnp.sum(value, axis=0, keepdims=True)

    small_copy(0).start()
    ff_part(10)

    def make_grad(which, source):
        @pl.loop(0, tiles)
        def _(j):
            ga[tile_at(which * tiles + j, TILE), :] = mm_tn(
                tok[:, tile_at(j, TILE)], source[...]
            ).astype(bf16)

        core_a(which).start()

    make_grad(2, dvl)
    ff_part(11)
    make_grad(0, dql)
    ff_part(12)
    make_grad(1, dkl)
    ff_part(13)
    for m in (3, 2, 0, 1):
        fill_px(m)
    start_folds(0)
    ff_part(14)

    @pl.loop(0, tiles)
    def _(j):
        cols = tile_at(j, TILE)
        dres[:, cols] += (
            mm_nt(dql[...], wa[cols, :])
            + mm_nt(dkl[...], wa[tile_at(tiles + j, TILE), :])
            + mm_nt(dvl[...], wa[tile_at(2 * tiles + j, TILE), :])
        )

    token_out = pltpu.make_async_copy(dres, dtok_h, o_sem.at[1])
    token_out.start()
    start_folds(1)
    ring_spread(ff_streams, 5)
    ring_first(a_streams)
    swap_small(0)

    def spread_gather(s):
        for cut in range(FF_CUTS):
            ring_spread(a_streams[cut::A_CUTS], s)
            ring_gather(ff_streams[cut::FF_CUTS], s - 1)

    start_folds(2)
    ring_spread(a_streams, 0)
    ring_spread(ff_streams, 6, True)
    swap_small(1)

    def spread_fold(s):
        start_folds(s + 2)
        spread_gather(s)

    pl.loop(1, 3)(spread_fold)
    swap_small(2)
    pl.loop(3, 6)(spread_fold)
    swap_small(3)
    ring_spread(a_streams, 6, True)
    ring_gather(ff_streams, 5)
    ring_gather(a_streams, 0)
    ring_gather(ff_streams, 6, True)
    own_ff = part_rows(core, units)
    back_ff = peer_copy(ff_o.at[own_ff, :], ff_o.at[own_ff, :], sems, 10, sibling)
    back_ff.start()
    near_ff = out_copy(ff_o, ff_h, own_ff, 2)
    near_ff.start()
    cross_over(0, first=True)
    side_done(0, 0)
    swap_small(4)
    small_out = pltpu.make_async_copy(smalls.at[len(swaps)], small_h, o_sem.at[6])
    small_out.start()

    def gather_one(s):
        ring_gather(a_streams, s)
        cross_over(s)
        side_done(0, s)
        side_done(1, s - 1)

    gather_one(1)
    back_ff.wait()
    far_ff = out_copy(ff_o, ff_h, part_rows(1 - core, units), 3)
    far_ff.start()
    pl.loop(2, 6)(gather_one)
    ring_gather(a_streams, 6, True)
    cross_over(6)
    side_done(0, 6)
    side_done(1, 5)
    cross_over(7, last=True)
    side_done(0, 7)
    side_done(1, 6)

    def drain(kind, source, total, sem):
        where = source.at[pl.ds(0, total), :]
        remote(where, where, sem, x_recv.at[0, 0], peer).wait_send()

    for kind, size in ((0, ff_size), (1, a_size)):
        drain(kind, sums[kind], 2 * (count - 1) * size, r_send.at[kind])
        drain(kind, outs[kind], 2 * (count - 1) * size, g_send.at[kind])
    drain(1, px, 2 * count * a_size, x_send.at[2])

    drain(1, a_o, 2 * count * a_size - 2 * (count - 1) * RING_ROWS, x_send.at[0])
    drain(1, a_o, 2 * (count - 1) * RING_ROWS, x_send.at[3])
    side_done(1, 7)
    drain(1, a_o, 4 * count * a_size, x_send.at[1])
    whole_a = pltpu.make_async_copy(a_o, a_h, o_sem.at[4])
    for copy in (result_out, token_out, near_ff, far_ff, small_out, whole_a):
        copy.wait()


def finish_kernel(halves, *refs):
    g_out, up, down, small, res, dtok = refs[:4], refs[4 : 4 + halves], *refs[4 + halves : 8 + halves]
    out = refs[8 + halves :]
    late = lax.axis_index("tensor") > 0
    for source, where in zip(g_out, (2, 4, 6, 8)):
        out[where][...] = source[...].astype(f32)
    width = res.shape[1]
    for piece in range(halves):
        out[12][:, piece * width : (piece + 1) * width] = up[piece][...].astype(f32)
    out[14][...] = down[...].astype(f32)

    @pl.when(pl.program_id(0) == 0)
    def _():
        out[0][...] = res[...]
        out[1][...] = dtok[...]
        for where, row in ((3, 6), (5, 7), (7, 8), (9, 2), (10, 0), (11, 1), (15, 5), (16, 3), (17, 4)):
            out[where][...] = small[row : row + 1, :].reshape(width)
        for piece in range(halves):
            line = jnp.where(
                late,
                small[9 + halves + piece : 10 + halves + piece, :],
                small[9 + piece : 10 + piece, :],
            )
            out[13][pl.ds(piece * width, width)] = line.reshape(width)


def finish(rows, width, units, res, dtok, ff, a, small):
    halves, steps = units // width, width // FINISH
    low = (FINISH, width)
    down_rows = units // steps

    def whole(shape):
        return pl.BlockSpec(shape, lambda i: (0,) * len(shape))

    def at_block(shape, start):
        return pl.BlockSpec(shape, lambda i: (start + i, 0))

    in_specs = [at_block(low, which * steps) for which in range(4)]
    in_specs += [at_block(low, units // FINISH + piece * steps) for piece in range(halves)]
    in_specs += [at_block((down_rows, width), 0), whole(small.shape), whole(res.shape), whole(dtok.shape)]
    matrix, line = (width, width), (width,)
    shapes = [
        (res.shape, bf16), (dtok.shape, f32), (matrix, f32), (line, f32), (matrix, f32), (line, f32),
        (matrix, f32), (line, f32), (matrix, f32), (line, f32), (line, f32), (line, f32),
        ((width, units), f32), ((units,), f32), ((units, width), f32), (line, f32), (line, f32), (line, f32),
    ]
    special = {
        2: at_block(low, 0), 4: at_block(low, 0), 6: at_block(low, 0), 8: at_block(low, 0),
        12: at_block((FINISH, units), 0), 14: at_block((down_rows, width), 0),
    }
    return pl.pallas_call(
        functools.partial(finish_kernel, halves),
        grid=(steps,),
        out_shape=shaped(*shapes),
        in_specs=in_specs,
        out_specs=tuple(special.get(i, whole(shape)) for i, (shape, _) in enumerate(shapes)),
        compiler_params=pltpu.CompilerParams(vmem_limit_bytes=62 << 20),
        name="finish",
    )(*([a] * 4), *([ff] * (halves + 1)), small, res, dtok)


def shaped(*items):
    return tuple(jax.ShapeDtypeStruct(shape, kind) for shape, kind in items)


def pair_device(
    tokens,
    positions,
    span_sizes,
    w_query,
    b_query,
    w_key,
    b_key,
    w_value,
    b_value,
    w_out,
    b_out,
    norm1_gain,
    norm1_bias,
    w_up,
    b_up,
    w_down,
    b_down,
    norm2_gain,
    norm2_bias,
    out_grad,
):
    rows, width = tokens.shape
    units = w_up.shape[1]
    pairs = width // LANES
    halves = units // width
    count = lax.axis_size("dp") // 2
    swaps = 2 + count.bit_length() - 1
    streams = 2 * (FF_CUTS + A_CUTS)
    ff_part, a_part = units // count // 2, width // count // 2
    lines = 9 + 2 * halves
    lines += -lines % 8

    def low(*shape):
        return pltpu.VMEM(shape, bf16)

    def wide(*shape):
        return pltpu.VMEM(shape, f32)

    def sem(*shape):
        return pltpu.SemaphoreType.DMA(shape)

    state, zrows = (pairs, 2, HD, LANES), (pairs, 8, LANES)
    own, pair = (rows, width), (2 * rows, width)
    scratch = dict(
        tok=low(*own), places=pltpu.VMEM(positions.shape, jnp.int32), span=pltpu.SMEM((1, 1), jnp.int32),
        og=low(*own), **{name: low(width) for name in LINES}, bup_line=low(units),
        wa=low(4 * width, width), wff=low(2 * units, width), vec=wide(9 + halves + -(9 + halves) % 8, width),
        hbuf=low(*pair), act=low(2 * rows, units), slope=wide(2 * rows, units), dbuf=low(*pair),
        dpre=low(2 * rows, units), hid=wide(*own), numer=wide(*own), denom=wide(*own),
        tsend=low(*state), trecv=low(*state), zsend=wide(*zrows), zrecv=wide(*zrows),
        bsend=low(*own), brecv=low(*own), res=low(*own), gff=low(2 * units, width),
        dhs=low(*own), dhr=low(*own), dho=wide(*own), mixb=low(*own), mixf=wide(*own), inv=wide(*own),
        rq=low(*own), rk=low(*own), vv=low(*own), nrm=wide(*own), scl=wide(rows, LANES),
        st=low(*state), zst=wide(*zrows), dres=wide(*own), dlow=low(*own), dn=low(*own), xs=low(*own),
        dsend=low(*state), drecv=low(*state), dzs=wide(*zrows), dzr=wide(*zrows),
        dql=low(*own), dkl=low(*own), dvl=low(*own),
        ctab=wide(rows, rows), cosb=wide(rows, LANES), sinb=wide(rows, LANES),
        acc=wide(24, width), bup=wide(8, units),
        cr_ff=low(units, width), cr_a=low(2 * width, width), px=low(width, width),
        xr=low(count, 2, a_part, width), rs_ff=low(count - 1, 2, ff_part, width),
        rs_a=low(count - 1, 2, a_part, width), ff_o=low(2 * units, width), a_o=low(4 * width, width),
        smalls=wide(swaps + 1, lines, width), small_r=wide(swaps, lines, width),
        send=sem(26), recv=sem(26), r_send=sem(2), r_recv=sem(streams, count - 1),
        g_send=sem(2), g_recv=sem(streams, count - 1), x_send=sem(4), x_recv=sem(2, count),
        t_recv=sem(2, count - 1),
        s_recv=sem(4, count), y_recv=sem(2, count),
        m_send=sem(swaps), m_recv=sem(swaps), w_sem=sem(5 + halves), o_sem=sem(7), l_sem=sem(14),
    )
    anywhere = pl.BlockSpec(memory_space=pl.ANY)
    outs = shaped(
        (own, bf16), (own, f32), ((2 * units, width), bf16), ((4 * width, width), bf16),
        ((lines, width), f32),
    )
    res, dtok, ff, a, small = pl.pallas_call(
        functools.partial(block_kernel, count),
        out_shape=outs,
        in_specs=[anywhere] * 20,
        out_specs=tuple([anywhere] * len(outs)),
        scratch_shapes=list(scratch.values()),
        compiler_params=pltpu.CompilerParams(
            collective_id=0, has_side_effects=True, vmem_limit_bytes=62 << 20
        ),
        name="block",
    )(
        tokens, positions, span_sizes.reshape(1, 1), b_query, b_key, b_value, b_out, norm1_gain,
        norm1_bias, b_down, norm2_gain, norm2_bias, b_up, out_grad,
        w_query, w_key, w_value, w_out, w_up, w_down,
    )
    return finish(rows, width, units, res, dtok, ff, a, small)


def pick(mesh):
    def per_device(*args):
        tokens, span_sizes, w_up = args[0], args[2], args[13]
        rows, width = tokens.shape
        units = w_up.shape[1]
        fits = (
            mesh.shape["tensor"] == 2
            and mesh.shape["dp"] == 16
            and span_sizes.shape[0] == 1
            and rows % TILE == 0
            and width == HEADS * HD
            and width % TILE == 0
            and units == 2 * width
        )
        return pair_device(*args) if fits else general_device(*args)

    return per_device


def solution(mesh):
    return jax.shard_map(
        pick(mesh),
        mesh=mesh,
        in_specs=(
            P(("dp", "tensor"), None),
            P("dp"),
            P("dp"),
            P(),
            P(),
            P(),
            P(),
            P(),
            P(),
            P(),
            P(),
            P(),
            P(),
            P(None, "tensor"),
            P("tensor"),
            P("tensor", None),
            P(),
            P(),
            P(),
            P(("dp", "tensor"), None),
        ),
        out_specs=(
            P(("dp", "tensor"), None),
            P(("dp", "tensor"), None),
            P(),
            P(),
            P(),
            P(),
            P(),
            P(),
            P(),
            P(),
            P(),
            P(),
            P(None, "tensor"),
            P("tensor"),
            P("tensor", None),
            P(),
            P(),
            P(),
        ),
        check_vma=False,
    )
```
